32 devices in a mesh: dp: 8 (over y, x, core), mp: 4 (over z).
Axes of the slice: x: 2, y: 2, z: 4, core: 2. Of those that a mesh axis runs over, the one named last changes fastest.
Arguments:
- frames_long: bfloat16 [8, 1024, 768], P('dp', 'mp'), may hold values from -6 to 6
- frames_short: bfloat16 [16, 512, 768], P('dp', 'mp'), may hold values from -6 to 6
- length_long: int32 [8], P('dp'), may hold values from 513 to 1024, as said below
- length_short: int32 [16], P('dp'), may hold values from 257 to 512, as said below
- input_proj: bfloat16 [3, 768, 768], P(None, 'dp', 'mp'), may hold values from -0.21875 to 0.21875
- output_proj: bfloat16 [768, 768], P('mp', 'dp'), may hold values from -0.875 to 0.875
- expand_weight: bfloat16 [768, 3072], P('dp', 'mp'), may hold values from -0.21875 to 0.21875
- shrink_weight: bfloat16 [3072, 768], P('mp', 'dp'), may hold values from -0.109375 to 0.109375
- head_bias: bfloat16 [2, 4, 192], P(None, 'mp', 'dp'), may hold values from -3 to 3
- expand_bias: bfloat16 [4, 768], P('mp', 'dp'), may hold values from -3 to 3
- row_params: float32 [6, 768], P(None, ('dp', 'mp')), may hold values from 0.25 to 1.75
- cotangent_long: bfloat16 [8, 1024, 768], P('dp', 'mp'), may hold values from -6 to 6
- cotangent_short: bfloat16 [16, 512, 768], P('dp', 'mp'), may hold values from -6 to 6
Outputs:
- result_long: bfloat16 [8, 1024, 768], P('dp', 'mp')
- result_short: bfloat16 [16, 512, 768], P('dp', 'mp')
- frames_grad_long: float32 [8, 1024, 768], P('dp', 'mp')
- frames_grad_short: float32 [16, 512, 768], P('dp', 'mp')
- input_proj_grad: float32 [3, 768, 768], P(None, 'dp', 'mp')
- output_proj_grad: float32 [768, 768], P('mp', 'dp')
- expand_grad: float32 [768, 3072], P('dp', 'mp')
- shrink_grad: float32 [3072, 768], P('mp', 'dp')
- head_bias_grad: float32 [2, 4, 192], P(None, 'mp', 'dp')
- expand_bias_grad: float32 [4, 768], P('mp', 'dp')
- row_params_grad: float32 [6, 768], P(None, ('dp', 'mp'))
The draws below stay inside these ranges and needn't reach their ends.
Inputs may be any that keep to these rules, and one draw needn't show every extreme that they name: `length_long`: lengths of the long bucket; some clip has exactly 1024. `length_short`: lengths of the short bucket; some clip has exactly 512.
All inputs are finite; a program needn't handle non-finite values.
Results may differ from the reference program's by a relative error of at most 0.02.
Values may be sent and summed in bfloat16 or wider, within the bound.
No kernel may reach another device: no remote copies, remote signals or barrier semaphores. Data moves between devices by JAX's collectives and lax.ppermute only.
A program may use at most 128 MiB of HBM per device.

```python
import jax
import jax.numpy as jnp
from jax import lax

D = 768
FF = 3072
HEAD = 64
LL = 1024
LS = 512
RL_DEV = 1
RS_DEV = 2
ROWS_L = 8
ROWS_S = 16
N_MP = 4


def draw_length_long(key, part):
    first_key, second_key = jax.random.split(key)
    drawn = jax.random.randint(first_key, (ROWS_L,), LL // 2 + 1, LL + 1)
    full_at = jax.random.randint(second_key, (), 0, ROWS_L)
    return jnp.where(jnp.arange(ROWS_L) == full_at, LL, drawn).astype(jnp.int32)


def draw_length_short(key, part):
    first_key, second_key = jax.random.split(key)
    drawn = jax.random.randint(first_key, (ROWS_S,), LS // 2 + 1, LS + 1)
    full_at = jax.random.randint(second_key, (), 0, ROWS_S)
    return jnp.where(jnp.arange(ROWS_S) == full_at, LS, drawn).astype(jnp.int32)


def spiked(array, stream_key, source, target, shards_of, factor):
    def block_of(dim):
        return (jnp.arange(array.shape[dim]) // (array.shape[dim] // shards_of)).reshape((-1,) + (1,) * (array.ndim - 1 - dim))

    first = jax.random.permutation(stream_key, shards_of)[block_of(target)]
    other_side = (block_of(target) + shards_of // 2) % shards_of
    return jnp.where((block_of(source) == first) | (block_of(source) == other_side), factor * array, array)


def shard_levels(stream_key, shape, pieces, smallest, largest):
    gain = 1.0
    for dim, parts in pieces:
        steps = jax.random.uniform(jax.random.fold_in(jax.random.fold_in(stream_key, 6), dim), (parts,), jnp.float32, smallest / len(pieces), largest / len(pieces))
        gain = gain * jnp.repeat(jnp.exp(steps), shape[dim] // parts).reshape((-1,) + (1,) * (len(shape) - 1 - dim))
    return gain


def noise(own_key, extent, width, bound, shards=(), kind=jnp.bfloat16):
    loudness = shard_levels(own_key, extent, shards, -0.22, 0.18) if shards else 1.0
    result = jax.random.normal(own_key, extent, jnp.float32) * width * loudness
    return jnp.minimum(jnp.maximum(result, -bound), bound).astype(kind)


def gaussian_with(rng, shape, width, limit, cuts, heavy, held_as=jnp.bfloat16):
    result = width * jax.random.normal(rng, shape, jnp.float32)
    if cuts:
        result = result * shard_levels(rng, shape, cuts, -0.22, 0.18)
    return jnp.clip(spiked(result, jax.random.fold_in(rng, 3), *heavy), -limit, limit).astype(held_as)


def setup_inputs(seed: int = 0) -> dict:
    seeds = jax.random.split(jax.random.key(seed), 14)
    return {
        "frames_long": noise(seeds[0], (ROWS_L, LL, D), 1.0, 6.0, ((0, 8), (1, 4))),
        "frames_short": noise(seeds[1], (ROWS_S, LS, D), 1.0, 6.0, ((0, 8), (1, 4))),
        "length_long": draw_length_long(jax.random.fold_in(seeds[13], 71), 0),
        "length_short": draw_length_short(jax.random.fold_in(seeds[13], 71), 0),
        "input_proj": noise(seeds[4], (3, D, D), D ** -0.5, 0.21875, ((1, 8), (2, 4))),
        "output_proj": noise(seeds[5], (D, D), (D // 16) ** -0.5, 0.875, ((0, 4), (1, 8))),
        "expand_weight": noise(seeds[6], (D, FF), D ** -0.5, 0.21875, ((0, 8), (1, 4))),
        "shrink_weight": noise(seeds[7], (FF, D), FF ** -0.5, 0.109375, ((0, 4), (1, 8))),
        "head_bias": noise(seeds[8], (2, N_MP, D // N_MP), 0.5, 3.0, ((1, 4), (2, 8))),
        "expand_bias": noise(seeds[9], (N_MP, FF // N_MP), 0.5, 3.0, ((0, 4), (1, 8))),
        "row_params": jnp.clip(1.0 + 0.15 * jax.random.normal(seeds[10], (6, D), jnp.float32), 0.25, 1.75),
        "cotangent_long": gaussian_with(seeds[11], (ROWS_L, LL, D), 1.0, 6.0, ((0, 8), (1, 4)), (0, 2, 8, 2.0)),
        "cotangent_short": gaussian_with(seeds[12], (ROWS_S, LS, D), 1.0, 6.0, ((0, 8), (1, 4)), (0, 2, 8, 2.0)),
    }


EPS = 1e-05
PRECISE = lax.Precision.HIGHEST
NEG_FILL = -1e+30

@jax.custom_vjp
def low(v):
    return lax.optimization_barrier(v.astype(jnp.bfloat16)).astype(jnp.float32)

@jax.custom_vjp
def low_back(v):
    return v

def low_keep(v):
    return (low(v), None)

def low_pass(kept, grad):
    return (grad,)

def back_keep(v):
    return (v, None)

def back_low(kept, grad):
    return (low(grad),)
low.defvjp(low_keep, low_pass)
low_back.defvjp(back_keep, back_low)

def matmul_high(left, right):
    return jnp.matmul(left, right, precision=PRECISE)

def norm_rows(values, gain_row, shift_row):
    center = values - lax.optimization_barrier(jnp.mean(values, axis=-1, keepdims=True))
    inv_dev = lax.rsqrt(lax.optimization_barrier(jnp.mean(center * center, axis=-1, keepdims=True)) + EPS)
    return center * inv_dev * gain_row + shift_row

def block_rows(params, frames, lengths):
    input_proj, output_proj, expand_weight, shrink_weight, head_bias, expand_bias, row_params = params
    row_count, seq_len, width_model = frames.shape
    local_width = width_model // N_MP
    local_units = FF // N_MP
    head_local = local_width // HEAD
    key_mask = jnp.arange(seq_len)[None, :] < lengths[:, None]
    heads_shape = (row_count, seq_len, head_local, HEAD)
    attention = jnp.zeros(frames.shape, jnp.float32)
    for group_index in range(N_MP):
        first_col = group_index * local_width
        last_col = first_col + local_width
        frames_in = low_back(frames)
        queries = low(low_back(matmul_high(frames_in, input_proj[0][:, first_col:last_col]) + head_bias[0, group_index]))
        key_rows = low(low_back(matmul_high(frames_in, input_proj[1][:, first_col:last_col])))
        value_rows = low(low_back(matmul_high(frames_in, input_proj[2][:, first_col:last_col]) + head_bias[1, group_index]))
        scores = jnp.einsum('rqhd,rkhd->rhqk', queries.reshape(heads_shape), key_rows.reshape(heads_shape), precision=PRECISE) * HEAD ** (-0.5)
        scores = jnp.where(key_mask[:, None, None, :], low_back(scores), NEG_FILL)
        soft_rows = jax.nn.softmax(scores, axis=-1)
        mixed_rows = jnp.einsum('rhqk,rkhd->rqhd', low(soft_rows), value_rows.reshape(heads_shape), precision=PRECISE)
        mixed_rows = low(low_back(mixed_rows.reshape(row_count, seq_len, local_width)))
        attention = attention + low(matmul_high(mixed_rows, output_proj[first_col:last_col, :]))
    attention = low_back(attention)
    normed_h = norm_rows(frames + attention + row_params[0], row_params[1], row_params[2])
    normed_low = low(normed_h)
    feed_out = jnp.zeros(frames.shape, jnp.float32)
    for group_index in range(N_MP):
        first_unit = group_index * local_units
        last_unit = first_unit + local_units
        feed_in = low_back(normed_low)
        up_pre = low_back(matmul_high(feed_in, expand_weight[:, first_unit:last_unit]) + expand_bias[group_index])
        activated = low(jax.nn.gelu(up_pre, approximate=False))
        feed_out = feed_out + low(matmul_high(activated, shrink_weight[first_unit:last_unit, :]))
    feed_out = low_back(feed_out)
    return norm_rows(normed_h + feed_out + row_params[3], row_params[4], row_params[5])

def run_bucket(params, frames, lengths, per_step):
    row_total, seq_len, width_model = frames.shape
    batches = frames.reshape(row_total // per_step, per_step, seq_len, width_model)
    length_batches = lengths.reshape(row_total // per_step, per_step)

    def one_batch(batch_pair):
        return block_rows(params, batch_pair[0], batch_pair[1])
    step_fn = jax.checkpoint(one_batch)
    return lax.map(step_fn, (batches, length_batches)).reshape(frames.shape)

def reference(frames_long, frames_short, length_long, length_short, input_proj, output_proj, expand_weight, shrink_weight, head_bias, expand_bias, row_params, cotangent_long, cotangent_short):
    params = tuple((array_in.astype(jnp.float32) for array_in in (input_proj, output_proj, expand_weight, shrink_weight, head_bias, expand_bias, row_params)))

    def forward(params_in, long_in, short_in):
        return (run_bucket(params_in, long_in, length_long, RL_DEV), run_bucket(params_in, short_in, length_short, RS_DEV))
    outputs, pullback = jax.vjp(forward, params, frames_long.astype(jnp.float32), frames_short.astype(jnp.float32))
    param_grads, grad_long, grad_short = pullback((cotangent_long.astype(jnp.float32), cotangent_short.astype(jnp.float32)))
    return (outputs[0].astype(jnp.bfloat16), outputs[1].astype(jnp.bfloat16), grad_long, grad_short, param_grads[0], param_grads[1], param_grads[2], param_grads[3], param_grads[4], param_grads[5], param_grads[6])
```

```python
import functools

import jax
import jax.numpy as jnp
from jax import lax
from jax.experimental import pallas as pl
from jax.experimental.pallas import tpu as pltpu
from jax.sharding import PartitionSpec as P

HEAD = 64
EPS = 1e-05
NEG_FILL = -1e30
SCALE = HEAD ** (-0.5)
N_MP = 4
LANES = 128
Q_TILE = 256
F32 = jnp.float32
BF16 = jnp.bfloat16
NT = (((1,), (1,)), ((), ()))
NN = (((1,), (0,)), ((), ()))
TN = (((0,), (0,)), ((), ()))


def dot(left, right, dims):
    return lax.dot_general(left, right, dims, preferred_element_type=F32)


def mp_swap(value, step):
    return lax.ppermute(value, "mp", [(i, i ^ step) for i in range(N_MP)])


def dp_swap(value, target):
    size = lax.axis_size("dp")
    return lax.ppermute(value, "dp", [(i, target(i)) for i in range(size)])


def core_swap(value):
    return dp_swap(value, lambda i: i ^ 1)


def to_clips(long_rows, short_rows, core, depth):
    block = short_rows.shape[1]
    keep = lax.dynamic_slice_in_dim(long_rows, core * block, block, 0)
    away = lax.dynamic_slice_in_dim(long_rows, (1 - core) * block, block, 0)
    back = core_swap(away)
    first = jnp.where(core == 0, keep, back)
    second = jnp.where(core == 0, back, keep)
    blocks = jnp.stack([first, second, short_rows[0], short_rows[1]])
    parts = []
    for step in range(N_MP):
        piece = lax.dynamic_index_in_dim(blocks, depth ^ step, 0, keepdims=False)
        parts.append(piece if step == 0 else mp_swap(piece, step))
    return jnp.concatenate(parts, axis=0)


def from_clips(rows, core, depth):
    block = rows.shape[0] // N_MP
    parts = []
    for step in range(N_MP):
        piece = rows[step * block : (step + 1) * block]
        parts.append(piece if step == 0 else mp_swap(piece, step))
    blocks = jnp.stack(parts)
    first, second, short_a, short_b = (
        lax.dynamic_index_in_dim(blocks, depth ^ i, 0, keepdims=False) for i in range(N_MP)
    )
    keep = jnp.where(core == 0, first, second)
    away = jnp.where(core == 0, second, first)
    back = core_swap(away)
    low = jnp.where(core == 0, keep, back)
    high = jnp.where(core == 0, back, keep)
    return jnp.concatenate([low, high], axis=0)[None], jnp.stack([short_a, short_b])


def bit_of(core_index, late):
    even = 4 if late else 2
    return even if core_index == 0 else 6 - even


def slot_table(mine):
    core = mine % 2
    early = jnp.where(core == 0, 2, 4)
    late = 6 - early
    relative = [0, early, late, 6, 1, 1 ^ late, 1 ^ early, 7]
    return jnp.stack([mine ^ r for r in relative]).astype(jnp.int32)


def place_kernel(n_pieces, table, *refs):
    pieces, out, sems = refs[:n_pieces], refs[n_pieces], refs[n_pieces + 1]
    at = 0
    copies = []
    for piece in pieces:
        for k in range(piece.shape[0]):
            copy = pltpu.make_async_copy(piece.at[k], out.at[table[at]], sems.at[at])
            copy.start()
            copies.append(copy)
            at += 1
    for copy in copies:
        copy.wait()


def place(pieces, table):
    total = sum(p.shape[0] for p in pieces)
    _, rows, cols = pieces[0].shape
    out = pl.pallas_call(
        functools.partial(place_kernel, len(pieces)),
        out_shape=jax.ShapeDtypeStruct((total, rows, cols), pieces[0].dtype),
        grid_spec=pltpu.PrefetchScalarGridSpec(
            num_scalar_prefetch=1,
            grid=(1,),
            in_specs=[pl.BlockSpec(memory_space=pl.ANY)] * len(pieces),
            out_specs=pl.BlockSpec(memory_space=pl.ANY),
            scratch_shapes=[pltpu.SemaphoreType.DMA((total,))],
        ),
        name="place",
    )(table, *pieces)
    return out.reshape(total * rows, cols)


def mp_gather(shard):
    return [shard] + [mp_swap(shard, step) for step in range(1, N_MP)]


def dp_gather(slab):
    size = lax.axis_size("dp")
    if size != 8:
        return lax.all_gather(slab, "dp", axis=0, tiled=True)
    own = slab[None]
    one = dp_swap(own, lambda i: i ^ bit_of(i % 2, False))
    two = dp_swap(jnp.concatenate([own, one]), lambda i: i ^ bit_of(i % 2, True))
    rest = core_swap(jnp.concatenate([own, one, two]))
    return place([own, one, two, rest], slot_table(lax.axis_index("dp")))


def dp_scatter(grad):
    size = lax.axis_size("dp")
    if size != 8:
        return lax.psum_scatter(grad, "dp", scatter_dimension=0, tiled=True)
    rows, cols = grad.shape
    table = slot_table(lax.axis_index("dp"))
    slots = grad.reshape(size, rows // size, cols)

    def pick(indices):
        return jnp.stack(
            [lax.dynamic_index_in_dim(slots, table[i], 0, keepdims=False) for i in indices]
        )

    away = pick((4, 5, 6, 7)).astype(BF16)
    keep = pick((0, 1, 2, 3))
    total = keep + core_swap(away).astype(F32)
    away = dp_swap(total[2:].astype(BF16), lambda i: i ^ bit_of(i % 2, True))
    total = total[:2] + away.astype(F32)
    away = dp_swap(total[1].astype(BF16), lambda i: i ^ bit_of(i % 2, False))
    return total[0] + away.astype(F32)


def mp_scatter(parts):
    total = parts[0]
    for step in range(1, N_MP):
        total = total + mp_swap(parts[step].astype(BF16), step).astype(F32)
    return total


def attend_kernel(q_ref, k_ref, v_ref, kp_ref, vp_ref, bias_ref, o_ref, lse_ref):
    rows = q_ref.shape[0]
    keys = jnp.concatenate([k_ref[...], kp_ref[...]], axis=0)
    values = jnp.concatenate([v_ref[...], vp_ref[...]], axis=0)
    bias = bias_ref[...]
    tile = min(rows, Q_TILE)
    low = lax.broadcasted_iota(jnp.int32, (tile, LANES), 1) < HEAD
    for start in range(0, rows, tile):
        q = q_ref[start : start + tile, :]
        outs, logs = [], []
        for half in range(2):
            here = low if half == 0 else ~low
            q_here = jnp.where(here, q, jnp.zeros_like(q))
            scores = dot(q_here, keys, NT) + bias
            top = jnp.max(scores, axis=-1, keepdims=True)
            raised = jnp.exp(scores - top)
            total = jnp.sum(raised, axis=-1, keepdims=True)
            mixed = dot(raised.astype(BF16), values, NN)
            outs.append(mixed / total)
            logs.append(top + jnp.log(total))
        o_ref[start : start + tile, :] = jnp.where(low, outs[0], outs[1]).astype(BF16)
        lse_ref[start : start + tile, :] = jnp.where(low, logs[0], logs[1])


def attend(qkv, kv_other, bias):
    rows, width = qkv.shape[0], qkv.shape[1] // 3
    pairs = width // LANES
    spec = lambda base: pl.BlockSpec((rows, LANES), lambda p: (0, base + p))
    return pl.pallas_call(
        attend_kernel,
        out_shape=(
            jax.ShapeDtypeStruct((rows, width), BF16),
            jax.ShapeDtypeStruct((rows, width), F32),
        ),
        grid=(pairs,),
        in_specs=[
            spec(0),
            spec(pairs),
            spec(2 * pairs),
            spec(0),
            spec(pairs),
            pl.BlockSpec((1, 2 * rows), lambda p: (0, 0)),
        ],
        out_specs=(spec(0), spec(0)),
        compiler_params=pltpu.CompilerParams(vmem_limit_bytes=56 << 20),
        name="attend",
    )(qkv, qkv, qkv, kv_other, kv_other, bias)


def attend_back_kernel(
    q_ref, k_ref, v_ref, kp_ref, vp_ref, bias_ref, o_ref, lse_ref, do_ref,
    dq_ref, dk_ref, dv_ref, dkp_ref, dvp_ref,
):
    rows = q_ref.shape[0]
    keys = jnp.concatenate([k_ref[...], kp_ref[...]], axis=0)
    values = jnp.concatenate([v_ref[...], vp_ref[...]], axis=0)
    bias = bias_ref[...]
    tile = min(rows, Q_TILE)
    low = lax.broadcasted_iota(jnp.int32, (tile, LANES), 1) < HEAD
    dk = jnp.zeros((LANES, 2 * rows), F32)
    dv = jnp.zeros((LANES, 2 * rows), F32)
    for start in range(0, rows, tile):
        at = slice(start, start + tile)
        q, do = q_ref[at, :], do_ref[at, :]
        product = o_ref[at, :].astype(F32) * do.astype(F32)
        lse = lse_ref[at, :]
        outs = []
        for half in range(2):
            here = low if half == 0 else ~low
            q_here = jnp.where(here, q, jnp.zeros_like(q))
            do_here = jnp.where(here, do, jnp.zeros_like(do))
            inner = jnp.sum(jnp.where(here, product, 0.0), axis=-1, keepdims=True)
            log = lse[:, half * HEAD : half * HEAD + 1]
            soft = jnp.exp(dot(q_here, keys, NT) + bias - log)
            grad = (soft * (dot(do_here, values, NT) - inner)).astype(BF16)
            outs.append(dot(grad, keys, NN))
            dk = dk + dot(q_here, grad, TN)
            dv = dv + dot(do_here, soft.astype(BF16), TN)
        dq_ref[at, :] = (jnp.where(low, outs[0], outs[1]) * SCALE).astype(BF16)
    dk, dv = dk.T, dv.T
    dk_ref[...] = dk[:rows]
    dkp_ref[...] = dk[rows:].astype(BF16)
    dv_ref[...] = dv[:rows]
    dvp_ref[...] = dv[rows:].astype(BF16)


def attend_back(qkv, kv_other, bias, out, lse, grad_out):
    rows, width = out.shape
    pairs = width // LANES
    spec = lambda base: pl.BlockSpec((rows, LANES), lambda p: (0, base + p))
    shape = lambda kind: jax.ShapeDtypeStruct((rows, width), kind)
    return pl.pallas_call(
        attend_back_kernel,
        out_shape=(shape(BF16), shape(F32), shape(F32), shape(BF16), shape(BF16)),
        grid=(pairs,),
        in_specs=[
            spec(0),
            spec(pairs),
            spec(2 * pairs),
            spec(0),
            spec(pairs),
            pl.BlockSpec((1, 2 * rows), lambda p: (0, 0)),
            spec(0),
            spec(0),
            spec(0),
        ],
        out_specs=(spec(0),) * 5,
        compiler_params=pltpu.CompilerParams(vmem_limit_bytes=56 << 20),
        name="attend_back",
    )(qkv, qkv, qkv, kv_other, kv_other, bias, out, lse, grad_out)


def gelu_parts(v):
    cdf = 0.5 * (1.0 + lax.erf(v * (2.0 ** -0.5)))
    pdf = jnp.exp(-0.5 * v * v) * 0.3989422804014327
    return v * cdf, cdf + v * pdf


def norm(values):
    center = values - jnp.mean(values, axis=-1, keepdims=True)
    inv_dev = lax.rsqrt(jnp.mean(center * center, axis=-1, keepdims=True) + EPS)
    return center * inv_dev, inv_dev


def norm_back(scaled, normed, inv_dev):
    return inv_dev * (
        scaled
        - jnp.mean(scaled, axis=-1, keepdims=True)
        - normed * jnp.mean(scaled * normed, axis=-1, keepdims=True)
    )


def on_device(
    frames_long,
    frames_short,
    length_long,
    length_short,
    input_proj,
    output_proj,
    expand_weight,
    shrink_weight,
    head_bias,
    expand_bias,
    row_params,
    cotangent_long,
    cotangent_short,
):
    mine = lax.axis_index("dp")
    depth = lax.axis_index("mp")
    n_dp = lax.axis_size("dp")
    core = mine % 2
    block = frames_short.shape[1]
    group = input_proj.shape[2]
    units = expand_weight.shape[1]
    width = group * N_MP
    shard = input_proj.shape[1]

    row_size, head_size = row_params.size, head_bias.size
    small = jnp.concatenate(
        [
            row_params.reshape(-1),
            head_bias.astype(F32).reshape(-1),
            expand_bias.astype(F32).reshape(-1),
            length_long.astype(F32),
            length_short.astype(F32),
        ]
    )
    pad = -small.size % LANES
    small = jnp.pad(small, (0, pad))[None]

    joined = jnp.concatenate(
        [input_proj[0], input_proj[1], input_proj[2], output_proj.T], axis=1
    )
    attn_parts = mp_gather(joined)
    order = [p[:, i * group : (i + 1) * group] for i in range(4) for p in attn_parts]
    attn_w = dp_gather(jnp.concatenate(order, axis=1))
    up_w = dp_gather(jnp.concatenate(mp_gather(expand_weight), axis=1))
    down_w = dp_gather(jnp.concatenate(mp_gather(shrink_weight.T), axis=1))

    everything = lax.all_gather(small, ("dp", "mp"), axis=0, tiled=True).reshape(
        n_dp, N_MP, -1
    )
    rows_of = everything[:, :, :row_size].reshape(n_dp, N_MP, 6, -1)
    row_vals = rows_of.transpose(2, 0, 1, 3).reshape(6, 1, width)
    relative = depth ^ jnp.arange(N_MP)
    at = row_size
    heads_of = everything[:, :, at : at + head_size].reshape(n_dp, N_MP, 2, -1)
    heads_of = heads_of.transpose(2, 1, 0, 3).reshape(2, N_MP, group)
    heads_of = jnp.take(heads_of, relative, axis=1).reshape(2, 1, width)
    at += head_size
    up_b = everything[:, :, at : at + expand_bias.size].transpose(1, 0, 2)
    up_b = jnp.take(up_b.reshape(N_MP, units), relative, axis=0).reshape(1, N_MP * units)
    at += expand_bias.size
    lengths = lax.dynamic_slice(everything, (mine - core, 0, at), (2, 1, 3))[:, 0]
    by_depth = jnp.stack([lengths[0, 0], lengths[1, 0], lengths[core, 1], lengths[core, 2]])
    length = by_depth[depth]

    is_long = depth < 2
    source = jnp.repeat(relative, block)
    inside = jnp.tile(jnp.arange(block), N_MP)
    stride = jnp.where(is_long, 2 * block, block)
    lead = jnp.where(is_long, block, 0)
    frame = (source * stride + inside).astype(F32)
    own_bias = jnp.where(frame + lead * core < length, 0.0, NEG_FILL)
    other_bias = jnp.where(
        is_long & (frame + lead * (1 - core) < length), 0.0, NEG_FILL
    )
    bias = jnp.concatenate([own_bias, other_bias])[None].astype(F32)

    x_low = to_clips(frames_long[0], frames_short, core, depth)
    cot = to_clips(cotangent_long[0], cotangent_short, core, depth)
    x = x_low.astype(F32)
    project = dot(x_low, attn_w[:, : 3 * width], NN)
    queries = ((project[:, :width] + heads_of[0]).astype(BF16) * SCALE).astype(BF16)
    kv = jnp.concatenate(
        [project[:, width : 2 * width], project[:, 2 * width :] + heads_of[1]], axis=1
    ).astype(BF16)
    qkv = jnp.concatenate([queries, kv], axis=1)
    kv_other = core_swap(kv)
    mixed, lse = attend(qkv, kv_other, bias)
    out_w = attn_w[:, 3 * width :]
    attention = dot(mixed, out_w, NT)
    n1, r1 = norm(x + attention + row_vals[0])
    h = n1 * row_vals[1] + row_vals[2]
    h_low = h.astype(BF16)
    act, slope = gelu_parts(dot(h_low, up_w, NN) + up_b)
    act = act.astype(BF16)
    n2, r2 = norm(h + dot(act, down_w, NT) + row_vals[3])
    result = (n2 * row_vals[4] + row_vals[5]).astype(BF16)
    result_long, result_short = from_clips(result, core, depth)

    gy = cot.astype(F32)
    dz = norm_back(gy * row_vals[4], n2, r2)
    df = dz.astype(BF16)
    du = (dot(df, down_w, NN) * slope).astype(BF16)
    g_down = dot(df, act, TN)
    g_up = dot(h_low, du, TN)
    dh = dz + dot(du, up_w, NT)
    da = norm_back(dh * row_vals[1], n1, r1)
    da_low = da.astype(BF16)
    do = dot(da_low, out_w, NN).astype(BF16)
    dq, dk, dv, dk_other, dv_other = attend_back(qkv, kv_other, bias, mixed, lse, do)
    back = core_swap(jnp.concatenate([dk_other, dv_other], axis=1)).astype(F32)
    dkv = (jnp.concatenate([dk, dv], axis=1) + back).astype(BF16)
    dqkv = jnp.concatenate([dq, dkv], axis=1)
    dx = dot(dqkv, attn_w[:, : 3 * width], NT)
    frames_grad = (da + dx).astype(BF16)
    grad_long, grad_short = from_clips(frames_grad, core, depth)

    g_attn = jnp.concatenate([dot(x_low, dqkv, TN), dot(da_low, mixed, TN)], axis=1)

    def halves(value):
        return [value[:, i * units : (i + 1) * units] for i in range(N_MP)]

    up_share = mp_scatter(halves(dp_scatter(g_up)))
    down_share = mp_scatter(halves(dp_scatter(g_down))).T
    attn_sum = dp_scatter(g_attn)
    attn_parts = [
        jnp.concatenate(
            [
                attn_sum[:, i * width + j * group : i * width + (j + 1) * group]
                for i in range(4)
            ],
            axis=1,
        )
        for j in range(N_MP)
    ]
    attn_share = mp_scatter(attn_parts)
    input_share = jnp.stack([attn_share[:, i * group : (i + 1) * group] for i in range(3)])
    output_share = attn_share[:, 3 * group :].T

    def total(value):
        return jnp.sum(value, axis=0)

    row_grads = jnp.stack(
        [total(da), total(dh * n1), total(dh), total(dz), total(gy * n2), total(gy)]
    )
    head_grads = jnp.stack([total(dq.astype(F32)), total(dkv[:, width:].astype(F32))])
    head_grads = jnp.take(head_grads.reshape(2, N_MP, group), relative, axis=1)
    up_b_grads = jnp.take(total(du.astype(F32)).reshape(N_MP, units), relative, axis=0)
    small_grads = jnp.concatenate(
        [
            row_grads.reshape(6, n_dp, N_MP, -1).transpose(1, 2, 0, 3).reshape(n_dp, N_MP, -1),
            head_grads.reshape(2, N_MP, n_dp, -1).transpose(2, 1, 0, 3).reshape(n_dp, N_MP, -1),
            up_b_grads.reshape(N_MP, n_dp, -1).transpose(1, 0, 2),
        ],
        axis=2,
    )
    small_share = lax.psum_scatter(
        jnp.pad(
            small_grads.reshape(n_dp * N_MP, -1),
            ((0, 0), (0, -small_grads.shape[2] % LANES)),
        ),
        ("dp", "mp"),
        scatter_dimension=0,
        tiled=True,
    )[0]
    return (
        result_long,
        result_short,
        grad_long.astype(F32),
        grad_short.astype(F32),
        input_share,
        output_share,
        up_share,
        down_share,
        small_share[row_size : row_size + head_size].reshape(2, 1, -1),
        small_share[row_size + head_size : row_size + head_size + expand_bias.size][None],
        small_share[:row_size].reshape(6, -1),
    )


def solution(mesh):
    return jax.shard_map(
        on_device,
        mesh=mesh,
        in_specs=(
            P("dp", "mp", None),
            P("dp", "mp", None),
            P("dp"),
            P("dp"),
            P(None, "dp", "mp"),
            P("mp", "dp"),
            P("dp", "mp"),
            P("mp", "dp"),
            P(None, "mp", "dp"),
            P("mp", "dp"),
            P(None, ("dp", "mp")),
            P("dp", "mp", None),
            P("dp", "mp", None),
        ),
        out_specs=(
            P("dp", "mp", None),
            P("dp", "mp", None),
            P("dp", "mp", None),
            P("dp", "mp", None),
            P(None, "dp", "mp"),
            P("mp", "dp"),
            P("dp", "mp"),
            P("mp", "dp"),
            P(None, "mp", "dp"),
            P("mp", "dp"),
            P(None, ("dp", "mp")),
        ),
        check_vma=False,
    )
```

```python
import functools

import jax
import jax.numpy as jnp
from jax import lax
from jax.experimental import pallas as pl
from jax.experimental.pallas import tpu as pltpu
from jax.sharding import PartitionSpec as P

HEAD = 64
EPS = 1e-05
NEG_FILL = -1e30
SCALE = HEAD ** (-0.5)
N_MP = 4
LANES = 128
Q_TILE = 256
F32 = jnp.float32
BF16 = jnp.bfloat16
NT = (((1,), (1,)), ((), ()))
NN = (((1,), (0,)), ((), ()))
TN = (((0,), (0,)), ((), ()))


def dot(left, right, dims):
    return lax.dot_general(left, right, dims, preferred_element_type=F32)


def mp_swap(value, step):
    return lax.ppermute(value, "mp", [(i, i ^ step) for i in range(N_MP)])


def dp_swap(value, target):
    size = lax.axis_size("dp")
    return lax.ppermute(value, "dp", [(i, target(i)) for i in range(size)])


def core_swap(value):
    return dp_swap(value, lambda i: i ^ 1)


def to_clips(long_rows, short_rows, core, depth):
    block = short_rows.shape[1]
    keep = lax.dynamic_slice_in_dim(long_rows, core * block, block, 0)
    away = lax.dynamic_slice_in_dim(long_rows, (1 - core) * block, block, 0)
    back = core_swap(away)
    first = jnp.where(core == 0, keep, back)
    second = jnp.where(core == 0, back, keep)
    blocks = jnp.stack([first, second, short_rows[0], short_rows[1]])
    parts = []
    for step in range(N_MP):
        piece = lax.dynamic_index_in_dim(blocks, depth ^ step, 0, keepdims=False)
        parts.append(piece if step == 0 else mp_swap(piece, step))
    return jnp.concatenate(parts, axis=0)


def from_clips(rows, core, depth):
    block = rows.shape[0] // N_MP
    parts = []
    for step in range(N_MP):
        piece = rows[step * block : (step + 1) * block]
        parts.append(piece if step == 0 else mp_swap(piece, step))
    blocks = jnp.stack(parts)
    first, second, short_a, short_b = (
        lax.dynamic_index_in_dim(blocks, depth ^ i, 0, keepdims=False) for i in range(N_MP)
    )
    keep = jnp.where(core == 0, first, second)
    away = jnp.where(core == 0, second, first)
    back = core_swap(away)
    low = jnp.where(core == 0, keep, back)
    high = jnp.where(core == 0, back, keep)
    return jnp.concatenate([low, high], axis=0)[None], jnp.stack([short_a, short_b])


def flip(index, late):
    return index ^ ((4 if late else 2) if index % 2 == 0 else (2 if late else 4))


def block_table(mine, size):
    if size != 8:
        return jnp.zeros((1,), jnp.int32)
    early = jnp.where(mine % 2 == 0, 2, 4)
    late = 6 - early
    relative = [0, early, late, 6, 1, 1 ^ late, 1 ^ early, 7]
    return jnp.stack([mine ^ r for r in relative]).astype(jnp.int32)


def dp_gather(slab):
    if lax.axis_size("dp") != 8:
        return [lax.all_gather(slab, "dp", axis=0, tiled=True)]
    early = lambda i: flip(i, False)
    late = lambda i: flip(i, True)
    one = dp_swap(slab, early)
    two = dp_swap(slab, late)
    three = dp_swap(one, late)
    plane = [slab, one, two, three]
    return plane + [core_swap(piece) for piece in plane]


def mp_gather(shard):
    return [shard] + [mp_swap(shard, step) for step in range(1, N_MP)]


def dp_scatter(parts):
    if len(parts) == 1:
        return lax.psum_scatter(parts[0][0], "dp", scatter_dimension=0, tiled=True)
    keep, away = parts
    total = keep.astype(F32) + core_swap(away).astype(F32)
    back = dp_swap(total[2:].astype(BF16), lambda i: flip(i, True))
    total = total[:2] + back.astype(F32)
    back = dp_swap(total[1].astype(BF16), lambda i: flip(i, False))
    return total[0] + back.astype(F32)


def mp_scatter(parts):
    total = parts[0]
    for step in range(1, N_MP):
        total = total + mp_swap(parts[step].astype(BF16), step).astype(F32)
    return total


def small_gather(value, mine, depth):
    size = lax.axis_size("dp")
    if size != 8:
        whole = lax.all_gather(value[None], ("dp", "mp"), axis=0, tiled=True)
        return whole.reshape((size, N_MP) + value.shape)
    slab = jnp.stack(mp_gather(value))
    blocks = jnp.stack(dp_gather(slab))
    places = jnp.array([[0, 4, 1, 6, 2, 5, 3, 7], [0, 4, 2, 5, 1, 6, 3, 7]], jnp.int32)
    where = places[mine % 2][mine ^ jnp.arange(size)]
    flat = where[:, None] * N_MP + (depth ^ jnp.arange(N_MP))[None, :]
    blocks = blocks.reshape((size * N_MP,) + value.shape)
    return jnp.take(blocks, flat.reshape(-1), axis=0).reshape((size, N_MP) + value.shape)


def small_sum(value):
    size = lax.axis_size("dp")
    if size != 8:
        return lax.psum(value, ("dp", "mp"))
    for bit in (1, 2, 4):
        value = value + dp_swap(value, lambda i: i ^ bit)
    total = value
    for step in range(1, N_MP):
        total = total + mp_swap(value, step)
    return total


class Weights:
    def __init__(self, pieces, table, held, sems, lo, tile):
        self.held, self.tile = held, tile
        self.copies = []
        for t in range(held.shape[2] // tile):
            row = []
            for k, piece in enumerate(pieces):
                copy = pltpu.make_async_copy(
                    piece.at[:, pl.ds(lo + t * tile, tile)],
                    held.at[table[k], :, pl.ds(t * tile, tile)],
                    sems.at[t, k],
                )
                copy.start()
                row.append(copy)
            self.copies.append(row)

    def get(self, t):
        for copy in self.copies[t]:
            copy.wait()
        at = t * self.tile
        count, rows, _ = self.held.shape
        return self.held[:, :, at : at + self.tile].reshape(count * rows, self.tile)


def weight_scratch(pieces, cols, tile):
    return [
        pltpu.VMEM((len(pieces), pieces[0].shape[0], cols), BF16),
        pltpu.SemaphoreType.DMA((cols // tile, len(pieces))),
    ]


def grad_shapes(pieces, cols):
    count, rows = len(pieces), pieces[0].shape[0]
    if count == 1:
        return [jax.ShapeDtypeStruct((1, rows, cols), F32)]
    return [jax.ShapeDtypeStruct((count // 2, rows, cols), BF16)] * 2


def store_grad(value, table, held, outs, at):
    held[...] = value.reshape(held.shape)
    for r in range(held.shape[0]):
        out = outs[r // outs[0].shape[0]]
        out[r % out.shape[0], :, at : at + held.shape[2]] = held[table[r]].astype(out.dtype)


def call(body, name, outs, arrays, table, pieces, scratch):
    vmem = pl.BlockSpec(memory_space=pltpu.VMEM)
    return pl.pallas_call(
        body,
        out_shape=tuple(outs),
        in_specs=[pl.BlockSpec(memory_space=pltpu.SMEM)]
        + [vmem] * len(arrays)
        + [pl.BlockSpec(memory_space=pl.ANY)] * len(pieces),
        out_specs=(vmem,) * len(outs),
        scratch_shapes=scratch,
        compiler_params=pltpu.CompilerParams(vmem_limit_bytes=56 << 20),
        name=name,
    )(table, *arrays, *pieces)


def like(shape, kind):
    return jax.ShapeDtypeStruct(shape, kind)


def attend_kernel(q_ref, k_ref, v_ref, kp_ref, vp_ref, bias_ref, o_ref, lse_ref):
    rows = q_ref.shape[0]
    keys = jnp.concatenate([k_ref[...], kp_ref[...]], axis=0)
    values = jnp.concatenate([v_ref[...], vp_ref[...]], axis=0)
    bias = bias_ref[...]
    tile = min(rows, Q_TILE)
    low = lax.broadcasted_iota(jnp.int32, (tile, LANES), 1) < HEAD
    for start in range(0, rows, tile):
        q = q_ref[start : start + tile, :]
        outs, logs = [], []
        for half in range(2):
            here = low if half == 0 else ~low
            q_here = jnp.where(here, q, jnp.zeros_like(q))
            scores = dot(q_here, keys, NT) + bias
            top = jnp.max(scores, axis=-1, keepdims=True)
            raised = jnp.exp(scores - top)
            total = jnp.sum(raised, axis=-1, keepdims=True)
            mixed = dot(raised.astype(BF16), values, NN)
            outs.append(mixed / total)
            logs.append(top + jnp.log(total))
        o_ref[start : start + tile, :] = jnp.where(low, outs[0], outs[1]).astype(BF16)
        lse_ref[start : start + tile, :] = jnp.where(low, logs[0], logs[1])


def attend(qkv, kv_other, bias):
    rows, width = qkv.shape[0], qkv.shape[1] // 3
    pairs = width // LANES
    spec = lambda base: pl.BlockSpec((rows, LANES), lambda p: (0, base + p))
    return pl.pallas_call(
        attend_kernel,
        out_shape=(
            jax.ShapeDtypeStruct((rows, width), BF16),
            jax.ShapeDtypeStruct((rows, width), F32),
        ),
        grid=(pairs,),
        in_specs=[
            spec(0),
            spec(pairs),
            spec(2 * pairs),
            spec(0),
            spec(pairs),
            pl.BlockSpec((1, 2 * rows), lambda p: (0, 0)),
        ],
        out_specs=(spec(0), spec(0)),
        compiler_params=pltpu.CompilerParams(vmem_limit_bytes=56 << 20),
        name="attend",
    )(qkv, qkv, qkv, kv_other, kv_other, bias)


def attend_back_kernel(
    q_ref, k_ref, v_ref, kp_ref, vp_ref, bias_ref, o_ref, lse_ref, do_ref,
    dq_ref, dk_ref, dv_ref, dkp_ref, dvp_ref,
):
    rows = q_ref.shape[0]
    keys = jnp.concatenate([k_ref[...], kp_ref[...]], axis=0)
    values = jnp.concatenate([v_ref[...], vp_ref[...]], axis=0)
    bias = bias_ref[...]
    tile = min(rows, Q_TILE)
    low = lax.broadcasted_iota(jnp.int32, (tile, LANES), 1) < HEAD
    dk = jnp.zeros((LANES, 2 * rows), F32)
    dv = jnp.zeros((LANES, 2 * rows), F32)
    for start in range(0, rows, tile):
        at = slice(start, start + tile)
        q, do = q_ref[at, :], do_ref[at, :]
        product = o_ref[at, :].astype(F32) * do.astype(F32)
        lse = lse_ref[at, :]
        outs = []
        for half in range(2):
            here = low if half == 0 else ~low
            q_here = jnp.where(here, q, jnp.zeros_like(q))
            do_here = jnp.where(here, do, jnp.zeros_like(do))
            inner = jnp.sum(jnp.where(here, product, 0.0), axis=-1, keepdims=True)
            log = lse[:, half * HEAD : half * HEAD + 1]
            soft = jnp.exp(dot(q_here, keys, NT) + bias - log)
            grad = (soft * (dot(do_here, values, NT) - inner)).astype(BF16)
            outs.append(dot(grad, keys, NN))
            dk = dk + dot(q_here, grad, TN)
            dv = dv + dot(do_here, soft.astype(BF16), TN)
        dq_ref[at, :] = (jnp.where(low, outs[0], outs[1]) * SCALE).astype(BF16)
    dk, dv = dk.T, dv.T
    dk_ref[...] = dk[:rows]
    dkp_ref[...] = dk[rows:].astype(BF16)
    dv_ref[...] = dv[:rows]
    dvp_ref[...] = dv[rows:].astype(BF16)


def attend_back(qkv, kv_other, bias, out, lse, grad_out):
    rows, width = out.shape
    pairs = width // LANES
    spec = lambda base: pl.BlockSpec((rows, LANES), lambda p: (0, base + p))
    shape = lambda kind: jax.ShapeDtypeStruct((rows, width), kind)
    return pl.pallas_call(
        attend_back_kernel,
        out_shape=(shape(BF16), shape(F32), shape(F32), shape(BF16), shape(BF16)),
        grid=(pairs,),
        in_specs=[
            spec(0),
            spec(pairs),
            spec(2 * pairs),
            spec(0),
            spec(pairs),
            pl.BlockSpec((1, 2 * rows), lambda p: (0, 0)),
            spec(0),
            spec(0),
            spec(0),
        ],
        out_specs=(spec(0),) * 5,
        compiler_params=pltpu.CompilerParams(vmem_limit_bytes=56 << 20),
        name="attend_back",
    )(qkv, qkv, qkv, kv_other, kv_other, bias, out, lse, grad_out)


def gelu_parts(v):
    cdf = 0.5 * (1.0 + lax.erf(v * (2.0 ** -0.5)))
    pdf = jnp.exp(-0.5 * v * v) * 0.3989422804014327
    return v * cdf, cdf + v * pdf


def norm(values):
    center = values - jnp.mean(values, axis=-1, keepdims=True)
    inv_dev = lax.rsqrt(jnp.mean(center * center, axis=-1, keepdims=True) + EPS)
    return center * inv_dev, inv_dev


def norm_back(scaled, normed, inv_dev):
    return inv_dev * (
        scaled
        - jnp.mean(scaled, axis=-1, keepdims=True)
        - normed * jnp.mean(scaled * normed, axis=-1, keepdims=True)
    )


def total(value):
    return jnp.sum(value, axis=0, keepdims=True)


def project(x, head_rows, table, pieces):
    rows, width = x.shape
    n = len(pieces)

    def body(table, x_ref, bias_ref, *refs):
        pieces, (qkv_ref, kv_ref, held, sems) = refs[:n], refs[n:]
        weights = Weights(pieces, table, held, sems, 0, width)
        x = x_ref[...]
        for i in range(3):
            value = dot(x, weights.get(i), NN) + bias_ref[i : i + 1, :]
            value = value.astype(BF16)
            if i == 0:
                value = (value.astype(F32) * SCALE).astype(BF16)
            else:
                kv_ref[:, (i - 1) * width : i * width] = value
            qkv_ref[:, i * width : (i + 1) * width] = value

    return call(
        body,
        "project",
        [like((rows, 3 * width), BF16), like((rows, 2 * width), BF16)],
        [x, head_rows],
        table,
        pieces,
        weight_scratch(pieces, 3 * width, width),
    )


def mix_and_expand(x, mixed, row_vals, up_b, table, out_pieces, up_pieces):
    rows, width = x.shape
    hidden = up_b.shape[1]
    tile = hidden // 6
    n = len(out_pieces)

    def body(table, x_ref, mixed_ref, rows_ref, up_b_ref, *refs):
        out_p, up_p = refs[:n], refs[n : 2 * n]
        n1_ref, r1_ref, h_ref, act_ref, slope_ref, w_out, sems_out, w_up, sems_up = refs[2 * n :]
        out_w = Weights(out_p, table, w_out, sems_out, 3 * width, width)
        up_w = Weights(up_p, table, w_up, sems_up, 0, tile)
        attention = dot(mixed_ref[...], out_w.get(0), NT)
        n1, r1 = norm(x_ref[...].astype(F32) + attention + rows_ref[0:1, :])
        n1_ref[...] = n1
        r1_ref[...] = jnp.broadcast_to(r1, r1_ref.shape)
        h_ref[...] = (n1 * rows_ref[1:2, :] + rows_ref[2:3, :]).astype(BF16)
        for t in range(hidden // tile):
            at = slice(t * tile, (t + 1) * tile)
            u = dot(h_ref[...], up_w.get(t), NN) + up_b_ref[:, at]
            act, slope = gelu_parts(u)
            act_ref[:, at] = act.astype(BF16)
            slope_ref[:, at] = slope.astype(BF16)

    return call(
        body,
        "mix_and_expand",
        [
            like((rows, width), F32),
            like((rows, LANES), F32),
            like((rows, width), BF16),
            like((rows, hidden), BF16),
            like((rows, hidden), BF16),
        ],
        [x, mixed, row_vals, up_b],
        table,
        list(out_pieces) + list(up_pieces),
        weight_scratch(out_pieces, width, width) + weight_scratch(up_pieces, hidden, tile),
    )


def shrink_and_turn(n1, act, cot, row_vals, table, pieces):
    rows, width = n1.shape
    hidden = act.shape[1]
    tile = hidden // 6
    n = len(pieces)
    grads = grad_shapes(pieces, hidden)

    def body(table, n1_ref, act_ref, cot_ref, rows_ref, *refs):
        pieces, (result_ref, dz_ref, df_ref, sums_ref) = refs[:n], refs[n : n + 4]
        grad_refs = refs[n + 4 : n + 4 + len(grads)]
        held, sems, slot = refs[n + 4 + len(grads) :]
        weights = Weights(pieces, table, held, sems, 0, tile)
        feed = jnp.zeros((rows, width), F32)
        for t in range(hidden // tile):
            feed = feed + dot(act_ref[:, t * tile : (t + 1) * tile], weights.get(t), NT)
        h = n1_ref[...] * rows_ref[1:2, :] + rows_ref[2:3, :]
        n2, r2 = norm(h + feed + rows_ref[3:4, :])
        result_ref[...] = (n2 * rows_ref[4:5, :] + rows_ref[5:6, :]).astype(BF16)
        gy = cot_ref[...].astype(F32)
        dz = norm_back(gy * rows_ref[4:5, :], n2, r2)
        dz_ref[...] = dz
        df_ref[...] = dz.astype(BF16)
        sums_ref[0:1, :] = total(dz)
        sums_ref[1:2, :] = total(gy * n2)
        sums_ref[2:3, :] = total(gy)
        for t in range(hidden // tile):
            at = t * tile
            grad = dot(df_ref[...], act_ref[:, at : at + tile], TN)
            store_grad(grad, table, slot, grad_refs, at)

    return call(
        body,
        "shrink_and_turn",
        [
            like((rows, width), BF16),
            like((rows, width), F32),
            like((rows, width), BF16),
            like((8, width), F32),
        ]
        + grads,
        [n1, act, cot, row_vals],
        table,
        pieces,
        weight_scratch(pieces, hidden, tile)
        + [pltpu.VMEM((n, pieces[0].shape[0], tile), F32)],
    )


def hidden_back(df, slope, h_low, table, pieces):
    rows, width = df.shape
    hidden = slope.shape[1]
    tile = hidden // 6
    n = len(pieces)
    grads = grad_shapes(pieces, hidden)

    def body(table, df_ref, slope_ref, h_ref, *refs):
        pieces, (du_ref, sums_ref) = refs[:n], refs[n : n + 2]
        grad_refs = refs[n + 2 : n + 2 + len(grads)]
        held, sems, slot = refs[n + 2 + len(grads) :]
        weights = Weights(pieces, table, held, sems, 0, tile)
        for t in range(hidden // tile):
            at = slice(t * tile, (t + 1) * tile)
            du = dot(df_ref[...], weights.get(t), NN) * slope_ref[:, at].astype(F32)
            du = du.astype(BF16)
            du_ref[:, at] = du
            sums_ref[:, at] = total(du.astype(F32))
            store_grad(dot(h_ref[...], du, TN), table, slot, grad_refs, t * tile)

    return call(
        body,
        "hidden_back",
        [like((rows, hidden), BF16), like((1, hidden), F32)] + grads,
        [df, slope, h_low],
        table,
        pieces,
        weight_scratch(pieces, hidden, tile)
        + [pltpu.VMEM((n, pieces[0].shape[0], tile), F32)],
    )


def expand_back(dz, du, n1, r1, row_vals, table, up_pieces, out_pieces):
    rows, width = dz.shape
    hidden = du.shape[1]
    tile = hidden // 6
    n = len(up_pieces)

    def body(table, dz_ref, du_ref, n1_ref, r1_ref, rows_ref, *refs):
        up_p, out_p = refs[:n], refs[n : 2 * n]
        da_ref, low_ref, do_ref, sums_ref, w_up, sems_up, w_out, sems_out = refs[2 * n :]
        up_w = Weights(up_p, table, w_up, sems_up, 0, tile)
        out_w = Weights(out_p, table, w_out, sems_out, 3 * width, width)
        dh = dz_ref[...]
        for t in range(hidden // tile):
            dh = dh + dot(du_ref[:, t * tile : (t + 1) * tile], up_w.get(t), NT)
        n1 = n1_ref[...]
        da = norm_back(dh * rows_ref[1:2, :], n1, r1_ref[:, :1])
        da_ref[...] = da
        low_ref[...] = da.astype(BF16)
        sums_ref[0:1, :] = total(da)
        sums_ref[1:2, :] = total(dh * n1)
        sums_ref[2:3, :] = total(dh)
        do_ref[...] = dot(low_ref[...], out_w.get(0), NN).astype(BF16)

    return call(
        body,
        "expand_back",
        [
            like((rows, width), F32),
            like((rows, width), BF16),
            like((rows, width), BF16),
            like((8, width), F32),
        ],
        [dz, du, n1, r1, row_vals],
        table,
        list(up_pieces) + list(out_pieces),
        weight_scratch(up_pieces, hidden, tile) + weight_scratch(out_pieces, width, width),
    )


def project_grads(x, mixed, da_low, dq, dkv_own, dkv_back, table, pieces):
    rows, width = x.shape
    n = len(pieces)
    grads = grad_shapes(pieces, 4 * width)

    def body(table, x_ref, mixed_ref, da_ref, dq_ref, own_ref, back_ref, *refs):
        dqkv_ref, sums_ref = refs[:2]
        grad_refs, (slot,) = refs[2 : 2 + len(grads)], refs[2 + len(grads) :]
        dqkv_ref[:, :width] = dq_ref[...]
        dqkv_ref[:, width:] = (own_ref[...] + back_ref[...].astype(F32)).astype(BF16)
        sums_ref[...] = total(dqkv_ref[...].astype(F32))
        for i in range(4):
            if i < 3:
                grad = dot(x_ref[...], dqkv_ref[:, i * width : (i + 1) * width], TN)
            else:
                grad = dot(da_ref[...], mixed_ref[...], TN)
            store_grad(grad, table, slot, grad_refs, i * width)

    return call(
        body,
        "project_grads",
        [like((rows, 3 * width), BF16), like((1, 3 * width), F32)] + grads,
        [x, mixed, da_low, dq, dkv_own, dkv_back],
        table,
        [],
        [pltpu.VMEM((n, pieces[0].shape[0], width), F32)],
    )


def project_back(da, dqkv, table, pieces):
    rows, width = da.shape
    n = len(pieces)

    def body(table, da_ref, dqkv_ref, *refs):
        pieces, (out_ref, held, sems) = refs[:n], refs[n:]
        weights = Weights(pieces, table, held, sems, 0, width)
        value = da_ref[...]
        for i in range(3):
            value = value + dot(dqkv_ref[:, i * width : (i + 1) * width], weights.get(i), NT)
        out_ref[...] = value.astype(BF16)

    return call(
        body,
        "project_back",
        [like((rows, width), BF16)],
        [da, dqkv],
        table,
        pieces,
        weight_scratch(pieces, 3 * width, width),
    )[0]


def on_device(
    frames_long,
    frames_short,
    length_long,
    length_short,
    input_proj,
    output_proj,
    expand_weight,
    shrink_weight,
    head_bias,
    expand_bias,
    row_params,
    cotangent_long,
    cotangent_short,
):
    mine = lax.axis_index("dp")
    depth = lax.axis_index("mp")
    n_dp = lax.axis_size("dp")
    core = mine % 2
    block = frames_short.shape[1]
    group = input_proj.shape[2]
    units = expand_weight.shape[1]
    width = group * N_MP
    table = block_table(mine, n_dp)
    relative = depth ^ jnp.arange(N_MP)

    joined = jnp.concatenate(
        [input_proj[0], input_proj[1], input_proj[2], output_proj.T], axis=1
    )
    attn_parts = mp_gather(joined)
    order = [p[:, i * group : (i + 1) * group] for i in range(4) for p in attn_parts]
    attn_p = dp_gather(jnp.concatenate(order, axis=1))
    up_p = dp_gather(jnp.concatenate(mp_gather(expand_weight), axis=1))
    down_p = dp_gather(jnp.concatenate(mp_gather(shrink_weight.T), axis=1))

    row_size, head_size, up_size = row_params.size, head_bias.size, expand_bias.size
    small = jnp.concatenate(
        [
            row_params.reshape(-1),
            head_bias.astype(F32).reshape(-1),
            expand_bias.astype(F32).reshape(-1),
            length_long.astype(F32),
            length_short.astype(F32),
        ]
    )
    small = jnp.pad(small, (0, -small.size % LANES)).reshape(-1, LANES)
    small = small_gather(small, mine, depth).reshape(n_dp, N_MP, -1)
    row_vals = small[:, :, :row_size].reshape(n_dp, N_MP, 6, -1)
    row_vals = row_vals.transpose(2, 0, 1, 3).reshape(6, width)
    at = row_size
    heads = small[:, :, at : at + head_size].reshape(n_dp, N_MP, 2, -1)
    heads = heads.transpose(2, 1, 0, 3).reshape(2, N_MP, group)
    heads = jnp.take(heads, relative, axis=1).reshape(2, width)
    head_rows = jnp.stack([heads[0], jnp.zeros_like(heads[0]), heads[1]])
    at += head_size
    up_b = small[:, :, at : at + up_size].transpose(1, 0, 2).reshape(N_MP, units)
    up_b = jnp.take(up_b, relative, axis=0).reshape(1, N_MP * units)
    at += up_size
    lengths = lax.dynamic_slice(small, (mine - core, 0, at), (2, 1, 3))[:, 0]
    by_depth = jnp.stack([lengths[0, 0], lengths[1, 0], lengths[core, 1], lengths[core, 2]])
    length = by_depth[depth]

    is_long = depth < 2
    source = jnp.repeat(relative, block)
    inside = jnp.tile(jnp.arange(block), N_MP)
    stride = jnp.where(is_long, 2 * block, block)
    lead = jnp.where(is_long, block, 0)
    frame = (source * stride + inside).astype(F32)
    own_bias = jnp.where(frame + lead * core < length, 0.0, NEG_FILL)
    other_bias = jnp.where(
        is_long & (frame + lead * (1 - core) < length), 0.0, NEG_FILL
    )
    bias = jnp.concatenate([own_bias, other_bias])[None].astype(F32)

    x = to_clips(frames_long[0], frames_short, core, depth)
    cot = to_clips(cotangent_long[0], cotangent_short, core, depth)
    qkv, kv = project(x, head_rows, table, attn_p)
    kv_other = core_swap(kv)
    mixed, lse = attend(qkv, kv_other, bias)
    n1, r1, h_low, act, slope = mix_and_expand(
        x, mixed, row_vals, up_b, table, attn_p, up_p
    )
    result, dz, df, sums_two, *g_down = shrink_and_turn(
        n1, act, cot, row_vals, table, down_p
    )
    result_long, result_short = from_clips(result, core, depth)

    du, up_b_sums, *g_up = hidden_back(df, slope, h_low, table, down_p)
    da, da_low, do, sums_one = expand_back(
        dz, du, n1, r1, row_vals, table, up_p, attn_p
    )
    dq, dk, dv, dk_other, dv_other = attend_back(qkv, kv_other, bias, mixed, lse, do)
    back = core_swap(jnp.concatenate([dk_other, dv_other], axis=1))
    dqkv, head_sums, *g_attn = project_grads(
        x, mixed, da_low, dq, jnp.concatenate([dk, dv], axis=1), back, table, attn_p
    )
    frames_grad = project_back(da, dqkv, table, attn_p)
    grad_long, grad_short = from_clips(frames_grad, core, depth)

    def by_units(value):
        return [value[:, i * units : (i + 1) * units] for i in range(N_MP)]

    down_share = mp_scatter(by_units(dp_scatter(g_down))).T
    up_share = mp_scatter(by_units(dp_scatter(g_up)))
    attn_sum = dp_scatter(g_attn)
    attn_parts = [
        jnp.concatenate(
            [
                attn_sum[:, i * width + j * group : i * width + (j + 1) * group]
                for i in range(4)
            ],
            axis=1,
        )
        for j in range(N_MP)
    ]
    attn_share = mp_scatter(attn_parts)
    input_share = jnp.stack([attn_share[:, i * group : (i + 1) * group] for i in range(3)])
    output_share = attn_share[:, 3 * group :].T

    head_sums = jnp.stack([head_sums[0, :width], head_sums[0, 2 * width :]])
    head_sums = jnp.take(head_sums.reshape(2, N_MP, group), relative, axis=1)
    up_b_sums = jnp.take(up_b_sums.reshape(N_MP, units), relative, axis=0)
    small = jnp.concatenate(
        [
            sums_one[:3].reshape(-1),
            sums_two[:3].reshape(-1),
            head_sums.reshape(-1),
            up_b_sums.reshape(-1),
        ]
    )
    small = small_sum(small.reshape(-1, LANES)).reshape(-1)
    row_grads = small[: 6 * width].reshape(6, width)
    row_cols = width // (n_dp * N_MP)
    row_share = lax.dynamic_slice(row_grads, (0, (mine * N_MP + depth) * row_cols), (6, row_cols))
    head_grads = small[6 * width : 8 * width].reshape(2, N_MP, group)
    head_cols = group // n_dp
    head_share = lax.dynamic_slice(head_grads, (0, depth, mine * head_cols), (2, 1, head_cols))
    up_b_grads = small[8 * width :].reshape(N_MP, units)
    up_cols = units // n_dp
    up_b_share = lax.dynamic_slice(up_b_grads, (depth, mine * up_cols), (1, up_cols))
    return (
        result_long,
        result_short,
        grad_long.astype(F32),
        grad_short.astype(F32),
        input_share,
        output_share,
        up_share,
        down_share,
        head_share,
        up_b_share,
        row_share,
    )


def solution(mesh):
    return jax.shard_map(
        on_device,
        mesh=mesh,
        in_specs=(
            P("dp", "mp", None),
            P("dp", "mp", None),
            P("dp"),
            P("dp"),
            P(None, "dp", "mp"),
            P("mp", "dp"),
            P("dp", "mp"),
            P("mp", "dp"),
            P(None, "mp", "dp"),
            P("mp", "dp"),
            P(None, ("dp", "mp")),
            P("dp", "mp", None),
            P("dp", "mp", None),
        ),
        out_specs=(
            P("dp", "mp", None),
            P("dp", "mp", None),
            P("dp", "mp", None),
            P("dp", "mp", None),
            P(None, "dp", "mp"),
            P("mp", "dp"),
            P("dp", "mp"),
            P("mp", "dp"),
            P(None, "mp", "dp"),
            P("mp", "dp"),
            P(None, ("dp", "mp")),
        ),
        check_vma=False,
    )
```

```python
import functools

import jax
import jax.numpy as jnp
from jax import lax
from jax.experimental import pallas as pl
from jax.experimental.pallas import tpu as pltpu
from jax.sharding import PartitionSpec as P

HEAD = 64
EPS = 1e-05
NEG_FILL = -1e30
SCALE = HEAD ** (-0.5)
N_MP = 4
WIDTH = 768
SHARED = 16
LANES = 128
Q_TILE = 256
F32 = jnp.float32
BF16 = jnp.bfloat16
NT = (((1,), (1,)), ((), ()))
NN = (((1,), (0,)), ((), ()))
TN = (((0,), (0,)), ((), ()))


def dot(left, right, dims):
    return lax.dot_general(left, right, dims, preferred_element_type=F32)


def mp_swap(value, step):
    return lax.ppermute(value, "mp", [(i, i ^ step) for i in range(N_MP)])


def dp_swap(value, target):
    size = lax.axis_size("dp")
    return lax.ppermute(value, "dp", [(i, target(i)) for i in range(size)])


def core_swap(value):
    return dp_swap(value, lambda i: i ^ 1)


def clip_blocks(long_rows, short_rows, core):
    block = short_rows.shape[1]
    keep = lax.dynamic_slice_in_dim(long_rows, core * block, block, 0)
    away = lax.dynamic_slice_in_dim(long_rows, (1 - core) * block, block, 0)
    back = core_swap(away)
    first = jnp.where(core == 0, keep, back)
    second = jnp.where(core == 0, back, keep)
    return jnp.stack([first, second, short_rows[0], short_rows[1]])


def to_clips(blocks, depth):
    parts = []
    for step in range(N_MP):
        piece = lax.dynamic_index_in_dim(blocks, depth ^ step, 0, keepdims=False)
        parts.append(piece if step == 0 else mp_swap(piece, step))
    return parts


def from_clips(rows):
    block = rows.shape[0] // N_MP
    parts = []
    for step in range(N_MP):
        piece = rows[step * block : (step + 1) * block]
        parts.append(piece if step == 0 else mp_swap(piece, step))
    return parts


def frames_of(parts, core, depth):
    blocks = jnp.stack(parts)
    first, second, short_a, short_b = (
        lax.dynamic_index_in_dim(blocks, depth ^ i, 0, keepdims=False) for i in range(N_MP)
    )
    keep = jnp.where(core == 0, first, second)
    away = jnp.where(core == 0, second, first)
    back = core_swap(away)
    low = jnp.where(core == 0, keep, back)
    high = jnp.where(core == 0, back, keep)
    return jnp.concatenate([low, high], axis=0)[None], jnp.stack([short_a, short_b])


def flip(index, late):
    return index ^ ((4 if late else 2) if index % 2 == 0 else (2 if late else 4))


def block_table(mine, size):
    if size != 8:
        return jnp.zeros((1,), jnp.int32)
    early = jnp.where(mine % 2 == 0, 2, 4)
    late = 6 - early
    relative = [0, early, late, 6, 1, 1 ^ late, 1 ^ early, 7]
    return jnp.stack([mine ^ r for r in relative]).astype(jnp.int32)


def early(i):
    return flip(i, False)


def late(i):
    return flip(i, True)


def tie(*values):
    return lax.optimization_barrier(values)


def swap_plane(plane):
    return plane + [core_swap(piece) for piece in plane]


def to_slab(parts):
    return jnp.concatenate(parts, axis=1)


def mp_gather(shard):
    return [shard] + [mp_swap(shard, step) for step in range(1, N_MP)]


def scatter_core(parts):
    keep, away = parts
    return keep.astype(F32) + core_swap(away).astype(F32)


def next_away(total, blocks, rows):
    return total[blocks // 2 * rows :].astype(BF16)


def next_total(total, back, blocks, rows):
    keep = jnp.concatenate([total[: blocks // 2 * rows], total[blocks * rows :]])
    return keep + back.astype(F32)


def mp_away(parts):
    return [mp_swap(parts[step].astype(BF16), step) for step in range(1, N_MP)]


def mp_total(own, backs):
    for back in backs:
        own = own + back.astype(F32)
    return own


def block_rows(pieces):
    return WIDTH // len(pieces)


class Weights:
    def __init__(self, pieces, table, held, sems, lo, tile):
        self.held, self.tile = held, tile
        self.copies = []
        for t in range(held.shape[2] // tile):
            row = []
            for k, piece in enumerate(pieces):
                copy = pltpu.make_async_copy(
                    piece.at[pl.ds(0, held.shape[1]), pl.ds(lo + t * tile, tile)],
                    held.at[table[k], :, pl.ds(t * tile, tile)],
                    sems.at[t, k],
                )
                copy.start()
                row.append(copy)
            self.copies.append(row)

    def get(self, t):
        for copy in self.copies[t]:
            copy.wait()
        at = t * self.tile
        count, rows, _ = self.held.shape
        return self.held[:, :, at : at + self.tile].reshape(count * rows, self.tile)


def weight_scratch(pieces, cols, tile):
    return [
        pltpu.VMEM((len(pieces), block_rows(pieces), cols), BF16),
        pltpu.SemaphoreType.DMA((cols // tile, len(pieces))),
    ]


def grad_shapes(pieces, cols, extra=0):
    count, rows = len(pieces), block_rows(pieces)
    if count == 1:
        return [jax.ShapeDtypeStruct((rows, cols), F32)]
    return [jax.ShapeDtypeStruct((count // 2 * rows + extra, cols), BF16)] * 2


def store_grad(value, table, held, outs, at):
    held[...] = value.reshape(held.shape)
    count, rows, cols = held.shape
    half = count // len(outs)
    for r in range(count):
        out, row = outs[r // half], r % half * rows
        out[row : row + rows, at : at + cols] = held[table[r]].astype(out.dtype)


def cost(micros):
    return pl.CostEstimate(
        flops=int(micros * 1.1e9), bytes_accessed=int(micros * 1e5), transcendentals=0
    )


def call(body, name, micros, outs, arrays, table, pieces, scratch):
    vmem = pl.BlockSpec(memory_space=pltpu.VMEM)
    return pl.pallas_call(
        body,
        out_shape=tuple(outs),
        in_specs=[pl.BlockSpec(memory_space=pltpu.SMEM)]
        + [vmem] * len(arrays)
        + [pl.BlockSpec(memory_space=pl.ANY)] * len(pieces),
        out_specs=(vmem,) * len(outs),
        scratch_shapes=scratch,
        compiler_params=pltpu.CompilerParams(vmem_limit_bytes=56 << 20),
        cost_estimate=cost(micros),
        name=name,
    )(table, *arrays, *pieces)


def like(shape, kind):
    return jax.ShapeDtypeStruct(shape, kind)


def attend_kernel(q_ref, k_ref, v_ref, kp_ref, vp_ref, bias_ref, o_ref, lse_ref):
    rows = q_ref.shape[0]
    keys = jnp.concatenate([k_ref[...], kp_ref[...]], axis=0)
    values = jnp.concatenate([v_ref[...], vp_ref[...]], axis=0)
    bias = bias_ref[...]
    tile = min(rows, Q_TILE)
    low = lax.broadcasted_iota(jnp.int32, (tile, LANES), 1) < HEAD
    for start in range(0, rows, tile):
        q = q_ref[start : start + tile, :]
        outs, logs = [], []
        for half in range(2):
            here = low if half == 0 else ~low
            q_here = jnp.where(here, q, jnp.zeros_like(q))
            scores = dot(q_here, keys, NT) + bias
            top = jnp.max(scores, axis=-1, keepdims=True)
            raised = jnp.exp(scores - top)
            total = jnp.sum(raised, axis=-1, keepdims=True)
            mixed = dot(raised.astype(BF16), values, NN)
            outs.append(mixed / total)
            logs.append(top + jnp.log(total))
        o_ref[start : start + tile, :] = jnp.where(low, outs[0], outs[1]).astype(BF16)
        lse_ref[start : start + tile, :] = jnp.where(low, logs[0], logs[1])


def attend(qkv, kv_other, bias):
    rows, width = qkv.shape[0], qkv.shape[1] // 3
    pairs = width // LANES
    spec = lambda base: pl.BlockSpec((rows, LANES), lambda p: (0, base + p))
    return pl.pallas_call(
        attend_kernel,
        out_shape=(
            jax.ShapeDtypeStruct((rows, width), BF16),
            jax.ShapeDtypeStruct((rows, width), F32),
        ),
        grid=(pairs,),
        in_specs=[
            spec(0),
            spec(pairs),
            spec(2 * pairs),
            spec(0),
            spec(pairs),
            pl.BlockSpec((1, 2 * rows), lambda p: (0, 0)),
        ],
        out_specs=(spec(0), spec(0)),
        compiler_params=pltpu.CompilerParams(vmem_limit_bytes=56 << 20),
        cost_estimate=cost(15),
        name="attend",
    )(qkv, qkv, qkv, kv_other, kv_other, bias)


def attend_back_kernel(
    q_ref, k_ref, v_ref, kp_ref, vp_ref, bias_ref, o_ref, lse_ref, do_ref,
    dq_ref, dk_ref, dv_ref, dkp_ref, dvp_ref,
):
    rows = q_ref.shape[0]
    keys = jnp.concatenate([k_ref[...], kp_ref[...]], axis=0)
    values = jnp.concatenate([v_ref[...], vp_ref[...]], axis=0)
    bias = bias_ref[...]
    tile = min(rows, Q_TILE)
    low = lax.broadcasted_iota(jnp.int32, (tile, LANES), 1) < HEAD
    dk = jnp.zeros((LANES, 2 * rows), F32)
    dv = jnp.zeros((LANES, 2 * rows), F32)
    for start in range(0, rows, tile):
        at = slice(start, start + tile)
        q, do = q_ref[at, :], do_ref[at, :]
        product = o_ref[at, :].astype(F32) * do.astype(F32)
        lse = lse_ref[at, :]
        outs = []
        for half in range(2):
            here = low if half == 0 else ~low
            q_here = jnp.where(here, q, jnp.zeros_like(q))
            do_here = jnp.where(here, do, jnp.zeros_like(do))
            inner = jnp.sum(jnp.where(here, product, 0.0), axis=-1, keepdims=True)
            log = lse[:, half * HEAD : half * HEAD + 1]
            soft = jnp.exp(dot(q_here, keys, NT) + bias - log)
            grad = (soft * (dot(do_here, values, NT) - inner)).astype(BF16)
            outs.append(dot(grad, keys, NN))
            dk = dk + dot(q_here, grad, TN)
            dv = dv + dot(do_here, soft.astype(BF16), TN)
        dq_ref[at, :] = (jnp.where(low, outs[0], outs[1]) * SCALE).astype(BF16)
    dk, dv = dk.T, dv.T
    dk_ref[...] = dk[:rows]
    dkp_ref[...] = dk[rows:].astype(BF16)
    dv_ref[...] = dv[:rows]
    dvp_ref[...] = dv[rows:].astype(BF16)


def attend_back(qkv, kv_other, bias, out, lse, grad_out):
    rows, width = out.shape
    pairs = width // LANES
    spec = lambda base: pl.BlockSpec((rows, LANES), lambda p: (0, base + p))
    shape = lambda kind: jax.ShapeDtypeStruct((rows, width), kind)
    return pl.pallas_call(
        attend_back_kernel,
        out_shape=(shape(BF16), shape(F32), shape(F32), shape(BF16), shape(BF16)),
        grid=(pairs,),
        in_specs=[
            spec(0),
            spec(pairs),
            spec(2 * pairs),
            spec(0),
            spec(pairs),
            pl.BlockSpec((1, 2 * rows), lambda p: (0, 0)),
            spec(0),
            spec(0),
            spec(0),
        ],
        out_specs=(spec(0),) * 5,
        compiler_params=pltpu.CompilerParams(vmem_limit_bytes=56 << 20),
        cost_estimate=cost(18),
        name="attend_back",
    )(qkv, qkv, qkv, kv_other, kv_other, bias, out, lse, grad_out)


def gelu_parts(v):
    cdf = 0.5 * (1.0 + lax.erf(v * (2.0 ** -0.5)))
    pdf = jnp.exp(-0.5 * v * v) * 0.3989422804014327
    return v * cdf, cdf + v * pdf


def norm(values):
    center = values - jnp.mean(values, axis=-1, keepdims=True)
    inv_dev = lax.rsqrt(jnp.mean(center * center, axis=-1, keepdims=True) + EPS)
    return center * inv_dev, inv_dev


def norm_back(scaled, normed, inv_dev):
    return inv_dev * (
        scaled
        - jnp.mean(scaled, axis=-1, keepdims=True)
        - normed * jnp.mean(scaled * normed, axis=-1, keepdims=True)
    )


def total(value):
    return jnp.sum(value, axis=0, keepdims=True)


def project(x, head_rows, table, pieces):
    rows, width = x.shape
    n = len(pieces)

    def body(table, x_ref, bias_ref, *refs):
        pieces, (qkv_ref, kv_ref, held, sems) = refs[:n], refs[n:]
        weights = Weights(pieces, table, held, sems, 0, width)
        x = x_ref[...]
        for i in range(3):
            value = dot(x, weights.get(i), NN) + bias_ref[i : i + 1, :]
            value = value.astype(BF16)
            if i == 0:
                value = (value.astype(F32) * SCALE).astype(BF16)
            else:
                kv_ref[:, (i - 1) * width : i * width] = value
            qkv_ref[:, i * width : (i + 1) * width] = value

    return call(
        body,
        "project",
        7,
        [like((rows, 3 * width), BF16), like((rows, 2 * width), BF16)],
        [x, head_rows],
        table,
        pieces,
        weight_scratch(pieces, 3 * width, width),
    )


def mix_and_expand(x, mixed, row_vals, up_b, table, out_pieces, up_pieces):
    rows, width = x.shape
    hidden = up_b.shape[1]
    tile = hidden // 6
    n = len(out_pieces)

    def body(table, x_ref, mixed_ref, rows_ref, up_b_ref, *refs):
        out_p, up_p = refs[:n], refs[n : 2 * n]
        n1_ref, r1_ref, h_ref, act_ref, slope_ref, w_out, sems_out, w_up, sems_up = refs[2 * n :]
        out_w = Weights(out_p, table, w_out, sems_out, 3 * width, width)
        up_w = Weights(up_p, table, w_up, sems_up, 0, tile)
        attention = dot(mixed_ref[...], out_w.get(0), NT)
        n1, r1 = norm(x_ref[...].astype(F32) + attention + rows_ref[0:1, :])
        n1_ref[...] = n1
        r1_ref[...] = jnp.broadcast_to(r1, r1_ref.shape)
        h_ref[...] = (n1 * rows_ref[1:2, :] + rows_ref[2:3, :]).astype(BF16)
        for t in range(hidden // tile):
            at = slice(t * tile, (t + 1) * tile)
            u = dot(h_ref[...], up_w.get(t), NN) + up_b_ref[:, at]
            act, slope = gelu_parts(u)
            act_ref[:, at] = act.astype(BF16)
            slope_ref[:, at] = slope.astype(BF16)

    return call(
        body,
        "mix_and_expand",
        14,
        [
            like((rows, width), F32),
            like((rows, LANES), F32),
            like((rows, width), BF16),
            like((rows, hidden), BF16),
            like((rows, hidden), BF16),
        ],
        [x, mixed, row_vals, up_b],
        table,
        list(out_pieces) + list(up_pieces),
        weight_scratch(out_pieces, width, width) + weight_scratch(up_pieces, hidden, tile),
    )


def shrink_and_turn(n1, act, cot, row_vals, table, pieces):
    rows, width = n1.shape
    hidden = act.shape[1]
    tile = hidden // 6
    n = len(pieces)
    grads = grad_shapes(pieces, hidden)

    def body(table, n1_ref, act_ref, cot_ref, rows_ref, *refs):
        pieces, (result_ref, dz_ref, df_ref, sums_ref) = refs[:n], refs[n : n + 4]
        grad_refs = refs[n + 4 : n + 4 + len(grads)]
        held, sems, slot = refs[n + 4 + len(grads) :]
        weights = Weights(pieces, table, held, sems, 0, tile)
        feed = jnp.zeros((rows, width), F32)
        for t in range(hidden // tile):
            feed = feed + dot(act_ref[:, t * tile : (t + 1) * tile], weights.get(t), NT)
        h = n1_ref[...] * rows_ref[1:2, :] + rows_ref[2:3, :]
        n2, r2 = norm(h + feed + rows_ref[3:4, :])
        result_ref[...] = (n2 * rows_ref[4:5, :] + rows_ref[5:6, :]).astype(BF16)
        gy = cot_ref[...].astype(F32)
        dz = norm_back(gy * rows_ref[4:5, :], n2, r2)
        dz_ref[...] = dz
        df_ref[...] = dz.astype(BF16)
        sums_ref[0:1, :] = total(dz)
        sums_ref[1:2, :] = total(gy * n2)
        sums_ref[2:3, :] = total(gy)
        for t in range(hidden // tile):
            at = t * tile
            grad = dot(df_ref[...], act_ref[:, at : at + tile], TN)
            store_grad(grad, table, slot, grad_refs, at)

    return call(
        body,
        "shrink_and_turn",
        16,
        [
            like((rows, width), BF16),
            like((rows, width), F32),
            like((rows, width), BF16),
            like((8, width), F32),
        ]
        + grads,
        [n1, act, cot, row_vals],
        table,
        pieces,
        weight_scratch(pieces, hidden, tile)
        + [pltpu.VMEM((n, block_rows(pieces), tile), F32)],
    )


def hidden_back(df, slope, h_low, table, pieces):
    rows, width = df.shape
    hidden = slope.shape[1]
    tile = hidden // 6
    n = len(pieces)
    grads = grad_shapes(pieces, hidden)

    def body(table, df_ref, slope_ref, h_ref, *refs):
        pieces, (du_ref, sums_ref) = refs[:n], refs[n : n + 2]
        grad_refs = refs[n + 2 : n + 2 + len(grads)]
        held, sems, slot = refs[n + 2 + len(grads) :]
        weights = Weights(pieces, table, held, sems, 0, tile)
        for t in range(hidden // tile):
            at = slice(t * tile, (t + 1) * tile)
            du = dot(df_ref[...], weights.get(t), NN) * slope_ref[:, at].astype(F32)
            du = du.astype(BF16)
            du_ref[:, at] = du
            sums_ref[:, at] = total(du.astype(F32))
            store_grad(dot(h_ref[...], du, TN), table, slot, grad_refs, t * tile)

    return call(
        body,
        "hidden_back",
        14,
        [like((rows, hidden), BF16), like((1, hidden), F32)] + grads,
        [df, slope, h_low],
        table,
        pieces,
        weight_scratch(pieces, hidden, tile)
        + [pltpu.VMEM((n, block_rows(pieces), tile), F32)],
    )


def expand_back(dz, du, n1, r1, row_vals, table, up_pieces, out_pieces):
    rows, width = dz.shape
    hidden = du.shape[1]
    tile = hidden // 6
    n = len(up_pieces)

    def body(table, dz_ref, du_ref, n1_ref, r1_ref, rows_ref, *refs):
        up_p, out_p = refs[:n], refs[n : 2 * n]
        da_ref, low_ref, do_ref, sums_ref, w_up, sems_up, w_out, sems_out = refs[2 * n :]
        up_w = Weights(up_p, table, w_up, sems_up, 0, tile)
        out_w = Weights(out_p, table, w_out, sems_out, 3 * width, width)
        dh = dz_ref[...]
        for t in range(hidden // tile):
            dh = dh + dot(du_ref[:, t * tile : (t + 1) * tile], up_w.get(t), NT)
        n1 = n1_ref[...]
        da = norm_back(dh * rows_ref[1:2, :], n1, r1_ref[:, :1])
        da_ref[...] = da
        low_ref[...] = da.astype(BF16)
        sums_ref[0:1, :] = total(da)
        sums_ref[1:2, :] = total(dh * n1)
        sums_ref[2:3, :] = total(dh)
        do_ref[...] = dot(low_ref[...], out_w.get(0), NN).astype(BF16)

    return call(
        body,
        "expand_back",
        12,
        [
            like((rows, width), F32),
            like((rows, width), BF16),
            like((rows, width), BF16),
            like((8, width), F32),
        ],
        [dz, du, n1, r1, row_vals],
        table,
        list(up_pieces) + list(out_pieces),
        weight_scratch(up_pieces, hidden, tile) + weight_scratch(out_pieces, width, width),
    )


def project_grads(x, mixed, da_low, dq, own, back, sums, table, pieces):
    rows, width = x.shape
    n = len(pieces)
    grads = grad_shapes(pieces, 4 * width, SHARED)
    shared = [like((SHARED, 4 * width), F32)]

    def body(table, x_ref, mixed_ref, da_ref, dq_ref, own_ref, back_ref, *refs):
        one_ref, two_ref, up_b_ref, dqkv_ref, shared_ref = refs[:5]
        grad_refs, (slot,) = refs[5 : 5 + len(grads)], refs[5 + len(grads) :]
        dqkv_ref[:, :width] = dq_ref[...]
        dqkv_ref[:, width:] = (own_ref[...] + back_ref[...].astype(F32)).astype(BF16)
        heads = total(dqkv_ref[...].astype(F32))
        shared_ref[...] = jnp.zeros_like(shared_ref)
        shared_ref[0:1, :] = up_b_ref[...]
        for i in range(3):
            shared_ref[1:2, i * width : (i + 1) * width] = one_ref[i : i + 1, :]
        shared_ref[1:2, 3 * width :] = two_ref[0:1, :]
        shared_ref[2:3, :width] = two_ref[1:2, :]
        shared_ref[2:3, width : 2 * width] = two_ref[2:3, :]
        shared_ref[2:3, 2 * width : 3 * width] = heads[:, :width]
        shared_ref[2:3, 3 * width :] = heads[:, 2 * width :]
        if len(grads) > 1:
            for grad_ref in grad_refs:
                grad_ref[grad_ref.shape[0] - SHARED :, :] = shared_ref[...].astype(BF16)
        for i in range(4):
            if i < 3:
                grad = dot(x_ref[...], dqkv_ref[:, i * width : (i + 1) * width], TN)
            else:
                grad = dot(da_ref[...], mixed_ref[...], TN)
            store_grad(grad, table, slot, grad_refs, i * width)

    return call(
        body,
        "project_grads",
        9,
        [like((rows, 3 * width), BF16)] + shared + grads,
        [x, mixed, da_low, dq, own, back, *sums],
        table,
        [],
        [pltpu.VMEM((n, block_rows(pieces), width), F32)],
    )


def project_back(da, dqkv, table, pieces):
    rows, width = da.shape
    n = len(pieces)

    def body(table, da_ref, dqkv_ref, *refs):
        pieces, (out_ref, held, sems) = refs[:n], refs[n:]
        weights = Weights(pieces, table, held, sems, 0, width)
        value = da_ref[...]
        for i in range(3):
            value = value + dot(dqkv_ref[:, i * width : (i + 1) * width], weights.get(i), NT)
        out_ref[...] = value.astype(BF16)

    return call(
        body,
        "project_back",
        8,
        [like((rows, width), BF16)],
        [da, dqkv],
        table,
        pieces,
        weight_scratch(pieces, 3 * width, width),
    )[0]


def small_block(row_params, head_bias, expand_bias, lengths, mine, depth):
    high = lax.reduce_precision(row_params, 8, 7)
    values = jnp.concatenate([high, row_params - high]).astype(BF16)
    out = jnp.zeros((SHARED, WIDTH), BF16)
    rank = mine * N_MP + depth
    out = lax.dynamic_update_slice(out, values, (0, rank * values.shape[1]))
    heads = head_bias[:, 0]
    out = lax.dynamic_update_slice(out, heads, (12, mine * heads.shape[1]))
    out = lax.dynamic_update_slice(out, expand_bias, (14, mine * expand_bias.shape[1]))
    counts = jnp.concatenate([lengths // 32, lengths % 32]).astype(BF16)[None]
    return lax.dynamic_update_slice(out, counts, (15, mine * counts.shape[1]))


def on_device(
    frames_long,
    frames_short,
    length_long,
    length_short,
    input_proj,
    output_proj,
    expand_weight,
    shrink_weight,
    head_bias,
    expand_bias,
    row_params,
    cotangent_long,
    cotangent_short,
):
    mine = lax.axis_index("dp")
    depth = lax.axis_index("mp")
    n_dp = lax.axis_size("dp")
    fast = n_dp == 8
    core = mine % 2
    block = frames_short.shape[1]
    shard, group = input_proj.shape[1:]
    units = expand_weight.shape[1]
    width = group * N_MP
    table = block_table(mine, n_dp)

    joined = jnp.concatenate(
        [input_proj[0], input_proj[1], input_proj[2], output_proj.T], axis=1
    )
    shrink_t = shrink_weight.T
    attn_parts = mp_gather(joined)
    lengths = jnp.concatenate([length_long, length_short])
    small = small_block(row_params, head_bias, expand_bias, lengths, mine, depth)
    small_parts = mp_gather(small)
    x_blocks = clip_blocks(frames_long[0], frames_short, core)
    cot_blocks = clip_blocks(cotangent_long[0], cotangent_short, core)
    *attn_parts, expand_weight, x_blocks = tie(*attn_parts, expand_weight, x_blocks)
    order = [p[:, i * group : (i + 1) * group] for i in range(4) for p in attn_parts]
    attn_slab = jnp.concatenate([to_slab(order), to_slab(small_parts)])
    up_parts = mp_gather(expand_weight)
    if fast:
        attn_one = dp_swap(attn_slab, early)
        attn_two = dp_swap(attn_slab, late)
        attn_one, attn_two, *up_parts, x_blocks = tie(attn_one, attn_two, *up_parts, x_blocks)
        up_slab = to_slab(up_parts)
        attn_three = dp_swap(attn_one, late)
        x_parts = to_clips(x_blocks, depth)
        up_one = dp_swap(up_slab, early)
        up_two = dp_swap(up_slab, late)
        attn_p = swap_plane([attn_slab, attn_one, attn_two, attn_three])
        up_one, up_two, *x_parts, shrink_t, attn_p[7] = tie(
            up_one, up_two, *x_parts, shrink_t, attn_p[7]
        )
        up_three = dp_swap(up_one, late)
        down_slab = to_slab(mp_gather(shrink_t))
        up_p = swap_plane([up_slab, up_one, up_two, up_three])
        small = sum(p[shard:].astype(F32) for p in attn_p)
    else:
        x_parts = to_clips(x_blocks, depth)
        gather = lambda slab: lax.all_gather(slab, "dp", axis=0)
        whole = gather(attn_slab)
        small = jnp.sum(whole[:, shard:].astype(F32), axis=0)
        attn_p = [whole[:, :shard].reshape(width, 4 * width)]
        up_p = [gather(to_slab(up_parts)).reshape(width, -1)]
        down_p = [gather(to_slab(mp_gather(shrink_t))).reshape(width, -1)]

    by_group = [small[:, i * width : (i + 1) * width] for i in range(N_MP)]
    row_vals = sum(part[:6] + part[6:12] for part in by_group)
    heads = jnp.concatenate([part[12:14, :group] for part in by_group], axis=1)
    head_rows = jnp.stack([heads[0], jnp.zeros_like(heads[0]), heads[1]])
    up_b = small[14:15]
    counts = lax.dynamic_slice(small, (15, (mine - core) * 6), (1, 12)).reshape(2, 2, 3)
    counts = counts[:, 0] * 32 + counts[:, 1]
    by_depth = jnp.stack([counts[0, 0], counts[1, 0], counts[core, 1], counts[core, 2]])
    length = by_depth[depth]

    is_long = depth < 2
    source = jnp.repeat(depth ^ jnp.arange(N_MP), block)
    inside = jnp.tile(jnp.arange(block), N_MP)
    stride = jnp.where(is_long, 2 * block, block)
    lead = jnp.where(is_long, block, 0)
    frame = (source * stride + inside).astype(F32)
    own_bias = jnp.where(frame + lead * core < length, 0.0, NEG_FILL)
    other_bias = jnp.where(
        is_long & (frame + lead * (1 - core) < length), 0.0, NEG_FILL
    )
    bias = jnp.concatenate([own_bias, other_bias])[None].astype(F32)

    x = jnp.concatenate(x_parts, axis=0)
    qkv, kv = project(x, head_rows, table, attn_p)
    kv_other = core_swap(kv)
    if fast:
        qkv, kv_other, down_slab, up_p[3], cot_blocks = tie(
            qkv, kv_other, down_slab, up_p[3], cot_blocks
        )
        down_one = dp_swap(down_slab, early)
        down_two = dp_swap(down_slab, late)
    cot_parts = to_clips(cot_blocks, depth)
    mixed, lse = attend(qkv, kv_other, bias)
    if fast:
        mixed, down_one, down_two, *cot_parts = tie(mixed, down_one, down_two, *cot_parts)
        down_three = dp_swap(down_one, late)
        down_p = swap_plane([down_slab, down_one, down_two, down_three])
    cot = jnp.concatenate(cot_parts, axis=0)
    n1, r1, h_low, act, slope = mix_and_expand(
        x, mixed, row_vals, up_b, table, attn_p, up_p
    )
    result, dz, df, sums_two, *g_down = shrink_and_turn(
        n1, act, cot, row_vals, table, down_p
    )
    result_parts = from_clips(result)

    du, up_b_sums, *g_up = hidden_back(df, slope, h_low, table, down_p)
    if fast:
        t_down = scatter_core(g_down)
        a_down = next_away(t_down, 4, shard)
        dz, a_down = tie(dz, a_down)
        b_down = dp_swap(a_down, late)
    da, da_low, do, sums_one = expand_back(
        dz, du, n1, r1, row_vals, table, up_p, attn_p
    )
    if fast:
        t_up = scatter_core(g_up)
        a_up = next_away(t_up, 4, shard)
        t_down = next_total(t_down, b_down, 4, shard)
        a_down = next_away(t_down, 2, shard)
        do, a_up, a_down, *result_parts = tie(do, a_up, a_down, *result_parts)
        b_up = dp_swap(a_up, late)
        b_down = dp_swap(a_down, early)
    result_long, result_short = frames_of(result_parts, core, depth)
    dq, dk, dv, dk_other, dv_other = attend_back(qkv, kv_other, bias, mixed, lse, do)
    back = core_swap(jnp.concatenate([dk_other, dv_other], axis=1))

    def by_units(value):
        return [value[:, i * units : (i + 1) * units] for i in range(N_MP)]

    own = jnp.concatenate([dk, dv], axis=1)
    if fast:
        t_up = next_total(t_up, b_up, 4, shard)
        a_up = next_away(t_up, 2, shard)
        s_down = by_units(next_total(t_down, b_down, 2, shard))
        back, a_up, *s_down = tie(back, a_up, *s_down)
        b_up = dp_swap(a_up, early)
        z_down = mp_away(s_down)
    sums = [sums_one, sums_two, up_b_sums]
    dqkv, shared, *g_attn = project_grads(
        x, mixed, da_low, dq, own, back, sums, table, attn_p
    )
    if fast:
        s_up = by_units(next_total(t_up, b_up, 2, shard))
        dqkv, *s_up = tie(dqkv, *s_up)
        z_up = mp_away(s_up)
    frames_grad = project_back(da, dqkv, table, attn_p)
    grad_parts = from_clips(frames_grad)
    if fast:
        t_attn = scatter_core(g_attn)
        b_attn = dp_swap(next_away(t_attn, 4, shard), late)
        t_attn = next_total(t_attn, b_attn, 4, shard)
        b_attn = dp_swap(next_away(t_attn, 2, shard), early)
        s_attn = next_total(t_attn, b_attn, 2, shard)
    else:
        scatter = lambda g: lax.psum_scatter(g[0], "dp", scatter_dimension=0, tiled=True)
        s_down = by_units(scatter(g_down))
        z_down = mp_away(s_down)
        s_up = by_units(scatter(g_up))
        z_up = mp_away(s_up)
        s_attn = jnp.concatenate([scatter(g_attn), lax.psum(shared, "dp")])
    grad_long, grad_short = frames_of(grad_parts, core, depth)

    def of_group(j):
        main, rest = s_attn[:shard], s_attn[shard:]
        cols = [i * width + j * group for i in range(4)]
        main = jnp.concatenate([main[:, c : c + group] for c in cols], axis=1)
        up_row = rest[0:1, j * units : (j + 1) * units]
        rows = jnp.concatenate([rest[1].reshape(4, width), rest[2, : 2 * width].reshape(2, width)])
        head = jnp.concatenate(
            [rest[2:3, c : c + group] for c in (2 * width + j * group, 3 * width + j * group)],
            axis=1,
        )
        head = jnp.pad(head, ((0, SHARED - 7 - 1), (0, width - 2 * group)))
        return jnp.concatenate([main, up_row, rows, head])

    attn_parts = [of_group(j) for j in range(N_MP)]
    attn_share = mp_total(attn_parts[0], mp_away(attn_parts))
    down_share = mp_total(s_down[0], z_down).T
    up_share = mp_total(s_up[0], z_up)
    input_share = jnp.stack(
        [attn_share[:shard, i * group : (i + 1) * group] for i in range(3)]
    )
    output_share = attn_share[:shard, 3 * group :].T
    rest = attn_share[shard:]
    up_cols, head_cols, row_cols = units // n_dp, group // n_dp, width // (n_dp * N_MP)
    up_b_share = lax.dynamic_slice(rest, (0, mine * up_cols), (1, up_cols))
    row_share = lax.dynamic_slice(rest, (1, (mine * N_MP + depth) * row_cols), (6, row_cols))
    head_share = lax.dynamic_slice(
        rest[7, : 2 * group].reshape(2, 1, group), (0, 0, mine * head_cols), (2, 1, head_cols)
    )
    return (
        result_long,
        result_short,
        grad_long.astype(F32),
        grad_short.astype(F32),
        input_share,
        output_share,
        up_share,
        down_share,
        head_share,
        up_b_share,
        row_share,
    )


def solution(mesh):
    return jax.shard_map(
        on_device,
        mesh=mesh,
        in_specs=(
            P("dp", "mp", None),
            P("dp", "mp", None),
            P("dp"),
            P("dp"),
            P(None, "dp", "mp"),
            P("mp", "dp"),
            P("dp", "mp"),
            P("mp", "dp"),
            P(None, "mp", "dp"),
            P("mp", "dp"),
            P(None, ("dp", "mp")),
            P("dp", "mp", None),
            P("dp", "mp", None),
        ),
        out_specs=(
            P("dp", "mp", None),
            P("dp", "mp", None),
            P("dp", "mp", None),
            P("dp", "mp", None),
            P(None, "dp", "mp"),
            P("mp", "dp"),
            P("dp", "mp"),
            P("mp", "dp"),
            P(None, "mp", "dp"),
            P("mp", "dp"),
            P(None, ("dp", "mp")),
        ),
        check_vma=False,
    )
```

```python
import functools

import jax
import jax.numpy as jnp
from jax import lax
from jax.experimental import pallas as pl
from jax.experimental.pallas import tpu as pltpu
from jax.sharding import PartitionSpec as P

HEAD = 64
EPS = 1e-05
NEG_FILL = -1e30
SCALE = HEAD ** (-0.5)
N_MP = 4
CS = 0.3
WIDTH = 768
SMALL = 16
SHARED = 8
LANES = 128
Q_TILE = 256
F32 = jnp.float32
BF16 = jnp.bfloat16
NT = (((1,), (1,)), ((), ()))
NN = (((1,), (0,)), ((), ()))
TN = (((0,), (0,)), ((), ()))


def dot(left, right, dims):
    return lax.dot_general(left, right, dims, preferred_element_type=F32)


def mp_swap(value, step):
    return lax.ppermute(value, "mp", [(i, i ^ step) for i in range(N_MP)])


def dp_swap(value, target):
    size = lax.axis_size("dp")
    return lax.ppermute(value, "dp", [(i, target(i)) for i in range(size)])


def core_swap(value):
    return dp_swap(value, lambda i: i ^ 1)


def clip_blocks(long_rows, short_rows, core):
    block = short_rows.shape[1]
    keep = lax.dynamic_slice_in_dim(long_rows, core * block, block, 0)
    away = lax.dynamic_slice_in_dim(long_rows, (1 - core) * block, block, 0)
    back = core_swap(away)
    first = jnp.where(core == 0, keep, back)
    second = jnp.where(core == 0, back, keep)
    return jnp.stack([first, second, short_rows[0], short_rows[1]])


def clip_pieces(blocks, depth):
    return [
        lax.dynamic_index_in_dim(blocks, depth ^ step, 0, keepdims=False) for step in range(N_MP)
    ]


def to_clips(blocks, depth):
    pieces = clip_pieces(blocks, depth)
    return pieces[:1] + [mp_swap(pieces[step], step) for step in range(1, N_MP)]


def from_clips(rows):
    block = rows.shape[0] // N_MP
    parts = []
    for step in range(N_MP):
        piece = rows[step * block : (step + 1) * block]
        parts.append(piece if step == 0 else mp_swap(piece, step))
    return parts


def frames_of(parts, core, depth):
    blocks = jnp.stack(parts)
    first, second, short_a, short_b = (
        lax.dynamic_index_in_dim(blocks, depth ^ i, 0, keepdims=False) for i in range(N_MP)
    )
    keep = jnp.where(core == 0, first, second)
    away = jnp.where(core == 0, second, first)
    back = core_swap(away)
    low = jnp.where(core == 0, keep, back)
    high = jnp.where(core == 0, back, keep)
    return jnp.concatenate([low, high], axis=0)[None], jnp.stack([short_a, short_b])


def flip(index, late):
    return index ^ ((4 if late else 2) if index % 2 == 0 else (2 if late else 4))


def block_table(mine, size):
    if size != 8:
        return jnp.zeros((1,), jnp.int32)
    early = jnp.where(mine % 2 == 0, 2, 4)
    late = 6 - early
    relative = [0, early, late, 6, 1, 1 ^ late, 1 ^ early, 7]
    return jnp.stack([mine ^ r for r in relative]).astype(jnp.int32)


def early(i):
    return flip(i, False)


def late(i):
    return flip(i, True)


def tie(*values):
    return lax.optimization_barrier(values)


def swap_plane(plane):
    return plane + [core_swap(piece) for piece in plane]


def to_slab(parts):
    return jnp.concatenate(parts, axis=1)


def mp_gather(shard):
    return [shard] + [mp_swap(shard, step) for step in range(1, N_MP)]


def half_sums(keep, back):
    half = keep.shape[0] // 2
    add = lambda at: (keep[at].astype(F32) + back[at].astype(F32)).astype(BF16)
    return add(slice(0, half)), add(slice(half, None))


def mp_away(parts):
    return [mp_swap(parts[step].astype(BF16), step) for step in range(1, N_MP)]


def mp_total(own, backs):
    for back in backs:
        own = own + back.astype(F32)
    return own


def block_rows(pieces):
    return WIDTH // len(pieces)


class Weights:
    def __init__(self, pieces, table, held, sems, lo, tile):
        self.held, self.tile = held, tile
        self.copies = []
        for t in range(held.shape[2] // tile):
            row = []
            for k, piece in enumerate(pieces):
                copy = pltpu.make_async_copy(
                    piece.at[pl.ds(0, held.shape[1]), pl.ds(lo + t * tile, tile)],
                    held.at[table[k], :, pl.ds(t * tile, tile)],
                    sems.at[t, k],
                )
                copy.start()
                row.append(copy)
            self.copies.append(row)

    def get(self, t):
        for copy in self.copies[t]:
            copy.wait()
        at = t * self.tile
        count, rows, _ = self.held.shape
        return self.held[:, :, at : at + self.tile].reshape(count * rows, self.tile)


def weight_scratch(pieces, cols, tile):
    return [
        pltpu.VMEM((len(pieces), block_rows(pieces), cols), BF16),
        pltpu.SemaphoreType.DMA((cols // tile, len(pieces))),
    ]


def grad_shapes(pieces, cols, extra=0):
    count, rows = len(pieces), block_rows(pieces)
    if count == 1:
        return [jax.ShapeDtypeStruct((1, rows, cols), F32)]
    return [jax.ShapeDtypeStruct((count // 2, rows + extra, cols), BF16)] * 2


def turn_scratch(pieces, rows):
    return [pltpu.VMEM((len(pieces), block_rows(pieces), rows), BF16)] * 2


def turn(value, table, plain, turned):
    plain[...] = value.T.reshape(plain.shape)
    for r in range(plain.shape[0]):
        turned[r] = plain[table[r]]


def store_grad(turned, right, outs, at):
    count, rows, _ = turned.shape
    grad = dot(turned[...].reshape(count * rows, -1), right, NN)
    half, cols = count // len(outs), right.shape[1]
    for r in range(count):
        out = outs[r // half]
        out[r % half, :rows, at : at + cols] = grad[r * rows : (r + 1) * rows].astype(out.dtype)


def cost(micros):
    return pl.CostEstimate(
        flops=int(micros * 1.1e9 * CS), bytes_accessed=int(micros * 1e5 * CS), transcendentals=0
    )


def call(body, name, micros, outs, arrays, table, pieces, scratch):
    vmem = pl.BlockSpec(memory_space=pltpu.VMEM)
    return pl.pallas_call(
        body,
        out_shape=tuple(outs),
        in_specs=[pl.BlockSpec(memory_space=pltpu.SMEM)]
        + [vmem] * len(arrays)
        + [pl.BlockSpec(memory_space=pl.ANY)] * len(pieces),
        out_specs=(vmem,) * len(outs),
        scratch_shapes=scratch,
        compiler_params=pltpu.CompilerParams(vmem_limit_bytes=56 << 20),
        cost_estimate=cost(micros),
        name=name,
    )(table, *arrays, *pieces)


def like(shape, kind):
    return jax.ShapeDtypeStruct(shape, kind)


def attend_kernel(q_ref, k_ref, v_ref, kp_ref, vp_ref, bias_ref, o_ref, lse_ref):
    rows = q_ref.shape[0]
    keys = jnp.concatenate([k_ref[...], kp_ref[...]], axis=0)
    values = jnp.concatenate([v_ref[...], vp_ref[...]], axis=0)
    bias = bias_ref[...]
    tile = min(rows, Q_TILE)
    low = lax.broadcasted_iota(jnp.int32, (tile, LANES), 1) < HEAD
    for start in range(0, rows, tile):
        q = q_ref[start : start + tile, :]
        outs, logs = [], []
        for half in range(2):
            here = low if half == 0 else ~low
            q_here = jnp.where(here, q, jnp.zeros_like(q))
            scores = dot(q_here, keys, NT) + bias
            top = jnp.max(scores, axis=-1, keepdims=True)
            raised = jnp.exp(scores - top)
            total = jnp.sum(raised, axis=-1, keepdims=True)
            mixed = dot(raised.astype(BF16), values, NN)
            outs.append(mixed / total)
            logs.append(top + jnp.log(total))
        o_ref[start : start + tile, :] = jnp.where(low, outs[0], outs[1]).astype(BF16)
        lse_ref[start : start + tile, :] = jnp.where(low, logs[0], logs[1])


def attend(qkv, kv_other, bias):
    rows, width = qkv.shape[0], qkv.shape[1] // 3
    pairs = width // LANES
    spec = lambda base: pl.BlockSpec((rows, LANES), lambda p: (0, base + p))
    return pl.pallas_call(
        attend_kernel,
        out_shape=(
            jax.ShapeDtypeStruct((rows, width), BF16),
            jax.ShapeDtypeStruct((rows, width), F32),
        ),
        grid=(pairs,),
        in_specs=[
            spec(0),
            spec(pairs),
            spec(2 * pairs),
            spec(0),
            spec(pairs),
            pl.BlockSpec((1, 2 * rows), lambda p: (0, 0)),
        ],
        out_specs=(spec(0), spec(0)),
        compiler_params=pltpu.CompilerParams(vmem_limit_bytes=56 << 20),
        cost_estimate=cost(15),
        name="attend",
    )(qkv, qkv, qkv, kv_other, kv_other, bias)


def attend_back_kernel(
    q_ref, k_ref, v_ref, kp_ref, vp_ref, bias_ref, o_ref, lse_ref, do_ref,
    dq_ref, dk_ref, dv_ref, dkp_ref, dvp_ref,
):
    rows = q_ref.shape[0]
    keys = jnp.concatenate([k_ref[...], kp_ref[...]], axis=0)
    values = jnp.concatenate([v_ref[...], vp_ref[...]], axis=0)
    bias = bias_ref[...]
    tile = min(rows, Q_TILE)
    low = lax.broadcasted_iota(jnp.int32, (tile, LANES), 1) < HEAD
    dk = jnp.zeros((LANES, 2 * rows), F32)
    dv = jnp.zeros((LANES, 2 * rows), F32)
    for start in range(0, rows, tile):
        at = slice(start, start + tile)
        q, do = q_ref[at, :], do_ref[at, :]
        product = o_ref[at, :].astype(F32) * do.astype(F32)
        lse = lse_ref[at, :]
        outs = []
        for half in range(2):
            here = low if half == 0 else ~low
            q_here = jnp.where(here, q, jnp.zeros_like(q))
            do_here = jnp.where(here, do, jnp.zeros_like(do))
            inner = jnp.sum(jnp.where(here, product, 0.0), axis=-1, keepdims=True)
            log = lse[:, half * HEAD : half * HEAD + 1]
            soft = jnp.exp(dot(q_here, keys, NT) + bias - log)
            grad = (soft * (dot(do_here, values, NT) - inner)).astype(BF16)
            outs.append(dot(grad, keys, NN))
            dk = dk + dot(q_here, grad, TN)
            dv = dv + dot(do_here, soft.astype(BF16), TN)
        dq_ref[at, :] = (jnp.where(low, outs[0], outs[1]) * SCALE).astype(BF16)
    dk, dv = dk.T, dv.T
    dk_ref[...] = dk[:rows]
    dkp_ref[...] = dk[rows:].astype(BF16)
    dv_ref[...] = dv[:rows]
    dvp_ref[...] = dv[rows:].astype(BF16)


def attend_back(qkv, kv_other, bias, out, lse, grad_out):
    rows, width = out.shape
    pairs = width // LANES
    spec = lambda base: pl.BlockSpec((rows, LANES), lambda p: (0, base + p))
    shape = lambda kind: jax.ShapeDtypeStruct((rows, width), kind)
    return pl.pallas_call(
        attend_back_kernel,
        out_shape=(shape(BF16), shape(F32), shape(F32), shape(BF16), shape(BF16)),
        grid=(pairs,),
        in_specs=[
            spec(0),
            spec(pairs),
            spec(2 * pairs),
            spec(0),
            spec(pairs),
            pl.BlockSpec((1, 2 * rows), lambda p: (0, 0)),
            spec(0),
            spec(0),
            spec(0),
        ],
        out_specs=(spec(0),) * 5,
        compiler_params=pltpu.CompilerParams(vmem_limit_bytes=56 << 20),
        cost_estimate=cost(18),
        name="attend_back",
    )(qkv, qkv, qkv, kv_other, kv_other, bias, out, lse, grad_out)


def gelu_parts(v):
    cdf = 0.5 * (1.0 + lax.erf(v * (2.0 ** -0.5)))
    pdf = jnp.exp(-0.5 * v * v) * 0.3989422804014327
    return v * cdf, cdf + v * pdf


def norm(values):
    center = values - jnp.mean(values, axis=-1, keepdims=True)
    inv_dev = lax.rsqrt(jnp.mean(center * center, axis=-1, keepdims=True) + EPS)
    return center * inv_dev, inv_dev


def norm_back(scaled, normed, inv_dev):
    return inv_dev * (
        scaled
        - jnp.mean(scaled, axis=-1, keepdims=True)
        - normed * jnp.mean(scaled * normed, axis=-1, keepdims=True)
    )


def total(value):
    return jnp.sum(value, axis=0, keepdims=True)


def project(x, head_rows, table, pieces):
    rows, width = x.shape
    n = len(pieces)

    def body(table, x_ref, bias_ref, *refs):
        pieces, (qkv_ref, kv_ref, held, sems) = refs[:n], refs[n:]
        weights = Weights(pieces, table, held, sems, 0, width)
        x = x_ref[...]
        for i in range(3):
            value = dot(x, weights.get(i), NN) + bias_ref[i : i + 1, :]
            value = value.astype(BF16)
            if i == 0:
                value = (value.astype(F32) * SCALE).astype(BF16)
            else:
                kv_ref[:, (i - 1) * width : i * width] = value
            qkv_ref[:, i * width : (i + 1) * width] = value

    return call(
        body,
        "project",
        7,
        [like((rows, 3 * width), BF16), like((rows, 2 * width), BF16)],
        [x, head_rows],
        table,
        pieces,
        weight_scratch(pieces, 3 * width, width),
    )


def mix_and_expand(x, mixed, row_vals, up_b, table, out_pieces, up_pieces):
    rows, width = x.shape
    hidden = up_b.shape[1]
    tile = hidden // 6
    n = len(out_pieces)

    def body(table, x_ref, mixed_ref, rows_ref, up_b_ref, *refs):
        out_p, up_p = refs[:n], refs[n : 2 * n]
        n1_ref, r1_ref, h_ref, act_ref, slope_ref, w_out, sems_out, w_up, sems_up = refs[2 * n :]
        out_w = Weights(out_p, table, w_out, sems_out, 3 * width, width)
        up_w = Weights(up_p, table, w_up, sems_up, 0, tile)
        attention = dot(mixed_ref[...], out_w.get(0), NT)
        n1, r1 = norm(x_ref[...].astype(F32) + attention + rows_ref[0:1, :])
        n1_ref[...] = n1
        r1_ref[...] = jnp.broadcast_to(r1, r1_ref.shape)
        h_ref[...] = (n1 * rows_ref[1:2, :] + rows_ref[2:3, :]).astype(BF16)
        for t in range(hidden // tile):
            at = slice(t * tile, (t + 1) * tile)
            u = dot(h_ref[...], up_w.get(t), NN) + up_b_ref[:, at]
            act, slope = gelu_parts(u)
            act_ref[:, at] = act.astype(BF16)
            slope_ref[:, at] = slope.astype(BF16)

    return call(
        body,
        "mix_and_expand",
        14,
        [
            like((rows, width), F32),
            like((rows, LANES), F32),
            like((rows, width), BF16),
            like((rows, hidden), BF16),
            like((rows, hidden), BF16),
        ],
        [x, mixed, row_vals, up_b],
        table,
        list(out_pieces) + list(up_pieces),
        weight_scratch(out_pieces, width, width) + weight_scratch(up_pieces, hidden, tile),
    )


def shrink_and_turn(n1, act, cot, row_vals, table, pieces):
    rows, width = n1.shape
    hidden = act.shape[1]
    tile = hidden // 6
    n = len(pieces)
    grads = grad_shapes(pieces, hidden)

    def body(table, n1_ref, act_ref, cot_ref, rows_ref, *refs):
        pieces, (result_ref, dz_ref, df_ref, sums_ref) = refs[:n], refs[n : n + 4]
        grad_refs = refs[n + 4 : n + 4 + len(grads)]
        held, sems, plain, turned = refs[n + 4 + len(grads) :]
        weights = Weights(pieces, table, held, sems, hidden, tile)
        feed = jnp.zeros((rows, width), F32)
        for t in range(hidden // tile):
            feed = feed + dot(act_ref[:, t * tile : (t + 1) * tile], weights.get(t), NT)
        h = n1_ref[...] * rows_ref[1:2, :] + rows_ref[2:3, :]
        n2, r2 = norm(h + feed + rows_ref[3:4, :])
        result_ref[...] = (n2 * rows_ref[4:5, :] + rows_ref[5:6, :]).astype(BF16)
        gy = cot_ref[...].astype(F32)
        dz = norm_back(gy * rows_ref[4:5, :], n2, r2)
        dz_ref[...] = dz
        df = dz.astype(BF16)
        df_ref[...] = df
        sums_ref[0:1, :] = total(dz)
        sums_ref[1:2, :] = total(gy * n2)
        sums_ref[2:3, :] = total(gy)
        turn(df, table, plain, turned)
        for t in range(hidden // tile):
            at = t * tile
            store_grad(turned, act_ref[:, at : at + tile], grad_refs, at)

    return call(
        body,
        "shrink_and_turn",
        16,
        [
            like((rows, width), BF16),
            like((rows, width), F32),
            like((rows, width), BF16),
            like((8, width), F32),
        ]
        + grads,
        [n1, act, cot, row_vals],
        table,
        pieces,
        weight_scratch(pieces, hidden, tile) + turn_scratch(pieces, rows),
    )


def hidden_back(df, slope, table, pieces):
    rows, width = df.shape
    hidden = slope.shape[1]
    tile = hidden // 6
    n = len(pieces)

    def body(table, df_ref, slope_ref, *refs):
        pieces, (du_ref, sums_ref, held, sems) = refs[:n], refs[n:]
        weights = Weights(pieces, table, held, sems, hidden, tile)
        for t in range(hidden // tile):
            at = slice(t * tile, (t + 1) * tile)
            du = dot(df_ref[...], weights.get(t), NN) * slope_ref[:, at].astype(F32)
            du = du.astype(BF16)
            du_ref[:, at] = du
            sums_ref[:, at] = total(du.astype(F32))

    return call(
        body,
        "hidden_back",
        8,
        [like((rows, hidden), BF16), like((1, hidden), F32)],
        [df, slope],
        table,
        pieces,
        weight_scratch(pieces, hidden, tile),
    )


def expand_back(dz, du, n1, r1, row_vals, table, up_pieces, out_pieces):
    rows, width = dz.shape
    hidden = du.shape[1]
    tile = hidden // 6
    n = len(up_pieces)

    def body(table, dz_ref, du_ref, n1_ref, r1_ref, rows_ref, *refs):
        up_p, out_p = refs[:n], refs[n : 2 * n]
        da_ref, low_ref, do_ref, sums_ref, w_up, sems_up, w_out, sems_out = refs[2 * n :]
        up_w = Weights(up_p, table, w_up, sems_up, 0, tile)
        out_w = Weights(out_p, table, w_out, sems_out, 3 * width, width)
        dh = dz_ref[...]
        for t in range(hidden // tile):
            dh = dh + dot(du_ref[:, t * tile : (t + 1) * tile], up_w.get(t), NT)
        n1 = n1_ref[...]
        da = norm_back(dh * rows_ref[1:2, :], n1, r1_ref[:, :1])
        da_ref[...] = da
        low_ref[...] = da.astype(BF16)
        sums_ref[0:1, :] = total(da)
        sums_ref[1:2, :] = total(dh * n1)
        sums_ref[2:3, :] = total(dh)
        do_ref[...] = dot(low_ref[...], out_w.get(0), NN).astype(BF16)

    return call(
        body,
        "expand_back",
        12,
        [
            like((rows, width), F32),
            like((rows, width), BF16),
            like((rows, width), BF16),
            like((8, width), F32),
        ],
        [dz, du, n1, r1, row_vals],
        table,
        list(up_pieces) + list(out_pieces),
        weight_scratch(up_pieces, hidden, tile) + weight_scratch(out_pieces, width, width),
    )


def share_rows(shared_ref, grad_refs, rows):
    if len(grad_refs) > 1:
        for grad_ref in grad_refs:
            for r in range(grad_ref.shape[0]):
                grad_ref[r, rows:, :] = shared_ref[...].astype(BF16)


def middle_grads(h_low, du, da_low, mixed, sums, table, pieces):
    rows, width = h_low.shape
    hidden = du.shape[1]
    tile = hidden // 6
    cols = hidden + width
    grads = grad_shapes(pieces, cols, SHARED)

    def body(table, h_ref, du_ref, da_ref, mixed_ref, *refs):
        one_ref, two_ref, up_b_ref, shared_ref = refs[:4]
        grad_refs = refs[4 : 4 + len(grads)]
        plain, turned = refs[4 + len(grads) :]
        shared_ref[...] = jnp.zeros_like(shared_ref)
        shared_ref[0:1, :hidden] = up_b_ref[...]
        for j in range(hidden // width):
            at = slice(j * width, (j + 1) * width)
            shared_ref[1:4, at] = one_ref[:3, :]
            shared_ref[4:7, at] = two_ref[:3, :]
        share_rows(shared_ref, grad_refs, block_rows(pieces))
        turn(h_ref[...], table, plain, turned)
        for t in range(hidden // tile):
            at = t * tile
            store_grad(turned, du_ref[:, at : at + tile], grad_refs, at)
        turn(da_ref[...], table, plain, turned)
        store_grad(turned, mixed_ref[...], grad_refs, hidden)

    return call(
        body,
        "middle_grads",
        10,
        [like((SHARED, cols), F32)] + grads,
        [h_low, du, da_low, mixed, *sums],
        table,
        [],
        turn_scratch(pieces, rows),
    )


def project_grads(x, dq, own, back, table, pieces):
    rows, width = x.shape
    grads = grad_shapes(pieces, 3 * width, SHARED)

    def body(table, x_ref, dq_ref, own_ref, back_ref, *refs):
        dqkv_ref, shared_ref = refs[:2]
        grad_refs = refs[2 : 2 + len(grads)]
        plain, turned = refs[2 + len(grads) :]
        dqkv_ref[:, :width] = dq_ref[...]
        dqkv_ref[:, width:] = (own_ref[...] + back_ref[...].astype(F32)).astype(BF16)
        shared_ref[...] = jnp.zeros_like(shared_ref)
        shared_ref[0:1, :] = total(dqkv_ref[...].astype(F32))
        share_rows(shared_ref, grad_refs, block_rows(pieces))
        turn(x_ref[...], table, plain, turned)
        for i in range(3):
            at = i * width
            store_grad(turned, dqkv_ref[:, at : at + width], grad_refs, at)

    return call(
        body,
        "project_grads",
        8,
        [like((rows, 3 * width), BF16), like((SHARED, 3 * width), F32)] + grads,
        [x, dq, own, back],
        table,
        [],
        turn_scratch(pieces, rows),
    )


def project_back(da, dqkv, table, pieces):
    rows, width = da.shape
    n = len(pieces)

    def body(table, da_ref, dqkv_ref, *refs):
        pieces, (out_ref, held, sems) = refs[:n], refs[n:]
        weights = Weights(pieces, table, held, sems, 0, width)
        value = da_ref[...]
        for i in range(3):
            value = value + dot(dqkv_ref[:, i * width : (i + 1) * width], weights.get(i), NT)
        out_ref[...] = value.astype(BF16)

    return call(
        body,
        "project_back",
        8,
        [like((rows, width), BF16)],
        [da, dqkv],
        table,
        pieces,
        weight_scratch(pieces, 3 * width, width),
    )[0]


def small_block(row_params, head_bias, expand_bias, mine, depth):
    high = lax.reduce_precision(row_params, 8, 7)
    values = jnp.concatenate([high, row_params - high]).astype(BF16)
    out = jnp.zeros((SMALL, WIDTH), BF16)
    rank = mine * N_MP + depth
    out = lax.dynamic_update_slice(out, values, (0, rank * values.shape[1]))
    heads = head_bias[:, 0]
    out = lax.dynamic_update_slice(out, heads, (12, mine * heads.shape[1]))
    return lax.dynamic_update_slice(out, expand_bias, (14, mine * expand_bias.shape[1]))


def key_bias(length_long, length_short, block, core, depth):
    lengths = jnp.concatenate([length_long, length_short])
    other = core_swap(lengths)
    longs = jnp.where(core == 0, jnp.stack([lengths[0], other[0]]), jnp.stack([other[0], lengths[0]]))
    length = jnp.concatenate([longs, lengths[1:]])[depth]
    is_long = depth < 2
    place = lax.broadcasted_iota(jnp.int32, (1, 2 * N_MP * block), 1)
    row = place % (N_MP * block)
    is_own = place < N_MP * block
    source = (row // block) ^ depth
    whose = jnp.where(is_own, core, 1 - core)
    frame = row % block + jnp.where(is_long, (2 * source + whose) * block, source * block)
    counted = (frame < length) & (is_own | is_long)
    return jnp.where(counted, 0.0, NEG_FILL).astype(F32)


def on_device(
    frames_long,
    frames_short,
    length_long,
    length_short,
    input_proj,
    output_proj,
    expand_weight,
    shrink_weight,
    head_bias,
    expand_bias,
    row_params,
    cotangent_long,
    cotangent_short,
):
    mine = lax.axis_index("dp")
    depth = lax.axis_index("mp")
    n_dp = lax.axis_size("dp")
    fast = n_dp == 8
    core = mine % 2
    block = frames_short.shape[1]
    shard, group = input_proj.shape[1:]
    units = expand_weight.shape[1]
    width = group * N_MP
    hidden = units * N_MP
    table = block_table(mine, n_dp)

    joined = jnp.concatenate(
        [input_proj[0], input_proj[1], input_proj[2], output_proj.T], axis=1
    )
    small = small_block(row_params, head_bias, expand_bias, mine, depth)
    attn_parts = mp_gather(jnp.concatenate([joined, small]))
    x_blocks = clip_blocks(frames_long[0], frames_short, core)
    cot_blocks = clip_blocks(cotangent_long[0], cotangent_short, core)
    bias = key_bias(length_long, length_short, block, core, depth)
    feed_shard = jnp.concatenate([expand_weight, shrink_weight.T], axis=1)
    *attn_parts, feed_shard, bias, x_blocks, cot_blocks = tie(
        *attn_parts, feed_shard, bias, x_blocks, cot_blocks
    )
    order = [p[:shard, i * group : (i + 1) * group] for i in range(4) for p in attn_parts]
    attn_slab = jnp.concatenate([to_slab(order), to_slab([p[shard:] for p in attn_parts])])
    feed_parts = mp_gather(feed_shard)
    feed_order = [p[:, i * units : (i + 1) * units] for i in range(2) for p in feed_parts]
    if fast:
        attn_one = dp_swap(attn_slab, early)
        attn_two = dp_swap(attn_slab, late)
        attn_slab, attn_one, attn_two, x_blocks, *feed_order = tie(
            attn_slab, attn_one, attn_two, x_blocks, *feed_order
        )
        attn_p = [attn_slab, attn_one, attn_two, dp_swap(attn_one, late)]
        feed_slab = to_slab(feed_order)
        feed_one = dp_swap(feed_slab, early)
        feed_two = dp_swap(feed_slab, late)
        x_pieces = clip_pieces(x_blocks, depth)
        x_far = mp_swap(x_pieces[3], 3)
        backs = [core_swap(piece) for piece in attn_p + [feed_slab]]
        *backs, x_pieces[1], x_pieces[2] = tie(*backs, x_pieces[1], x_pieces[2])
        x_parts = [x_pieces[0], mp_swap(x_pieces[1], 1), mp_swap(x_pieces[2], 2), x_far]
        attn_p += backs[:4]
        feed_own = backs[4]
        small = sum(p[shard:].astype(F32) for p in attn_p)
    else:
        x_parts = to_clips(x_blocks, depth)
        gather = lambda slab: lax.all_gather(slab, "dp", axis=0)
        whole = gather(attn_slab)
        small = jnp.sum(whole[:, shard:].astype(F32), axis=0)
        attn_p = [whole[:, :shard].reshape(width, 4 * width)]
        feed_p = [gather(to_slab(feed_order)).reshape(width, 2 * hidden)]

    by_group = [small[:, i * width : (i + 1) * width] for i in range(N_MP)]
    row_vals = sum(part[:6] + part[6:12] for part in by_group)
    heads = jnp.concatenate([part[12:14, :group] for part in by_group], axis=1)
    head_rows = jnp.stack([heads[0], jnp.zeros_like(heads[0]), heads[1]])
    up_b = small[14:15]

    x = jnp.concatenate(x_parts, axis=0)
    qkv, kv = project(x, head_rows, table, attn_p)
    if fast:
        kv, feed_one, feed_two = tie(kv, feed_one, feed_two)
    kv_other = core_swap(kv)
    if fast:
        feed_three = dp_swap(feed_one, late)
        feed_p = [feed_slab, feed_one, feed_two]
        feed_back = [feed_own, core_swap(feed_one), core_swap(feed_two)]
        qkv, kv_other, cot_blocks, row_vals, up_b, *feed_back = tie(
            qkv, kv_other, cot_blocks, row_vals, up_b, *feed_back
        )
    cot_parts = to_clips(cot_blocks, depth)
    mixed, lse = attend(qkv, kv_other, bias)
    if fast:
        mixed, feed_three, *cot_parts = tie(mixed, feed_three, *cot_parts)
        feed_p = feed_p + [feed_three] + feed_back + [core_swap(feed_three)]
    n1, r1, h_low, act, slope = mix_and_expand(
        x, mixed, row_vals, up_b, table, attn_p, feed_p
    )
    cot = jnp.concatenate(cot_parts, axis=0)
    result, dz, df, sums_two, *g_down = shrink_and_turn(
        n1, act, cot, row_vals, table, feed_p
    )

    def by_group_of(value, sizes):
        starts = [N_MP * sum(sizes[:i]) for i in range(len(sizes))]
        return [
            jnp.concatenate(
                [value[:, a + j * n : a + (j + 1) * n] for a, n in zip(starts, sizes)], axis=1
            )
            for j in range(N_MP)
        ]

    def last_sum(keep, back):
        return keep[0].astype(F32) + back[0].astype(F32)

    result_parts = from_clips(result)
    du, up_b_sums = hidden_back(df, slope, table, feed_p)
    if fast:
        du, result_parts[3], b_down = tie(du, result_parts[3], core_swap(g_down[1]))
        k_down, a_down = half_sums(g_down[0], b_down)
        dz, a_down = tie(dz, a_down)
        b_down = dp_swap(a_down, late)
    da, da_low, do, sums_one = expand_back(
        dz, du, n1, r1, row_vals, table, feed_p, attn_p
    )
    if fast:
        da_low, b_down, *result_parts = tie(da_low, b_down, *result_parts)
        k_down, a_down = half_sums(k_down, b_down)
        da_low, a_down = tie(da_low, a_down)
        b_down = dp_swap(a_down, early)
    sums = [sums_one, sums_two, up_b_sums]
    mid_shared, *g_mid = middle_grads(h_low, du, da_low, mixed, sums, table, attn_p)
    if fast:
        *g_mid, b_down = tie(*g_mid, b_down)
        b_mid = core_swap(g_mid[1])
        s_down = by_group_of(last_sum(k_down, b_down), [units])
        b_mid, *s_down = tie(b_mid, *s_down)
        k_mid, a_mid = half_sums(g_mid[0], b_mid)
        do, a_mid, *s_down = tie(do, a_mid, *s_down)
        b_mid = dp_swap(a_mid, late)
        z_down = mp_away(s_down)
    dq, dk, dv, dk_other, dv_other = attend_back(qkv, kv_other, bias, mixed, lse, do)
    if fast:
        dk_other, b_mid, *z_down = tie(dk_other, b_mid, *z_down)
    back = core_swap(jnp.concatenate([dk_other, dv_other], axis=1))
    own = jnp.concatenate([dk, dv], axis=1)
    if fast:
        k_mid, a_mid = half_sums(k_mid, b_mid)
        back, a_mid = tie(back, a_mid)
        b_mid = dp_swap(a_mid, early)
    result_long, result_short = frames_of(result_parts, core, depth)
    dqkv, attn_shared, *g_attn = project_grads(x, dq, own, back, table, attn_p)
    if fast:
        *g_attn, b_mid = tie(*g_attn, b_mid)
        b_attn = core_swap(g_attn[1])
        s_mid = by_group_of(last_sum(k_mid, b_mid), [units, group])
        dqkv, *s_mid = tie(dqkv, *s_mid)
        z_mid = mp_away(s_mid)
    frames_grad = project_back(da, dqkv, table, attn_p)
    if fast:
        frames_grad, b_attn, *z_mid = tie(frames_grad, b_attn, *z_mid)
    grad_parts = from_clips(frames_grad)
    if fast:
        k_attn, a_attn = half_sums(g_attn[0], b_attn)
        k_attn, a_attn = half_sums(k_attn, dp_swap(a_attn, late))
        s_attn = last_sum(k_attn, dp_swap(a_attn, early))
    else:
        scatter = lambda g: lax.psum_scatter(g[0][0], "dp", scatter_dimension=0, tiled=True)
        s_down = by_group_of(scatter(g_down), [units])
        z_down = mp_away(s_down)
        s_mid = jnp.concatenate([scatter(g_mid), lax.psum(mid_shared, "dp")])
        s_mid = by_group_of(s_mid, [units, group])
        z_mid = mp_away(s_mid)
        s_attn = jnp.concatenate([scatter(g_attn), lax.psum(attn_shared, "dp")])
    s_attn = by_group_of(s_attn, [group] * 3)
    mid_share = mp_total(s_mid[0], z_mid)
    grad_long, grad_short = frames_of(grad_parts, core, depth)
    attn_share = mp_total(s_attn[0], mp_away(s_attn))
    down_share = mp_total(s_down[0], z_down).T
    up_share = mid_share[:shard, :units]
    output_share = mid_share[:shard, units:].T
    input_share = jnp.stack(
        [attn_share[:shard, i * group : (i + 1) * group] for i in range(3)]
    )
    up_cols, head_cols, row_cols = units // n_dp, group // n_dp, width // (n_dp * N_MP)
    rank = mine * N_MP + depth
    up_b_share = lax.dynamic_slice(mid_share, (shard, mine * up_cols), (1, up_cols))
    row_share = lax.dynamic_slice(mid_share, (shard + 1, rank * row_cols), (6, row_cols))
    head_share = jnp.stack(
        [
            lax.dynamic_slice(attn_share, (shard, at + mine * head_cols), (1, head_cols))
            for at in (0, 2 * group)
        ]
    )
    return (
        result_long,
        result_short,
        grad_long.astype(F32),
        grad_short.astype(F32),
        input_share,
        output_share,
        up_share,
        down_share,
        head_share,
        up_b_share,
        row_share,
    )


def solution(mesh):
    return jax.shard_map(
        on_device,
        mesh=mesh,
        in_specs=(
            P("dp", "mp", None),
            P("dp", "mp", None),
            P("dp"),
            P("dp"),
            P(None, "dp", "mp"),
            P("mp", "dp"),
            P("dp", "mp"),
            P("mp", "dp"),
            P(None, "mp", "dp"),
            P("mp", "dp"),
            P(None, ("dp", "mp")),
            P("dp", "mp", None),
            P("dp", "mp", None),
        ),
        out_specs=(
            P("dp", "mp", None),
            P("dp", "mp", None),
            P("dp", "mp", None),
            P("dp", "mp", None),
            P(None, "dp", "mp"),
            P("mp", "dp"),
            P("dp", "mp"),
            P("mp", "dp"),
            P(None, "mp", "dp"),
            P("mp", "dp"),
            P(None, ("dp", "mp")),
        ),
        check_vma=False,
    )
```

```python
import functools

import jax
import jax.numpy as jnp
from jax import lax
from jax.experimental import pallas as pl
from jax.experimental.pallas import tpu as pltpu
from jax.sharding import PartitionSpec as P

HEAD = 64
EPS = 1e-05
NEG_FILL = -1e30
SCALE = HEAD ** (-0.5)
N_MP = 4
PARTS = 1
CS = 0.3
WIDTH = 768
SMALL = 16
SHARED = 8
LANES = 128
Q_TILE = 256
F32 = jnp.float32
BF16 = jnp.bfloat16
NT = (((1,), (1,)), ((), ()))
NN = (((1,), (0,)), ((), ()))
TN = (((0,), (0,)), ((), ()))


def dot(left, right, dims):
    return lax.dot_general(left, right, dims, preferred_element_type=F32)


def mp_swap(value, step):
    return lax.ppermute(value, "mp", [(i, i ^ step) for i in range(N_MP)])


def dp_swap(value, target):
    size = lax.axis_size("dp")
    return lax.ppermute(value, "dp", [(i, target(i)) for i in range(size)])


def core_swap(value):
    return dp_swap(value, lambda i: i ^ 1)


def clip_blocks(long_rows, short_rows, core):
    block = short_rows.shape[1]
    keep = lax.dynamic_slice_in_dim(long_rows, core * block, block, 0)
    away = lax.dynamic_slice_in_dim(long_rows, (1 - core) * block, block, 0)
    back = core_swap(away)
    first = jnp.where(core == 0, keep, back)
    second = jnp.where(core == 0, back, keep)
    return jnp.stack([first, second, short_rows[0], short_rows[1]])


def clip_pieces(blocks, depth):
    return [
        lax.dynamic_index_in_dim(blocks, depth ^ step, 0, keepdims=False) for step in range(N_MP)
    ]


def to_clips(blocks, depth):
    pieces = clip_pieces(blocks, depth)
    return pieces[:1] + [mp_swap(pieces[step], step) for step in range(1, N_MP)]


def from_clips(rows):
    block = rows.shape[0] // N_MP
    parts = []
    for step in range(N_MP):
        piece = rows[step * block : (step + 1) * block]
        parts.append(piece if step == 0 else mp_swap(piece, step))
    return parts


def frames_of(parts, core, depth):
    blocks = jnp.stack(parts)
    first, second, short_a, short_b = (
        lax.dynamic_index_in_dim(blocks, depth ^ i, 0, keepdims=False) for i in range(N_MP)
    )
    keep = jnp.where(core == 0, first, second)
    away = jnp.where(core == 0, second, first)
    back = core_swap(away)
    low = jnp.where(core == 0, keep, back)
    high = jnp.where(core == 0, back, keep)
    return jnp.concatenate([low, high], axis=0)[None], jnp.stack([short_a, short_b])


def flip(index, late):
    return index ^ ((4 if late else 2) if index % 2 == 0 else (2 if late else 4))


def block_table(mine, size):
    if size != 8:
        return jnp.zeros((1,), jnp.int32)
    early = jnp.where(mine % 2 == 0, 2, 4)
    late = 6 - early
    relative = [0, early, late, 6, 1, 1 ^ late, 1 ^ early, 7]
    return jnp.stack([mine ^ r for r in relative]).astype(jnp.int32)


def early(i):
    return flip(i, False)


def late(i):
    return flip(i, True)


def tie(*values):
    return lax.optimization_barrier(values)


def swap_plane(plane):
    return plane + [core_swap(piece) for piece in plane]


def to_slab(parts):
    return jnp.concatenate(parts, axis=1)


def mp_gather(shard):
    return [shard] + [mp_swap(shard, step) for step in range(1, N_MP)]


def half_sums(keep, back):
    half = keep.shape[0] // 2
    add = lambda at: (keep[at].astype(F32) + back[at].astype(F32)).astype(BF16)
    return add(slice(0, half)), add(slice(half, None))


def mp_away(parts):
    return [mp_swap(parts[step].astype(BF16), step) for step in range(1, N_MP)]


def mp_scatter(parts, depth):
    stack = jnp.stack(parts).astype(BF16)
    stack = jnp.stack(
        [lax.dynamic_index_in_dim(stack, depth ^ i, 0, keepdims=False) for i in range(N_MP)]
    )
    return lax.psum_scatter(stack, "mp", scatter_dimension=0, tiled=True)[0].astype(F32)


def mp_total(own, backs):
    for back in backs:
        own = own + back.astype(F32)
    return own


def block_rows(pieces):
    return WIDTH // len(pieces)


class Weights:
    def __init__(self, pieces, table, held, sems, lo, tile):
        self.held, self.tile = held, tile
        cols, parts = held.shape[2], sems.shape[0]
        self.span, self.copies = cols // parts, []
        for t in range(parts):
            row = []
            for k, piece in enumerate(pieces):
                copy = pltpu.make_async_copy(
                    piece.at[pl.ds(0, held.shape[1]), pl.ds(lo + t * self.span, self.span)],
                    held.at[table[k], :, pl.ds(t * self.span, self.span)],
                    sems.at[t, k],
                )
                copy.start()
                row.append(copy)
            self.copies.append(row)
        self.waited = 0

    def get(self, t):
        at = t * self.tile
        while self.waited * self.span < at + self.tile:
            for copy in self.copies[self.waited]:
                copy.wait()
            self.waited += 1
        count, rows, _ = self.held.shape
        return self.held[:, :, at : at + self.tile].reshape(count * rows, self.tile)


def weight_scratch(pieces, cols, parts=1):
    return [
        pltpu.VMEM((len(pieces), block_rows(pieces), cols), BF16),
        pltpu.SemaphoreType.DMA((parts, len(pieces))),
    ]


def grad_shapes(pieces, cols, extra=0):
    count, rows = len(pieces), block_rows(pieces)
    if count == 1:
        return [jax.ShapeDtypeStruct((1, rows, cols), F32)]
    return [jax.ShapeDtypeStruct((count // 2, rows + extra, cols), BF16)] * 2


def turn_scratch(pieces, rows):
    return [pltpu.VMEM((len(pieces), block_rows(pieces), rows), BF16)] * 2


def turn(value, table, plain, turned):
    plain[...] = value.T.reshape(plain.shape)
    for r in range(plain.shape[0]):
        turned[r] = plain[table[r]]


def stage_scratch(pieces, cols):
    return [
        pltpu.VMEM((g.shape[0], block_rows(pieces), cols), g.dtype)
        for g in grad_shapes(pieces, cols)
    ]


def store_grad(turned, right, stages, at, writes=None, outs=None):
    count, rows, _ = turned.shape
    grad = dot(turned[...].reshape(count * rows, -1), right, NN)
    half, cols = count // len(stages), right.shape[1]
    for r in range(count):
        stage = stages[r // half]
        part = grad[r * rows : (r + 1) * rows].astype(stage.dtype)
        stage[r % half, :rows, at : at + cols] = part
    if writes is not None:
        for stage, out in zip(stages, outs):
            writes.start(
                stage.at[:, :, pl.ds(at, cols)],
                out.at[:, pl.ds(0, rows), pl.ds(at, cols)],
            )


class Writes:
    def __init__(self, sems):
        self.sems, self.copies = sems, []

    def start(self, source, target):
        copy = pltpu.make_async_copy(source, target, self.sems.at[len(self.copies)])
        copy.start()
        self.copies.append(copy)

    def finish(self):
        for copy in self.copies:
            copy.wait()


class Reads:
    def __init__(self, sources, targets, sems):
        self.targets, self.copies = targets, []
        for i, (source, target) in enumerate(zip(sources, targets)):
            copy = pltpu.make_async_copy(source, target, sems.at[i])
            copy.start()
            self.copies.append(copy)

    def get(self, i):
        self.copies[i].wait()
        return self.targets[i]


def read_scratch(arrays):
    return [pltpu.VMEM(a.shape, a.dtype) for a in arrays] + [
        pltpu.SemaphoreType.DMA((len(arrays),))
    ]


def cost(micros):
    return pl.CostEstimate(
        flops=int(micros * 1.1e9 * CS), bytes_accessed=int(micros * 1e5 * CS), transcendentals=0
    )


def call(body, name, micros, outs, arrays, table, pieces, scratch, far=0):
    vmem = pl.BlockSpec(memory_space=pltpu.VMEM)
    away = pl.BlockSpec(memory_space=pl.ANY)
    return pl.pallas_call(
        body,
        out_shape=tuple(outs),
        in_specs=[pl.BlockSpec(memory_space=pltpu.SMEM)]
        + [vmem] * len(arrays)
        + [away] * len(pieces),
        out_specs=(vmem,) * (len(outs) - far) + (away,) * far,
        scratch_shapes=scratch,
        compiler_params=pltpu.CompilerParams(vmem_limit_bytes=56 << 20),
        cost_estimate=cost(micros),
        name=name,
    )(table, *arrays, *pieces)


def like(shape, kind):
    return jax.ShapeDtypeStruct(shape, kind)


def attend_kernel(q_ref, k_ref, v_ref, kp_ref, vp_ref, bias_ref, o_ref, lse_ref):
    rows = q_ref.shape[0]
    keys = jnp.concatenate([k_ref[...], kp_ref[...]], axis=0)
    values = jnp.concatenate([v_ref[...], vp_ref[...]], axis=0)
    bias = bias_ref[...]
    tile = min(rows, Q_TILE)
    low = lax.broadcasted_iota(jnp.int32, (tile, LANES), 1) < HEAD
    for start in range(0, rows, tile):
        q = q_ref[start : start + tile, :]
        outs, logs = [], []
        for half in range(2):
            here = low if half == 0 else ~low
            q_here = jnp.where(here, q, jnp.zeros_like(q))
            scores = dot(q_here, keys, NT) + bias
            top = jnp.max(scores, axis=-1, keepdims=True)
            raised = jnp.exp(scores - top)
            total = jnp.sum(raised, axis=-1, keepdims=True)
            mixed = dot(raised.astype(BF16), values, NN)
            outs.append(mixed / total)
            logs.append(top + jnp.log(total))
        o_ref[start : start + tile, :] = jnp.where(low, outs[0], outs[1]).astype(BF16)
        lse_ref[start : start + tile, :] = jnp.where(low, logs[0], logs[1])


def attend(qkv, kv_other, bias):
    rows, width = qkv.shape[0], qkv.shape[1] // 3
    pairs = width // LANES
    spec = lambda base: pl.BlockSpec((rows, LANES), lambda p: (0, base + p))
    return pl.pallas_call(
        attend_kernel,
        out_shape=(
            jax.ShapeDtypeStruct((rows, width), BF16),
            jax.ShapeDtypeStruct((rows, width), F32),
        ),
        grid=(pairs,),
        in_specs=[
            spec(0),
            spec(pairs),
            spec(2 * pairs),
            spec(0),
            spec(pairs),
            pl.BlockSpec((1, 2 * rows), lambda p: (0, 0)),
        ],
        out_specs=(spec(0), spec(0)),
        compiler_params=pltpu.CompilerParams(vmem_limit_bytes=56 << 20),
        cost_estimate=cost(15),
        name="attend",
    )(qkv, qkv, qkv, kv_other, kv_other, bias)


def attend_back_kernel(
    q_ref, k_ref, v_ref, kp_ref, vp_ref, bias_ref, o_ref, lse_ref, do_ref,
    dq_ref, own_ref, other_ref,
):
    rows = q_ref.shape[0]
    keys = jnp.concatenate([k_ref[...], kp_ref[...]], axis=0)
    values = jnp.concatenate([v_ref[...], vp_ref[...]], axis=0)
    bias = bias_ref[...]
    tile = min(rows, Q_TILE)
    low = lax.broadcasted_iota(jnp.int32, (tile, LANES), 1) < HEAD
    dk = jnp.zeros((LANES, 2 * rows), F32)
    dv = jnp.zeros((LANES, 2 * rows), F32)
    for start in range(0, rows, tile):
        at = slice(start, start + tile)
        q, do = q_ref[at, :], do_ref[at, :]
        product = o_ref[at, :].astype(F32) * do.astype(F32)
        lse = lse_ref[at, :]
        outs = []
        for half in range(2):
            here = low if half == 0 else ~low
            q_here = jnp.where(here, q, jnp.zeros_like(q))
            do_here = jnp.where(here, do, jnp.zeros_like(do))
            inner = jnp.sum(jnp.where(here, product, 0.0), axis=-1, keepdims=True)
            log = lse[:, half * HEAD : half * HEAD + 1]
            soft = jnp.exp(dot(q_here, keys, NT) + bias - log)
            grad = (soft * (dot(do_here, values, NT) - inner)).astype(BF16)
            outs.append(dot(grad, keys, NN))
            dk = dk + dot(q_here, grad, TN)
            dv = dv + dot(do_here, soft.astype(BF16), TN)
        dq_ref[at, :] = (jnp.where(low, outs[0], outs[1]) * SCALE).astype(BF16)
    for i, value in enumerate((dk.T, dv.T)):
        at = slice(i * LANES, (i + 1) * LANES)
        own_ref[:, at] = value[:rows]
        other_ref[:, at] = value[rows:].astype(BF16)


def attend_back(qkv, kv_other, bias, out, lse, grad_out, first, count):
    rows, width = out.shape
    pairs = width // LANES
    spec = lambda base: pl.BlockSpec((rows, LANES), lambda p: (0, base + first + p))
    result = lambda cols: pl.BlockSpec((rows, cols), lambda p: (0, p))
    return pl.pallas_call(
        attend_back_kernel,
        out_shape=(
            jax.ShapeDtypeStruct((rows, count * LANES), BF16),
            jax.ShapeDtypeStruct((rows, 2 * count * LANES), F32),
            jax.ShapeDtypeStruct((rows, 2 * count * LANES), BF16),
        ),
        grid=(count,),
        in_specs=[
            spec(0),
            spec(pairs),
            spec(2 * pairs),
            spec(0),
            spec(pairs),
            pl.BlockSpec((1, 2 * rows), lambda p: (0, 0)),
            spec(0),
            spec(0),
            spec(0),
        ],
        out_specs=(result(LANES), result(2 * LANES), result(2 * LANES)),
        compiler_params=pltpu.CompilerParams(vmem_limit_bytes=56 << 20),
        cost_estimate=cost(3 * count),
        name="attend_back",
    )(qkv, qkv, qkv, kv_other, kv_other, bias, out, lse, grad_out)


def gelu_parts(v):
    cdf = 0.5 * (1.0 + lax.erf(v * (2.0 ** -0.5)))
    pdf = jnp.exp(-0.5 * v * v) * 0.3989422804014327
    return v * cdf, cdf + v * pdf


def norm(values):
    center = values - jnp.mean(values, axis=-1, keepdims=True)
    inv_dev = lax.rsqrt(jnp.mean(center * center, axis=-1, keepdims=True) + EPS)
    return center * inv_dev, inv_dev


def norm_back(scaled, normed, inv_dev):
    return inv_dev * (
        scaled
        - jnp.mean(scaled, axis=-1, keepdims=True)
        - normed * jnp.mean(scaled * normed, axis=-1, keepdims=True)
    )


def total(value):
    return jnp.sum(value, axis=0, keepdims=True)


def project(x, head_rows, table, pieces):
    rows, width = x.shape
    n = len(pieces)

    def body(table, x_ref, bias_ref, *refs):
        pieces, (qkv_ref, kv_ref, held, sems) = refs[:n], refs[n:]
        weights = Weights(pieces, table, held, sems, 0, width)
        x = x_ref[...]
        for i in range(3):
            value = dot(x, weights.get(i), NN) + bias_ref[i : i + 1, :]
            value = value.astype(BF16)
            if i == 0:
                value = (value.astype(F32) * SCALE).astype(BF16)
            else:
                kv_ref[:, (i - 1) * width : i * width] = value
            qkv_ref[:, i * width : (i + 1) * width] = value

    return call(
        body,
        "project",
        7,
        [like((rows, 3 * width), BF16), like((rows, 2 * width), BF16)],
        [x, head_rows],
        table,
        pieces,
        weight_scratch(pieces, 3 * width, 3),
    )


def feed_forward(x, mixed, cot, row_vals, up_b, table, out_pieces, feed_pieces):
    rows, width = x.shape
    hidden = up_b.shape[1]
    count = 6
    tile = hidden // count
    n = len(out_pieces)
    grads = grad_shapes(feed_pieces, hidden)
    g = len(grads)

    def body(table, x_ref, mixed_ref, cot_ref, rows_ref, up_b_ref, *refs):
        out_p, up_p, refs = refs[:n], refs[n : 2 * n], refs[2 * n :]
        sums_ref, r1_ref, n1_out, h_out, slope_out, result_out, dz_out, df_out = refs[:8]
        grad_outs, refs = refs[8 : 8 + g], refs[8 + g :]
        w_out, sems_out, w_up, sems_up, w_down, sems_down, plain, turned = refs[:8]
        n1_ref, h_ref, act_ref, slope_ref, result_ref, dz_ref, df_ref = refs[8:15]
        stages, sems = refs[15 : 15 + g], refs[15 + g]
        writes = Writes(sems)
        out_w = Weights(out_p, table, w_out, sems_out, 3 * width, width)
        up_w = Weights(up_p, table, w_up, sems_up, 0, tile)
        down_w = Weights(up_p, table, w_down, sems_down, hidden, tile)
        attention = dot(mixed_ref[...], out_w.get(0), NT)
        n1, r1 = norm(x_ref[...].astype(F32) + attention + rows_ref[0:1, :])
        n1_ref[...] = n1
        r1_ref[...] = jnp.broadcast_to(r1, r1_ref.shape)
        h_ref[...] = (n1 * rows_ref[1:2, :] + rows_ref[2:3, :]).astype(BF16)
        writes.start(n1_ref, n1_out)
        writes.start(h_ref, h_out)
        spans = [slice(t * tile, (t + 1) * tile) for t in range(count)]
        feed = jnp.zeros((rows, width), F32)
        u = dot(h_ref[...], up_w.get(0), NN)
        for t, at in enumerate(spans):
            down = down_w.get(t)
            later = dot(h_ref[...], up_w.get(t + 1), NN) if t + 1 < count else None
            act, slope = gelu_parts(u + up_b_ref[:, at])
            act_ref[:, at] = act.astype(BF16)
            slope_ref[:, at] = slope.astype(BF16)
            writes.start(slope_ref.at[:, pl.ds(at.start, tile)], slope_out.at[:, pl.ds(at.start, tile)])
            feed = feed + dot(act_ref[:, at], down, NT)
            u = later
        h = n1_ref[...] * rows_ref[1:2, :] + rows_ref[2:3, :]
        n2, r2 = norm(h + feed + rows_ref[3:4, :])
        result_ref[...] = (n2 * rows_ref[4:5, :] + rows_ref[5:6, :]).astype(BF16)
        writes.start(result_ref, result_out)
        gy = cot_ref[...].astype(F32)
        dz = norm_back(gy * rows_ref[4:5, :], n2, r2)
        dz_ref[...] = dz
        writes.start(dz_ref, dz_out)
        df_ref[...] = dz.astype(BF16)
        writes.start(df_ref, df_out)
        sums_ref[0:1, :] = total(dz)
        sums_ref[1:2, :] = total(gy * n2)
        sums_ref[2:3, :] = total(gy)
        turn(df_ref[...], table, plain, turned)
        for at in spans:
            store_grad(turned, act_ref[:, at], stages, at.start, writes, grad_outs)
        writes.finish()

    return call(
        body,
        "feed_forward",
        20,
        [
            like((8, width), F32),
            like((rows, LANES), F32),
            like((rows, width), F32),
            like((rows, width), BF16),
            like((rows, hidden), BF16),
            like((rows, width), BF16),
            like((rows, width), F32),
            like((rows, width), BF16),
        ]
        + grads,
        [x, mixed, cot, row_vals, up_b],
        table,
        list(out_pieces) + list(feed_pieces),
        weight_scratch(out_pieces, width)
        + weight_scratch(feed_pieces, hidden, PARTS)
        + weight_scratch(feed_pieces, hidden, PARTS)
        + turn_scratch(feed_pieces, rows)
        + [
            pltpu.VMEM((rows, width), F32),
            pltpu.VMEM((rows, width), BF16),
            pltpu.VMEM((rows, hidden), BF16),
            pltpu.VMEM((rows, hidden), BF16),
            pltpu.VMEM((rows, width), BF16),
            pltpu.VMEM((rows, width), F32),
            pltpu.VMEM((rows, width), BF16),
        ]
        + stage_scratch(feed_pieces, hidden)
        + [pltpu.SemaphoreType.DMA((5 + count * (1 + g),))],
        far=6 + g,
    )


def hidden_back(df, slope, table, pieces):
    rows, width = df.shape
    hidden = slope.shape[1]
    count = 6
    tile = hidden // count
    n = len(pieces)

    def body(table, df_far, slope_far, *refs):
        pieces, (sums_ref, du_out, df_ref, slope_ref, read_sems) = refs[:n], refs[n : n + 5]
        held, sems, du_ref, write_sems = refs[n + 5 :]
        reads = Reads([df_far], [df_ref], read_sems)
        weights = Weights(pieces, table, held, sems, hidden, tile)
        late = pltpu.make_async_copy(slope_far, slope_ref, read_sems.at[1])
        late.start()
        writes = Writes(write_sems)
        df = reads.get(0)[...]
        dact = dot(df, weights.get(0), NN)
        late.wait()
        for t in range(count):
            at = slice(t * tile, (t + 1) * tile)
            later = dot(df, weights.get(t + 1), NN) if t + 1 < count else None
            du = (dact * slope_ref[:, at].astype(F32)).astype(BF16)
            du_ref[:, at] = du
            writes.start(du_ref.at[:, pl.ds(t * tile, tile)], du_out.at[:, pl.ds(t * tile, tile)])
            sums_ref[:, at] = total(du.astype(F32))
            dact = later
        writes.finish()

    return call(
        body,
        "hidden_back",
        7,
        [like((1, hidden), F32), like((rows, hidden), BF16)],
        [],
        table,
        [df, slope] + list(pieces),
        read_scratch([df, slope])
        + weight_scratch(pieces, hidden, PARTS)
        + [pltpu.VMEM((rows, hidden), BF16), pltpu.SemaphoreType.DMA((count,))],
        far=1,
    )


def expand_back(du, dz, h_low, n1, r1, mixed, row_vals, sums, table, out_pieces, up_pieces):
    rows, width = dz.shape
    hidden = du.shape[1]
    count = 6
    tile = hidden // count
    cols = hidden + width
    n = len(out_pieces)
    grads = grad_shapes(up_pieces, cols, SHARED)
    g = len(grads)
    big = [h_low, du, dz, n1, mixed]

    def body(table, r1_ref, rows_ref, two_ref, up_b_ref, *refs):
        far, refs = refs[:5], refs[5:]
        out_p, up_p, refs = refs[:n], refs[n : 2 * n], refs[2 * n :]
        shared_ref, da_ref, do_ref = refs[:3]
        grad_outs, refs = refs[3 : 3 + g], refs[3 + g :]
        near, read_sems, refs = refs[:5], refs[5], refs[6:]
        w_out, sems_out, w_up, sems_up, plain, turned, low_ref = refs[:7]
        stages, shared_low, sems = refs[7 : 7 + g], refs[7 + g], refs[8 + g]
        reads = Reads(far, near, read_sems)
        writes = Writes(sems)
        up_w = Weights(up_p, table, w_up, sems_up, 0, tile)
        out_w = Weights(out_p, table, w_out, sems_out, 3 * width, width)
        shared_ref[...] = jnp.zeros_like(shared_ref)
        shared_ref[0:1, :hidden] = up_b_ref[...]
        turn(reads.get(0)[...], table, plain, turned)
        du_ref = reads.get(1)
        dh = reads.get(2)[...]
        for t in range(count):
            at = slice(t * tile, (t + 1) * tile)
            store_grad(turned, du_ref[:, at], stages, t * tile, writes, grad_outs)
        for t in range(count):
            at = slice(t * tile, (t + 1) * tile)
            dh = dh + dot(du_ref[:, at], up_w.get(t), NT)
        n1 = reads.get(3)[...]
        da = norm_back(dh * rows_ref[1:2, :], n1, r1_ref[:, :1])
        da_ref[...] = da
        low_ref[...] = da.astype(BF16)
        do_ref[...] = dot(low_ref[...], out_w.get(0), NN).astype(BF16)
        own = [total(da), total(dh * n1), total(dh)]
        for j in range(hidden // width):
            at = slice(j * width, (j + 1) * width)
            for i in range(3):
                shared_ref[1 + i : 2 + i, at] = own[i]
            shared_ref[4:7, at] = two_ref[:3, :]
        if g > 1:
            shared_low[...] = shared_ref[...].astype(BF16)
            for out in grad_outs:
                for r in range(out.shape[0]):
                    writes.start(shared_low, out.at[r, pl.ds(block_rows(up_pieces), SHARED)])
        turn(low_ref[...], table, plain, turned)
        store_grad(turned, reads.get(4)[...], stages, hidden, writes, grad_outs)
        writes.finish()

    return call(
        body,
        "expand_back",
        14,
        [
            like((SHARED, cols), F32),
            like((rows, width), F32),
            like((rows, width), BF16),
        ]
        + grads,
        [r1, row_vals, *sums],
        table,
        big + list(out_pieces) + list(up_pieces),
        read_scratch(big)
        + weight_scratch(out_pieces, width)
        + weight_scratch(up_pieces, hidden, PARTS)
        + turn_scratch(up_pieces, rows)
        + [pltpu.VMEM((rows, width), BF16)]
        + stage_scratch(up_pieces, cols)
        + [
            pltpu.VMEM((SHARED, cols), BF16),
            pltpu.SemaphoreType.DMA((g * (count + 1) + len(up_pieces),)),
        ],
        far=g,
    )


def project_grads(x, parts, table, pieces):
    rows, width = x.shape
    grads = grad_shapes(pieces, 3 * width, SHARED)
    flat = [value for part in parts for value in part]
    g = len(grads)

    def body(table, x_ref, *refs):
        part_refs, refs = refs[: len(flat)], refs[len(flat) :]
        dqkv_ref, shared_ref = refs[:2]
        grad_outs, refs = refs[2 : 2 + g], refs[2 + g :]
        plain, turned = refs[:2]
        stages, shared_low, sems = refs[2 : 2 + g], refs[2 + g], refs[3 + g]
        writes = Writes(sems)
        turn(x_ref[...], table, plain, turned)
        pair = 0
        for i in range(0, len(flat), 3):
            q_ref, own_ref, back_ref = part_refs[i : i + 3]
            cols = q_ref.shape[1]
            dqkv_ref[:, pair * LANES : pair * LANES + cols] = q_ref[...]
            for p in range(cols // LANES):
                for which in range(2):
                    at = slice((2 * p + which) * LANES, (2 * p + which + 1) * LANES)
                    to = (which + 1) * width + (pair + p) * LANES
                    value = own_ref[:, at] + back_ref[:, at].astype(F32)
                    dqkv_ref[:, to : to + LANES] = value.astype(BF16)
            pair += cols // LANES
        for i in range(3):
            at = i * width
            store_grad(turned, dqkv_ref[:, at : at + width], stages, at, writes, grad_outs)
        shared_ref[...] = jnp.zeros_like(shared_ref)
        shared_ref[0:1, :] = total(dqkv_ref[...].astype(F32))
        if g > 1:
            shared_low[...] = shared_ref[...].astype(BF16)
            for out in grad_outs:
                for r in range(out.shape[0]):
                    writes.start(shared_low, out.at[r, pl.ds(block_rows(pieces), SHARED)])
        writes.finish()

    return call(
        body,
        "project_grads",
        7,
        [like((rows, 3 * width), BF16), like((SHARED, 3 * width), F32)] + grads,
        [x] + flat,
        table,
        [],
        turn_scratch(pieces, rows)
        + stage_scratch(pieces, 3 * width)
        + [
            pltpu.VMEM((SHARED, 3 * width), BF16),
            pltpu.SemaphoreType.DMA((3 * g + len(pieces),)),
        ],
        far=g,
    )


def project_back(da, dqkv, table, pieces):
    rows, width = da.shape
    n = len(pieces)

    def body(table, da_ref, dqkv_ref, *refs):
        pieces, (out_ref, held, sems) = refs[:n], refs[n:]
        weights = Weights(pieces, table, held, sems, 0, width)
        value = da_ref[...]
        for i in range(3):
            value = value + dot(dqkv_ref[:, i * width : (i + 1) * width], weights.get(i), NT)
        out_ref[...] = value.astype(BF16)

    return call(
        body,
        "project_back",
        8,
        [like((rows, width), BF16)],
        [da, dqkv],
        table,
        pieces,
        weight_scratch(pieces, 3 * width, 3),
    )[0]


def small_block(row_params, head_bias, expand_bias, mine, depth):
    high = lax.reduce_precision(row_params, 8, 7)
    values = jnp.concatenate([high, row_params - high]).astype(BF16)
    out = jnp.zeros((SMALL, WIDTH), BF16)
    rank = mine * N_MP + depth
    out = lax.dynamic_update_slice(out, values, (0, rank * values.shape[1]))
    heads = head_bias[:, 0]
    out = lax.dynamic_update_slice(out, heads, (12, mine * heads.shape[1]))
    return lax.dynamic_update_slice(out, expand_bias, (14, mine * expand_bias.shape[1]))


def key_bias(length_long, length_short, block, core, depth):
    lengths = jnp.concatenate([length_long, length_short])
    other = core_swap(lengths)
    longs = jnp.where(core == 0, jnp.stack([lengths[0], other[0]]), jnp.stack([other[0], lengths[0]]))
    length = jnp.concatenate([longs, lengths[1:]])[depth]
    is_long = depth < 2
    place = lax.broadcasted_iota(jnp.int32, (1, 2 * N_MP * block), 1)
    row = place % (N_MP * block)
    is_own = place < N_MP * block
    source = (row // block) ^ depth
    whose = jnp.where(is_own, core, 1 - core)
    frame = row % block + jnp.where(is_long, (2 * source + whose) * block, source * block)
    counted = (frame < length) & (is_own | is_long)
    return jnp.where(counted, 0.0, NEG_FILL).astype(F32)


def on_device(
    frames_long,
    frames_short,
    length_long,
    length_short,
    input_proj,
    output_proj,
    expand_weight,
    shrink_weight,
    head_bias,
    expand_bias,
    row_params,
    cotangent_long,
    cotangent_short,
):
    mine = lax.axis_index("dp")
    depth = lax.axis_index("mp")
    n_dp = lax.axis_size("dp")
    fast = n_dp == 8
    core = mine % 2
    block = frames_short.shape[1]
    shard, group = input_proj.shape[1:]
    units = expand_weight.shape[1]
    width = group * N_MP
    hidden = units * N_MP
    table = block_table(mine, n_dp)

    joined = jnp.concatenate(
        [input_proj[0], input_proj[1], input_proj[2], output_proj.T], axis=1
    )
    small = small_block(row_params, head_bias, expand_bias, mine, depth)
    attn_parts = mp_gather(jnp.concatenate([joined, small]))
    x_blocks = clip_blocks(frames_long[0], frames_short, core)
    cot_blocks = clip_blocks(cotangent_long[0], cotangent_short, core)
    bias = key_bias(length_long, length_short, block, core, depth)
    feed_shard = jnp.concatenate([expand_weight, shrink_weight.T], axis=1)
    *attn_parts, feed_shard, bias, x_blocks, cot_blocks = tie(
        *attn_parts, feed_shard, bias, x_blocks, cot_blocks
    )
    order = [p[:shard, i * group : (i + 1) * group] for i in range(4) for p in attn_parts]
    attn_slab = jnp.concatenate([to_slab(order), to_slab([p[shard:] for p in attn_parts])])
    feed_parts = mp_gather(feed_shard)
    feed_order = [p[:, i * units : (i + 1) * units] for i in range(2) for p in feed_parts]
    if fast:
        attn_one = dp_swap(attn_slab, early)
        attn_two = dp_swap(attn_slab, late)
        attn_slab, attn_one, attn_two = tie(attn_slab, attn_one, attn_two)
        attn_p = [attn_slab, attn_one, attn_two, dp_swap(attn_one, late)]
        backs = [core_swap(piece) for piece in attn_p[:3]]
        x_pieces = clip_pieces(x_blocks, depth)
        both = tie(*backs, *x_pieces, *feed_order)
        backs, x_pieces, feed_order = both[:3], both[3:7], both[7:]
        feed_slab = to_slab(feed_order)
        feed_one = dp_swap(feed_slab, early)
        feed_two = dp_swap(feed_slab, late)
        x_parts = [x_pieces[0]] + [mp_swap(x_pieces[i], i) for i in range(1, N_MP)]
        attn_p += list(backs) + [core_swap(attn_p[3])]
        small = sum(p[shard:].astype(F32) for p in attn_p)
    else:
        x_parts = to_clips(x_blocks, depth)
        gather = lambda slab: lax.all_gather(slab, "dp", axis=0)
        whole = gather(attn_slab)
        small = jnp.sum(whole[:, shard:].astype(F32), axis=0)
        attn_p = [whole[:, :shard].reshape(width, 4 * width)]
        feed_p = [gather(to_slab(feed_order)).reshape(width, 2 * hidden)]

    by_group = [small[:, i * width : (i + 1) * width] for i in range(N_MP)]
    row_vals = sum(part[:6] + part[6:12] for part in by_group)
    heads = jnp.concatenate([part[12:14, :group] for part in by_group], axis=1)
    head_rows = jnp.stack([heads[0], jnp.zeros_like(heads[0]), heads[1]])
    up_b = small[14:15]

    x = jnp.concatenate(x_parts, axis=0)
    qkv, kv = project(x, head_rows, table, attn_p)
    if fast:
        kv, feed_one, feed_two = tie(kv, feed_one, feed_two)
    kv_other = core_swap(kv)
    if fast:
        feed_three = dp_swap(feed_one, late)
        feed_p = [feed_slab, feed_one, feed_two]
        feed_back = [core_swap(feed_slab), core_swap(feed_one), core_swap(feed_two)]
        qkv, kv_other, cot_blocks, row_vals, up_b, *feed_back = tie(
            qkv, kv_other, cot_blocks, row_vals, up_b, *feed_back
        )
    cot_parts = to_clips(cot_blocks, depth)
    mixed, lse = attend(qkv, kv_other, bias)
    if fast:
        mixed, feed_three, *cot_parts = tie(mixed, feed_three, *cot_parts)
        feed_p = feed_p + [feed_three] + feed_back + [core_swap(feed_three)]
    cot = jnp.concatenate(cot_parts, axis=0)
    sums_two, r1, n1, h_low, slope, result, dz, df, *g_down = feed_forward(
        x, mixed, cot, row_vals, up_b, table, attn_p, feed_p
    )

    def by_group_of(value, sizes):
        starts = [N_MP * sum(sizes[:i]) for i in range(len(sizes))]
        return [
            jnp.concatenate(
                [value[:, a + j * n : a + (j + 1) * n] for a, n in zip(starts, sizes)], axis=1
            )
            for j in range(N_MP)
        ]

    def last_sum(keep, back):
        return keep[0].astype(F32) + back[0].astype(F32)

    result_parts = from_clips(result)
    up_b_sums, du = hidden_back(df, slope, table, feed_p)
    if fast:
        du, result_parts[3], b_down = tie(du, result_parts[3], core_swap(g_down[1]))
        k_down, a_down = half_sums(g_down[0], b_down)
        dz, a_down = tie(dz, a_down)
        b_down = dp_swap(a_down, late)
    sums = [sums_two, up_b_sums]
    mid_shared, da, do, *g_mid = expand_back(
        du, dz, h_low, n1, r1, mixed, row_vals, sums, table, attn_p, feed_p
    )
    if fast:
        do, b_down, *both = tie(do, b_down, *result_parts, *g_mid)
        result_parts, g_mid = both[:N_MP], both[N_MP:]
        k_down, a_down = half_sums(k_down, b_down)
        do, a_down = tie(do, a_down)
        b_down = dp_swap(a_down, early)
        b_mid = core_swap(g_mid[1])
    result_long, result_short = frames_of(result_parts, core, depth)
    pairs = width // LANES
    first = pairs // 3
    dq_a, own_a, other_a = attend_back(qkv, kv_other, bias, mixed, lse, do, 0, first)
    if fast:
        other_a, b_down, b_mid = tie(other_a, b_down, b_mid)
        k_mid, a_mid = half_sums(g_mid[0], b_mid)
        s_down = by_group_of(last_sum(k_down, b_down), [units])
        do, a_mid, *s_down = tie(do, a_mid, *s_down)
        b_mid = dp_swap(a_mid, late)
        down_share = mp_scatter(s_down, depth)
    back_a = core_swap(other_a)
    dq_b, own_b, other_b = attend_back(
        qkv, kv_other, bias, mixed, lse, do, first, pairs - first
    )
    if fast:
        other_b, back_a, b_mid = tie(other_b, back_a, b_mid)
    back_b = core_swap(other_b)
    if fast:
        k_mid, a_mid = half_sums(k_mid, b_mid)
        back_b, a_mid = tie(back_b, a_mid)
        b_mid = dp_swap(a_mid, early)
    parts = [(dq_a, own_a, back_a), (dq_b, own_b, back_b)]
    dqkv, attn_shared, *g_attn = project_grads(x, parts, table, attn_p)
    if fast:
        *g_attn, b_mid = tie(*g_attn, b_mid)
        b_attn = core_swap(g_attn[1])
        s_mid = by_group_of(last_sum(k_mid, b_mid), [units, group])
        mid_share = mp_scatter(s_mid, depth)
        k_attn, a_attn = half_sums(g_attn[0], b_attn)
        dqkv, a_attn = tie(dqkv, a_attn)
        b_attn = dp_swap(a_attn, late)
    frames_grad = project_back(da, dqkv, table, attn_p)
    if fast:
        frames_grad, b_attn = tie(frames_grad, b_attn)
        k_attn, a_attn = half_sums(k_attn, b_attn)
        frames_grad, a_attn = tie(frames_grad, a_attn)
    grad_parts = from_clips(frames_grad)
    if fast:
        b_attn, *grad_parts = tie(dp_swap(a_attn, early), *grad_parts)
        s_attn = last_sum(k_attn, b_attn)
    else:
        scatter = lambda g: lax.psum_scatter(g[0][0], "dp", scatter_dimension=0, tiled=True)
        down_share = mp_scatter(by_group_of(scatter(g_down), [units]), depth)
        s_mid = jnp.concatenate([scatter(g_mid), lax.psum(mid_shared, "dp")])
        mid_share = mp_scatter(by_group_of(s_mid, [units, group]), depth)
        s_attn = jnp.concatenate([scatter(g_attn), lax.psum(attn_shared, "dp")])
    s_attn = by_group_of(s_attn, [group] * 3)
    grad_long, grad_short = frames_of(grad_parts, core, depth)
    attn_share = mp_total(s_attn[0], mp_away(s_attn))
    down_share = down_share.T
    up_share = mid_share[:shard, :units]
    output_share = mid_share[:shard, units:].T
    input_share = jnp.stack(
        [attn_share[:shard, i * group : (i + 1) * group] for i in range(3)]
    )
    up_cols, head_cols, row_cols = units // n_dp, group // n_dp, width // (n_dp * N_MP)
    rank = mine * N_MP + depth
    up_b_share = lax.dynamic_slice(mid_share, (shard, mine * up_cols), (1, up_cols))
    row_share = lax.dynamic_slice(mid_share, (shard + 1, rank * row_cols), (6, row_cols))
    head_share = jnp.stack(
        [
            lax.dynamic_slice(attn_share, (shard, at + mine * head_cols), (1, head_cols))
            for at in (0, 2 * group)
        ]
    )
    return (
        result_long,
        result_short,
        grad_long.astype(F32),
        grad_short.astype(F32),
        input_share,
        output_share,
        up_share,
        down_share,
        head_share,
        up_b_share,
        row_share,
    )


def solution(mesh):
    return jax.shard_map(
        on_device,
        mesh=mesh,
        in_specs=(
            P("dp", "mp", None),
            P("dp", "mp", None),
            P("dp"),
            P("dp"),
            P(None, "dp", "mp"),
            P("mp", "dp"),
            P("dp", "mp"),
            P("mp", "dp"),
            P(None, "mp", "dp"),
            P("mp", "dp"),
            P(None, ("dp", "mp")),
            P("dp", "mp", None),
            P("dp", "mp", None),
        ),
        out_specs=(
            P("dp", "mp", None),
            P("dp", "mp", None),
            P("dp", "mp", None),
            P("dp", "mp", None),
            P(None, "dp", "mp"),
            P("mp", "dp"),
            P("dp", "mp"),
            P("mp", "dp"),
            P(None, "mp", "dp"),
            P("mp", "dp"),
            P(None, ("dp", "mp")),
        ),
        check_vma=False,
    )
```

```python
import functools

import jax
import jax.numpy as jnp
from jax import lax
from jax.experimental import pallas as pl
from jax.experimental.pallas import tpu as pltpu
from jax.sharding import PartitionSpec as P

HEAD = 64
EPS = 1e-05
NEG_FILL = -1e30
SCALE = HEAD ** (-0.5)
N_MP = 4
PARTS = 1
CS = 0.3
WIDTH = 768
SMALL = 8
SHARED = 8
LANES = 128
Q_TILE = 256
F32 = jnp.float32
BF16 = jnp.bfloat16
NT = (((1,), (1,)), ((), ()))
NN = (((1,), (0,)), ((), ()))
TN = (((0,), (0,)), ((), ()))


def dot(left, right, dims):
    return lax.dot_general(left, right, dims, preferred_element_type=F32)


def mp_swap(value, step):
    return lax.ppermute(value, "mp", [(i, i ^ step) for i in range(N_MP)])


def dp_swap(value, target):
    size = lax.axis_size("dp")
    return lax.ppermute(value, "dp", [(i, target(i)) for i in range(size)])


def core_swap(value):
    return dp_swap(value, lambda i: i ^ 1)


def clip_blocks(long_rows, short_rows, core):
    block = short_rows.shape[1]
    keep = lax.dynamic_slice_in_dim(long_rows, core * block, block, 0)
    away = lax.dynamic_slice_in_dim(long_rows, (1 - core) * block, block, 0)
    back = core_swap(away)
    first = jnp.where(core == 0, keep, back)
    second = jnp.where(core == 0, back, keep)
    return jnp.stack([first, second, short_rows[0], short_rows[1]])


def clip_pieces(blocks, depth):
    return [
        lax.dynamic_index_in_dim(blocks, depth ^ step, 0, keepdims=False) for step in range(N_MP)
    ]


def to_clips(blocks, depth):
    pieces = clip_pieces(blocks, depth)
    return pieces[:1] + [mp_swap(pieces[step], step) for step in range(1, N_MP)]


def from_clips(rows):
    block = rows.shape[0] // N_MP
    parts = []
    for step in range(N_MP):
        piece = rows[step * block : (step + 1) * block]
        parts.append(piece if step == 0 else mp_swap(piece, step))
    return parts


def frames_of(parts, core, depth):
    blocks = jnp.stack(parts)
    first, second, short_a, short_b = (
        lax.dynamic_index_in_dim(blocks, depth ^ i, 0, keepdims=False) for i in range(N_MP)
    )
    keep = jnp.where(core == 0, first, second)
    away = jnp.where(core == 0, second, first)
    back = core_swap(away)
    low = jnp.where(core == 0, keep, back)
    high = jnp.where(core == 0, back, keep)
    return jnp.concatenate([low, high], axis=0)[None], jnp.stack([short_a, short_b])


def flip(index, late):
    return index ^ ((4 if late else 2) if index % 2 == 0 else (2 if late else 4))


def block_table(mine, size):
    if size != 8:
        return jnp.zeros((1,), jnp.int32)
    early = jnp.where(mine % 2 == 0, 2, 4)
    late = 6 - early
    relative = [0, early, late, 6, 1, 1 ^ late, 1 ^ early, 7]
    return jnp.stack([mine ^ r for r in relative]).astype(jnp.int32)


def early(i):
    return flip(i, False)


def late(i):
    return flip(i, True)


def across(i):
    return i ^ 6


def tie(*values):
    return lax.optimization_barrier(values)


def swap_plane(plane):
    return plane + [core_swap(piece) for piece in plane]


def to_slab(parts):
    return jnp.concatenate(parts, axis=1)


def mp_gather(shard):
    return [shard] + [mp_swap(shard, step) for step in range(1, N_MP)]


def half_sums(keep, back):
    half = keep.shape[0] // 2
    add = lambda at: (keep[at].astype(F32) + back[at].astype(F32)).astype(BF16)
    return add(slice(0, half)), add(slice(half, None))


def mp_away(parts):
    return [mp_swap(parts[step].astype(BF16), step) for step in range(1, N_MP)]


def mp_total(own, backs):
    for back in backs:
        own = own + back.astype(F32)
    return own


def block_rows(pieces):
    return WIDTH // len(pieces)


class Weights:
    def __init__(self, pieces, table, held, sems, lo, tile):
        self.held, self.tile = held, tile
        cols, parts = held.shape[2], sems.shape[0]
        self.span, self.copies = cols // parts, []
        for t in range(parts):
            row = []
            for k, piece in enumerate(pieces):
                copy = pltpu.make_async_copy(
                    piece.at[pl.ds(0, held.shape[1]), pl.ds(lo + t * self.span, self.span)],
                    held.at[table[k], :, pl.ds(t * self.span, self.span)],
                    sems.at[t, k],
                )
                copy.start()
                row.append(copy)
            self.copies.append(row)
        self.waited = 0

    def get(self, t):
        at = t * self.tile
        while self.waited * self.span < at + self.tile:
            for copy in self.copies[self.waited]:
                copy.wait()
            self.waited += 1
        count, rows, _ = self.held.shape
        return self.held[:, :, at : at + self.tile].reshape(count * rows, self.tile)


def weight_scratch(pieces, cols, parts=1):
    return [
        pltpu.VMEM((len(pieces), block_rows(pieces), cols), BF16),
        pltpu.SemaphoreType.DMA((parts, len(pieces))),
    ]


def grad_shapes(pieces, cols, extra=0):
    count, rows = len(pieces), block_rows(pieces)
    if count == 1:
        return [jax.ShapeDtypeStruct((1, rows, cols), F32)]
    return [jax.ShapeDtypeStruct((count // 2, rows + extra, cols), BF16)] * 2


def turn_scratch(pieces, rows):
    return [pltpu.VMEM((len(pieces), block_rows(pieces), rows), BF16)] * 2


def turn(value, table, plain, turned):
    plain[...] = value.T.reshape(plain.shape)
    for r in range(plain.shape[0]):
        turned[r] = plain[table[r]]


def stage_scratch(pieces, cols):
    return [
        pltpu.VMEM((g.shape[0], block_rows(pieces), cols), g.dtype)
        for g in grad_shapes(pieces, cols)
    ]


def store_grad(turned, right, stages, at, writes=None, outs=None):
    count, rows, _ = turned.shape
    grad = dot(turned[...].reshape(count * rows, -1), right, NN)
    half, cols = count // len(stages), right.shape[1]
    for r in range(count):
        stage = stages[r // half]
        part = grad[r * rows : (r + 1) * rows].astype(stage.dtype)
        stage[r % half, :rows, at : at + cols] = part
    if writes is not None:
        for stage, out in zip(stages, outs):
            writes.start(
                stage.at[:, :, pl.ds(at, cols)],
                out.at[:, pl.ds(0, rows), pl.ds(at, cols)],
            )


class Writes:
    def __init__(self, sems):
        self.sems, self.copies = sems, []

    def start(self, source, target):
        copy = pltpu.make_async_copy(source, target, self.sems.at[len(self.copies)])
        copy.start()
        self.copies.append(copy)

    def finish(self):
        for copy in self.copies:
            copy.wait()


class Reads:
    def __init__(self, sources, targets, sems):
        self.targets, self.copies = targets, []
        for i, (source, target) in enumerate(zip(sources, targets)):
            copy = pltpu.make_async_copy(source, target, sems.at[i])
            copy.start()
            self.copies.append(copy)

    def get(self, i):
        self.copies[i].wait()
        return self.targets[i]


def read_scratch(arrays):
    return [pltpu.VMEM(a.shape, a.dtype) for a in arrays] + [
        pltpu.SemaphoreType.DMA((len(arrays),))
    ]


def cost(micros):
    return pl.CostEstimate(
        flops=int(micros * 1.1e9 * CS), bytes_accessed=int(micros * 1e5 * CS), transcendentals=0
    )


def call(body, name, micros, outs, arrays, table, pieces, scratch, far=0):
    vmem = pl.BlockSpec(memory_space=pltpu.VMEM)
    away = pl.BlockSpec(memory_space=pl.ANY)
    return pl.pallas_call(
        body,
        out_shape=tuple(outs),
        in_specs=[pl.BlockSpec(memory_space=pltpu.SMEM)]
        + [vmem] * len(arrays)
        + [away] * len(pieces),
        out_specs=(vmem,) * (len(outs) - far) + (away,) * far,
        scratch_shapes=scratch,
        compiler_params=pltpu.CompilerParams(vmem_limit_bytes=56 << 20),
        cost_estimate=cost(micros),
        name=name,
    )(table, *arrays, *pieces)


def like(shape, kind):
    return jax.ShapeDtypeStruct(shape, kind)


def attend_kernel(q_ref, k_ref, v_ref, kp_ref, vp_ref, bias_ref, o_ref, lse_ref):
    rows = q_ref.shape[0]
    keys = jnp.concatenate([k_ref[...], kp_ref[...]], axis=0)
    values = jnp.concatenate([v_ref[...], vp_ref[...]], axis=0)
    bias = bias_ref[...]
    tile = min(rows, Q_TILE)
    low = lax.broadcasted_iota(jnp.int32, (tile, LANES), 1) < HEAD
    for start in range(0, rows, tile):
        q = q_ref[start : start + tile, :]
        outs, logs = [], []
        for half in range(2):
            here = low if half == 0 else ~low
            q_here = jnp.where(here, q, jnp.zeros_like(q))
            scores = dot(q_here, keys, NT) + bias
            top = jnp.max(scores, axis=-1, keepdims=True)
            raised = jnp.exp(scores - top)
            total = jnp.sum(raised, axis=-1, keepdims=True)
            mixed = dot(raised.astype(BF16), values, NN)
            outs.append(mixed / total)
            logs.append(top + jnp.log(total))
        o_ref[start : start + tile, :] = jnp.where(low, outs[0], outs[1]).astype(BF16)
        lse_ref[start : start + tile, :] = jnp.where(low, logs[0], logs[1])


def attend(qkv, kv_other, bias):
    rows, width = qkv.shape[0], qkv.shape[1] // 3
    pairs = width // LANES
    spec = lambda base: pl.BlockSpec((rows, LANES), lambda p: (0, base + p))
    return pl.pallas_call(
        attend_kernel,
        out_shape=(
            jax.ShapeDtypeStruct((rows, width), BF16),
            jax.ShapeDtypeStruct((rows, width), F32),
        ),
        grid=(pairs,),
        in_specs=[
            spec(0),
            spec(pairs),
            spec(2 * pairs),
            spec(0),
            spec(pairs),
            pl.BlockSpec((1, 2 * rows), lambda p: (0, 0)),
        ],
        out_specs=(spec(0), spec(0)),
        compiler_params=pltpu.CompilerParams(vmem_limit_bytes=56 << 20),
        cost_estimate=cost(15),
        name="attend",
    )(qkv, qkv, qkv, kv_other, kv_other, bias)


def attend_back_kernel(
    q_ref, k_ref, v_ref, kp_ref, vp_ref, bias_ref, o_ref, lse_ref, do_ref,
    dq_ref, own_ref, other_ref,
):
    rows = q_ref.shape[0]
    keys = jnp.concatenate([k_ref[...], kp_ref[...]], axis=0)
    values = jnp.concatenate([v_ref[...], vp_ref[...]], axis=0)
    bias = bias_ref[...]
    tile = min(rows, Q_TILE)
    low = lax.broadcasted_iota(jnp.int32, (tile, LANES), 1) < HEAD
    dk = jnp.zeros((LANES, 2 * rows), F32)
    dv = jnp.zeros((LANES, 2 * rows), F32)
    for start in range(0, rows, tile):
        at = slice(start, start + tile)
        q, do = q_ref[at, :], do_ref[at, :]
        product = o_ref[at, :].astype(F32) * do.astype(F32)
        lse = lse_ref[at, :]
        outs = []
        for half in range(2):
            here = low if half == 0 else ~low
            q_here = jnp.where(here, q, jnp.zeros_like(q))
            do_here = jnp.where(here, do, jnp.zeros_like(do))
            inner = jnp.sum(jnp.where(here, product, 0.0), axis=-1, keepdims=True)
            log = lse[:, half * HEAD : half * HEAD + 1]
            soft = jnp.exp(dot(q_here, keys, NT) + bias - log)
            grad = (soft * (dot(do_here, values, NT) - inner)).astype(BF16)
            outs.append(dot(grad, keys, NN))
            dk = dk + dot(q_here, grad, TN)
            dv = dv + dot(do_here, soft.astype(BF16), TN)
        dq_ref[at, :] = (jnp.where(low, outs[0], outs[1]) * SCALE).astype(BF16)
    for i, value in enumerate((dk.T, dv.T)):
        at = slice(i * LANES, (i + 1) * LANES)
        own_ref[:, at] = value[:rows]
        other_ref[:, at] = value[rows:].astype(BF16)


def attend_back(qkv, kv_other, bias, out, lse, grad_out, first, count):
    rows, width = out.shape
    pairs = width // LANES
    spec = lambda base: pl.BlockSpec((rows, LANES), lambda p: (0, base + first + p))
    result = lambda cols: pl.BlockSpec((rows, cols), lambda p: (0, p))
    return pl.pallas_call(
        attend_back_kernel,
        out_shape=(
            jax.ShapeDtypeStruct((rows, count * LANES), BF16),
            jax.ShapeDtypeStruct((rows, 2 * count * LANES), F32),
            jax.ShapeDtypeStruct((rows, 2 * count * LANES), BF16),
        ),
        grid=(count,),
        in_specs=[
            spec(0),
            spec(pairs),
            spec(2 * pairs),
            spec(0),
            spec(pairs),
            pl.BlockSpec((1, 2 * rows), lambda p: (0, 0)),
            spec(0),
            spec(0),
            spec(0),
        ],
        out_specs=(result(LANES), result(2 * LANES), result(2 * LANES)),
        compiler_params=pltpu.CompilerParams(vmem_limit_bytes=56 << 20),
        cost_estimate=cost(3 * count),
        name="attend_back",
    )(qkv, qkv, qkv, kv_other, kv_other, bias, out, lse, grad_out)


def gelu_parts(v):
    cdf = 0.5 * (1.0 + lax.erf(v * (2.0 ** -0.5)))
    pdf = jnp.exp(-0.5 * v * v) * 0.3989422804014327
    return v * cdf, cdf + v * pdf


def norm(values):
    center = values - jnp.mean(values, axis=-1, keepdims=True)
    inv_dev = lax.rsqrt(jnp.mean(center * center, axis=-1, keepdims=True) + EPS)
    return center * inv_dev, inv_dev


def norm_back(scaled, normed, inv_dev):
    return inv_dev * (
        scaled
        - jnp.mean(scaled, axis=-1, keepdims=True)
        - normed * jnp.mean(scaled * normed, axis=-1, keepdims=True)
    )


def total(value):
    return jnp.sum(value, axis=0, keepdims=True)


def project(x, head_rows, table, pieces):
    rows, width = x.shape
    n = len(pieces)

    def body(table, x_ref, bias_ref, *refs):
        pieces, (qkv_ref, kv_ref, held, sems) = refs[:n], refs[n:]
        weights = Weights(pieces, table, held, sems, 0, width)
        x = x_ref[...]
        for i in range(3):
            value = dot(x, weights.get(i), NN) + bias_ref[i : i + 1, :]
            value = value.astype(BF16)
            if i == 0:
                value = (value.astype(F32) * SCALE).astype(BF16)
            else:
                kv_ref[:, (i - 1) * width : i * width] = value
            qkv_ref[:, i * width : (i + 1) * width] = value

    return call(
        body,
        "project",
        7,
        [like((rows, 3 * width), BF16), like((rows, 2 * width), BF16)],
        [x, head_rows],
        table,
        pieces,
        weight_scratch(pieces, 3 * width, 3),
    )


def feed_forward(x, mixed, cot, row_vals, up_b, table, out_pieces, feed_pieces):
    rows, width = x.shape
    hidden = up_b.shape[1]
    count = 6
    tile = hidden // count
    n = len(out_pieces)
    grads = grad_shapes(feed_pieces, hidden)
    g = len(grads)

    def body(table, x_ref, mixed_ref, cot_ref, rows_ref, up_b_ref, *refs):
        out_p, up_p, refs = refs[:n], refs[n : 2 * n], refs[2 * n :]
        sums_ref, r1_ref, n1_out, h_out, slope_out, result_out, dz_out, df_out = refs[:8]
        grad_outs, refs = refs[8 : 8 + g], refs[8 + g :]
        w_out, sems_out, w_up, sems_up, w_down, sems_down, plain, turned = refs[:8]
        n1_ref, h_ref, act_ref, slope_ref, result_ref, dz_ref, df_ref = refs[8:15]
        stages, sems = refs[15 : 15 + g], refs[15 + g]
        writes = Writes(sems)
        out_w = Weights(out_p, table, w_out, sems_out, 3 * width, width)
        up_w = Weights(up_p, table, w_up, sems_up, 0, tile)
        down_w = Weights(up_p, table, w_down, sems_down, hidden, tile)
        attention = dot(mixed_ref[...], out_w.get(0), NT)
        n1, r1 = norm(x_ref[...].astype(F32) + attention + rows_ref[0:1, :])
        n1_ref[...] = n1
        r1_ref[...] = jnp.broadcast_to(r1, r1_ref.shape)
        h_ref[...] = (n1 * rows_ref[1:2, :] + rows_ref[2:3, :]).astype(BF16)
        writes.start(n1_ref, n1_out)
        writes.start(h_ref, h_out)
        spans = [slice(t * tile, (t + 1) * tile) for t in range(count)]
        feed = jnp.zeros((rows, width), F32)
        u = dot(h_ref[...], up_w.get(0), NN)
        for t, at in enumerate(spans):
            down = down_w.get(t)
            later = dot(h_ref[...], up_w.get(t + 1), NN) if t + 1 < count else None
            act, slope = gelu_parts(u + up_b_ref[:, at])
            act_ref[:, at] = act.astype(BF16)
            slope_ref[:, at] = slope.astype(BF16)
            writes.start(slope_ref.at[:, pl.ds(at.start, tile)], slope_out.at[:, pl.ds(at.start, tile)])
            feed = feed + dot(act_ref[:, at], down, NT)
            u = later
        h = n1_ref[...] * rows_ref[1:2, :] + rows_ref[2:3, :]
        n2, r2 = norm(h + feed + rows_ref[3:4, :])
        result_ref[...] = (n2 * rows_ref[4:5, :] + rows_ref[5:6, :]).astype(BF16)
        writes.start(result_ref, result_out)
        gy = cot_ref[...].astype(F32)
        dz = norm_back(gy * rows_ref[4:5, :], n2, r2)
        dz_ref[...] = dz
        writes.start(dz_ref, dz_out)
        df_ref[...] = dz.astype(BF16)
        writes.start(df_ref, df_out)
        sums_ref[0:1, :] = total(dz)
        sums_ref[1:2, :] = total(gy * n2)
        sums_ref[2:3, :] = total(gy)
        turn(df_ref[...], table, plain, turned)
        for at in spans:
            store_grad(turned, act_ref[:, at], stages, at.start, writes, grad_outs)
        writes.finish()

    return call(
        body,
        "feed_forward",
        20,
        [
            like((8, width), F32),
            like((rows, LANES), F32),
            like((rows, width), F32),
            like((rows, width), BF16),
            like((rows, hidden), BF16),
            like((rows, width), BF16),
            like((rows, width), F32),
            like((rows, width), BF16),
        ]
        + grads,
        [x, mixed, cot, row_vals, up_b],
        table,
        list(out_pieces) + list(feed_pieces),
        weight_scratch(out_pieces, width)
        + weight_scratch(feed_pieces, hidden, PARTS)
        + weight_scratch(feed_pieces, hidden, PARTS)
        + turn_scratch(feed_pieces, rows)
        + [
            pltpu.VMEM((rows, width), F32),
            pltpu.VMEM((rows, width), BF16),
            pltpu.VMEM((rows, hidden), BF16),
            pltpu.VMEM((rows, hidden), BF16),
            pltpu.VMEM((rows, width), BF16),
            pltpu.VMEM((rows, width), F32),
            pltpu.VMEM((rows, width), BF16),
        ]
        + stage_scratch(feed_pieces, hidden)
        + [pltpu.SemaphoreType.DMA((5 + count * (1 + g),))],
        far=6 + g,
    )


def hidden_back(df, slope, table, pieces):
    rows, width = df.shape
    hidden = slope.shape[1]
    count = 6
    tile = hidden // count
    n = len(pieces)

    def body(table, df_far, slope_far, *refs):
        pieces, (sums_ref, du_out, df_ref, slope_ref, read_sems) = refs[:n], refs[n : n + 5]
        held, sems, du_ref, write_sems = refs[n + 5 :]
        reads = Reads([df_far], [df_ref], read_sems)
        weights = Weights(pieces, table, held, sems, hidden, tile)
        late = pltpu.make_async_copy(slope_far, slope_ref, read_sems.at[1])
        late.start()
        writes = Writes(write_sems)
        df = reads.get(0)[...]
        dact = dot(df, weights.get(0), NN)
        late.wait()
        for t in range(count):
            at = slice(t * tile, (t + 1) * tile)
            later = dot(df, weights.get(t + 1), NN) if t + 1 < count else None
            du = (dact * slope_ref[:, at].astype(F32)).astype(BF16)
            du_ref[:, at] = du
            writes.start(du_ref.at[:, pl.ds(t * tile, tile)], du_out.at[:, pl.ds(t * tile, tile)])
            sums_ref[:, at] = total(du.astype(F32))
            dact = later
        writes.finish()

    return call(
        body,
        "hidden_back",
        7,
        [like((1, hidden), F32), like((rows, hidden), BF16)],
        [],
        table,
        [df, slope] + list(pieces),
        read_scratch([df, slope])
        + weight_scratch(pieces, hidden, PARTS)
        + [pltpu.VMEM((rows, hidden), BF16), pltpu.SemaphoreType.DMA((count,))],
        far=1,
    )


def expand_back(du, dz, h_low, n1, r1, mixed, row_vals, sums, table, out_pieces, up_pieces):
    rows, width = dz.shape
    hidden = du.shape[1]
    count = 6
    tile = hidden // count
    cols = hidden + width
    n = len(out_pieces)
    grads = grad_shapes(up_pieces, cols, SHARED)
    g = len(grads)
    big = [h_low, du, dz, n1, mixed]

    def body(table, r1_ref, rows_ref, two_ref, up_b_ref, *refs):
        far, refs = refs[:5], refs[5:]
        out_p, up_p, refs = refs[:n], refs[n : 2 * n], refs[2 * n :]
        shared_ref, da_ref, do_ref = refs[:3]
        grad_outs, refs = refs[3 : 3 + g], refs[3 + g :]
        near, read_sems, refs = refs[:5], refs[5], refs[6:]
        w_out, sems_out, w_up, sems_up, plain, turned, low_ref = refs[:7]
        stages, shared_low, sems = refs[7 : 7 + g], refs[7 + g], refs[8 + g]
        reads = Reads(far, near, read_sems)
        writes = Writes(sems)
        up_w = Weights(up_p, table, w_up, sems_up, 0, tile)
        out_w = Weights(out_p, table, w_out, sems_out, 3 * width, width)
        shared_ref[...] = jnp.zeros_like(shared_ref)
        shared_ref[0:1, :hidden] = up_b_ref[...]
        turn(reads.get(0)[...], table, plain, turned)
        du_ref = reads.get(1)
        dh = reads.get(2)[...]
        for t in range(count):
            at = slice(t * tile, (t + 1) * tile)
            store_grad(turned, du_ref[:, at], stages, t * tile, writes, grad_outs)
        for t in range(count):
            at = slice(t * tile, (t + 1) * tile)
            dh = dh + dot(du_ref[:, at], up_w.get(t), NT)
        n1 = reads.get(3)[...]
        da = norm_back(dh * rows_ref[1:2, :], n1, r1_ref[:, :1])
        da_ref[...] = da
        low_ref[...] = da.astype(BF16)
        do_ref[...] = dot(low_ref[...], out_w.get(0), NN).astype(BF16)
        own = [total(da), total(dh * n1), total(dh)]
        for j in range(hidden // width):
            at = slice(j * width, (j + 1) * width)
            for i in range(3):
                shared_ref[1 + i : 2 + i, at] = own[i]
            shared_ref[4:7, at] = two_ref[:3, :]
        if g > 1:
            shared_low[...] = shared_ref[...].astype(BF16)
            for out in grad_outs:
                for r in range(out.shape[0]):
                    writes.start(shared_low, out.at[r, pl.ds(block_rows(up_pieces), SHARED)])
        turn(low_ref[...], table, plain, turned)
        store_grad(turned, reads.get(4)[...], stages, hidden, writes, grad_outs)
        writes.finish()

    return call(
        body,
        "expand_back",
        14,
        [
            like((SHARED, cols), F32),
            like((rows, width), F32),
            like((rows, width), BF16),
        ]
        + grads,
        [r1, row_vals, *sums],
        table,
        big + list(out_pieces) + list(up_pieces),
        read_scratch(big)
        + weight_scratch(out_pieces, width)
        + weight_scratch(up_pieces, hidden, PARTS)
        + turn_scratch(up_pieces, rows)
        + [pltpu.VMEM((rows, width), BF16)]
        + stage_scratch(up_pieces, cols)
        + [
            pltpu.VMEM((SHARED, cols), BF16),
            pltpu.SemaphoreType.DMA((g * (count + 1) + len(up_pieces),)),
        ],
        far=g,
    )


def project_grads(x, parts, table, pieces):
    rows, width = x.shape
    grads = grad_shapes(pieces, 3 * width, SHARED)
    flat = [value for part in parts for value in part]
    g = len(grads)

    def body(table, x_ref, *refs):
        part_refs, refs = refs[: len(flat)], refs[len(flat) :]
        dqkv_ref, shared_ref = refs[:2]
        grad_outs, refs = refs[2 : 2 + g], refs[2 + g :]
        plain, turned = refs[:2]
        stages, shared_low, sems = refs[2 : 2 + g], refs[2 + g], refs[3 + g]
        writes = Writes(sems)
        turn(x_ref[...], table, plain, turned)
        pair = 0
        for i in range(0, len(flat), 3):
            q_ref, own_ref, back_ref = part_refs[i : i + 3]
            cols = q_ref.shape[1]
            dqkv_ref[:, pair * LANES : pair * LANES + cols] = q_ref[...]
            for p in range(cols // LANES):
                for which in range(2):
                    at = slice((2 * p + which) * LANES, (2 * p + which + 1) * LANES)
                    to = (which + 1) * width + (pair + p) * LANES
                    value = own_ref[:, at] + back_ref[:, at].astype(F32)
                    dqkv_ref[:, to : to + LANES] = value.astype(BF16)
            pair += cols // LANES
        for i in range(3):
            at = i * width
            store_grad(turned, dqkv_ref[:, at : at + width], stages, at, writes, grad_outs)
        shared_ref[...] = jnp.zeros_like(shared_ref)
        shared_ref[0:1, :] = total(dqkv_ref[...].astype(F32))
        if g > 1:
            shared_low[...] = shared_ref[...].astype(BF16)
            for out in grad_outs:
                for r in range(out.shape[0]):
                    writes.start(shared_low, out.at[r, pl.ds(block_rows(pieces), SHARED)])
        writes.finish()

    return call(
        body,
        "project_grads",
        7,
        [like((rows, 3 * width), BF16), like((SHARED, 3 * width), F32)] + grads,
        [x] + flat,
        table,
        [],
        turn_scratch(pieces, rows)
        + stage_scratch(pieces, 3 * width)
        + [
            pltpu.VMEM((SHARED, 3 * width), BF16),
            pltpu.SemaphoreType.DMA((3 * g + len(pieces),)),
        ],
        far=g,
    )


def project_back(da, dqkv, table, pieces):
    rows, width = da.shape
    n = len(pieces)

    def body(table, da_ref, dqkv_ref, *refs):
        pieces, (out_ref, held, sems) = refs[:n], refs[n:]
        weights = Weights(pieces, table, held, sems, 0, width)
        value = da_ref[...]
        for i in range(3):
            value = value + dot(dqkv_ref[:, i * width : (i + 1) * width], weights.get(i), NT)
        out_ref[...] = value.astype(BF16)

    return call(
        body,
        "project_back",
        8,
        [like((rows, width), BF16)],
        [da, dqkv],
        table,
        pieces,
        weight_scratch(pieces, 3 * width, 3),
    )[0]


def at_column(values, rows, width, column):
    return lax.dynamic_update_slice(jnp.zeros((rows, width), values.dtype), values, (0, column))


def small_block(row_params, expand_bias, mine, depth):
    high = lax.reduce_precision(row_params, 8, 7)
    column = (mine * N_MP + depth) * row_params.shape[1]
    high_low = [
        at_column(part.astype(BF16), 6, WIDTH, column) for part in (high, row_params - high)
    ]
    bias = at_column(expand_bias, 2, 2 * WIDTH, mine * expand_bias.shape[1])
    return jnp.concatenate([jnp.concatenate(high_low, axis=1), bias])


def key_bias(length_long, length_short, block, core, depth):
    lengths = jnp.concatenate([length_long, length_short])
    other = core_swap(lengths)
    longs = jnp.where(core == 0, jnp.stack([lengths[0], other[0]]), jnp.stack([other[0], lengths[0]]))
    length = jnp.concatenate([longs, lengths[1:]])[depth]
    is_long = depth < 2
    place = lax.broadcasted_iota(jnp.int32, (1, 2 * N_MP * block), 1)
    row = place % (N_MP * block)
    is_own = place < N_MP * block
    source = (row // block) ^ depth
    whose = jnp.where(is_own, core, 1 - core)
    frame = row % block + jnp.where(is_long, (2 * source + whose) * block, source * block)
    counted = (frame < length) & (is_own | is_long)
    return jnp.where(counted, 0.0, NEG_FILL).astype(F32)


def on_device(
    frames_long,
    frames_short,
    length_long,
    length_short,
    input_proj,
    output_proj,
    expand_weight,
    shrink_weight,
    head_bias,
    expand_bias,
    row_params,
    cotangent_long,
    cotangent_short,
):
    mine = lax.axis_index("dp")
    depth = lax.axis_index("mp")
    n_dp = lax.axis_size("dp")
    fast = n_dp == 8
    core = mine % 2
    block = frames_short.shape[1]
    shard, group = input_proj.shape[1:]
    units = expand_weight.shape[1]
    width = group * N_MP
    hidden = units * N_MP
    table = block_table(mine, n_dp)

    joined = jnp.concatenate(
        [input_proj[0], input_proj[1], input_proj[2], output_proj.T], axis=1
    )
    heads = at_column(head_bias[:, 0], SMALL, WIDTH, mine * head_bias.shape[2])
    attn_parts = mp_gather(jnp.concatenate([joined, heads]))
    x_blocks = clip_blocks(frames_long[0], frames_short, core)
    cot_blocks = clip_blocks(cotangent_long[0], cotangent_short, core)
    bias = key_bias(length_long, length_short, block, core, depth)
    feed_shard = jnp.concatenate(
        [
            jnp.concatenate([expand_weight, shrink_weight.T], axis=1),
            small_block(row_params, expand_bias, mine, depth),
        ]
    )
    *attn_parts, feed_shard, bias, x_blocks, cot_blocks = tie(
        *attn_parts, feed_shard, bias, x_blocks, cot_blocks
    )
    order = [p[:shard, i * group : (i + 1) * group] for i in range(4) for p in attn_parts]
    attn_slab = jnp.concatenate([to_slab(order), to_slab([p[shard:] for p in attn_parts])])
    feed_parts = mp_gather(feed_shard)
    feed_order = [p[:, i * units : (i + 1) * units] for i in range(2) for p in feed_parts]
    if fast:
        attn_p = [attn_slab] + [dp_swap(attn_slab, to) for to in (early, late, across)]
        x_pieces = clip_pieces(x_blocks, depth)
        attn_p += [core_swap(piece) for piece in attn_p]
        both = tie(*attn_p, *x_pieces, *feed_order)
        attn_p, x_pieces, feed_order = both[:8], both[8:12], both[12:]
        feed_slab = to_slab(feed_order)
        feed_one = dp_swap(feed_slab, early)
        feed_two = dp_swap(feed_slab, late)
        x_parts = [x_pieces[0]] + [mp_swap(x_pieces[i], i) for i in range(1, N_MP)]
        *x_parts, cot_blocks = tie(*x_parts, cot_blocks)
        heads = sum(p[shard:].astype(F32) for p in attn_p)
    else:
        x_parts = to_clips(x_blocks, depth)
        gather = lambda slab: lax.all_gather(slab, "dp", axis=0)
        whole = gather(attn_slab)
        heads = jnp.sum(whole[:, shard:].astype(F32), axis=0)
        attn_p = [whole[:, :shard].reshape(width, 4 * width)]
        whole = gather(to_slab(feed_order))
        small = jnp.sum(whole[:, shard:].astype(F32), axis=0)
        feed_p = [whole[:, :shard].reshape(width, 2 * hidden)]
    cot_parts = to_clips(cot_blocks, depth)
    heads = jnp.concatenate(
        [heads[:2, i * width : i * width + group] for i in range(N_MP)], axis=1
    )
    head_rows = jnp.stack([heads[0], jnp.zeros_like(heads[0]), heads[1]])

    x = jnp.concatenate(x_parts, axis=0)
    qkv, kv = project(x, head_rows, table, attn_p)
    if fast:
        kv, feed_one, feed_two, cot_parts[3] = tie(kv, feed_one, feed_two, cot_parts[3])
    kv_other = core_swap(kv)
    if fast:
        feed_three = dp_swap(feed_one, late)
        feed_p = [feed_slab, feed_one, feed_two]
    mixed, lse = attend(qkv, kv_other, bias)
    if fast:
        mixed, feed_three, *cot_parts = tie(mixed, feed_three, *cot_parts)
        feed_p = feed_p + [feed_three]
        feed_p = feed_p + [core_swap(piece) for piece in feed_p]
        small = sum(p[shard:].astype(F32) for p in feed_p)
    by_group = [small[:6, i * width : (i + 1) * width] for i in range(2 * N_MP)]
    row_vals = sum(by_group)
    up_b = small[6:7, :hidden]
    cot = jnp.concatenate(cot_parts, axis=0)
    sums_two, r1, n1, h_low, slope, result, dz, df, *g_down = feed_forward(
        x, mixed, cot, row_vals, up_b, table, attn_p, feed_p
    )

    def by_group_of(value, sizes):
        starts = [N_MP * sum(sizes[:i]) for i in range(len(sizes))]
        return [
            jnp.concatenate(
                [value[:, a + j * n : a + (j + 1) * n] for a, n in zip(starts, sizes)], axis=1
            )
            for j in range(N_MP)
        ]

    def last_sum(keep, back):
        return keep[0].astype(F32) + back[0].astype(F32)

    result_parts = from_clips(result)
    up_b_sums, du = hidden_back(df, slope, table, feed_p)
    if fast:
        du, result_parts[3], b_down = tie(du, result_parts[3], core_swap(g_down[1]))
        k_down, a_down = half_sums(g_down[0], b_down)
        dz, a_down = tie(dz, a_down)
        b_down = dp_swap(a_down, late)
    sums = [sums_two, up_b_sums]
    mid_shared, da, do, *g_mid = expand_back(
        du, dz, h_low, n1, r1, mixed, row_vals, sums, table, attn_p, feed_p
    )
    if fast:
        do, b_down, *both = tie(do, b_down, *result_parts, *g_mid)
        result_parts, g_mid = both[:N_MP], both[N_MP:]
        k_down, a_down = half_sums(k_down, b_down)
        do, a_down = tie(do, a_down)
        b_down = dp_swap(a_down, early)
        b_mid = core_swap(g_mid[1])
    result_long, result_short = frames_of(result_parts, core, depth)
    pairs = width // LANES
    first = pairs // 3
    dq_a, own_a, other_a = attend_back(qkv, kv_other, bias, mixed, lse, do, 0, first)
    if fast:
        other_a, b_down, b_mid = tie(other_a, b_down, b_mid)
        k_mid, a_mid = half_sums(g_mid[0], b_mid)
        s_down = by_group_of(last_sum(k_down, b_down), [units])
        do, a_mid, *s_down = tie(do, a_mid, *s_down)
        b_mid = dp_swap(a_mid, late)
        z_down = mp_away(s_down)
    back_a = core_swap(other_a)
    dq_b, own_b, other_b = attend_back(
        qkv, kv_other, bias, mixed, lse, do, first, pairs - first
    )
    if fast:
        other_b, back_a, b_mid, *z_down = tie(other_b, back_a, b_mid, *z_down)
    back_b = core_swap(other_b)
    if fast:
        k_mid, a_mid = half_sums(k_mid, b_mid)
        back_b, a_mid = tie(back_b, a_mid)
        b_mid = dp_swap(a_mid, early)
    parts = [(dq_a, own_a, back_a), (dq_b, own_b, back_b)]
    dqkv, attn_shared, *g_attn = project_grads(x, parts, table, attn_p)
    if fast:
        *g_attn, b_mid = tie(*g_attn, b_mid)
        b_attn = core_swap(g_attn[1])
        s_mid = by_group_of(last_sum(k_mid, b_mid), [units, group])
        k_attn, a_attn = half_sums(g_attn[0], b_attn)
        dqkv, a_attn, *s_mid = tie(dqkv, a_attn, *s_mid)
        b_attn = dp_swap(a_attn, late)
        z_mid = mp_away(s_mid)
    frames_grad = project_back(da, dqkv, table, attn_p)
    if fast:
        frames_grad, b_attn = tie(frames_grad, b_attn)
        k_attn, a_attn = half_sums(k_attn, b_attn)
        frames_grad, a_attn = tie(frames_grad, a_attn)
    grad_parts = from_clips(frames_grad)
    if fast:
        b_attn, *grad_parts = tie(dp_swap(a_attn, early), *grad_parts)
        s_attn = last_sum(k_attn, b_attn)
    else:
        scatter = lambda g: lax.psum_scatter(g[0][0], "dp", scatter_dimension=0, tiled=True)
        s_down = by_group_of(scatter(g_down), [units])
        z_down = mp_away(s_down)
        s_mid = jnp.concatenate([scatter(g_mid), lax.psum(mid_shared, "dp")])
        s_mid = by_group_of(s_mid, [units, group])
        z_mid = mp_away(s_mid)
        s_attn = jnp.concatenate([scatter(g_attn), lax.psum(attn_shared, "dp")])
    s_attn = by_group_of(s_attn, [group] * 3)
    grad_long, grad_short = frames_of(grad_parts, core, depth)
    attn_share = mp_total(s_attn[0], mp_away(s_attn))
    down_share = mp_total(s_down[0], z_down).T
    mid_share = mp_total(s_mid[0], z_mid)
    up_share = mid_share[:shard, :units]
    output_share = mid_share[:shard, units:].T
    input_share = jnp.stack(
        [attn_share[:shard, i * group : (i + 1) * group] for i in range(3)]
    )
    up_cols, head_cols, row_cols = units // n_dp, group // n_dp, width // (n_dp * N_MP)
    rank = mine * N_MP + depth
    up_b_share = lax.dynamic_slice(mid_share, (shard, mine * up_cols), (1, up_cols))
    row_share = lax.dynamic_slice(mid_share, (shard + 1, rank * row_cols), (6, row_cols))
    head_share = jnp.stack(
        [
            lax.dynamic_slice(attn_share, (shard, at + mine * head_cols), (1, head_cols))
            for at in (0, 2 * group)
        ]
    )
    return (
        result_long,
        result_short,
        grad_long.astype(F32),
        grad_short.astype(F32),
        input_share,
        output_share,
        up_share,
        down_share,
        head_share,
        up_b_share,
        row_share,
    )


def solution(mesh):
    return jax.shard_map(
        on_device,
        mesh=mesh,
        in_specs=(
            P("dp", "mp", None),
            P("dp", "mp", None),
            P("dp"),
            P("dp"),
            P(None, "dp", "mp"),
            P("mp", "dp"),
            P("dp", "mp"),
            P("mp", "dp"),
            P(None, "mp", "dp"),
            P("mp", "dp"),
            P(None, ("dp", "mp")),
            P("dp", "mp", None),
            P("dp", "mp", None),
        ),
        out_specs=(
            P("dp", "mp", None),
            P("dp", "mp", None),
            P("dp", "mp", None),
            P("dp", "mp", None),
            P(None, "dp", "mp"),
            P("mp", "dp"),
            P("dp", "mp"),
            P("mp", "dp"),
            P(None, "mp", "dp"),
            P("mp", "dp"),
            P(None, ("dp", "mp")),
        ),
        check_vma=False,
    )
```

```python
import functools

import jax
import jax.numpy as jnp
from jax import lax
from jax.experimental import pallas as pl
from jax.experimental.pallas import tpu as pltpu
from jax.sharding import PartitionSpec as P

HEAD = 64
EPS = 1e-05
NEG_FILL = -1e30
SCALE = HEAD ** (-0.5)
N_MP = 4
PARTS = 1
CS = 0.3
WIDTH = 768
SMALL = 8
SHARED = 8
LANES = 128
Q_TILE = 256
F32 = jnp.float32
BF16 = jnp.bfloat16
NT = (((1,), (1,)), ((), ()))
NN = (((1,), (0,)), ((), ()))
TN = (((0,), (0,)), ((), ()))


def dot(left, right, dims):
    return lax.dot_general(left, right, dims, preferred_element_type=F32)


def mp_swap(value, step):
    return lax.ppermute(value, "mp", [(i, i ^ step) for i in range(N_MP)])


def dp_swap(value, target):
    size = lax.axis_size("dp")
    return lax.ppermute(value, "dp", [(i, target(i)) for i in range(size)])


def core_swap(value):
    return dp_swap(value, lambda i: i ^ 1)


def clip_blocks(long_rows, short_rows, core):
    block = short_rows.shape[1]
    keep = lax.dynamic_slice_in_dim(long_rows, core * block, block, 0)
    away = lax.dynamic_slice_in_dim(long_rows, (1 - core) * block, block, 0)
    back = core_swap(away)
    first = jnp.where(core == 0, keep, back)
    second = jnp.where(core == 0, back, keep)
    return jnp.stack([first, second, short_rows[0], short_rows[1]])


def clip_pieces(blocks, depth):
    return [
        lax.dynamic_index_in_dim(blocks, depth ^ step, 0, keepdims=False) for step in range(N_MP)
    ]


def to_clips(blocks, depth):
    pieces = clip_pieces(blocks, depth)
    return pieces[:1] + [mp_swap(pieces[step], step) for step in range(1, N_MP)]


def from_clips(rows):
    block = rows.shape[0] // N_MP
    parts = []
    for step in range(N_MP):
        piece = rows[step * block : (step + 1) * block]
        parts.append(piece if step == 0 else mp_swap(piece, step))
    return parts


def frames_of(parts, core, depth):
    blocks = jnp.stack(parts)
    first, second, short_a, short_b = (
        lax.dynamic_index_in_dim(blocks, depth ^ i, 0, keepdims=False) for i in range(N_MP)
    )
    keep = jnp.where(core == 0, first, second)
    away = jnp.where(core == 0, second, first)
    back = core_swap(away)
    low = jnp.where(core == 0, keep, back)
    high = jnp.where(core == 0, back, keep)
    return jnp.concatenate([low, high], axis=0)[None], jnp.stack([short_a, short_b])


def flip(index, late):
    return index ^ ((4 if late else 2) if index % 2 == 0 else (2 if late else 4))


def block_table(mine, size):
    if size != 8:
        return jnp.zeros((1,), jnp.int32)
    early = jnp.where(mine % 2 == 0, 2, 4)
    late = 6 - early
    relative = [0, early, late, 6, 1, 1 ^ late, 1 ^ early, 7]
    return jnp.stack([mine ^ r for r in relative]).astype(jnp.int32)


def early(i):
    return flip(i, False)


def late(i):
    return flip(i, True)


def across(i):
    return i ^ 6


def tie(*values):
    return lax.optimization_barrier(values)


def swap_plane(plane):
    return plane + [core_swap(piece) for piece in plane]


def to_slab(parts):
    return jnp.concatenate(parts, axis=1)


def mp_gather(shard):
    return [shard] + [mp_swap(shard, step) for step in range(1, N_MP)]


def half_sums(keep, back):
    half = keep.shape[0] // 2
    add = lambda at: (keep[at].astype(F32) + back[at].astype(F32)).astype(BF16)
    return add(slice(0, half)), add(slice(half, None))


def mp_away(parts):
    return [mp_swap(parts[step].astype(BF16), step) for step in range(1, N_MP)]


def mp_total(own, backs):
    for back in backs:
        own = own + back.astype(F32)
    return own


def block_rows(pieces):
    return WIDTH // len(pieces)


class Weights:
    def __init__(self, pieces, table, held, sems, lo, tile):
        self.held, self.tile = held, tile
        cols, parts = held.shape[2], sems.shape[0]
        self.span, self.copies = cols // parts, []
        for t in range(parts):
            row = []
            for k, piece in enumerate(pieces):
                copy = pltpu.make_async_copy(
                    piece.at[pl.ds(0, held.shape[1]), pl.ds(lo + t * self.span, self.span)],
                    held.at[table[k], :, pl.ds(t * self.span, self.span)],
                    sems.at[t, k],
                )
                copy.start()
                row.append(copy)
            self.copies.append(row)
        self.waited = 0

    def get(self, t):
        at = t * self.tile
        while self.waited * self.span < at + self.tile:
            for copy in self.copies[self.waited]:
                copy.wait()
            self.waited += 1
        count, rows, _ = self.held.shape
        return self.held[:, :, at : at + self.tile].reshape(count * rows, self.tile)


def weight_scratch(pieces, cols, parts=1):
    return [
        pltpu.VMEM((len(pieces), block_rows(pieces), cols), BF16),
        pltpu.SemaphoreType.DMA((parts, len(pieces))),
    ]


def grad_shapes(pieces, cols, extra=0):
    count, rows = len(pieces), block_rows(pieces)
    if count == 1:
        return [jax.ShapeDtypeStruct((1, rows, cols), F32)]
    return [jax.ShapeDtypeStruct((count // 2, rows + extra, cols), BF16)] * 2


def turn_scratch(pieces, rows):
    return [pltpu.VMEM((len(pieces), block_rows(pieces), rows), BF16)] * 2


def turn(value, table, plain, turned):
    plain[...] = value.T.reshape(plain.shape)
    for r in range(plain.shape[0]):
        turned[r] = plain[table[r]]


def stage_scratch(pieces, cols):
    return [
        pltpu.VMEM((g.shape[0], block_rows(pieces), cols), g.dtype)
        for g in grad_shapes(pieces, cols)
    ]


def store_grad(turned, right, stages, at, writes=None, outs=None):
    count, rows, _ = turned.shape
    grad = dot(turned[...].reshape(count * rows, -1), right, NN)
    half, cols = count // len(stages), right.shape[1]
    for r in range(count):
        stage = stages[r // half]
        part = grad[r * rows : (r + 1) * rows].astype(stage.dtype)
        stage[r % half, :rows, at : at + cols] = part
    if writes is not None:
        for stage, out in zip(stages, outs):
            writes.start(
                stage.at[:, :, pl.ds(at, cols)],
                out.at[:, pl.ds(0, rows), pl.ds(at, cols)],
            )


class Writes:
    def __init__(self, sems):
        self.sems, self.copies = sems, []

    def start(self, source, target):
        copy = pltpu.make_async_copy(source, target, self.sems.at[len(self.copies)])
        copy.start()
        self.copies.append(copy)

    def finish(self):
        for copy in self.copies:
            copy.wait()


class Reads:
    def __init__(self, sources, targets, sems):
        self.targets, self.copies = targets, []
        for i, (source, target) in enumerate(zip(sources, targets)):
            copy = pltpu.make_async_copy(source, target, sems.at[i])
            copy.start()
            self.copies.append(copy)

    def get(self, i):
        self.copies[i].wait()
        return self.targets[i]


def read_scratch(arrays):
    return [pltpu.VMEM(a.shape, a.dtype) for a in arrays] + [
        pltpu.SemaphoreType.DMA((len(arrays),))
    ]


def cost(micros):
    return pl.CostEstimate(
        flops=int(micros * 1.1e9 * CS), bytes_accessed=int(micros * 1e5 * CS), transcendentals=0
    )


def call(body, name, micros, outs, arrays, table, pieces, scratch, far=0):
    vmem = pl.BlockSpec(memory_space=pltpu.VMEM)
    away = pl.BlockSpec(memory_space=pl.ANY)
    return pl.pallas_call(
        body,
        out_shape=tuple(outs),
        in_specs=[pl.BlockSpec(memory_space=pltpu.SMEM)]
        + [vmem] * len(arrays)
        + [away] * len(pieces),
        out_specs=(vmem,) * (len(outs) - far) + (away,) * far,
        scratch_shapes=scratch,
        compiler_params=pltpu.CompilerParams(vmem_limit_bytes=60 << 20),
        cost_estimate=cost(micros),
        name=name,
    )(table, *arrays, *pieces)


def like(shape, kind):
    return jax.ShapeDtypeStruct(shape, kind)


def attend_kernel(q_ref, k_ref, v_ref, kp_ref, vp_ref, bias_ref, o_ref, lse_ref):
    rows = q_ref.shape[0]
    keys = jnp.concatenate([k_ref[...], kp_ref[...]], axis=0)
    values = jnp.concatenate([v_ref[...], vp_ref[...]], axis=0)
    bias = bias_ref[...]
    tile = min(rows, Q_TILE)
    low = lax.broadcasted_iota(jnp.int32, (tile, LANES), 1) < HEAD
    for start in range(0, rows, tile):
        q = q_ref[start : start + tile, :]
        outs, logs = [], []
        for half in range(2):
            here = low if half == 0 else ~low
            q_here = jnp.where(here, q, jnp.zeros_like(q))
            scores = dot(q_here, keys, NT) + bias
            top = jnp.max(scores, axis=-1, keepdims=True)
            raised = jnp.exp(scores - top)
            total = jnp.sum(raised, axis=-1, keepdims=True)
            mixed = dot(raised.astype(BF16), values, NN)
            outs.append(mixed / total)
            logs.append(top + jnp.log(total))
        o_ref[start : start + tile, :] = jnp.where(low, outs[0], outs[1]).astype(BF16)
        lse_ref[start : start + tile, :] = jnp.where(low, logs[0], logs[1])


def attend(qkv, kv_other, bias):
    rows, width = qkv.shape[0], qkv.shape[1] // 3
    pairs = width // LANES
    spec = lambda base: pl.BlockSpec((rows, LANES), lambda p: (0, base + p))
    return pl.pallas_call(
        attend_kernel,
        out_shape=(
            jax.ShapeDtypeStruct((rows, width), BF16),
            jax.ShapeDtypeStruct((rows, width), F32),
        ),
        grid=(pairs,),
        in_specs=[
            spec(0),
            spec(pairs),
            spec(2 * pairs),
            spec(0),
            spec(pairs),
            pl.BlockSpec((1, 2 * rows), lambda p: (0, 0)),
        ],
        out_specs=(spec(0), spec(0)),
        compiler_params=pltpu.CompilerParams(vmem_limit_bytes=56 << 20),
        cost_estimate=cost(15),
        name="attend",
    )(qkv, qkv, qkv, kv_other, kv_other, bias)


def attend_back_kernel(
    q_ref, k_ref, v_ref, kp_ref, vp_ref, bias_ref, o_ref, lse_ref, do_ref,
    dq_ref, own_ref, other_ref,
):
    rows = q_ref.shape[0]
    keys = jnp.concatenate([k_ref[...], kp_ref[...]], axis=0)
    values = jnp.concatenate([v_ref[...], vp_ref[...]], axis=0)
    bias = bias_ref[...]
    tile = min(rows, Q_TILE)
    low = lax.broadcasted_iota(jnp.int32, (tile, LANES), 1) < HEAD
    dk = jnp.zeros((LANES, 2 * rows), F32)
    dv = jnp.zeros((LANES, 2 * rows), F32)
    for start in range(0, rows, tile):
        at = slice(start, start + tile)
        q, do = q_ref[at, :], do_ref[at, :]
        product = o_ref[at, :].astype(F32) * do.astype(F32)
        lse = lse_ref[at, :]
        outs = []
        for half in range(2):
            here = low if half == 0 else ~low
            q_here = jnp.where(here, q, jnp.zeros_like(q))
            do_here = jnp.where(here, do, jnp.zeros_like(do))
            inner = jnp.sum(jnp.where(here, product, 0.0), axis=-1, keepdims=True)
            log = lse[:, half * HEAD : half * HEAD + 1]
            soft = jnp.exp(dot(q_here, keys, NT) + bias - log)
            grad = (soft * (dot(do_here, values, NT) - inner)).astype(BF16)
            outs.append(dot(grad, keys, NN))
            dk = dk + dot(q_here, grad, TN)
            dv = dv + dot(do_here, soft.astype(BF16), TN)
        dq_ref[at, :] = (jnp.where(low, outs[0], outs[1]) * SCALE).astype(BF16)
    for i, value in enumerate((dk.T, dv.T)):
        at = slice(i * LANES, (i + 1) * LANES)
        own_ref[:, at] = value[:rows]
        other_ref[:, at] = value[rows:].astype(BF16)


def attend_back(qkv, kv_other, bias, out, lse, grad_out, first, count):
    rows, width = out.shape
    pairs = width // LANES
    spec = lambda base: pl.BlockSpec((rows, LANES), lambda p: (0, base + first + p))
    result = lambda cols: pl.BlockSpec((rows, cols), lambda p: (0, p))
    return pl.pallas_call(
        attend_back_kernel,
        out_shape=(
            jax.ShapeDtypeStruct((rows, count * LANES), BF16),
            jax.ShapeDtypeStruct((rows, 2 * count * LANES), F32),
            jax.ShapeDtypeStruct((rows, 2 * count * LANES), BF16),
        ),
        grid=(count,),
        in_specs=[
            spec(0),
            spec(pairs),
            spec(2 * pairs),
            spec(0),
            spec(pairs),
            pl.BlockSpec((1, 2 * rows), lambda p: (0, 0)),
            spec(0),
            spec(0),
            spec(0),
        ],
        out_specs=(result(LANES), result(2 * LANES), result(2 * LANES)),
        compiler_params=pltpu.CompilerParams(vmem_limit_bytes=56 << 20),
        cost_estimate=cost(3 * count),
        name="attend_back",
    )(qkv, qkv, qkv, kv_other, kv_other, bias, out, lse, grad_out)


def gelu_parts(v):
    cdf = 0.5 * (1.0 + lax.erf(v * (2.0 ** -0.5)))
    pdf = jnp.exp(-0.5 * v * v) * 0.3989422804014327
    return v * cdf, cdf + v * pdf


def norm(values):
    center = values - jnp.mean(values, axis=-1, keepdims=True)
    inv_dev = lax.rsqrt(jnp.mean(center * center, axis=-1, keepdims=True) + EPS)
    return center * inv_dev, inv_dev


def norm_back(scaled, normed, inv_dev):
    return inv_dev * (
        scaled
        - jnp.mean(scaled, axis=-1, keepdims=True)
        - normed * jnp.mean(scaled * normed, axis=-1, keepdims=True)
    )


def total(value):
    return jnp.sum(value, axis=0, keepdims=True)


def project(x_parts, head_rows, table, pieces):
    block, width = x_parts[0].shape
    rows = block * len(x_parts)
    n = len(pieces)

    def body(table, *refs):
        part_refs, bias_ref, refs = refs[:N_MP], refs[N_MP], refs[N_MP + 1 :]
        pieces, (x_ref, qkv_ref, kv_ref, held, sems) = refs[:n], refs[n:]
        weights = Weights(pieces, table, held, sems, 0, width)
        for i, part in enumerate(part_refs):
            x_ref[i * block : (i + 1) * block, :] = part[...]
        x = x_ref[...]
        for i in range(3):
            value = dot(x, weights.get(i), NN) + bias_ref[i : i + 1, :]
            value = value.astype(BF16)
            if i == 0:
                value = (value.astype(F32) * SCALE).astype(BF16)
            else:
                kv_ref[:, (i - 1) * width : i * width] = value
            qkv_ref[:, i * width : (i + 1) * width] = value

    return call(
        body,
        "project",
        7,
        [
            like((rows, width), BF16),
            like((rows, 3 * width), BF16),
            like((rows, 2 * width), BF16),
        ],
        list(x_parts) + [head_rows],
        table,
        pieces,
        weight_scratch(pieces, 3 * width, 3),
    )


def feed(x, mixed, cot_parts, smalls, small_row, table, out_pieces, feed_pieces):
    rows, width = x.shape
    hidden = feed_pieces[0].shape[1] // 2
    count = 6
    tile = hidden // count
    spans = [slice(t * tile, (t + 1) * tile) for t in range(count)]
    cols = hidden + width
    n = len(out_pieces)
    down_grads = grad_shapes(feed_pieces, hidden)
    mid_grads = grad_shapes(feed_pieces, cols, SHARED)
    g = len(mid_grads)

    def body(table, x_ref, mixed_ref, *refs):
        cot_far, small_far, refs = refs[:N_MP], refs[N_MP : N_MP + n], refs[N_MP + n :]
        out_p, up_p, refs = refs[:n], refs[n : 2 * n], refs[2 * n :]
        shared_ref, result_out, da_out, do_out = refs[:4]
        down_outs, mid_outs, refs = refs[4 : 4 + g], refs[4 + g : 4 + 2 * g], refs[4 + 2 * g :]
        w_out, sems_out, w_up, sems_up, w_down, sems_down = refs[:6]
        plain, turned, plain_h, turned_h = refs[6:10]
        small_ref, cot_ref, read_sems = refs[10:13]
        n1_ref, dz_ref, h_ref, act_ref, slope_ref, result_ref, low_ref, do_ref = refs[13:21]
        down_stages, mid_stages = refs[21 : 21 + g], refs[21 + g : 21 + 2 * g]
        shared_low, sems = refs[21 + 2 * g :]
        out_w = Weights(out_p, table, w_out, sems_out, 3 * width, width)
        smalls = [small.at[pl.ds(small_row, SMALL)] for small in small_far]
        reads = Reads(smalls, [small_ref.at[i] for i in range(n)], read_sems)
        up_w = Weights(up_p, table, w_up, sems_up, 0, tile)
        down_w = Weights(up_p, table, w_down, sems_down, hidden, tile)
        block = rows // N_MP
        cots = Reads(
            cot_far,
            [cot_ref.at[pl.ds(i * block, block)] for i in range(N_MP)],
            read_sems.at[pl.ds(n, N_MP)],
        )
        writes = Writes(sems)

        attention = dot(mixed_ref[...], out_w.get(0), NT)
        for i in range(n):
            reads.get(i)
        small = jnp.sum(small_ref[...].astype(F32), axis=0)
        row_vals = sum(small[:, i * width : (i + 1) * width] for i in range(2 * N_MP))
        row = lambda i: row_vals[i : i + 1, :]
        up_b = small[6:7, :hidden]
        n1, r1 = norm(x_ref[...].astype(F32) + attention + row(0))
        n1_ref[...] = n1
        h_ref[...] = (n1 * row(1) + row(2)).astype(BF16)
        feed = jnp.zeros((rows, width), F32)
        u = dot(h_ref[...], up_w.get(0), NN)
        for t, at in enumerate(spans):
            down = down_w.get(t)
            later = dot(h_ref[...], up_w.get(t + 1), NN) if t + 1 < count else None
            act, slope = gelu_parts(u + up_b[:, at])
            act_ref[:, at] = act.astype(BF16)
            slope_ref[:, at] = slope.astype(BF16)
            feed = feed + dot(act_ref[:, at], down, NT)
            u = later
        h = n1_ref[...] * row(1) + row(2)
        n2, r2 = norm(h + feed + row(3))
        result_ref[...] = (n2 * row(4) + row(5)).astype(BF16)
        writes.start(result_ref, result_out)
        for i in range(N_MP):
            cots.get(i)
        gy = cot_ref[...].astype(F32)
        dz = norm_back(gy * row(4), n2, r2)
        dz_ref[...] = dz
        low_ref[...] = dz.astype(BF16)
        sums = [total(dz), total(gy * n2), total(gy)]

        turn(low_ref[...], table, plain, turned)
        turn(h_ref[...], table, plain_h, turned_h)
        shared_ref[...] = jnp.zeros_like(shared_ref)
        dh = dz_ref[...]
        for t, at in enumerate(spans):
            dact = dot(low_ref[...], down_w.get(t), NN)
            store_grad(turned, act_ref[:, at], down_stages, at.start, writes, down_outs)
            du = (dact * slope_ref[:, at].astype(F32)).astype(BF16)
            shared_ref[0:1, at] = total(du.astype(F32))
            dh = dh + dot(du, up_w.get(t), NT)
            store_grad(turned_h, du, mid_stages, at.start, writes, mid_outs)
        n1 = n1_ref[...]
        da = norm_back(dh * row(1), n1, r1)
        dz_ref[...] = da
        writes.start(dz_ref, da_out)
        low_ref[...] = da.astype(BF16)
        do_ref[...] = dot(low_ref[...], out_w.get(0), NN).astype(BF16)
        writes.start(do_ref, do_out)
        sums = [total(da), total(dh * n1), total(dh)] + sums
        for j in range(hidden // width):
            for i, value in enumerate(sums):
                shared_ref[1 + i : 2 + i, j * width : (j + 1) * width] = value
        if g > 1:
            shared_low[...] = shared_ref[...].astype(BF16)
            for out in mid_outs:
                for r in range(out.shape[0]):
                    writes.start(shared_low, out.at[r, pl.ds(block_rows(feed_pieces), SHARED)])
        turn(low_ref[...], table, plain, turned)
        store_grad(turned, mixed_ref[...], mid_stages, hidden, writes, mid_outs)
        writes.finish()

    near = [((rows, width), F32)] * 2 + [((rows, width), BF16)]
    near += [((rows, hidden), BF16)] * 2 + [((rows, width), BF16)] * 3
    return call(
        body,
        "feed",
        33,
        [
            like((SHARED, cols), F32),
            like((rows, width), BF16),
            like((rows, width), F32),
            like((rows, width), BF16),
        ]
        + down_grads
        + mid_grads,
        [x, mixed],
        table,
        list(cot_parts) + list(smalls) + list(out_pieces) + list(feed_pieces),
        weight_scratch(out_pieces, width)
        + weight_scratch(feed_pieces, hidden) * 2
        + turn_scratch(feed_pieces, rows) * 2
        + [
            pltpu.VMEM((n, SMALL, 2 * hidden), BF16),
            pltpu.VMEM((rows, width), BF16),
            pltpu.SemaphoreType.DMA((n + N_MP,)),
        ]
        + [pltpu.VMEM(*spec) for spec in near]
        + stage_scratch(feed_pieces, hidden)
        + stage_scratch(feed_pieces, cols)
        + [
            pltpu.VMEM((SHARED, cols), BF16),
            pltpu.SemaphoreType.DMA((3 + g * (2 * count + 1) + n,)),
        ],
        far=3 + 2 * g,
    )


def project_grads(x, parts, table, pieces):
    rows, width = x.shape
    grads = grad_shapes(pieces, 3 * width, SHARED)
    flat = [value for part in parts for value in part]
    g = len(grads)

    def body(table, x_ref, *refs):
        part_refs, refs = refs[: len(flat)], refs[len(flat) :]
        dqkv_ref, shared_ref = refs[:2]
        grad_outs, refs = refs[2 : 2 + g], refs[2 + g :]
        plain, turned = refs[:2]
        stages, shared_low, sems = refs[2 : 2 + g], refs[2 + g], refs[3 + g]
        writes = Writes(sems)
        turn(x_ref[...], table, plain, turned)
        pair = 0
        for i in range(0, len(flat), 3):
            q_ref, own_ref, back_ref = part_refs[i : i + 3]
            cols = q_ref.shape[1]
            dqkv_ref[:, pair * LANES : pair * LANES + cols] = q_ref[...]
            for p in range(cols // LANES):
                for which in range(2):
                    at = slice((2 * p + which) * LANES, (2 * p + which + 1) * LANES)
                    to = (which + 1) * width + (pair + p) * LANES
                    value = own_ref[:, at] + back_ref[:, at].astype(F32)
                    dqkv_ref[:, to : to + LANES] = value.astype(BF16)
            pair += cols // LANES
        for i in range(3):
            at = i * width
            store_grad(turned, dqkv_ref[:, at : at + width], stages, at, writes, grad_outs)
        shared_ref[...] = jnp.zeros_like(shared_ref)
        shared_ref[0:1, :] = total(dqkv_ref[...].astype(F32))
        if g > 1:
            shared_low[...] = shared_ref[...].astype(BF16)
            for out in grad_outs:
                for r in range(out.shape[0]):
                    writes.start(shared_low, out.at[r, pl.ds(block_rows(pieces), SHARED)])
        writes.finish()

    return call(
        body,
        "project_grads",
        7,
        [like((rows, 3 * width), BF16), like((SHARED, 3 * width), F32)] + grads,
        [x] + flat,
        table,
        [],
        turn_scratch(pieces, rows)
        + stage_scratch(pieces, 3 * width)
        + [
            pltpu.VMEM((SHARED, 3 * width), BF16),
            pltpu.SemaphoreType.DMA((3 * g + len(pieces),)),
        ],
        far=g,
    )


def project_back(da, dqkv, table, pieces):
    rows, width = da.shape
    n = len(pieces)

    def body(table, da_ref, dqkv_ref, *refs):
        pieces, (out_ref, held, sems) = refs[:n], refs[n:]
        weights = Weights(pieces, table, held, sems, 0, width)
        value = da_ref[...]
        for i in range(3):
            value = value + dot(dqkv_ref[:, i * width : (i + 1) * width], weights.get(i), NT)
        out_ref[...] = value.astype(BF16)

    return call(
        body,
        "project_back",
        8,
        [like((rows, width), BF16)],
        [da, dqkv],
        table,
        pieces,
        weight_scratch(pieces, 3 * width, 3),
    )[0]


def at_column(values, rows, width, column):
    return lax.dynamic_update_slice(jnp.zeros((rows, width), values.dtype), values, (0, column))


def small_block(row_params, expand_bias, mine, depth):
    high = lax.reduce_precision(row_params, 8, 7)
    column = (mine * N_MP + depth) * row_params.shape[1]
    high_low = [
        at_column(part.astype(BF16), 6, WIDTH, column) for part in (high, row_params - high)
    ]
    bias = at_column(expand_bias, 2, 2 * WIDTH, mine * expand_bias.shape[1])
    return jnp.concatenate([jnp.concatenate(high_low, axis=1), bias])


def key_bias(length_long, length_short, block, core, depth):
    lengths = jnp.concatenate([length_long, length_short])
    other = core_swap(lengths)
    longs = jnp.where(core == 0, jnp.stack([lengths[0], other[0]]), jnp.stack([other[0], lengths[0]]))
    length = jnp.concatenate([longs, lengths[1:]])[depth]
    is_long = depth < 2
    place = lax.broadcasted_iota(jnp.int32, (1, 2 * N_MP * block), 1)
    row = place % (N_MP * block)
    is_own = place < N_MP * block
    source = (row // block) ^ depth
    whose = jnp.where(is_own, core, 1 - core)
    frame = row % block + jnp.where(is_long, (2 * source + whose) * block, source * block)
    counted = (frame < length) & (is_own | is_long)
    return jnp.where(counted, 0.0, NEG_FILL).astype(F32)


def on_device(
    frames_long,
    frames_short,
    length_long,
    length_short,
    input_proj,
    output_proj,
    expand_weight,
    shrink_weight,
    head_bias,
    expand_bias,
    row_params,
    cotangent_long,
    cotangent_short,
):
    mine = lax.axis_index("dp")
    depth = lax.axis_index("mp")
    n_dp = lax.axis_size("dp")
    fast = n_dp == 8
    core = mine % 2
    block = frames_short.shape[1]
    shard, group = input_proj.shape[1:]
    units = expand_weight.shape[1]
    width = group * N_MP
    hidden = units * N_MP
    table = block_table(mine, n_dp)

    joined = jnp.concatenate(
        [input_proj[0], input_proj[1], input_proj[2], output_proj.T], axis=1
    )
    heads = at_column(head_bias[:, 0], SMALL, WIDTH, mine * head_bias.shape[2])
    attn_parts = mp_gather(jnp.concatenate([joined, heads]))
    x_blocks = clip_blocks(frames_long[0], frames_short, core)
    cot_blocks = clip_blocks(cotangent_long[0], cotangent_short, core)
    bias = key_bias(length_long, length_short, block, core, depth)
    feed_shard = jnp.concatenate(
        [
            jnp.concatenate([expand_weight, shrink_weight.T], axis=1),
            small_block(row_params, expand_bias, mine, depth),
        ]
    )
    *attn_parts, feed_shard, bias, x_blocks, cot_blocks = tie(
        *attn_parts, feed_shard, bias, x_blocks, cot_blocks
    )
    order = [p[:shard, i * group : (i + 1) * group] for i in range(4) for p in attn_parts]
    attn_slab = jnp.concatenate([to_slab(order), to_slab([p[shard:] for p in attn_parts])])
    feed_parts = mp_gather(feed_shard)

    def feed_slab_of(parts):
        return to_slab([p[:, i * units : (i + 1) * units] for i in range(2) for p in parts])

    if fast:
        near = [dp_swap(attn_slab, to) for to in (early, late)]
        far_slab, feed_parts[1] = tie(attn_slab, feed_parts[1])
        attn_p = [attn_slab] + near + [dp_swap(far_slab, across)]
        x_pieces = clip_pieces(x_blocks, depth)
        both = tie(*attn_p, *x_pieces, *feed_parts)
        attn_p, x_pieces, feed_parts = both[:4], both[4:8], both[8:]
        x_parts = [x_pieces[0]] + [mp_swap(x_pieces[i], i) for i in range(1, N_MP)]
        both = tie(*[core_swap(piece) for piece in attn_p], feed_slab_of(feed_parts))
        attn_p, feed_slab = list(attn_p) + list(both[:4]), both[4]
        feed_one = dp_swap(feed_slab, early)
        feed_two = dp_swap(feed_slab, late)
        *x_parts, cot_blocks, own_slab = tie(*x_parts, cot_blocks, feed_slab)
        heads = sum(p[shard:].astype(F32) for p in attn_p)
    else:
        x_parts = to_clips(x_blocks, depth)
        gather = lambda slab: lax.all_gather(slab, "dp", axis=0)
        whole = gather(attn_slab)
        heads = jnp.sum(whole[:, shard:].astype(F32), axis=0)
        attn_p = [whole[:, :shard].reshape(width, 4 * width)]
        whole = gather(feed_slab_of(feed_parts))
        small = jnp.sum(whole[:, shard:].astype(F32), axis=0)
        feed_p = [whole[:, :shard].reshape(width, 2 * hidden)]
    cot_parts = to_clips(cot_blocks, depth)
    heads = jnp.concatenate(
        [heads[:2, i * width : i * width + group] for i in range(N_MP)], axis=1
    )
    head_rows = jnp.stack([heads[0], jnp.zeros_like(heads[0]), heads[1]])

    x, qkv, kv = project(x_parts, head_rows, table, attn_p)
    if fast:
        kv, feed_one, feed_two, cot_parts[3], own_slab = tie(
            kv, feed_one, feed_two, cot_parts[3], core_swap(own_slab)
        )
    kv_other = core_swap(kv)
    if fast:
        feed_three = dp_swap(feed_one, late)
        feed_p = [feed_slab, feed_one, feed_two]
        backs = [own_slab] + [core_swap(piece) for piece in feed_p[1:]]
    mixed, lse = attend(qkv, kv_other, bias)
    if fast:
        mixed, feed_three, *both = tie(mixed, feed_three, *backs, *cot_parts)
        backs, cot_parts = both[:3], both[3:]
        feed_p = feed_p + [feed_three] + backs + [core_swap(feed_three)]
        smalls, small_row = feed_p, shard
    else:
        smalls, small_row = [small.astype(BF16)], 0
    outs = feed(x, mixed, cot_parts, smalls, small_row, table, attn_p, feed_p)
    mid_shared, result, da, do, *grads = outs
    g_down, g_mid = grads[: len(grads) // 2], grads[len(grads) // 2 :]

    def by_group_of(value, sizes):
        starts = [N_MP * sum(sizes[:i]) for i in range(len(sizes))]
        return [
            jnp.concatenate(
                [value[:, a + j * n : a + (j + 1) * n] for a, n in zip(starts, sizes)], axis=1
            )
            for j in range(N_MP)
        ]

    def last_sum(keep, back):
        return keep[0].astype(F32) + back[0].astype(F32)

    result_parts = from_clips(result)
    if fast:
        k_down, a_down = half_sums(g_down[0], core_swap(g_down[1]))
        b_mid = core_swap(g_mid[1])
        do, a_down = tie(do, a_down)
        b_down = dp_swap(a_down, late)
        k_mid, a_mid = half_sums(g_mid[0], b_mid)
        do, a_mid = tie(do, a_mid)
        b_mid = dp_swap(a_mid, late)
    pairs = width // LANES
    first = pairs // 3
    dq_a, own_a, other_a = attend_back(qkv, kv_other, bias, mixed, lse, do, 0, first)
    if fast:
        other_a, b_down, result_parts[3] = tie(other_a, b_down, result_parts[3])
        k_down, a_down = half_sums(k_down, b_down)
        do, a_down = tie(do, a_down)
        b_down = dp_swap(a_down, early)
    back_a = core_swap(other_a)
    dq_b, own_b, other_b = attend_back(
        qkv, kv_other, bias, mixed, lse, do, first, pairs - first
    )
    if fast:
        other_b, back_a, b_mid, b_down, *result_parts = tie(
            other_b, back_a, b_mid, b_down, *result_parts
        )
    back_b = core_swap(other_b)
    if fast:
        s_down = by_group_of(last_sum(k_down, b_down), [units])
        k_mid, a_mid = half_sums(k_mid, b_mid)
        back_b, a_mid, *s_down = tie(back_b, a_mid, *s_down)
        b_mid = dp_swap(a_mid, early)
        z_down = mp_away(s_down)
    result_long, result_short = frames_of(result_parts, core, depth)
    parts = [(dq_a, own_a, back_a), (dq_b, own_b, back_b)]
    dqkv, attn_shared, *g_attn = project_grads(x, parts, table, attn_p)
    if fast:
        *both, b_mid = tie(*g_attn, *z_down, b_mid)
        g_attn, z_down = both[:2], both[2:]
        b_attn = core_swap(g_attn[1])
        s_mid = by_group_of(last_sum(k_mid, b_mid), [units, group])
        k_attn, a_attn = half_sums(g_attn[0], b_attn)
        dqkv, a_attn, *s_mid = tie(dqkv, a_attn, *s_mid)
        b_attn = dp_swap(a_attn, late)
        z_mid = mp_away(s_mid)
    frames_grad = project_back(da, dqkv, table, attn_p)
    if fast:
        frames_grad, b_attn = tie(frames_grad, b_attn)
        k_attn, a_attn = half_sums(k_attn, b_attn)
        frames_grad, a_attn = tie(frames_grad, a_attn)
    grad_parts = from_clips(frames_grad)
    if fast:
        b_attn, *grad_parts = tie(dp_swap(a_attn, early), *grad_parts)
        s_attn = last_sum(k_attn, b_attn)
    else:
        scatter = lambda g: lax.psum_scatter(g[0][0], "dp", scatter_dimension=0, tiled=True)
        s_down = by_group_of(scatter(g_down), [units])
        z_down = mp_away(s_down)
        s_mid = jnp.concatenate([scatter(g_mid), lax.psum(mid_shared, "dp")])
        s_mid = by_group_of(s_mid, [units, group])
        z_mid = mp_away(s_mid)
        s_attn = jnp.concatenate([scatter(g_attn), lax.psum(attn_shared, "dp")])
    s_attn = by_group_of(s_attn, [group] * 3)
    grad_long, grad_short = frames_of(grad_parts, core, depth)
    attn_share = mp_total(s_attn[0], mp_away(s_attn))
    down_share = mp_total(s_down[0], z_down).T
    mid_share = mp_total(s_mid[0], z_mid)
    up_share = mid_share[:shard, :units]
    output_share = mid_share[:shard, units:].T
    input_share = jnp.stack(
        [attn_share[:shard, i * group : (i + 1) * group] for i in range(3)]
    )
    up_cols, head_cols, row_cols = units // n_dp, group // n_dp, width // (n_dp * N_MP)
    rank = mine * N_MP + depth
    up_b_share = lax.dynamic_slice(mid_share, (shard, mine * up_cols), (1, up_cols))
    row_share = lax.dynamic_slice(mid_share, (shard + 1, rank * row_cols), (6, row_cols))
    head_share = jnp.stack(
        [
            lax.dynamic_slice(attn_share, (shard, at + mine * head_cols), (1, head_cols))
            for at in (0, 2 * group)
        ]
    )
    return (
        result_long,
        result_short,
        grad_long.astype(F32),
        grad_short.astype(F32),
        input_share,
        output_share,
        up_share,
        down_share,
        head_share,
        up_b_share,
        row_share,
    )


def solution(mesh):
    return jax.shard_map(
        on_device,
        mesh=mesh,
        in_specs=(
            P("dp", "mp", None),
            P("dp", "mp", None),
            P("dp"),
            P("dp"),
            P(None, "dp", "mp"),
            P("mp", "dp"),
            P("dp", "mp"),
            P("mp", "dp"),
            P(None, "mp", "dp"),
            P("mp", "dp"),
            P(None, ("dp", "mp")),
            P("dp", "mp", None),
            P("dp", "mp", None),
        ),
        out_specs=(
            P("dp", "mp", None),
            P("dp", "mp", None),
            P("dp", "mp", None),
            P("dp", "mp", None),
            P(None, "dp", "mp"),
            P("mp", "dp"),
            P("dp", "mp"),
            P("mp", "dp"),
            P(None, "mp", "dp"),
            P("mp", "dp"),
            P(None, ("dp", "mp")),
        ),
        check_vma=False,
    )
```

```python
import functools

import jax
import jax.numpy as jnp
from jax import lax
from jax.experimental import pallas as pl
from jax.experimental.pallas import tpu as pltpu
from jax.sharding import PartitionSpec as P

HEAD = 64
EPS = 1e-05
NEG_FILL = -1e30
SCALE = HEAD ** (-0.5)
N_MP = 4
PARTS = 1
CS = 0.3
WIDTH = 768
SMALL = 8
SHARED = 8
LANES = 128
Q_TILE = 256
F32 = jnp.float32
BF16 = jnp.bfloat16
NT = (((1,), (1,)), ((), ()))
NN = (((1,), (0,)), ((), ()))
TN = (((0,), (0,)), ((), ()))


def dot(left, right, dims):
    return lax.dot_general(left, right, dims, preferred_element_type=F32)


def mp_swap(value, step):
    return lax.ppermute(value, "mp", [(i, i ^ step) for i in range(N_MP)])


def dp_swap(value, target):
    size = lax.axis_size("dp")
    return lax.ppermute(value, "dp", [(i, target(i)) for i in range(size)])


def core_swap(value):
    return dp_swap(value, lambda i: i ^ 1)


def clip_blocks(long_rows, short_rows, core):
    block = short_rows.shape[1]
    keep = lax.dynamic_slice_in_dim(long_rows, core * block, block, 0)
    away = lax.dynamic_slice_in_dim(long_rows, (1 - core) * block, block, 0)
    back = core_swap(away)
    first = jnp.where(core == 0, keep, back)
    second = jnp.where(core == 0, back, keep)
    return jnp.stack([first, second, short_rows[0], short_rows[1]])


def clip_pieces(blocks, depth):
    return [
        lax.dynamic_index_in_dim(blocks, depth ^ step, 0, keepdims=False) for step in range(N_MP)
    ]


def to_clips(blocks, depth):
    pieces = clip_pieces(blocks, depth)
    return pieces[:1] + [mp_swap(pieces[step], step) for step in range(1, N_MP)]


def from_clips(rows):
    block = rows.shape[0] // N_MP
    parts = []
    for step in range(N_MP):
        piece = rows[step * block : (step + 1) * block]
        parts.append(piece if step == 0 else mp_swap(piece, step))
    return parts


def frames_of(parts, core, depth):
    blocks = jnp.stack(parts)
    first, second, short_a, short_b = (
        lax.dynamic_index_in_dim(blocks, depth ^ i, 0, keepdims=False) for i in range(N_MP)
    )
    keep = jnp.where(core == 0, first, second)
    away = jnp.where(core == 0, second, first)
    back = core_swap(away)
    low = jnp.where(core == 0, keep, back)
    high = jnp.where(core == 0, back, keep)
    return jnp.concatenate([low, high], axis=0)[None], jnp.stack([short_a, short_b])


def flip(index, late):
    return index ^ ((4 if late else 2) if index % 2 == 0 else (2 if late else 4))


def block_table(mine, size):
    if size != 8:
        return jnp.zeros((1,), jnp.int32)
    early = jnp.where(mine % 2 == 0, 2, 4)
    late = 6 - early
    relative = [0, early, late, 6, 1, 1 ^ late, 1 ^ early, 7]
    return jnp.stack([mine ^ r for r in relative]).astype(jnp.int32)


def early(i):
    return flip(i, False)


def late(i):
    return flip(i, True)


def across(i):
    return i ^ 6


def tie(*values):
    return lax.optimization_barrier(values)


def swap_plane(plane):
    return plane + [core_swap(piece) for piece in plane]


def to_slab(parts):
    return jnp.concatenate(parts, axis=1)


def mp_gather(shard):
    return [shard] + [mp_swap(shard, step) for step in range(1, N_MP)]


def half_sums(keep, back):
    half = keep.shape[0] // 2
    add = lambda at: (keep[at].astype(F32) + back[at].astype(F32)).astype(BF16)
    return add(slice(0, half)), add(slice(half, None))


def mp_away(parts):
    return [mp_swap(parts[step].astype(BF16), step) for step in range(1, N_MP)]


def mp_total(own, backs):
    for back in backs:
        own = own + back.astype(F32)
    return own


def blocks_of(pieces):
    step = pieces[0].shape[0]
    return [(p, k * step) for p in pieces for k in range(p.shape[0] // step)]


def block_rows(pieces):
    return WIDTH // len(blocks_of(pieces))


class Weights:
    def __init__(self, pieces, table, held, sems, lo, tile):
        self.held, self.tile = held, tile
        cols, parts = held.shape[2], sems.shape[0]
        self.span, self.copies = cols // parts, []
        for t in range(parts):
            row = []
            for k, (piece, first) in enumerate(blocks_of(pieces)):
                copy = pltpu.make_async_copy(
                    piece.at[pl.ds(first, held.shape[1]), pl.ds(lo + t * self.span, self.span)],
                    held.at[table[k], :, pl.ds(t * self.span, self.span)],
                    sems.at[t, k],
                )
                copy.start()
                row.append(copy)
            self.copies.append(row)
        self.waited = 0

    def get(self, t):
        at = t * self.tile
        while self.waited * self.span < at + self.tile:
            for copy in self.copies[self.waited]:
                copy.wait()
            self.waited += 1
        count, rows, _ = self.held.shape
        return self.held[:, :, at : at + self.tile].reshape(count * rows, self.tile)


def weight_scratch(pieces, cols, parts=1):
    return [
        pltpu.VMEM((len(blocks_of(pieces)), block_rows(pieces), cols), BF16),
        pltpu.SemaphoreType.DMA((parts, len(blocks_of(pieces)))),
    ]


def grad_shapes(pieces, cols, extra=0):
    count, rows = len(blocks_of(pieces)), block_rows(pieces)
    if count == 1:
        return [jax.ShapeDtypeStruct((1, rows, cols), F32)]
    return [jax.ShapeDtypeStruct((count // 2, rows + extra, cols), BF16)] * 2


def turn_scratch(pieces, rows):
    return [pltpu.VMEM((len(blocks_of(pieces)), block_rows(pieces), rows), BF16)] * 2


def turn(value, table, plain, turned):
    plain[...] = value.T.reshape(plain.shape)
    for r in range(plain.shape[0]):
        turned[r] = plain[table[r]]


def stage_scratch(pieces, cols):
    return [
        pltpu.VMEM((g.shape[0], block_rows(pieces), cols), g.dtype)
        for g in grad_shapes(pieces, cols)
    ]


def store_grad(turned, right, stages, at, writes=None, outs=None):
    count, rows, _ = turned.shape
    grad = dot(turned[...].reshape(count * rows, -1), right, NN)
    half, cols = count // len(stages), right.shape[1]
    for r in range(count):
        stage = stages[r // half]
        part = grad[r * rows : (r + 1) * rows].astype(stage.dtype)
        stage[r % half, :rows, at : at + cols] = part
    if writes is not None:
        for stage, out in zip(stages, outs):
            writes.start(
                stage.at[:, :, pl.ds(at, cols)],
                out.at[:, pl.ds(0, rows), pl.ds(at, cols)],
            )


class Writes:
    def __init__(self, sems):
        self.sems, self.copies = sems, []

    def start(self, source, target):
        copy = pltpu.make_async_copy(source, target, self.sems.at[len(self.copies)])
        copy.start()
        self.copies.append(copy)

    def finish(self):
        for copy in self.copies:
            copy.wait()


class Reads:
    def __init__(self, sources, targets, sems):
        self.targets, self.copies = targets, []
        for i, (source, target) in enumerate(zip(sources, targets)):
            copy = pltpu.make_async_copy(source, target, sems.at[i])
            copy.start()
            self.copies.append(copy)

    def get(self, i):
        self.copies[i].wait()
        return self.targets[i]


def read_scratch(arrays):
    return [pltpu.VMEM(a.shape, a.dtype) for a in arrays] + [
        pltpu.SemaphoreType.DMA((len(arrays),))
    ]


def cost(micros):
    return pl.CostEstimate(
        flops=int(micros * 1.1e9 * CS), bytes_accessed=int(micros * 1e5 * CS), transcendentals=0
    )


def call(body, name, micros, outs, arrays, table, pieces, scratch, far=0):
    vmem = pl.BlockSpec(memory_space=pltpu.VMEM)
    away = pl.BlockSpec(memory_space=pl.ANY)
    return pl.pallas_call(
        body,
        out_shape=tuple(outs),
        in_specs=[pl.BlockSpec(memory_space=pltpu.SMEM)]
        + [vmem] * len(arrays)
        + [away] * len(pieces),
        out_specs=(vmem,) * (len(outs) - far) + (away,) * far,
        scratch_shapes=scratch,
        compiler_params=pltpu.CompilerParams(vmem_limit_bytes=60 << 20),
        cost_estimate=cost(micros),
        name=name,
    )(table, *arrays, *pieces)


def like(shape, kind):
    return jax.ShapeDtypeStruct(shape, kind)


def attend_kernel(q_ref, k_ref, v_ref, kp_ref, vp_ref, bias_ref, o_ref, lse_ref):
    rows = q_ref.shape[0]
    keys = jnp.concatenate([k_ref[...], kp_ref[...]], axis=0)
    values = jnp.concatenate([v_ref[...], vp_ref[...]], axis=0)
    bias = bias_ref[...]
    tile = min(rows, Q_TILE)
    low = lax.broadcasted_iota(jnp.int32, (tile, LANES), 1) < HEAD
    for start in range(0, rows, tile):
        q = q_ref[start : start + tile, :]
        outs, logs = [], []
        for half in range(2):
            here = low if half == 0 else ~low
            q_here = jnp.where(here, q, jnp.zeros_like(q))
            scores = dot(q_here, keys, NT) + bias
            top = jnp.max(scores, axis=-1, keepdims=True)
            raised = jnp.exp(scores - top)
            total = jnp.sum(raised, axis=-1, keepdims=True)
            mixed = dot(raised.astype(BF16), values, NN)
            outs.append(mixed / total)
            logs.append(top + jnp.log(total))
        o_ref[start : start + tile, :] = jnp.where(low, outs[0], outs[1]).astype(BF16)
        lse_ref[start : start + tile, :] = jnp.where(low, logs[0], logs[1])


def attend(qkv, kv_other, bias):
    rows, width = qkv.shape[0], qkv.shape[1] // 3
    pairs = width // LANES
    spec = lambda base: pl.BlockSpec((rows, LANES), lambda p: (0, base + p))
    return pl.pallas_call(
        attend_kernel,
        out_shape=(
            jax.ShapeDtypeStruct((rows, width), BF16),
            jax.ShapeDtypeStruct((rows, width), F32),
        ),
        grid=(pairs,),
        in_specs=[
            spec(0),
            spec(pairs),
            spec(2 * pairs),
            spec(0),
            spec(pairs),
            pl.BlockSpec((1, 2 * rows), lambda p: (0, 0)),
        ],
        out_specs=(spec(0), spec(0)),
        compiler_params=pltpu.CompilerParams(vmem_limit_bytes=56 << 20),
        cost_estimate=cost(15),
        name="attend",
    )(qkv, qkv, qkv, kv_other, kv_other, bias)


def attend_back_kernel(
    q_ref, k_ref, v_ref, kp_ref, vp_ref, bias_ref, o_ref, lse_ref, do_ref,
    dq_ref, own_ref, other_ref,
):
    rows = q_ref.shape[0]
    keys = jnp.concatenate([k_ref[...], kp_ref[...]], axis=0)
    values = jnp.concatenate([v_ref[...], vp_ref[...]], axis=0)
    bias = bias_ref[...]
    tile = min(rows, Q_TILE)
    low = lax.broadcasted_iota(jnp.int32, (tile, LANES), 1) < HEAD
    dk = jnp.zeros((LANES, 2 * rows), F32)
    dv = jnp.zeros((LANES, 2 * rows), F32)
    for start in range(0, rows, tile):
        at = slice(start, start + tile)
        q, do = q_ref[at, :], do_ref[at, :]
        product = o_ref[at, :].astype(F32) * do.astype(F32)
        lse = lse_ref[at, :]
        outs = []
        for half in range(2):
            here = low if half == 0 else ~low
            q_here = jnp.where(here, q, jnp.zeros_like(q))
            do_here = jnp.where(here, do, jnp.zeros_like(do))
            inner = jnp.sum(jnp.where(here, product, 0.0), axis=-1, keepdims=True)
            log = lse[:, half * HEAD : half * HEAD + 1]
            soft = jnp.exp(dot(q_here, keys, NT) + bias - log)
            grad = (soft * (dot(do_here, values, NT) - inner)).astype(BF16)
            outs.append(dot(grad, keys, NN))
            dk = dk + dot(q_here, grad, TN)
            dv = dv + dot(do_here, soft.astype(BF16), TN)
        dq_ref[at, :] = (jnp.where(low, outs[0], outs[1]) * SCALE).astype(BF16)
    for i, value in enumerate((dk.T, dv.T)):
        at = slice(i * LANES, (i + 1) * LANES)
        own_ref[:, at] = value[:rows]
        other_ref[:, at] = value[rows:].astype(BF16)


def attend_back(qkv, kv_other, bias, out, lse, grad_out, first, count):
    rows, width = out.shape
    pairs = width // LANES
    spec = lambda base: pl.BlockSpec((rows, LANES), lambda p: (0, base + first + p))
    result = lambda cols: pl.BlockSpec((rows, cols), lambda p: (0, p))
    return pl.pallas_call(
        attend_back_kernel,
        out_shape=(
            jax.ShapeDtypeStruct((rows, count * LANES), BF16),
            jax.ShapeDtypeStruct((rows, 2 * count * LANES), F32),
            jax.ShapeDtypeStruct((rows, 2 * count * LANES), BF16),
        ),
        grid=(count,),
        in_specs=[
            spec(0),
            spec(pairs),
            spec(2 * pairs),
            spec(0),
            spec(pairs),
            pl.BlockSpec((1, 2 * rows), lambda p: (0, 0)),
            spec(0),
            spec(0),
            spec(0),
        ],
        out_specs=(result(LANES), result(2 * LANES), result(2 * LANES)),
        compiler_params=pltpu.CompilerParams(vmem_limit_bytes=56 << 20),
        cost_estimate=cost(3 * count),
        name="attend_back",
    )(qkv, qkv, qkv, kv_other, kv_other, bias, out, lse, grad_out)


def gelu_parts(v):
    cdf = 0.5 * (1.0 + lax.erf(v * (2.0 ** -0.5)))
    pdf = jnp.exp(-0.5 * v * v) * 0.3989422804014327
    return v * cdf, cdf + v * pdf


def norm(values):
    center = values - jnp.mean(values, axis=-1, keepdims=True)
    inv_dev = lax.rsqrt(jnp.mean(center * center, axis=-1, keepdims=True) + EPS)
    return center * inv_dev, inv_dev


def norm_back(scaled, normed, inv_dev):
    return inv_dev * (
        scaled
        - jnp.mean(scaled, axis=-1, keepdims=True)
        - normed * jnp.mean(scaled * normed, axis=-1, keepdims=True)
    )


def total(value):
    return jnp.sum(value, axis=0, keepdims=True)


def join(parts, starts, size, micros):
    rows, cols = parts[0].shape[0], len(starts) * len(parts) * size

    def body(*refs):
        parts, out = refs[:-1], refs[-1]
        at = 0
        for start in starts:
            for part in parts:
                out[:, at : at + size] = part[:, start : start + size]
                at += size

    vmem = pl.BlockSpec(memory_space=pltpu.VMEM)
    return pl.pallas_call(
        body,
        out_shape=like((rows, cols), parts[0].dtype),
        in_specs=[vmem] * len(parts),
        out_specs=vmem,
        cost_estimate=cost(micros),
        name="join",
    )(*parts)


def project(x_parts, head_row, table, pieces):
    block, width = x_parts[0].shape
    rows = block * len(x_parts)
    n = len(pieces)

    def body(table, *refs):
        part_refs, bias_ref, refs = refs[:N_MP], refs[N_MP], refs[N_MP + 1 :]
        pieces, (x_ref, qkv_ref, kv_ref, held, sems) = refs[:n], refs[n:]
        weights = Weights(pieces, table, held, sems, 0, width)
        for i, part in enumerate(part_refs):
            x_ref[i * block : (i + 1) * block, :] = part[...]
        x = x_ref[...]
        for i in range(3):
            value = dot(x, weights.get(i), NN) + bias_ref[:, i * width : (i + 1) * width]
            value = value.astype(BF16)
            if i == 0:
                value = (value.astype(F32) * SCALE).astype(BF16)
            else:
                kv_ref[:, (i - 1) * width : i * width] = value
            qkv_ref[:, i * width : (i + 1) * width] = value

    return call(
        body,
        "project",
        7,
        [
            like((rows, width), BF16),
            like((rows, 3 * width), BF16),
            like((rows, 2 * width), BF16),
        ],
        list(x_parts) + [head_row],
        table,
        pieces,
        weight_scratch(pieces, 3 * width, 3),
    )


def feed(x, mixed, cot_parts, smalls, small_row, table, out_pieces, feed_pieces):
    rows, width = x.shape
    hidden = feed_pieces[0].shape[1] // 2
    count = 6
    tile = hidden // count
    spans = [slice(t * tile, (t + 1) * tile) for t in range(count)]
    cols = hidden + width
    n_out, n_up, n = len(out_pieces), len(feed_pieces), len(smalls)
    down_grads = grad_shapes(feed_pieces, hidden)
    mid_grads = grad_shapes(feed_pieces, cols, SHARED)
    g = len(mid_grads)

    def body(table, x_ref, mixed_ref, *refs):
        cot_far, small_far, refs = refs[:N_MP], refs[N_MP : N_MP + n], refs[N_MP + n :]
        out_p, up_p = refs[:n_out], refs[n_out : n_out + n_up]
        refs = refs[n_out + n_up :]
        shared_ref, result_out, da_out, do_out = refs[:4]
        down_outs, mid_outs, refs = refs[4 : 4 + g], refs[4 + g : 4 + 2 * g], refs[4 + 2 * g :]
        w_out, sems_out, w_up, sems_up, w_down, sems_down = refs[:6]
        plain, turned, plain_h, turned_h = refs[6:10]
        small_ref, cot_ref, read_sems = refs[10:13]
        n1_ref, dz_ref, h_ref, act_ref, slope_ref, result_ref, low_ref, do_ref = refs[13:21]
        down_stages, mid_stages = refs[21 : 21 + g], refs[21 + g : 21 + 2 * g]
        shared_low, sems = refs[21 + 2 * g :]
        out_w = Weights(out_p, table, w_out, sems_out, 3 * width, width)
        smalls = [small.at[pl.ds(small_row, SMALL)] for small in small_far]
        reads = Reads(smalls, [small_ref.at[i] for i in range(n)], read_sems)
        up_w = Weights(up_p, table, w_up, sems_up, 0, tile)
        down_w = Weights(up_p, table, w_down, sems_down, hidden, tile)
        block = rows // N_MP
        cots = Reads(
            cot_far,
            [cot_ref.at[pl.ds(i * block, block)] for i in range(N_MP)],
            read_sems.at[pl.ds(n, N_MP)],
        )
        writes = Writes(sems)

        attention = dot(mixed_ref[...], out_w.get(0), NT)
        for i in range(n):
            reads.get(i)
        small = jnp.sum(small_ref[...].astype(F32), axis=0)
        row_vals = sum(small[:, i * width : (i + 1) * width] for i in range(2 * N_MP))
        row = lambda i: row_vals[i : i + 1, :]
        up_b = small[6:7, :hidden]
        n1, r1 = norm(x_ref[...].astype(F32) + attention + row(0))
        n1_ref[...] = n1
        h_ref[...] = (n1 * row(1) + row(2)).astype(BF16)
        feed = jnp.zeros((rows, width), F32)
        u = dot(h_ref[...], up_w.get(0), NN)
        for t, at in enumerate(spans):
            down = down_w.get(t)
            later = dot(h_ref[...], up_w.get(t + 1), NN) if t + 1 < count else None
            act, slope = gelu_parts(u + up_b[:, at])
            act_ref[:, at] = act.astype(BF16)
            slope_ref[:, at] = slope.astype(BF16)
            feed = feed + dot(act_ref[:, at], down, NT)
            u = later
        h = n1_ref[...] * row(1) + row(2)
        n2, r2 = norm(h + feed + row(3))
        result_ref[...] = (n2 * row(4) + row(5)).astype(BF16)
        writes.start(result_ref, result_out)
        for i in range(N_MP):
            cots.get(i)
        gy = cot_ref[...].astype(F32)
        dz = norm_back(gy * row(4), n2, r2)
        dz_ref[...] = dz
        low_ref[...] = dz.astype(BF16)
        sums = [total(dz), total(gy * n2), total(gy)]

        turn(low_ref[...], table, plain, turned)
        turn(h_ref[...], table, plain_h, turned_h)
        shared_ref[...] = jnp.zeros_like(shared_ref)
        dh = dz_ref[...]
        for t, at in enumerate(spans):
            dact = dot(low_ref[...], down_w.get(t), NN)
            store_grad(turned, act_ref[:, at], down_stages, at.start, writes, down_outs)
            du = (dact * slope_ref[:, at].astype(F32)).astype(BF16)
            shared_ref[0:1, at] = total(du.astype(F32))
            dh = dh + dot(du, up_w.get(t), NT)
            store_grad(turned_h, du, mid_stages, at.start, writes, mid_outs)
        n1 = n1_ref[...]
        da = norm_back(dh * row(1), n1, r1)
        dz_ref[...] = da
        writes.start(dz_ref, da_out)
        low_ref[...] = da.astype(BF16)
        do_ref[...] = dot(low_ref[...], out_w.get(0), NN).astype(BF16)
        writes.start(do_ref, do_out)
        sums = [total(da), total(dh * n1), total(dh)] + sums
        for j in range(hidden // width):
            for i, value in enumerate(sums):
                shared_ref[1 + i : 2 + i, j * width : (j + 1) * width] = value
        if g > 1:
            shared_low[...] = shared_ref[...].astype(BF16)
            for out in mid_outs:
                for r in range(out.shape[0]):
                    writes.start(shared_low, out.at[r, pl.ds(block_rows(feed_pieces), SHARED)])
        turn(low_ref[...], table, plain, turned)
        store_grad(turned, mixed_ref[...], mid_stages, hidden, writes, mid_outs)
        writes.finish()

    near = [((rows, width), F32)] * 2 + [((rows, width), BF16)]
    near += [((rows, hidden), BF16)] * 2 + [((rows, width), BF16)] * 3
    return call(
        body,
        "feed",
        33,
        [
            like((SHARED, cols), F32),
            like((rows, width), BF16),
            like((rows, width), F32),
            like((rows, width), BF16),
        ]
        + down_grads
        + mid_grads,
        [x, mixed],
        table,
        list(cot_parts) + list(smalls) + list(out_pieces) + list(feed_pieces),
        weight_scratch(out_pieces, width)
        + weight_scratch(feed_pieces, hidden) * 2
        + turn_scratch(feed_pieces, rows) * 2
        + [
            pltpu.VMEM((n, SMALL, 2 * hidden), BF16),
            pltpu.VMEM((rows, width), BF16),
            pltpu.SemaphoreType.DMA((n + N_MP,)),
        ]
        + [pltpu.VMEM(*spec) for spec in near]
        + stage_scratch(feed_pieces, hidden)
        + stage_scratch(feed_pieces, cols)
        + [
            pltpu.VMEM((SHARED, cols), BF16),
            pltpu.SemaphoreType.DMA((3 + g * (2 * count + 1) + n_up,)),
        ],
        far=3 + 2 * g,
    )


def project_grads(x, parts, table, pieces):
    rows, width = x.shape
    grads = grad_shapes(pieces, 3 * width, SHARED)
    flat = [value for part in parts for value in part]
    g = len(grads)

    def body(table, x_ref, *refs):
        part_refs, refs = refs[: len(flat)], refs[len(flat) :]
        dqkv_ref, shared_ref = refs[:2]
        grad_outs, refs = refs[2 : 2 + g], refs[2 + g :]
        plain, turned = refs[:2]
        stages, shared_low, sems = refs[2 : 2 + g], refs[2 + g], refs[3 + g]
        writes = Writes(sems)
        turn(x_ref[...], table, plain, turned)
        pair = 0
        for i in range(0, len(flat), 3):
            q_ref, own_ref, back_ref = part_refs[i : i + 3]
            cols = q_ref.shape[1]
            dqkv_ref[:, pair * LANES : pair * LANES + cols] = q_ref[...]
            for p in range(cols // LANES):
                for which in range(2):
                    at = slice((2 * p + which) * LANES, (2 * p + which + 1) * LANES)
                    to = (which + 1) * width + (pair + p) * LANES
                    value = own_ref[:, at] + back_ref[:, at].astype(F32)
                    dqkv_ref[:, to : to + LANES] = value.astype(BF16)
            pair += cols // LANES
        for i in range(3):
            at = i * width
            store_grad(turned, dqkv_ref[:, at : at + width], stages, at, writes, grad_outs)
        shared_ref[...] = jnp.zeros_like(shared_ref)
        shared_ref[0:1, :] = total(dqkv_ref[...].astype(F32))
        if g > 1:
            shared_low[...] = shared_ref[...].astype(BF16)
            for out in grad_outs:
                for r in range(out.shape[0]):
                    writes.start(shared_low, out.at[r, pl.ds(block_rows(pieces), SHARED)])
        writes.finish()

    return call(
        body,
        "project_grads",
        7,
        [like((rows, 3 * width), BF16), like((SHARED, 3 * width), F32)] + grads,
        [x] + flat,
        table,
        [],
        turn_scratch(pieces, rows)
        + stage_scratch(pieces, 3 * width)
        + [
            pltpu.VMEM((SHARED, 3 * width), BF16),
            pltpu.SemaphoreType.DMA((3 * g + len(blocks_of(pieces)),)),
        ],
        far=g,
    )


def project_back(da, dqkv, table, pieces):
    rows, width = da.shape
    n = len(pieces)

    def body(table, da_ref, dqkv_ref, *refs):
        pieces, (out_ref, held, sems) = refs[:n], refs[n:]
        weights = Weights(pieces, table, held, sems, 0, width)
        value = da_ref[...]
        for i in range(3):
            value = value + dot(dqkv_ref[:, i * width : (i + 1) * width], weights.get(i), NT)
        out_ref[...] = value.astype(BF16)

    return call(
        body,
        "project_back",
        8,
        [like((rows, width), BF16)],
        [da, dqkv],
        table,
        pieces,
        weight_scratch(pieces, 3 * width, 3),
    )[0]


def at_column(values, rows, width, column):
    return lax.dynamic_update_slice(jnp.zeros((rows, width), values.dtype), values, (0, column))


def small_block(row_params, expand_bias, mine, depth):
    high = lax.reduce_precision(row_params, 8, 7)
    column = (mine * N_MP + depth) * row_params.shape[1]
    high_low = [
        at_column(part.astype(BF16), 6, WIDTH, column) for part in (high, row_params - high)
    ]
    bias = at_column(expand_bias, 2, 2 * WIDTH, mine * expand_bias.shape[1])
    return jnp.concatenate([jnp.concatenate(high_low, axis=1), bias])


def key_bias(length_long, length_short, block, core, depth):
    lengths = jnp.concatenate([length_long, length_short])
    other = core_swap(lengths)
    longs = jnp.where(core == 0, jnp.stack([lengths[0], other[0]]), jnp.stack([other[0], lengths[0]]))
    length = jnp.concatenate([longs, lengths[1:]])[depth]
    is_long = depth < 2
    place = lax.broadcasted_iota(jnp.int32, (1, 2 * N_MP * block), 1)
    row = place % (N_MP * block)
    is_own = place < N_MP * block
    source = (row // block) ^ depth
    whose = jnp.where(is_own, core, 1 - core)
    frame = row % block + jnp.where(is_long, (2 * source + whose) * block, source * block)
    counted = (frame < length) & (is_own | is_long)
    return jnp.where(counted, 0.0, NEG_FILL).astype(F32)


def on_device(
    frames_long,
    frames_short,
    length_long,
    length_short,
    input_proj,
    output_proj,
    expand_weight,
    shrink_weight,
    head_bias,
    expand_bias,
    row_params,
    cotangent_long,
    cotangent_short,
):
    mine = lax.axis_index("dp")
    depth = lax.axis_index("mp")
    n_dp = lax.axis_size("dp")
    fast = n_dp == 8
    core = mine % 2
    block = frames_short.shape[1]
    shard, group = input_proj.shape[1:]
    units = expand_weight.shape[1]
    width = group * N_MP
    hidden = units * N_MP
    table = block_table(mine, n_dp)

    joined = jnp.concatenate(
        [input_proj[0], input_proj[1], input_proj[2], output_proj.T], axis=1
    )
    none = jnp.zeros((SMALL, group), BF16)
    heads = [at_column(head_bias[i], SMALL, group, mine * head_bias.shape[2]) for i in range(2)]
    heads = jnp.concatenate([heads[0], none, heads[1], none], axis=1)
    attn_parts = mp_gather(jnp.concatenate([joined, heads]))
    x_blocks = clip_blocks(frames_long[0], frames_short, core)
    cot_blocks = clip_blocks(cotangent_long[0], cotangent_short, core)
    bias = key_bias(length_long, length_short, block, core, depth)
    feed_shard = jnp.concatenate(
        [
            jnp.concatenate([expand_weight, shrink_weight.T], axis=1),
            small_block(row_params, expand_bias, mine, depth),
        ]
    )
    *attn_parts, feed_shard, bias, x_blocks, cot_blocks = tie(
        *attn_parts, feed_shard, bias, x_blocks, cot_blocks
    )
    attn_slab = join(attn_parts, [i * group for i in range(4)], group, 10)
    feed_parts = mp_gather(feed_shard)
    if fast:
        attn_p = [attn_slab, dp_swap(attn_slab, early), dp_swap(attn_slab, late)]
        x_pieces = clip_pieces(x_blocks, depth)
        both = tie(*attn_p, *x_pieces, *feed_parts)
        attn_p, x_pieces, feed_parts = list(both[:3]), both[3:7], both[7:]
        x_parts = [x_pieces[0]] + [mp_swap(x_pieces[i], i) for i in range(1, N_MP)]
        three = dp_swap(attn_p[1], late)
        feed_slab, three, x_parts[1], x_parts[3] = tie(
            join(feed_parts, (0, units), units, 10), three, x_parts[1], x_parts[3]
        )
        attn_p.append(three)
        attn_p.append(core_swap(jnp.concatenate(attn_p)))
        feed_one = dp_swap(feed_slab, early)
        feed_two = dp_swap(feed_slab, late)
        *x_parts, cot_blocks, own_slab = tie(*x_parts, cot_blocks, feed_slab)
        heads = sum(
            p[first + shard : first + shard + SMALL].astype(F32) for p, first in blocks_of(attn_p)
        )
    else:
        x_parts = to_clips(x_blocks, depth)
        gather = lambda slab: lax.all_gather(slab, "dp", axis=0)
        whole = gather(attn_slab)
        heads = jnp.sum(whole[:, shard:].astype(F32), axis=0)
        attn_p = [whole[:, :shard].reshape(width, 4 * width)]
        whole = gather(join(feed_parts, (0, units), units, 10))
        small = jnp.sum(whole[:, shard:].astype(F32), axis=0)
        feed_p = [whole[:, :shard].reshape(width, 2 * hidden)]
    cot_parts = to_clips(cot_blocks, depth)
    head_row = heads[:1, : 3 * width]

    x, qkv, kv = project(x_parts, head_row, table, attn_p)
    if fast:
        kv, feed_one, feed_two, cot_parts[3], own_slab = tie(
            kv, feed_one, feed_two, cot_parts[3], core_swap(own_slab)
        )
    kv_other = core_swap(kv)
    if fast:
        feed_three = dp_swap(feed_one, late)
        feed_p = [feed_slab, feed_one, feed_two]
        backs = [own_slab] + [core_swap(piece) for piece in feed_p[1:]]
    mixed, lse = attend(qkv, kv_other, bias)
    if fast:
        mixed, feed_three, *both = tie(mixed, feed_three, *backs, *cot_parts)
        backs, cot_parts = both[:3], both[3:]
        feed_p = feed_p + [feed_three] + backs + [core_swap(feed_three)]
        smalls, small_row = feed_p, shard
    else:
        smalls, small_row = [small.astype(BF16)], 0
    outs = feed(x, mixed, cot_parts, smalls, small_row, table, attn_p, feed_p)
    mid_shared, result, da, do, *grads = outs
    g_down, g_mid = grads[: len(grads) // 2], grads[len(grads) // 2 :]

    def by_group_of(value, sizes):
        starts = [N_MP * sum(sizes[:i]) for i in range(len(sizes))]
        return [
            jnp.concatenate(
                [value[:, a + j * n : a + (j + 1) * n] for a, n in zip(starts, sizes)], axis=1
            )
            for j in range(N_MP)
        ]

    def last_sum(keep, back):
        return keep[0].astype(F32) + back[0].astype(F32)

    result_parts = from_clips(result)
    if fast:
        b_down, send = tie(core_swap(g_down[1]), g_mid[1])
        k_down, a_down = half_sums(g_down[0], b_down)
        do, a_down = tie(do, a_down)
        b_down = dp_swap(a_down, late)
        b_mid = core_swap(send)
    pairs = width // LANES
    first = pairs // 3
    dq_a, own_a, other_a = attend_back(qkv, kv_other, bias, mixed, lse, do, 0, first)
    if fast:
        other_a, b_down, b_mid, result_parts[3] = tie(other_a, b_down, b_mid, result_parts[3])
        k_down, a_down = half_sums(k_down, b_down)
        k_mid, a_mid = half_sums(g_mid[0], b_mid)
        do, a_down, a_mid = tie(do, a_down, a_mid)
        b_mid = dp_swap(a_mid, late)
        b_down = dp_swap(a_down, early)
    back_a = core_swap(other_a)
    dq_b, own_b, other_b = attend_back(
        qkv, kv_other, bias, mixed, lse, do, first, pairs - first
    )
    if fast:
        other_b, back_a, b_mid, b_down, *result_parts = tie(
            other_b, back_a, b_mid, b_down, *result_parts
        )
    back_b = core_swap(other_b)
    if fast:
        s_down = by_group_of(last_sum(k_down, b_down), [units])
        k_mid, a_mid = half_sums(k_mid, b_mid)
        back_b, a_mid, *s_down = tie(back_b, a_mid, *s_down)
        b_mid = dp_swap(a_mid, early)
        z_down = mp_away(s_down)
    result_long, result_short = frames_of(result_parts, core, depth)
    parts = [(dq_a, own_a, back_a), (dq_b, own_b, back_b)]
    dqkv, attn_shared, *g_attn = project_grads(x, parts, table, attn_p)
    if fast:
        *both, b_mid = tie(*g_attn, *z_down, b_mid)
        g_attn, z_down = both[:2], both[2:]
        b_attn = core_swap(g_attn[1])
        s_mid = by_group_of(last_sum(k_mid, b_mid), [units, group])
        k_attn, a_attn = half_sums(g_attn[0], b_attn)
        dqkv, a_attn, *s_mid = tie(dqkv, a_attn, *s_mid)
        b_attn = dp_swap(a_attn, late)
        z_mid = mp_away(s_mid)
    frames_grad = project_back(da, dqkv, table, attn_p)
    if fast:
        frames_grad, b_attn = tie(frames_grad, b_attn)
        k_attn, a_attn = half_sums(k_attn, b_attn)
        frames_grad, a_attn = tie(frames_grad, a_attn)
    grad_parts = from_clips(frames_grad)
    if fast:
        b_attn, *grad_parts = tie(dp_swap(a_attn, early), *grad_parts)
        s_attn = last_sum(k_attn, b_attn)
    else:
        scatter = lambda g: lax.psum_scatter(g[0][0], "dp", scatter_dimension=0, tiled=True)
        s_down = by_group_of(scatter(g_down), [units])
        z_down = mp_away(s_down)
        s_mid = jnp.concatenate([scatter(g_mid), lax.psum(mid_shared, "dp")])
        s_mid = by_group_of(s_mid, [units, group])
        z_mid = mp_away(s_mid)
        s_attn = jnp.concatenate([scatter(g_attn), lax.psum(attn_shared, "dp")])
    s_attn = by_group_of(s_attn, [group] * 3)
    grad_long, grad_short = frames_of(grad_parts, core, depth)
    attn_share = mp_total(s_attn[0], mp_away(s_attn))
    down_share = mp_total(s_down[0], z_down).T
    mid_share = mp_total(s_mid[0], z_mid)
    up_share = mid_share[:shard, :units]
    output_share = mid_share[:shard, units:].T
    input_share = jnp.stack(
        [attn_share[:shard, i * group : (i + 1) * group] for i in range(3)]
    )
    up_cols, head_cols, row_cols = units // n_dp, group // n_dp, width // (n_dp * N_MP)
    rank = mine * N_MP + depth
    up_b_share = lax.dynamic_slice(mid_share, (shard, mine * up_cols), (1, up_cols))
    row_share = lax.dynamic_slice(mid_share, (shard + 1, rank * row_cols), (6, row_cols))
    head_share = jnp.stack(
        [
            lax.dynamic_slice(attn_share, (shard, at + mine * head_cols), (1, head_cols))
            for at in (0, 2 * group)
        ]
    )
    return (
        result_long,
        result_short,
        grad_long.astype(F32),
        grad_short.astype(F32),
        input_share,
        output_share,
        up_share,
        down_share,
        head_share,
        up_b_share,
        row_share,
    )


def solution(mesh):
    return jax.shard_map(
        on_device,
        mesh=mesh,
        in_specs=(
            P("dp", "mp", None),
            P("dp", "mp", None),
            P("dp"),
            P("dp"),
            P(None, "dp", "mp"),
            P("mp", "dp"),
            P("dp", "mp"),
            P("mp", "dp"),
            P(None, "mp", "dp"),
            P("mp", "dp"),
            P(None, ("dp", "mp")),
            P("dp", "mp", None),
            P("dp", "mp", None),
        ),
        out_specs=(
            P("dp", "mp", None),
            P("dp", "mp", None),
            P("dp", "mp", None),
            P("dp", "mp", None),
            P(None, "dp", "mp"),
            P("mp", "dp"),
            P("dp", "mp"),
            P("mp", "dp"),
            P(None, "mp", "dp"),
            P("mp", "dp"),
            P(None, ("dp", "mp")),
        ),
        check_vma=False,
    )
```

```python
import functools

import jax
import jax.numpy as jnp
from jax import lax
from jax.experimental import pallas as pl
from jax.experimental.pallas import tpu as pltpu
from jax.sharding import PartitionSpec as P

HEAD = 64
EPS = 1e-05
NEG_FILL = -1e30
SCALE = HEAD ** (-0.5)
N_MP = 4
PARTS = 1
CS = 0.3
WIDTH = 768
SMALL = 8
SHARED = 8
LANES = 128
Q_TILE = 256
F32 = jnp.float32
BF16 = jnp.bfloat16
NT = (((1,), (1,)), ((), ()))
NN = (((1,), (0,)), ((), ()))
TN = (((0,), (0,)), ((), ()))


def dot(left, right, dims):
    return lax.dot_general(left, right, dims, preferred_element_type=F32)


def mp_swap(value, step):
    return lax.ppermute(value, "mp", [(i, i ^ step) for i in range(N_MP)])


def dp_swap(value, target):
    size = lax.axis_size("dp")
    return lax.ppermute(value, "dp", [(i, target(i)) for i in range(size)])


def core_swap(value):
    return dp_swap(value, lambda i: i ^ 1)


def clip_blocks(long_rows, short_rows, core):
    block = short_rows.shape[1]
    keep = lax.dynamic_slice_in_dim(long_rows, core * block, block, 0)
    away = lax.dynamic_slice_in_dim(long_rows, (1 - core) * block, block, 0)
    back = core_swap(away)
    first = jnp.where(core == 0, keep, back)
    second = jnp.where(core == 0, back, keep)
    return jnp.stack([first, second, short_rows[0], short_rows[1]])


def clip_pieces(blocks, depth):
    return [
        lax.dynamic_index_in_dim(blocks, depth ^ step, 0, keepdims=False) for step in range(N_MP)
    ]


def to_clips(blocks, depth):
    pieces = clip_pieces(blocks, depth)
    return pieces[:1] + [mp_swap(pieces[step], step) for step in range(1, N_MP)]


def from_clips(rows):
    block = rows.shape[0] // N_MP
    parts = []
    for step in range(N_MP):
        piece = rows[step * block : (step + 1) * block]
        parts.append(piece if step == 0 else mp_swap(piece, step))
    return parts


def frames_of(parts, core, depth):
    blocks = jnp.stack(parts)
    first, second, short_a, short_b = (
        lax.dynamic_index_in_dim(blocks, depth ^ i, 0, keepdims=False) for i in range(N_MP)
    )
    keep = jnp.where(core == 0, first, second)
    away = jnp.where(core == 0, second, first)
    back = core_swap(away)
    low = jnp.where(core == 0, keep, back)
    high = jnp.where(core == 0, back, keep)
    return jnp.concatenate([low, high], axis=0)[None], jnp.stack([short_a, short_b])


def flip(index, late):
    return index ^ ((4 if late else 2) if index % 2 == 0 else (2 if late else 4))


def block_table(mine, size):
    if size != 8:
        return jnp.zeros((1,), jnp.int32)
    early = jnp.where(mine % 2 == 0, 2, 4)
    late = 6 - early
    relative = [0, early, late, 6, 1, 1 ^ late, 1 ^ early, 7]
    return jnp.stack([mine ^ r for r in relative]).astype(jnp.int32)


def early(i):
    return flip(i, False)


def late(i):
    return flip(i, True)


def across(i):
    return i ^ 6


def tie(*values):
    return lax.optimization_barrier(values)


def swap_plane(plane):
    return plane + [core_swap(piece) for piece in plane]


def to_slab(parts):
    return jnp.concatenate(parts, axis=1)


def mp_gather(shard):
    return [shard] + [mp_swap(shard, step) for step in range(1, N_MP)]


def half_sums(keep, back):
    half = keep.shape[0] // 2
    add = lambda at: (keep[at].astype(F32) + back[at].astype(F32)).astype(BF16)
    return add(slice(0, half)), add(slice(half, None))


def mp_away(parts):
    return [mp_swap(parts[step].astype(BF16), step) for step in range(1, N_MP)]


def mp_total(own, backs):
    for back in backs:
        own = own + back.astype(F32)
    return own


def blocks_of(pieces):
    step = pieces[0].shape[0]
    return [(p, k * step) for p in pieces for k in range(p.shape[0] // step)]


def block_rows(pieces):
    return WIDTH // len(blocks_of(pieces))


class Weights:
    def __init__(self, pieces, table, held, sems, lo, tile):
        self.held, self.tile = held, tile
        cols, parts = held.shape[2], sems.shape[0]
        self.span, self.copies = cols // parts, []
        for t in range(parts):
            row = []
            for k, (piece, first) in enumerate(blocks_of(pieces)):
                copy = pltpu.make_async_copy(
                    piece.at[pl.ds(first, held.shape[1]), pl.ds(lo + t * self.span, self.span)],
                    held.at[table[k], :, pl.ds(t * self.span, self.span)],
                    sems.at[t, k],
                )
                copy.start()
                row.append(copy)
            self.copies.append(row)
        self.waited = 0

    def get(self, t):
        at = t * self.tile
        while self.waited * self.span < at + self.tile:
            for copy in self.copies[self.waited]:
                copy.wait()
            self.waited += 1
        count, rows, _ = self.held.shape
        return self.held[:, :, at : at + self.tile].reshape(count * rows, self.tile)


def weight_scratch(pieces, cols, parts=1):
    return [
        pltpu.VMEM((len(blocks_of(pieces)), block_rows(pieces), cols), BF16),
        pltpu.SemaphoreType.DMA((parts, len(blocks_of(pieces)))),
    ]


def grad_shapes(pieces, cols, extra=0):
    count, rows = len(blocks_of(pieces)), block_rows(pieces)
    if count == 1:
        return [jax.ShapeDtypeStruct((1, rows, cols), F32)]
    return [jax.ShapeDtypeStruct((count // 2, rows + extra, cols), BF16)] * 2


def turn_scratch(pieces, rows):
    return [pltpu.VMEM((len(blocks_of(pieces)), block_rows(pieces), rows), BF16)] * 2


def turn(value, table, plain, turned):
    plain[...] = value.T.reshape(plain.shape)
    for r in range(plain.shape[0]):
        turned[r] = plain[table[r]]


def stage_scratch(pieces, cols):
    return [
        pltpu.VMEM((g.shape[0], block_rows(pieces), cols), g.dtype)
        for g in grad_shapes(pieces, cols)
    ]


def store_grad(turned, right, stages, at, writes=None, outs=None):
    count, rows, _ = turned.shape
    grad = dot(turned[...].reshape(count * rows, -1), right, NN)
    half, cols = count // len(stages), right.shape[1]
    for r in range(count):
        stage = stages[r // half]
        part = grad[r * rows : (r + 1) * rows].astype(stage.dtype)
        stage[r % half, :rows, at : at + cols] = part
    if writes is not None:
        for stage, out in zip(stages, outs):
            writes.start(
                stage.at[:, :, pl.ds(at, cols)],
                out.at[:, pl.ds(0, rows), pl.ds(at, cols)],
            )


class Writes:
    def __init__(self, sems):
        self.sems, self.copies = sems, []

    def start(self, source, target):
        copy = pltpu.make_async_copy(source, target, self.sems.at[len(self.copies)])
        copy.start()
        self.copies.append(copy)

    def finish(self):
        for copy in self.copies:
            copy.wait()


class Reads:
    def __init__(self, sources, targets, sems):
        self.targets, self.copies = targets, []
        for i, (source, target) in enumerate(zip(sources, targets)):
            copy = pltpu.make_async_copy(source, target, sems.at[i])
            copy.start()
            self.copies.append(copy)

    def get(self, i):
        self.copies[i].wait()
        return self.targets[i]


def read_scratch(arrays):
    return [pltpu.VMEM(a.shape, a.dtype) for a in arrays] + [
        pltpu.SemaphoreType.DMA((len(arrays),))
    ]


def cost(micros):
    return pl.CostEstimate(
        flops=int(micros * 1.1e9 * CS), bytes_accessed=int(micros * 1e5 * CS), transcendentals=0
    )


def call(body, name, micros, outs, arrays, table, pieces, scratch, far=0):
    vmem = pl.BlockSpec(memory_space=pltpu.VMEM)
    away = pl.BlockSpec(memory_space=pl.ANY)
    return pl.pallas_call(
        body,
        out_shape=tuple(outs),
        in_specs=[pl.BlockSpec(memory_space=pltpu.SMEM)]
        + [vmem] * len(arrays)
        + [away] * len(pieces),
        out_specs=(vmem,) * (len(outs) - far) + (away,) * far,
        scratch_shapes=scratch,
        compiler_params=pltpu.CompilerParams(vmem_limit_bytes=60 << 20),
        cost_estimate=cost(micros),
        name=name,
    )(table, *arrays, *pieces)


def like(shape, kind):
    return jax.ShapeDtypeStruct(shape, kind)


def attend_kernel(q_ref, k_ref, v_ref, kp_ref, vp_ref, bias_ref, o_ref, lse_ref):
    rows = q_ref.shape[0]
    keys = jnp.concatenate([k_ref[...], kp_ref[...]], axis=0)
    values = jnp.concatenate([v_ref[...], vp_ref[...]], axis=0)
    bias = bias_ref[...]
    tile = min(rows, Q_TILE)
    low = lax.broadcasted_iota(jnp.int32, (tile, LANES), 1) < HEAD
    for start in range(0, rows, tile):
        q = q_ref[start : start + tile, :]
        outs, logs = [], []
        for half in range(2):
            here = low if half == 0 else ~low
            q_here = jnp.where(here, q, jnp.zeros_like(q))
            scores = dot(q_here, keys, NT) + bias
            top = jnp.max(scores, axis=-1, keepdims=True)
            raised = jnp.exp(scores - top)
            total = jnp.sum(raised, axis=-1, keepdims=True)
            mixed = dot(raised.astype(BF16), values, NN)
            outs.append(mixed / total)
            logs.append(top + jnp.log(total))
        o_ref[start : start + tile, :] = jnp.where(low, outs[0], outs[1]).astype(BF16)
        lse_ref[start : start + tile, :] = jnp.where(low, logs[0], logs[1])


def attend(qkv, kv_other, bias):
    rows, width = qkv.shape[0], qkv.shape[1] // 3
    pairs = width // LANES
    spec = lambda base: pl.BlockSpec((rows, LANES), lambda p: (0, base + p))
    return pl.pallas_call(
        attend_kernel,
        out_shape=(
            jax.ShapeDtypeStruct((rows, width), BF16),
            jax.ShapeDtypeStruct((rows, width), F32),
        ),
        grid=(pairs,),
        in_specs=[
            spec(0),
            spec(pairs),
            spec(2 * pairs),
            spec(0),
            spec(pairs),
            pl.BlockSpec((1, 2 * rows), lambda p: (0, 0)),
        ],
        out_specs=(spec(0), spec(0)),
        compiler_params=pltpu.CompilerParams(vmem_limit_bytes=56 << 20),
        cost_estimate=cost(15),
        name="attend",
    )(qkv, qkv, qkv, kv_other, kv_other, bias)


def attend_back_kernel(
    q_ref, k_ref, v_ref, kp_ref, vp_ref, bias_ref, o_ref, lse_ref, do_ref,
    dq_ref, own_ref, other_ref,
):
    rows = q_ref.shape[0]
    keys = jnp.concatenate([k_ref[...], kp_ref[...]], axis=0)
    values = jnp.concatenate([v_ref[...], vp_ref[...]], axis=0)
    bias = bias_ref[...]
    tile = min(rows, Q_TILE)
    low = lax.broadcasted_iota(jnp.int32, (tile, LANES), 1) < HEAD
    dk = jnp.zeros((LANES, 2 * rows), F32)
    dv = jnp.zeros((LANES, 2 * rows), F32)
    for start in range(0, rows, tile):
        at = slice(start, start + tile)
        q, do = q_ref[at, :], do_ref[at, :]
        product = o_ref[at, :].astype(F32) * do.astype(F32)
        lse = lse_ref[at, :]
        outs = []
        for half in range(2):
            here = low if half == 0 else ~low
            q_here = jnp.where(here, q, jnp.zeros_like(q))
            do_here = jnp.where(here, do, jnp.zeros_like(do))
            inner = jnp.sum(jnp.where(here, product, 0.0), axis=-1, keepdims=True)
            log = lse[:, half * HEAD : half * HEAD + 1]
            soft = jnp.exp(dot(q_here, keys, NT) + bias - log)
            grad = (soft * (dot(do_here, values, NT) - inner)).astype(BF16)
            outs.append(dot(grad, keys, NN))
            dk = dk + dot(q_here, grad, TN)
            dv = dv + dot(do_here, soft.astype(BF16), TN)
        dq_ref[at, :] = (jnp.where(low, outs[0], outs[1]) * SCALE).astype(BF16)
    for i, value in enumerate((dk.T, dv.T)):
        at = slice(i * LANES, (i + 1) * LANES)
        own_ref[:, at] = value[:rows]
        other_ref[:, at] = value[rows:].astype(BF16)


def attend_back(qkv, kv_other, bias, out, lse, grad_out, first, count):
    rows, width = out.shape
    pairs = width // LANES
    spec = lambda base: pl.BlockSpec((rows, LANES), lambda p: (0, base + first + p))
    result = lambda cols: pl.BlockSpec((rows, cols), lambda p: (0, p))
    return pl.pallas_call(
        attend_back_kernel,
        out_shape=(
            jax.ShapeDtypeStruct((rows, count * LANES), BF16),
            jax.ShapeDtypeStruct((rows, 2 * count * LANES), F32),
            jax.ShapeDtypeStruct((rows, 2 * count * LANES), BF16),
        ),
        grid=(count,),
        in_specs=[
            spec(0),
            spec(pairs),
            spec(2 * pairs),
            spec(0),
            spec(pairs),
            pl.BlockSpec((1, 2 * rows), lambda p: (0, 0)),
            spec(0),
            spec(0),
            spec(0),
        ],
        out_specs=(result(LANES), result(2 * LANES), result(2 * LANES)),
        compiler_params=pltpu.CompilerParams(vmem_limit_bytes=56 << 20),
        cost_estimate=cost(3 * count),
        name="attend_back",
    )(qkv, qkv, qkv, kv_other, kv_other, bias, out, lse, grad_out)


def gelu_parts(v):
    cdf = 0.5 * (1.0 + lax.erf(v * (2.0 ** -0.5)))
    pdf = jnp.exp(-0.5 * v * v) * 0.3989422804014327
    return v * cdf, cdf + v * pdf


def norm(values):
    center = values - jnp.mean(values, axis=-1, keepdims=True)
    inv_dev = lax.rsqrt(jnp.mean(center * center, axis=-1, keepdims=True) + EPS)
    return center * inv_dev, inv_dev


def norm_back(scaled, normed, inv_dev):
    return inv_dev * (
        scaled
        - jnp.mean(scaled, axis=-1, keepdims=True)
        - normed * jnp.mean(scaled * normed, axis=-1, keepdims=True)
    )


def total(value):
    return jnp.sum(value, axis=0, keepdims=True)


def join(parts, starts, size, micros):
    rows, cols = parts[0].shape[0], len(starts) * len(parts) * size

    def body(*refs):
        parts, out = refs[:-1], refs[-1]
        at = 0
        for start in starts:
            for part in parts:
                out[:, at : at + size] = part[:, start : start + size]
                at += size

    vmem = pl.BlockSpec(memory_space=pltpu.VMEM)
    return pl.pallas_call(
        body,
        out_shape=like((rows, cols), parts[0].dtype),
        in_specs=[vmem] * len(parts),
        out_specs=vmem,
        cost_estimate=cost(micros),
        name="join",
    )(*parts)


def project(x_parts, head_row, table, pieces):
    block, width = x_parts[0].shape
    rows = block * len(x_parts)
    n = len(pieces)

    def body(table, *refs):
        part_refs, bias_ref, refs = refs[:N_MP], refs[N_MP], refs[N_MP + 1 :]
        pieces, (x_ref, qkv_ref, kv_ref, held, sems) = refs[:n], refs[n:]
        weights = Weights(pieces, table, held, sems, 0, width)
        for i, part in enumerate(part_refs):
            x_ref[i * block : (i + 1) * block, :] = part[...]
        x = x_ref[...]
        for i in range(3):
            value = dot(x, weights.get(i), NN) + bias_ref[:, i * width : (i + 1) * width]
            value = value.astype(BF16)
            if i == 0:
                value = (value.astype(F32) * SCALE).astype(BF16)
            else:
                kv_ref[:, (i - 1) * width : i * width] = value
            qkv_ref[:, i * width : (i + 1) * width] = value

    return call(
        body,
        "project",
        7,
        [
            like((rows, width), BF16),
            like((rows, 3 * width), BF16),
            like((rows, 2 * width), BF16),
        ],
        list(x_parts) + [head_row],
        table,
        pieces,
        weight_scratch(pieces, 3 * width, 3),
    )


def feed(x, mixed, cot_parts, smalls, small_row, table, out_pieces, feed_pieces):
    rows, width = x.shape
    hidden = feed_pieces[0].shape[1] // 2
    count = 6
    tile = hidden // count
    spans = [slice(t * tile, (t + 1) * tile) for t in range(count)]
    cols = hidden + width
    n_out, n_up, n = len(out_pieces), len(feed_pieces), len(smalls)
    down_grads = grad_shapes(feed_pieces, hidden)
    mid_grads = grad_shapes(feed_pieces, cols, SHARED)
    g = len(mid_grads)

    def body(table, x_ref, mixed_ref, *refs):
        cot_far, small_far, refs = refs[:N_MP], refs[N_MP : N_MP + n], refs[N_MP + n :]
        out_p, up_p = refs[:n_out], refs[n_out : n_out + n_up]
        refs = refs[n_out + n_up :]
        shared_ref, result_out, da_out, do_out = refs[:4]
        down_outs, mid_outs, refs = refs[4 : 4 + g], refs[4 + g : 4 + 2 * g], refs[4 + 2 * g :]
        w_out, sems_out, w_up, sems_up, w_down, sems_down = refs[:6]
        plain, turned, plain_h, turned_h = refs[6:10]
        small_ref, cot_ref, read_sems = refs[10:13]
        n1_ref, dz_ref, h_ref, act_ref, slope_ref, result_ref, low_ref, do_ref = refs[13:21]
        down_stages, mid_stages = refs[21 : 21 + g], refs[21 + g : 21 + 2 * g]
        shared_low, sems = refs[21 + 2 * g :]
        out_w = Weights(out_p, table, w_out, sems_out, 3 * width, width)
        smalls = [small.at[pl.ds(small_row, SMALL)] for small in small_far]
        reads = Reads(smalls, [small_ref.at[i] for i in range(n)], read_sems)
        up_w = Weights(up_p, table, w_up, sems_up, 0, tile)
        down_w = Weights(up_p, table, w_down, sems_down, hidden, tile)
        block = rows // N_MP
        cots = Reads(
            cot_far,
            [cot_ref.at[pl.ds(i * block, block)] for i in range(N_MP)],
            read_sems.at[pl.ds(n, N_MP)],
        )
        writes = Writes(sems)

        attention = dot(mixed_ref[...], out_w.get(0), NT)
        for i in range(n):
            reads.get(i)
        small = jnp.sum(small_ref[...].astype(F32), axis=0)
        row_vals = sum(small[:, i * width : (i + 1) * width] for i in range(2 * N_MP))
        row = lambda i: row_vals[i : i + 1, :]
        up_b = small[6:7, :hidden]
        n1, r1 = norm(x_ref[...].astype(F32) + attention + row(0))
        n1_ref[...] = n1
        h_ref[...] = (n1 * row(1) + row(2)).astype(BF16)
        feed = jnp.zeros((rows, width), F32)
        u = dot(h_ref[...], up_w.get(0), NN)
        for t, at in enumerate(spans):
            down = down_w.get(t)
            later = dot(h_ref[...], up_w.get(t + 1), NN) if t + 1 < count else None
            act, slope = gelu_parts(u + up_b[:, at])
            act_ref[:, at] = act.astype(BF16)
            slope_ref[:, at] = slope.astype(BF16)
            feed = feed + dot(act_ref[:, at], down, NT)
            u = later
        h = n1_ref[...] * row(1) + row(2)
        n2, r2 = norm(h + feed + row(3))
        result_ref[...] = (n2 * row(4) + row(5)).astype(BF16)
        writes.start(result_ref, result_out)
        for i in range(N_MP):
            cots.get(i)
        gy = cot_ref[...].astype(F32)
        dz = norm_back(gy * row(4), n2, r2)
        dz_ref[...] = dz
        low_ref[...] = dz.astype(BF16)
        sums = [total(dz), total(gy * n2), total(gy)]

        turn(low_ref[...], table, plain, turned)
        turn(h_ref[...], table, plain_h, turned_h)
        shared_ref[...] = jnp.zeros_like(shared_ref)
        dh = dz_ref[...]
        for t, at in enumerate(spans):
            dact = dot(low_ref[...], down_w.get(t), NN)
            store_grad(turned, act_ref[:, at], down_stages, at.start, writes, down_outs)
            du = (dact * slope_ref[:, at].astype(F32)).astype(BF16)
            shared_ref[0:1, at] = total(du.astype(F32))
            dh = dh + dot(du, up_w.get(t), NT)
            store_grad(turned_h, du, mid_stages, at.start, writes, mid_outs)
        n1 = n1_ref[...]
        da = norm_back(dh * row(1), n1, r1)
        dz_ref[...] = da
        writes.start(dz_ref, da_out)
        low_ref[...] = da.astype(BF16)
        do_ref[...] = dot(low_ref[...], out_w.get(0), NN).astype(BF16)
        writes.start(do_ref, do_out)
        sums = [total(da), total(dh * n1), total(dh)] + sums
        for j in range(hidden // width):
            for i, value in enumerate(sums):
                shared_ref[1 + i : 2 + i, j * width : (j + 1) * width] = value
        if g > 1:
            shared_low[...] = shared_ref[...].astype(BF16)
            for out in mid_outs:
                for r in range(out.shape[0]):
                    writes.start(shared_low, out.at[r, pl.ds(block_rows(feed_pieces), SHARED)])
        turn(low_ref[...], table, plain, turned)
        store_grad(turned, mixed_ref[...], mid_stages, hidden, writes, mid_outs)
        writes.finish()

    near = [((rows, width), F32)] * 2 + [((rows, width), BF16)]
    near += [((rows, hidden), BF16)] * 2 + [((rows, width), BF16)] * 3
    return call(
        body,
        "feed",
        33,
        [
            like((SHARED, cols), F32),
            like((rows, width), BF16),
            like((rows, width), F32),
            like((rows, width), BF16),
        ]
        + down_grads
        + mid_grads,
        [x, mixed],
        table,
        list(cot_parts) + list(smalls) + list(out_pieces) + list(feed_pieces),
        weight_scratch(out_pieces, width)
        + weight_scratch(feed_pieces, hidden) * 2
        + turn_scratch(feed_pieces, rows) * 2
        + [
            pltpu.VMEM((n, SMALL, 2 * hidden), BF16),
            pltpu.VMEM((rows, width), BF16),
            pltpu.SemaphoreType.DMA((n + N_MP,)),
        ]
        + [pltpu.VMEM(*spec) for spec in near]
        + stage_scratch(feed_pieces, hidden)
        + stage_scratch(feed_pieces, cols)
        + [
            pltpu.VMEM((SHARED, cols), BF16),
            pltpu.SemaphoreType.DMA((3 + g * (2 * count + 1) + n_up,)),
        ],
        far=3 + 2 * g,
    )


def project_grads(x, parts, table, pieces):
    rows, width = x.shape
    grads = grad_shapes(pieces, 3 * width, SHARED)
    flat = [value for part in parts for value in part]
    g = len(grads)

    def body(table, x_ref, *refs):
        part_refs, refs = refs[: len(flat)], refs[len(flat) :]
        dqkv_ref, shared_ref = refs[:2]
        grad_outs, refs = refs[2 : 2 + g], refs[2 + g :]
        plain, turned = refs[:2]
        stages, shared_low, sems = refs[2 : 2 + g], refs[2 + g], refs[3 + g]
        writes = Writes(sems)
        turn(x_ref[...], table, plain, turned)
        pair = 0
        for i in range(0, len(flat), 3):
            q_ref, own_ref, back_ref = part_refs[i : i + 3]
            cols = q_ref.shape[1]
            dqkv_ref[:, pair * LANES : pair * LANES + cols] = q_ref[...]
            for p in range(cols // LANES):
                for which in range(2):
                    at = slice((2 * p + which) * LANES, (2 * p + which + 1) * LANES)
                    to = (which + 1) * width + (pair + p) * LANES
                    value = own_ref[:, at] + back_ref[:, at].astype(F32)
                    dqkv_ref[:, to : to + LANES] = value.astype(BF16)
            pair += cols // LANES
        for i in range(3):
            at = i * width
            store_grad(turned, dqkv_ref[:, at : at + width], stages, at, writes, grad_outs)
        shared_ref[...] = jnp.zeros_like(shared_ref)
        shared_ref[0:1, :] = total(dqkv_ref[...].astype(F32))
        if g > 1:
            shared_low[...] = shared_ref[...].astype(BF16)
            for out in grad_outs:
                for r in range(out.shape[0]):
                    writes.start(shared_low, out.at[r, pl.ds(block_rows(pieces), SHARED)])
        writes.finish()

    return call(
        body,
        "project_grads",
        7,
        [like((rows, 3 * width), BF16), like((SHARED, 3 * width), F32)] + grads,
        [x] + flat,
        table,
        [],
        turn_scratch(pieces, rows)
        + stage_scratch(pieces, 3 * width)
        + [
            pltpu.VMEM((SHARED, 3 * width), BF16),
            pltpu.SemaphoreType.DMA((3 * g + len(blocks_of(pieces)),)),
        ],
        far=g,
    )


def project_back(da, dqkv, table, pieces):
    rows, width = da.shape
    n = len(pieces)

    def body(table, da_ref, dqkv_ref, *refs):
        pieces, (out_ref, held, sems) = refs[:n], refs[n:]
        weights = Weights(pieces, table, held, sems, 0, width)
        value = da_ref[...]
        for i in range(3):
            value = value + dot(dqkv_ref[:, i * width : (i + 1) * width], weights.get(i), NT)
        out_ref[...] = value.astype(BF16)

    return call(
        body,
        "project_back",
        8,
        [like((rows, width), BF16)],
        [da, dqkv],
        table,
        pieces,
        weight_scratch(pieces, 3 * width, 3),
    )[0]


def at_column(values, rows, width, column):
    return lax.dynamic_update_slice(jnp.zeros((rows, width), values.dtype), values, (0, column))


def small_block(row_params, expand_bias, mine, depth):
    high = lax.reduce_precision(row_params, 8, 7)
    column = (mine * N_MP + depth) * row_params.shape[1]
    high_low = [
        at_column(part.astype(BF16), 6, WIDTH, column) for part in (high, row_params - high)
    ]
    bias = at_column(expand_bias, 2, 2 * WIDTH, mine * expand_bias.shape[1])
    return jnp.concatenate([jnp.concatenate(high_low, axis=1), bias])


def key_bias(length_long, length_short, block, core, depth):
    lengths = jnp.concatenate([length_long, length_short])
    other = core_swap(lengths)
    longs = jnp.where(core == 0, jnp.stack([lengths[0], other[0]]), jnp.stack([other[0], lengths[0]]))
    length = jnp.concatenate([longs, lengths[1:]])[depth]
    is_long = depth < 2
    place = lax.broadcasted_iota(jnp.int32, (1, 2 * N_MP * block), 1)
    row = place % (N_MP * block)
    is_own = place < N_MP * block
    source = (row // block) ^ depth
    whose = jnp.where(is_own, core, 1 - core)
    frame = row % block + jnp.where(is_long, (2 * source + whose) * block, source * block)
    counted = (frame < length) & (is_own | is_long)
    return jnp.where(counted, 0.0, NEG_FILL).astype(F32)


def on_device(
    frames_long,
    frames_short,
    length_long,
    length_short,
    input_proj,
    output_proj,
    expand_weight,
    shrink_weight,
    head_bias,
    expand_bias,
    row_params,
    cotangent_long,
    cotangent_short,
):
    mine = lax.axis_index("dp")
    depth = lax.axis_index("mp")
    n_dp = lax.axis_size("dp")
    fast = n_dp == 8
    core = mine % 2
    block = frames_short.shape[1]
    shard, group = input_proj.shape[1:]
    units = expand_weight.shape[1]
    width = group * N_MP
    hidden = units * N_MP
    table = block_table(mine, n_dp)

    joined = jnp.concatenate(
        [input_proj[0], input_proj[1], input_proj[2], output_proj.T], axis=1
    )
    none = jnp.zeros((SMALL, group), BF16)
    heads = [at_column(head_bias[i], SMALL, group, mine * head_bias.shape[2]) for i in range(2)]
    heads = jnp.concatenate([heads[0], none, heads[1], none], axis=1)
    attn_parts = mp_gather(jnp.concatenate([joined, heads]))
    x_blocks = clip_blocks(frames_long[0], frames_short, core)
    cot_blocks = clip_blocks(cotangent_long[0], cotangent_short, core)
    bias = key_bias(length_long, length_short, block, core, depth)
    feed_shard = jnp.concatenate(
        [
            jnp.concatenate([expand_weight, shrink_weight.T], axis=1),
            small_block(row_params, expand_bias, mine, depth),
        ]
    )
    *attn_parts, feed_shard, bias, x_blocks, cot_blocks = tie(
        *attn_parts, feed_shard, bias, x_blocks, cot_blocks
    )
    attn_slab = join(attn_parts, [i * group for i in range(4)], group, 10)
    feed_parts = mp_gather(feed_shard)
    if fast:
        attn_p = [attn_slab, dp_swap(attn_slab, early), dp_swap(attn_slab, late)]
        x_pieces = clip_pieces(x_blocks, depth)
        both = tie(*attn_p, *x_pieces, *feed_parts)
        attn_p, x_pieces, feed_parts = list(both[:3]), both[3:7], both[7:]
        x_parts = [x_pieces[0]] + [mp_swap(x_pieces[i], i) for i in range(1, N_MP)]
        three = dp_swap(attn_p[1], late)
        feed_slab, three, x_parts[1], x_parts[3] = tie(
            join(feed_parts, (0, units), units, 10), three, x_parts[1], x_parts[3]
        )
        attn_p.append(three)
        attn_p.append(core_swap(jnp.concatenate(attn_p)))
        feed_one = dp_swap(feed_slab, early)
        *x_parts, cot_blocks, own_slab, feed_one = tie(
            *x_parts, cot_blocks, feed_slab, feed_one
        )
        feed_two = dp_swap(own_slab, late)
        heads = sum(
            p[first + shard : first + shard + SMALL].astype(F32) for p, first in blocks_of(attn_p)
        )
    else:
        x_parts = to_clips(x_blocks, depth)
        gather = lambda slab: lax.all_gather(slab, "dp", axis=0)
        whole = gather(attn_slab)
        heads = jnp.sum(whole[:, shard:].astype(F32), axis=0)
        attn_p = [whole[:, :shard].reshape(width, 4 * width)]
        whole = gather(join(feed_parts, (0, units), units, 10))
        small = jnp.sum(whole[:, shard:].astype(F32), axis=0)
        feed_p = [whole[:, :shard].reshape(width, 2 * hidden)]
    cot_parts = to_clips(cot_blocks, depth)
    head_row = heads[:1, : 3 * width]

    x, qkv, kv = project(x_parts, head_row, table, attn_p)
    if fast:
        kv, feed_two, cot_parts[3], own_slab = tie(
            kv, feed_two, cot_parts[3], core_swap(own_slab)
        )
    kv_other = core_swap(kv)
    if fast:
        feed_three = dp_swap(feed_one, late)
        feed_p = [feed_slab, feed_one, feed_two]
        backs = [own_slab] + [core_swap(piece) for piece in feed_p[1:]]
    mixed, lse = attend(qkv, kv_other, bias)
    if fast:
        mixed, feed_three, *both = tie(mixed, feed_three, *backs, *cot_parts)
        backs, cot_parts = both[:3], both[3:]
        feed_p = feed_p + [feed_three] + backs + [core_swap(feed_three)]
        smalls, small_row = feed_p, shard
    else:
        smalls, small_row = [small.astype(BF16)], 0
    outs = feed(x, mixed, cot_parts, smalls, small_row, table, attn_p, feed_p)
    mid_shared, result, da, do, *grads = outs
    g_down, g_mid = grads[: len(grads) // 2], grads[len(grads) // 2 :]

    def by_group_of(value, sizes):
        starts = [N_MP * sum(sizes[:i]) for i in range(len(sizes))]
        return [
            jnp.concatenate(
                [value[:, a + j * n : a + (j + 1) * n] for a, n in zip(starts, sizes)], axis=1
            )
            for j in range(N_MP)
        ]

    def last_sum(keep, back):
        return keep[0].astype(F32) + back[0].astype(F32)

    result_parts = from_clips(result)
    if fast:
        b_down, send = tie(core_swap(g_down[1]), g_mid[1])
        k_down, a_down = half_sums(g_down[0], b_down)
        do, a_down = tie(do, a_down)
        b_down = dp_swap(a_down, late)
        b_mid = core_swap(send)
    pairs = width // LANES
    first = pairs // 2
    dq_a, own_a, other_a = attend_back(qkv, kv_other, bias, mixed, lse, do, 0, first)
    if fast:
        other_a, b_down, b_mid, result_parts[3] = tie(other_a, b_down, b_mid, result_parts[3])
        k_down, a_down = half_sums(k_down, b_down)
        k_mid, a_mid = half_sums(g_mid[0], b_mid)
        do, a_down, a_mid = tie(do, a_down, a_mid)
        b_mid = dp_swap(a_mid, late)
        b_down = dp_swap(a_down, early)
    back_a = core_swap(other_a)
    dq_b, own_b, other_b = attend_back(
        qkv, kv_other, bias, mixed, lse, do, first, pairs - first
    )
    if fast:
        other_b, back_a, b_down, *result_parts = tie(other_b, back_a, b_down, *result_parts)
        s_down = by_group_of(last_sum(k_down, b_down), [units])
    back_b = core_swap(other_b)
    if fast:
        back_b, *s_down = tie(back_b, *s_down)
        z_down = mp_away(s_down)
    parts = [(dq_a, own_a, back_a), (dq_b, own_b, back_b)]
    dqkv, attn_shared, *g_attn = project_grads(x, parts, table, attn_p)
    if fast:
        *both, b_mid = tie(*g_attn, *z_down, b_mid)
        g_attn, z_down = both[:2], both[2:]
        b_attn = core_swap(g_attn[1])
        k_mid, a_mid = half_sums(k_mid, b_mid)
        k_attn, a_attn = half_sums(g_attn[0], b_attn)
        dqkv, a_attn, a_mid = tie(dqkv, a_attn, a_mid)
        b_attn = dp_swap(a_attn, late)
        b_mid = dp_swap(a_mid, early)
    frames_grad = project_back(da, dqkv, table, attn_p)
    if fast:
        frames_grad, b_attn, b_mid = tie(frames_grad, b_attn, b_mid)
        k_attn, a_attn = half_sums(k_attn, b_attn)
        s_mid = by_group_of(last_sum(k_mid, b_mid), [units, group])
        frames_grad, a_attn, *s_mid = tie(frames_grad, a_attn, *s_mid)
    grad_parts = from_clips(frames_grad)
    if fast:
        b_attn, *grad_parts = tie(dp_swap(a_attn, early), *grad_parts)
        s_attn = last_sum(k_attn, b_attn)
        z_mid = mp_away(s_mid)
    else:
        scatter = lambda g: lax.psum_scatter(g[0][0], "dp", scatter_dimension=0, tiled=True)
        s_down = by_group_of(scatter(g_down), [units])
        z_down = mp_away(s_down)
        s_mid = jnp.concatenate([scatter(g_mid), lax.psum(mid_shared, "dp")])
        s_mid = by_group_of(s_mid, [units, group])
        z_mid = mp_away(s_mid)
        s_attn = jnp.concatenate([scatter(g_attn), lax.psum(attn_shared, "dp")])
    s_attn = by_group_of(s_attn, [group] * 3)
    grad_long, grad_short = frames_of(grad_parts, core, depth)
    result_long, result_short = frames_of(result_parts, core, depth)
    attn_share = mp_total(s_attn[0], mp_away(s_attn))
    down_share = mp_total(s_down[0], z_down).T
    mid_share = mp_total(s_mid[0], z_mid)
    up_share = mid_share[:shard, :units]
    output_share = mid_share[:shard, units:].T
    input_share = jnp.stack(
        [attn_share[:shard, i * group : (i + 1) * group] for i in range(3)]
    )
    up_cols, head_cols, row_cols = units // n_dp, group // n_dp, width // (n_dp * N_MP)
    rank = mine * N_MP + depth
    up_b_share = lax.dynamic_slice(mid_share, (shard, mine * up_cols), (1, up_cols))
    row_share = lax.dynamic_slice(mid_share, (shard + 1, rank * row_cols), (6, row_cols))
    head_share = jnp.stack(
        [
            lax.dynamic_slice(attn_share, (shard, at + mine * head_cols), (1, head_cols))
            for at in (0, 2 * group)
        ]
    )
    return (
        result_long,
        result_short,
        grad_long.astype(F32),
        grad_short.astype(F32),
        input_share,
        output_share,
        up_share,
        down_share,
        head_share,
        up_b_share,
        row_share,
    )


def solution(mesh):
    return jax.shard_map(
        on_device,
        mesh=mesh,
        in_specs=(
            P("dp", "mp", None),
            P("dp", "mp", None),
            P("dp"),
            P("dp"),
            P(None, "dp", "mp"),
            P("mp", "dp"),
            P("dp", "mp"),
            P("mp", "dp"),
            P(None, "mp", "dp"),
            P("mp", "dp"),
            P(None, ("dp", "mp")),
            P("dp", "mp", None),
            P("dp", "mp", None),
        ),
        out_specs=(
            P("dp", "mp", None),
            P("dp", "mp", None),
            P("dp", "mp", None),
            P("dp", "mp", None),
            P(None, "dp", "mp"),
            P("mp", "dp"),
            P("dp", "mp"),
            P("mp", "dp"),
            P(None, "mp", "dp"),
            P("mp", "dp"),
            P(None, ("dp", "mp")),
        ),
        check_vma=False,
    )
```

```python
import functools

import jax
import jax.numpy as jnp
from jax import lax
from jax.experimental import pallas as pl
from jax.experimental.pallas import tpu as pltpu
from jax.sharding import PartitionSpec as P

HEAD = 64
EPS = 1e-05
NEG_FILL = -1e30
SCALE = HEAD ** (-0.5)
N_MP = 4
PARTS = 1
CS = 0.3
WIDTH = 768
SMALL = 8
SHARED = 8
LANES = 128
Q_TILE = 256
F32 = jnp.float32
BF16 = jnp.bfloat16
NT = (((1,), (1,)), ((), ()))
NN = (((1,), (0,)), ((), ()))
TN = (((0,), (0,)), ((), ()))


def dot(left, right, dims):
    return lax.dot_general(left, right, dims, preferred_element_type=F32)


def mp_swap(value, step):
    return lax.ppermute(value, "mp", [(i, i ^ step) for i in range(N_MP)])


def dp_swap(value, target):
    size = lax.axis_size("dp")
    return lax.ppermute(value, "dp", [(i, target(i)) for i in range(size)])


def core_swap(value):
    return dp_swap(value, lambda i: i ^ 1)


def clip_blocks(long_rows, short_rows, core):
    block = short_rows.shape[1]
    keep = lax.dynamic_slice_in_dim(long_rows, core * block, block, 0)
    away = lax.dynamic_slice_in_dim(long_rows, (1 - core) * block, block, 0)
    back = core_swap(away)
    first = jnp.where(core == 0, keep, back)
    second = jnp.where(core == 0, back, keep)
    return jnp.stack([first, second, short_rows[0], short_rows[1]])


def clip_pieces(blocks, depth):
    return [
        lax.dynamic_index_in_dim(blocks, depth ^ step, 0, keepdims=False) for step in range(N_MP)
    ]


def to_clips(blocks, depth):
    pieces = clip_pieces(blocks, depth)
    return pieces[:1] + [mp_swap(pieces[step], step) for step in range(1, N_MP)]


def from_clips(rows):
    block = rows.shape[0] // N_MP
    parts = []
    for step in range(N_MP):
        piece = rows[step * block : (step + 1) * block]
        parts.append(piece if step == 0 else mp_swap(piece, step))
    return parts


def frames_of(parts, core, depth):
    blocks = jnp.stack(parts)
    first, second, short_a, short_b = (
        lax.dynamic_index_in_dim(blocks, depth ^ i, 0, keepdims=False) for i in range(N_MP)
    )
    keep = jnp.where(core == 0, first, second)
    away = jnp.where(core == 0, second, first)
    back = core_swap(away)
    low = jnp.where(core == 0, keep, back)
    high = jnp.where(core == 0, back, keep)
    return jnp.concatenate([low, high], axis=0)[None], jnp.stack([short_a, short_b])


def flip(index, late):
    return index ^ ((4 if late else 2) if index % 2 == 0 else (2 if late else 4))


def block_table(mine, size):
    if size != 8:
        return jnp.zeros((1,), jnp.int32)
    early = jnp.where(mine % 2 == 0, 2, 4)
    late = 6 - early
    relative = [0, early, late, 6, 1, 1 ^ late, 1 ^ early, 7]
    return jnp.stack([mine ^ r for r in relative]).astype(jnp.int32)


def early(i):
    return flip(i, False)


def late(i):
    return flip(i, True)


def across(i):
    return i ^ 6


def tie(*values):
    return lax.optimization_barrier(values)


def swap_plane(plane):
    return plane + [core_swap(piece) for piece in plane]


def to_slab(parts):
    return jnp.concatenate(parts, axis=1)


def mp_gather(shard):
    return [shard] + [mp_swap(shard, step) for step in range(1, N_MP)]


def half_sums(keep, back):
    half = keep.shape[0] // 2
    add = lambda at: (keep[at].astype(F32) + back[at].astype(F32)).astype(BF16)
    return add(slice(0, half)), add(slice(half, None))


def mp_away(parts):
    return [mp_swap(parts[step].astype(BF16), step) for step in range(1, N_MP)]


def mp_total(own, backs):
    for back in backs:
        own = own + back.astype(F32)
    return own


def blocks_of(pieces):
    step = pieces[0].shape[0]
    return [(p, k * step) for p in pieces for k in range(p.shape[0] // step)]


def block_rows(pieces):
    return WIDTH // len(blocks_of(pieces))


class Weights:
    def __init__(self, pieces, table, held, sems, lo, tile):
        self.held, self.tile = held, tile
        cols, parts = held.shape[2], sems.shape[0]
        self.span, self.copies = cols // parts, []
        for t in range(parts):
            row = []
            for k, (piece, first) in enumerate(blocks_of(pieces)):
                copy = pltpu.make_async_copy(
                    piece.at[pl.ds(first, held.shape[1]), pl.ds(lo + t * self.span, self.span)],
                    held.at[table[k], :, pl.ds(t * self.span, self.span)],
                    sems.at[t, k],
                )
                copy.start()
                row.append(copy)
            self.copies.append(row)
        self.waited = 0

    def get(self, t):
        at = t * self.tile
        while self.waited * self.span < at + self.tile:
            for copy in self.copies[self.waited]:
                copy.wait()
            self.waited += 1
        count, rows, _ = self.held.shape
        return self.held[:, :, at : at + self.tile].reshape(count * rows, self.tile)


def weight_scratch(pieces, cols, parts=1):
    return [
        pltpu.VMEM((len(blocks_of(pieces)), block_rows(pieces), cols), BF16),
        pltpu.SemaphoreType.DMA((parts, len(blocks_of(pieces)))),
    ]


def grad_shapes(pieces, cols, extra=0):
    count, rows = len(blocks_of(pieces)), block_rows(pieces)
    if count == 1:
        return [jax.ShapeDtypeStruct((1, rows, cols), F32)]
    return [jax.ShapeDtypeStruct((count // 2, rows + extra, cols), BF16)] * 2


def turn_scratch(pieces, rows):
    return [pltpu.VMEM((len(blocks_of(pieces)), block_rows(pieces), rows), BF16)] * 2


def turn(value, table, plain, turned):
    plain[...] = value.T.reshape(plain.shape)
    for r in range(plain.shape[0]):
        turned[r] = plain[table[r]]


def stage_scratch(pieces, cols):
    return [
        pltpu.VMEM((g.shape[0], block_rows(pieces), cols), g.dtype)
        for g in grad_shapes(pieces, cols)
    ]


def store_grad(turned, right, stages, at, writes=None, outs=None):
    count, rows, _ = turned.shape
    grad = dot(turned[...].reshape(count * rows, -1), right, NN)
    half, cols = count // len(stages), right.shape[1]
    for r in range(count):
        stage = stages[r // half]
        part = grad[r * rows : (r + 1) * rows].astype(stage.dtype)
        stage[r % half, :rows, at : at + cols] = part
    if writes is not None:
        for stage, out in zip(stages, outs):
            writes.start(
                stage.at[:, :, pl.ds(at, cols)],
                out.at[:, pl.ds(0, rows), pl.ds(at, cols)],
            )


class Writes:
    def __init__(self, sems):
        self.sems, self.copies = sems, []

    def start(self, source, target):
        copy = pltpu.make_async_copy(source, target, self.sems.at[len(self.copies)])
        copy.start()
        self.copies.append(copy)

    def finish(self):
        for copy in self.copies:
            copy.wait()


class Reads:
    def __init__(self, sources, targets, sems):
        self.targets, self.copies = targets, []
        for i, (source, target) in enumerate(zip(sources, targets)):
            copy = pltpu.make_async_copy(source, target, sems.at[i])
            copy.start()
            self.copies.append(copy)

    def get(self, i):
        self.copies[i].wait()
        return self.targets[i]


def read_scratch(arrays):
    return [pltpu.VMEM(a.shape, a.dtype) for a in arrays] + [
        pltpu.SemaphoreType.DMA((len(arrays),))
    ]


def cost(micros):
    return pl.CostEstimate(
        flops=int(micros * 1.1e9 * CS), bytes_accessed=int(micros * 1e5 * CS), transcendentals=0
    )


def call(body, name, micros, outs, arrays, table, pieces, scratch, far=0):
    vmem = pl.BlockSpec(memory_space=pltpu.VMEM)
    away = pl.BlockSpec(memory_space=pl.ANY)
    return pl.pallas_call(
        body,
        out_shape=tuple(outs),
        in_specs=[pl.BlockSpec(memory_space=pltpu.SMEM)]
        + [vmem] * len(arrays)
        + [away] * len(pieces),
        out_specs=(vmem,) * (len(outs) - far) + (away,) * far,
        scratch_shapes=scratch,
        compiler_params=pltpu.CompilerParams(vmem_limit_bytes=60 << 20),
        cost_estimate=cost(micros),
        name=name,
    )(table, *arrays, *pieces)


def like(shape, kind):
    return jax.ShapeDtypeStruct(shape, kind)


def attend_kernel(q_ref, k_ref, v_ref, kp_ref, vp_ref, bias_ref, o_ref, lse_ref):
    rows = q_ref.shape[0]
    keys = jnp.concatenate([k_ref[...], kp_ref[...]], axis=0)
    values = jnp.concatenate([v_ref[...], vp_ref[...]], axis=0)
    bias = bias_ref[...]
    tile = min(rows, Q_TILE)
    low = lax.broadcasted_iota(jnp.int32, (tile, LANES), 1) < HEAD
    for start in range(0, rows, tile):
        q = q_ref[start : start + tile, :]
        outs, logs = [], []
        for half in range(2):
            here = low if half == 0 else ~low
            q_here = jnp.where(here, q, jnp.zeros_like(q))
            scores = dot(q_here, keys, NT) + bias
            top = jnp.max(scores, axis=-1, keepdims=True)
            raised = jnp.exp(scores - top)
            total = jnp.sum(raised, axis=-1, keepdims=True)
            mixed = dot(raised.astype(BF16), values, NN)
            outs.append(mixed / total)
            logs.append(top + jnp.log(total))
        o_ref[start : start + tile, :] = jnp.where(low, outs[0], outs[1]).astype(BF16)
        lse_ref[start : start + tile, :] = jnp.where(low, logs[0], logs[1])


def attend(qkv, kv_other, bias):
    rows, width = qkv.shape[0], qkv.shape[1] // 3
    pairs = width // LANES
    spec = lambda base: pl.BlockSpec((rows, LANES), lambda p: (0, base + p))
    return pl.pallas_call(
        attend_kernel,
        out_shape=(
            jax.ShapeDtypeStruct((rows, width), BF16),
            jax.ShapeDtypeStruct((rows, width), F32),
        ),
        grid=(pairs,),
        in_specs=[
            spec(0),
            spec(pairs),
            spec(2 * pairs),
            spec(0),
            spec(pairs),
            pl.BlockSpec((1, 2 * rows), lambda p: (0, 0)),
        ],
        out_specs=(spec(0), spec(0)),
        compiler_params=pltpu.CompilerParams(vmem_limit_bytes=56 << 20),
        cost_estimate=cost(15),
        name="attend",
    )(qkv, qkv, qkv, kv_other, kv_other, bias)


def attend_back_kernel(
    q_ref, k_ref, v_ref, kp_ref, vp_ref, bias_ref, o_ref, lse_ref, do_ref,
    dq_ref, own_ref, other_ref,
):
    rows = q_ref.shape[0]
    keys = jnp.concatenate([k_ref[...], kp_ref[...]], axis=0)
    values = jnp.concatenate([v_ref[...], vp_ref[...]], axis=0)
    bias = bias_ref[...]
    tile = min(rows, Q_TILE)
    low = lax.broadcasted_iota(jnp.int32, (tile, LANES), 1) < HEAD
    dk = jnp.zeros((LANES, 2 * rows), F32)
    dv = jnp.zeros((LANES, 2 * rows), F32)
    for start in range(0, rows, tile):
        at = slice(start, start + tile)
        q, do = q_ref[at, :], do_ref[at, :]
        product = o_ref[at, :].astype(F32) * do.astype(F32)
        lse = lse_ref[at, :]
        outs = []
        for half in range(2):
            here = low if half == 0 else ~low
            q_here = jnp.where(here, q, jnp.zeros_like(q))
            do_here = jnp.where(here, do, jnp.zeros_like(do))
            inner = jnp.sum(jnp.where(here, product, 0.0), axis=-1, keepdims=True)
            log = lse[:, half * HEAD : half * HEAD + 1]
            soft = jnp.exp(dot(q_here, keys, NT) + bias - log)
            grad = (soft * (dot(do_here, values, NT) - inner)).astype(BF16)
            outs.append(dot(grad, keys, NN))
            dk = dk + dot(q_here, grad, TN)
            dv = dv + dot(do_here, soft.astype(BF16), TN)
        dq_ref[at, :] = (jnp.where(low, outs[0], outs[1]) * SCALE).astype(BF16)
    for i, value in enumerate((dk.T, dv.T)):
        at = slice(i * LANES, (i + 1) * LANES)
        own_ref[:, at] = value[:rows]
        other_ref[:, at] = value[rows:].astype(BF16)


def attend_back(qkv, kv_other, bias, out, lse, grad_out, first, count):
    rows, width = out.shape
    pairs = width // LANES
    spec = lambda base: pl.BlockSpec((rows, LANES), lambda p: (0, base + first + p))
    result = lambda cols: pl.BlockSpec((rows, cols), lambda p: (0, p))
    return pl.pallas_call(
        attend_back_kernel,
        out_shape=(
            jax.ShapeDtypeStruct((rows, count * LANES), BF16),
            jax.ShapeDtypeStruct((rows, 2 * count * LANES), F32),
            jax.ShapeDtypeStruct((rows, 2 * count * LANES), BF16),
        ),
        grid=(count,),
        in_specs=[
            spec(0),
            spec(pairs),
            spec(2 * pairs),
            spec(0),
            spec(pairs),
            pl.BlockSpec((1, 2 * rows), lambda p: (0, 0)),
            spec(0),
            spec(0),
            spec(0),
        ],
        out_specs=(result(LANES), result(2 * LANES), result(2 * LANES)),
        compiler_params=pltpu.CompilerParams(vmem_limit_bytes=56 << 20),
        cost_estimate=cost(3 * count),
        name="attend_back",
    )(qkv, qkv, qkv, kv_other, kv_other, bias, out, lse, grad_out)


def gelu_parts(v):
    cdf = 0.5 * (1.0 + lax.erf(v * (2.0 ** -0.5)))
    pdf = jnp.exp(-0.5 * v * v) * 0.3989422804014327
    return v * cdf, cdf + v * pdf


def norm(values):
    center = values - jnp.mean(values, axis=-1, keepdims=True)
    inv_dev = lax.rsqrt(jnp.mean(center * center, axis=-1, keepdims=True) + EPS)
    return center * inv_dev, inv_dev


def norm_back(scaled, normed, inv_dev):
    return inv_dev * (
        scaled
        - jnp.mean(scaled, axis=-1, keepdims=True)
        - normed * jnp.mean(scaled * normed, axis=-1, keepdims=True)
    )


def total(value):
    return jnp.sum(value, axis=0, keepdims=True)


def join(parts, starts, size, micros):
    rows, cols = parts[0].shape[0], len(starts) * len(parts) * size

    def body(*refs):
        parts, out = refs[:-1], refs[-1]
        at = 0
        for start in starts:
            for part in parts:
                out[:, at : at + size] = part[:, start : start + size]
                at += size

    vmem = pl.BlockSpec(memory_space=pltpu.VMEM)
    return pl.pallas_call(
        body,
        out_shape=like((rows, cols), parts[0].dtype),
        in_specs=[vmem] * len(parts),
        out_specs=vmem,
        cost_estimate=cost(micros),
        name="join",
    )(*parts)


def project(x_parts, head_row, table, pieces):
    block, width = x_parts[0].shape
    rows = block * len(x_parts)
    n = len(pieces)

    def body(table, *refs):
        part_refs, bias_ref, refs = refs[:N_MP], refs[N_MP], refs[N_MP + 1 :]
        pieces, (x_ref, qkv_ref, kv_ref, held, sems) = refs[:n], refs[n:]
        weights = Weights(pieces, table, held, sems, 0, width)
        for i, part in enumerate(part_refs):
            x_ref[i * block : (i + 1) * block, :] = part[...]
        x = x_ref[...]
        for i in range(3):
            value = dot(x, weights.get(i), NN) + bias_ref[:, i * width : (i + 1) * width]
            value = value.astype(BF16)
            if i == 0:
                value = (value.astype(F32) * SCALE).astype(BF16)
            else:
                kv_ref[:, (i - 1) * width : i * width] = value
            qkv_ref[:, i * width : (i + 1) * width] = value

    return call(
        body,
        "project",
        7,
        [
            like((rows, width), BF16),
            like((rows, 3 * width), BF16),
            like((rows, 2 * width), BF16),
        ],
        list(x_parts) + [head_row],
        table,
        pieces,
        weight_scratch(pieces, 3 * width, 3),
    )


def feed(x, mixed, cot_parts, smalls, small_row, table, out_pieces, feed_pieces):
    rows, width = x.shape
    hidden = feed_pieces[0].shape[1] // 2
    count = 6
    tile = hidden // count
    spans = [slice(t * tile, (t + 1) * tile) for t in range(count)]
    cols = hidden + width
    n_out, n_up, n = len(out_pieces), len(feed_pieces), len(smalls)
    down_grads = grad_shapes(feed_pieces, hidden)
    mid_grads = grad_shapes(feed_pieces, cols, SHARED)
    g = len(mid_grads)

    def body(table, x_ref, mixed_ref, *refs):
        cot_far, small_far, refs = refs[:N_MP], refs[N_MP : N_MP + n], refs[N_MP + n :]
        out_p, up_p = refs[:n_out], refs[n_out : n_out + n_up]
        refs = refs[n_out + n_up :]
        shared_ref, result_out, da_out, do_out = refs[:4]
        down_outs, mid_outs, refs = refs[4 : 4 + g], refs[4 + g : 4 + 2 * g], refs[4 + 2 * g :]
        w_out, sems_out, w_up, sems_up, w_down, sems_down = refs[:6]
        plain, turned, plain_h, turned_h = refs[6:10]
        small_ref, cot_ref, read_sems = refs[10:13]
        n1_ref, dz_ref, h_ref, act_ref, slope_ref, result_ref, low_ref, do_ref = refs[13:21]
        down_stages, mid_stages = refs[21 : 21 + g], refs[21 + g : 21 + 2 * g]
        shared_low, sems = refs[21 + 2 * g :]
        out_w = Weights(out_p, table, w_out, sems_out, 3 * width, width)
        smalls = [small.at[pl.ds(small_row, SMALL)] for small in small_far]
        reads = Reads(smalls, [small_ref.at[i] for i in range(n)], read_sems)
        up_w = Weights(up_p, table, w_up, sems_up, 0, tile)
        down_w = Weights(up_p, table, w_down, sems_down, hidden, tile)
        block = rows // N_MP
        cots = Reads(
            cot_far,
            [cot_ref.at[pl.ds(i * block, block)] for i in range(N_MP)],
            read_sems.at[pl.ds(n, N_MP)],
        )
        writes = Writes(sems)

        attention = dot(mixed_ref[...], out_w.get(0), NT)
        for i in range(n):
            reads.get(i)
        small = jnp.sum(small_ref[...].astype(F32), axis=0)
        row_vals = sum(small[:, i * width : (i + 1) * width] for i in range(2 * N_MP))
        row = lambda i: row_vals[i : i + 1, :]
        up_b = small[6:7, :hidden]
        n1, r1 = norm(x_ref[...].astype(F32) + attention + row(0))
        n1_ref[...] = n1
        h_ref[...] = (n1 * row(1) + row(2)).astype(BF16)
        feed = jnp.zeros((rows, width), F32)
        u = dot(h_ref[...], up_w.get(0), NN)
        for t, at in enumerate(spans):
            down = down_w.get(t)
            later = dot(h_ref[...], up_w.get(t + 1), NN) if t + 1 < count else None
            act, slope = gelu_parts(u + up_b[:, at])
            act_ref[:, at] = act.astype(BF16)
            slope_ref[:, at] = slope.astype(BF16)
            feed = feed + dot(act_ref[:, at], down, NT)
            u = later
        h = n1_ref[...] * row(1) + row(2)
        n2, r2 = norm(h + feed + row(3))
        result_ref[...] = (n2 * row(4) + row(5)).astype(BF16)
        writes.start(result_ref, result_out)
        for i in range(N_MP):
            cots.get(i)
        gy = cot_ref[...].astype(F32)
        dz = norm_back(gy * row(4), n2, r2)
        dz_ref[...] = dz
        low_ref[...] = dz.astype(BF16)
        sums = [total(dz), total(gy * n2), total(gy)]

        turn(low_ref[...], table, plain, turned)
        turn(h_ref[...], table, plain_h, turned_h)
        shared_ref[...] = jnp.zeros_like(shared_ref)
        dh = dz_ref[...]
        for t, at in enumerate(spans):
            dact = dot(low_ref[...], down_w.get(t), NN)
            store_grad(turned, act_ref[:, at], down_stages, at.start, writes, down_outs)
            du = (dact * slope_ref[:, at].astype(F32)).astype(BF16)
            shared_ref[0:1, at] = total(du.astype(F32))
            dh = dh + dot(du, up_w.get(t), NT)
            store_grad(turned_h, du, mid_stages, at.start, writes, mid_outs)
        n1 = n1_ref[...]
        da = norm_back(dh * row(1), n1, r1)
        dz_ref[...] = da
        writes.start(dz_ref, da_out)
        low_ref[...] = da.astype(BF16)
        do_ref[...] = dot(low_ref[...], out_w.get(0), NN).astype(BF16)
        writes.start(do_ref, do_out)
        sums = [total(da), total(dh * n1), total(dh)] + sums
        for j in range(hidden // width):
            for i, value in enumerate(sums):
                shared_ref[1 + i : 2 + i, j * width : (j + 1) * width] = value
        if g > 1:
            shared_low[...] = shared_ref[...].astype(BF16)
            for out in mid_outs:
                for r in range(out.shape[0]):
                    writes.start(shared_low, out.at[r, pl.ds(block_rows(feed_pieces), SHARED)])
        turn(low_ref[...], table, plain, turned)
        store_grad(turned, mixed_ref[...], mid_stages, hidden, writes, mid_outs)
        writes.finish()

    near = [((rows, width), F32)] * 2 + [((rows, width), BF16)]
    near += [((rows, hidden), BF16)] * 2 + [((rows, width), BF16)] * 3
    return call(
        body,
        "feed",
        33,
        [
            like((SHARED, cols), F32),
            like((rows, width), BF16),
            like((rows, width), F32),
            like((rows, width), BF16),
        ]
        + down_grads
        + mid_grads,
        [x, mixed],
        table,
        list(cot_parts) + list(smalls) + list(out_pieces) + list(feed_pieces),
        weight_scratch(out_pieces, width)
        + weight_scratch(feed_pieces, hidden) * 2
        + turn_scratch(feed_pieces, rows) * 2
        + [
            pltpu.VMEM((n, SMALL, 2 * hidden), BF16),
            pltpu.VMEM((rows, width), BF16),
            pltpu.SemaphoreType.DMA((n + N_MP,)),
        ]
        + [pltpu.VMEM(*spec) for spec in near]
        + stage_scratch(feed_pieces, hidden)
        + stage_scratch(feed_pieces, cols)
        + [
            pltpu.VMEM((SHARED, cols), BF16),
            pltpu.SemaphoreType.DMA((3 + g * (2 * count + 1) + n_up,)),
        ],
        far=3 + 2 * g,
    )


def project_back(da, parts, table, pieces):
    rows, width = da.shape
    n = len(pieces)
    flat = [value for part in parts for value in part]

    def body(table, da_ref, *refs):
        part_refs, refs = refs[: len(flat)], refs[len(flat) :]
        pieces, (out_ref, dqkv_ref, held, sems) = refs[:n], refs[n:]
        weights = Weights(pieces, table, held, sems, 0, width)
        pair = 0
        for i in range(0, len(flat), 3):
            q_ref, own_ref, back_ref = part_refs[i : i + 3]
            cols = q_ref.shape[1]
            dqkv_ref[:, pair * LANES : pair * LANES + cols] = q_ref[...]
            for p in range(cols // LANES):
                for which in range(2):
                    at = slice((2 * p + which) * LANES, (2 * p + which + 1) * LANES)
                    to = (which + 1) * width + (pair + p) * LANES
                    value = own_ref[:, at] + back_ref[:, at].astype(F32)
                    dqkv_ref[:, to : to + LANES] = value.astype(BF16)
            pair += cols // LANES
        value = da_ref[...]
        for i in range(3):
            value = value + dot(dqkv_ref[:, i * width : (i + 1) * width], weights.get(i), NT)
        out_ref[...] = value.astype(BF16)

    return call(
        body,
        "project_back",
        9,
        [like((rows, width), BF16), like((rows, 3 * width), BF16)],
        [da] + flat,
        table,
        pieces,
        weight_scratch(pieces, 3 * width, 3),
    )


def project_grads(x, dqkv, table, pieces):
    rows, width = x.shape
    grads = grad_shapes(pieces, 3 * width, SHARED)
    g = len(grads)

    def body(table, x_ref, dqkv_ref, *refs):
        shared_ref, grad_outs, refs = refs[0], refs[1 : 1 + g], refs[1 + g :]
        plain, turned = refs[:2]
        stages, shared_low, sems = refs[2 : 2 + g], refs[2 + g], refs[3 + g]
        writes = Writes(sems)
        turn(x_ref[...], table, plain, turned)
        for i in range(3):
            at = i * width
            store_grad(turned, dqkv_ref[:, at : at + width], stages, at, writes, grad_outs)
        shared_ref[...] = jnp.zeros_like(shared_ref)
        shared_ref[0:1, :] = total(dqkv_ref[...].astype(F32))
        if g > 1:
            shared_low[...] = shared_ref[...].astype(BF16)
            for out in grad_outs:
                for r in range(out.shape[0]):
                    writes.start(shared_low, out.at[r, pl.ds(block_rows(pieces), SHARED)])
        writes.finish()

    return call(
        body,
        "project_grads",
        7,
        [like((SHARED, 3 * width), F32)] + grads,
        [x, dqkv],
        table,
        [],
        turn_scratch(pieces, rows)
        + stage_scratch(pieces, 3 * width)
        + [
            pltpu.VMEM((SHARED, 3 * width), BF16),
            pltpu.SemaphoreType.DMA((3 * g + len(blocks_of(pieces)),)),
        ],
        far=g,
    )


def at_column(values, rows, width, column):
    return lax.dynamic_update_slice(jnp.zeros((rows, width), values.dtype), values, (0, column))


def small_block(row_params, expand_bias, mine, depth):
    high = lax.reduce_precision(row_params, 8, 7)
    column = (mine * N_MP + depth) * row_params.shape[1]
    high_low = [
        at_column(part.astype(BF16), 6, WIDTH, column) for part in (high, row_params - high)
    ]
    bias = at_column(expand_bias, 2, 2 * WIDTH, mine * expand_bias.shape[1])
    return jnp.concatenate([jnp.concatenate(high_low, axis=1), bias])


def key_bias(length_long, length_short, block, core, depth):
    lengths = jnp.concatenate([length_long, length_short])
    other = core_swap(lengths)
    longs = jnp.where(core == 0, jnp.stack([lengths[0], other[0]]), jnp.stack([other[0], lengths[0]]))
    length = jnp.concatenate([longs, lengths[1:]])[depth]
    is_long = depth < 2
    place = lax.broadcasted_iota(jnp.int32, (1, 2 * N_MP * block), 1)
    row = place % (N_MP * block)
    is_own = place < N_MP * block
    source = (row // block) ^ depth
    whose = jnp.where(is_own, core, 1 - core)
    frame = row % block + jnp.where(is_long, (2 * source + whose) * block, source * block)
    counted = (frame < length) & (is_own | is_long)
    return jnp.where(counted, 0.0, NEG_FILL).astype(F32)


def on_device(
    frames_long,
    frames_short,
    length_long,
    length_short,
    input_proj,
    output_proj,
    expand_weight,
    shrink_weight,
    head_bias,
    expand_bias,
    row_params,
    cotangent_long,
    cotangent_short,
):
    mine = lax.axis_index("dp")
    depth = lax.axis_index("mp")
    n_dp = lax.axis_size("dp")
    fast = n_dp == 8
    core = mine % 2
    block = frames_short.shape[1]
    shard, group = input_proj.shape[1:]
    units = expand_weight.shape[1]
    width = group * N_MP
    hidden = units * N_MP
    table = block_table(mine, n_dp)

    joined = jnp.concatenate(
        [input_proj[0], input_proj[1], input_proj[2], output_proj.T], axis=1
    )
    none = jnp.zeros((SMALL, group), BF16)
    heads = [at_column(head_bias[i], SMALL, group, mine * head_bias.shape[2]) for i in range(2)]
    heads = jnp.concatenate([heads[0], none, heads[1], none], axis=1)
    attn_parts = mp_gather(jnp.concatenate([joined, heads]))
    x_blocks = clip_blocks(frames_long[0], frames_short, core)
    cot_blocks = clip_blocks(cotangent_long[0], cotangent_short, core)
    bias = key_bias(length_long, length_short, block, core, depth)
    feed_shard = jnp.concatenate(
        [
            jnp.concatenate([expand_weight, shrink_weight.T], axis=1),
            small_block(row_params, expand_bias, mine, depth),
        ]
    )
    *attn_parts, feed_shard, bias, x_blocks, cot_blocks = tie(
        *attn_parts, feed_shard, bias, x_blocks, cot_blocks
    )
    attn_slab = join(attn_parts, [i * group for i in range(4)], group, 10)
    feed_parts = mp_gather(feed_shard)
    if fast:
        attn_p = [attn_slab, dp_swap(attn_slab, early), dp_swap(attn_slab, late)]
        x_pieces = clip_pieces(x_blocks, depth)
        both = tie(*attn_p, *x_pieces, *feed_parts)
        attn_p, x_pieces, feed_parts = list(both[:3]), both[3:7], both[7:]
        x_parts = [x_pieces[0]] + [mp_swap(x_pieces[i], i) for i in range(1, N_MP)]
        three = dp_swap(attn_p[1], late)
        feed_slab, three, x_parts[1], x_parts[3] = tie(
            join(feed_parts, (0, units), units, 10), three, x_parts[1], x_parts[3]
        )
        attn_p.append(three)
        attn_p.append(core_swap(jnp.concatenate(attn_p)))
        feed_one = dp_swap(feed_slab, early)
        *x_parts, cot_blocks, own_slab, feed_one = tie(
            *x_parts, cot_blocks, feed_slab, feed_one
        )
        feed_two = dp_swap(own_slab, late)
        heads = sum(
            p[first + shard : first + shard + SMALL].astype(F32) for p, first in blocks_of(attn_p)
        )
    else:
        x_parts = to_clips(x_blocks, depth)
        gather = lambda slab: lax.all_gather(slab, "dp", axis=0)
        whole = gather(attn_slab)
        heads = jnp.sum(whole[:, shard:].astype(F32), axis=0)
        attn_p = [whole[:, :shard].reshape(width, 4 * width)]
        whole = gather(join(feed_parts, (0, units), units, 10))
        small = jnp.sum(whole[:, shard:].astype(F32), axis=0)
        feed_p = [whole[:, :shard].reshape(width, 2 * hidden)]
    cot_parts = to_clips(cot_blocks, depth)
    head_row = heads[:1, : 3 * width]

    x, qkv, kv = project(x_parts, head_row, table, attn_p)
    if fast:
        kv, feed_two, cot_parts[3], own_slab = tie(
            kv, feed_two, cot_parts[3], core_swap(own_slab)
        )
    kv_other = core_swap(kv)
    if fast:
        feed_three = dp_swap(feed_one, late)
        feed_p = [feed_slab, feed_one, feed_two]
        backs = [own_slab] + [core_swap(piece) for piece in feed_p[1:]]
    mixed, lse = attend(qkv, kv_other, bias)
    if fast:
        mixed, feed_three, *both = tie(mixed, feed_three, *backs, *cot_parts)
        backs, cot_parts = both[:3], both[3:]
        feed_p = feed_p + [feed_three] + backs + [core_swap(feed_three)]
        smalls, small_row = feed_p, shard
    else:
        smalls, small_row = [small.astype(BF16)], 0
    outs = feed(x, mixed, cot_parts, smalls, small_row, table, attn_p, feed_p)
    mid_shared, result, da, do, *grads = outs
    g_down, g_mid = grads[: len(grads) // 2], grads[len(grads) // 2 :]

    def by_group_of(value, sizes):
        starts = [N_MP * sum(sizes[:i]) for i in range(len(sizes))]
        return [
            jnp.concatenate(
                [value[:, a + j * n : a + (j + 1) * n] for a, n in zip(starts, sizes)], axis=1
            )
            for j in range(N_MP)
        ]

    def last_sum(keep, back):
        return keep[0].astype(F32) + back[0].astype(F32)

    result_parts = from_clips(result)
    if fast:
        b_down, b_mid = core_swap(g_down[1]), core_swap(g_mid[1])
    pairs = width // LANES
    first = pairs // 2
    dq_a, own_a, other_a = attend_back(qkv, kv_other, bias, mixed, lse, do, 0, first)
    if fast:
        other_a, b_down, b_mid, result_parts[3] = tie(other_a, b_down, b_mid, result_parts[3])
        k_down, a_down = half_sums(g_down[0], b_down)
        do, a_down = tie(do, a_down)
        b_down = dp_swap(a_down, late)
        k_mid, a_mid = half_sums(g_mid[0], b_mid)
        do, a_mid = tie(do, a_mid)
        b_mid = dp_swap(a_mid, late)
    back_a = core_swap(other_a)
    dq_b, own_b, other_b = attend_back(
        qkv, kv_other, bias, mixed, lse, do, first, pairs - first
    )
    if fast:
        other_b, back_a, *result_parts = tie(other_b, back_a, *result_parts)
    back_b = core_swap(other_b)
    parts = [(dq_a, own_a, back_a), (dq_b, own_b, back_b)]
    frames_grad, dqkv = project_back(da, parts, table, attn_p)
    grad_parts = from_clips(frames_grad)
    if fast:
        dqkv, b_down, b_mid = tie(dqkv, b_down, b_mid)
        k_down, a_down = half_sums(k_down, b_down)
        k_mid, a_mid = half_sums(k_mid, b_mid)
        dqkv, a_down, a_mid = tie(dqkv, a_down, a_mid)
        b_down = dp_swap(a_down, early)
        b_mid = dp_swap(a_mid, early)
    attn_shared, *g_attn = project_grads(x, dqkv, table, attn_p)
    if fast:
        both = tie(*g_attn, b_down, b_mid, *grad_parts)
        g_attn, b_down, b_mid, grad_parts = both[:2], both[2], both[3], both[4:]
        b_attn = core_swap(g_attn[1])
        s_down = by_group_of(last_sum(k_down, b_down), [units])
        k_attn, a_attn = half_sums(g_attn[0], b_attn)
        a_attn, *s_down = tie(a_attn, *s_down)
        b_attn = dp_swap(a_attn, late)
        z_down = mp_away(s_down)
        s_mid = by_group_of(last_sum(k_mid, b_mid), [units, group])
        b_attn, *z_down = tie(b_attn, *z_down)
        k_attn, a_attn = half_sums(k_attn, b_attn)
        z_mid = mp_away(s_mid)
        b_attn, *z_mid = tie(dp_swap(a_attn, early), *z_mid)
        s_attn = last_sum(k_attn, b_attn)
    else:
        scatter = lambda g: lax.psum_scatter(g[0][0], "dp", scatter_dimension=0, tiled=True)
        s_down = by_group_of(scatter(g_down), [units])
        z_down = mp_away(s_down)
        s_mid = jnp.concatenate([scatter(g_mid), lax.psum(mid_shared, "dp")])
        s_mid = by_group_of(s_mid, [units, group])
        z_mid = mp_away(s_mid)
        s_attn = jnp.concatenate([scatter(g_attn), lax.psum(attn_shared, "dp")])
    s_attn = by_group_of(s_attn, [group] * 3)
    grad_long, grad_short = frames_of(grad_parts, core, depth)
    result_long, result_short = frames_of(result_parts, core, depth)
    attn_share = mp_total(s_attn[0], mp_away(s_attn))
    down_share = mp_total(s_down[0], z_down).T
    mid_share = mp_total(s_mid[0], z_mid)
    up_share = mid_share[:shard, :units]
    output_share = mid_share[:shard, units:].T
    input_share = jnp.stack(
        [attn_share[:shard, i * group : (i + 1) * group] for i in range(3)]
    )
    up_cols, head_cols, row_cols = units // n_dp, group // n_dp, width // (n_dp * N_MP)
    rank = mine * N_MP + depth
    up_b_share = lax.dynamic_slice(mid_share, (shard, mine * up_cols), (1, up_cols))
    row_share = lax.dynamic_slice(mid_share, (shard + 1, rank * row_cols), (6, row_cols))
    head_share = jnp.stack(
        [
            lax.dynamic_slice(attn_share, (shard, at + mine * head_cols), (1, head_cols))
            for at in (0, 2 * group)
        ]
    )
    return (
        result_long,
        result_short,
        grad_long.astype(F32),
        grad_short.astype(F32),
        input_share,
        output_share,
        up_share,
        down_share,
        head_share,
        up_b_share,
        row_share,
    )


def solution(mesh):
    return jax.shard_map(
        on_device,
        mesh=mesh,
        in_specs=(
            P("dp", "mp", None),
            P("dp", "mp", None),
            P("dp"),
            P("dp"),
            P(None, "dp", "mp"),
            P("mp", "dp"),
            P("dp", "mp"),
            P("mp", "dp"),
            P(None, "mp", "dp"),
            P("mp", "dp"),
            P(None, ("dp", "mp")),
            P("dp", "mp", None),
            P("dp", "mp", None),
        ),
        out_specs=(
            P("dp", "mp", None),
            P("dp", "mp", None),
            P("dp", "mp", None),
            P("dp", "mp", None),
            P(None, "dp", "mp"),
            P("mp", "dp"),
            P("dp", "mp"),
            P("mp", "dp"),
            P(None, "mp", "dp"),
            P("mp", "dp"),
            P(None, ("dp", "mp")),
        ),
        check_vma=False,
    )
```

```python
import functools

import jax
import jax.numpy as jnp
from jax import lax
from jax.experimental import pallas as pl
from jax.experimental.pallas import tpu as pltpu
from jax.sharding import PartitionSpec as P

HEAD = 64
EPS = 1e-05
NEG_FILL = -1e30
SCALE = HEAD ** (-0.5)
N_MP = 4
PARTS = 1
CS = 0.3
WIDTH = 768
SMALL = 8
SHARED = 8
LANES = 128
Q_TILE = 256
F32 = jnp.float32
BF16 = jnp.bfloat16
NT = (((1,), (1,)), ((), ()))
NN = (((1,), (0,)), ((), ()))
TN = (((0,), (0,)), ((), ()))


def dot(left, right, dims):
    return lax.dot_general(left, right, dims, preferred_element_type=F32)


def mp_swap(value, step):
    return lax.ppermute(value, "mp", [(i, i ^ step) for i in range(N_MP)])


def dp_swap(value, target):
    size = lax.axis_size("dp")
    return lax.ppermute(value, "dp", [(i, target(i)) for i in range(size)])


def core_swap(value):
    return dp_swap(value, lambda i: i ^ 1)


def clip_blocks(long_rows, short_rows, core):
    block = short_rows.shape[1]
    keep = lax.dynamic_slice_in_dim(long_rows, core * block, block, 0)
    away = lax.dynamic_slice_in_dim(long_rows, (1 - core) * block, block, 0)
    back = core_swap(away)
    first = jnp.where(core == 0, keep, back)
    second = jnp.where(core == 0, back, keep)
    return jnp.stack([first, second, short_rows[0], short_rows[1]])


def clip_pieces(blocks, depth):
    return [
        lax.dynamic_index_in_dim(blocks, depth ^ step, 0, keepdims=False) for step in range(N_MP)
    ]


def to_clips(blocks, depth):
    pieces = clip_pieces(blocks, depth)
    return pieces[:1] + [mp_swap(pieces[step], step) for step in range(1, N_MP)]


def from_clips(rows):
    block = rows.shape[0] // N_MP
    parts = []
    for step in range(N_MP):
        piece = rows[step * block : (step + 1) * block]
        parts.append(piece if step == 0 else mp_swap(piece, step))
    return parts


def frames_of(parts, core, depth):
    blocks = jnp.stack(parts)
    first, second, short_a, short_b = (
        lax.dynamic_index_in_dim(blocks, depth ^ i, 0, keepdims=False) for i in range(N_MP)
    )
    keep = jnp.where(core == 0, first, second)
    away = jnp.where(core == 0, second, first)
    back = core_swap(away)
    low = jnp.where(core == 0, keep, back)
    high = jnp.where(core == 0, back, keep)
    return jnp.concatenate([low, high], axis=0)[None], jnp.stack([short_a, short_b])


def flip(index, late):
    return index ^ ((4 if late else 2) if index % 2 == 0 else (2 if late else 4))


def block_table(mine, size):
    if size != 8:
        return jnp.zeros((1,), jnp.int32)
    early = jnp.where(mine % 2 == 0, 2, 4)
    late = 6 - early
    relative = [0, early, late, 6, 1, 1 ^ late, 1 ^ early, 7]
    return jnp.stack([mine ^ r for r in relative]).astype(jnp.int32)


def early(i):
    return flip(i, False)


def late(i):
    return flip(i, True)


def across(i):
    return i ^ 6


def tie(*values):
    return lax.optimization_barrier(values)


def swap_plane(plane):
    return plane + [core_swap(piece) for piece in plane]


def to_slab(parts):
    return jnp.concatenate(parts, axis=1)


def mp_gather(shard):
    return [shard] + [mp_swap(shard, step) for step in range(1, N_MP)]


def goes_on(terms):
    half = terms[0].shape[0] // 2
    return sum(term[half:].astype(F32) for term in terms).astype(BF16)


def stays(terms, back):
    half = terms[0].shape[0] // 2
    return [term[:half] for term in terms] + [back]


def mp_away(parts):
    return [mp_swap(parts[step].astype(BF16), step) for step in range(1, N_MP)]


def mp_total(own, backs):
    for back in backs:
        own = own + back.astype(F32)
    return own


def blocks_of(pieces):
    step = pieces[0].shape[0]
    return [(p, k * step) for p in pieces for k in range(p.shape[0] // step)]


def block_rows(pieces):
    return WIDTH // len(blocks_of(pieces))


class Weights:
    def __init__(self, pieces, table, held, sems, lo, tile):
        self.held, self.tile = held, tile
        cols, parts = held.shape[2], sems.shape[0]
        self.span, self.copies = cols // parts, []
        for t in range(parts):
            row = []
            for k, (piece, first) in enumerate(blocks_of(pieces)):
                copy = pltpu.make_async_copy(
                    piece.at[pl.ds(first, held.shape[1]), pl.ds(lo + t * self.span, self.span)],
                    held.at[table[k], :, pl.ds(t * self.span, self.span)],
                    sems.at[t, k],
                )
                copy.start()
                row.append(copy)
            self.copies.append(row)
        self.waited = 0

    def get(self, t):
        at = t * self.tile
        while self.waited * self.span < at + self.tile:
            for copy in self.copies[self.waited]:
                copy.wait()
            self.waited += 1
        count, rows, _ = self.held.shape
        return self.held[:, :, at : at + self.tile].reshape(count * rows, self.tile)


def weight_scratch(pieces, cols, parts=1):
    return [
        pltpu.VMEM((len(blocks_of(pieces)), block_rows(pieces), cols), BF16),
        pltpu.SemaphoreType.DMA((parts, len(blocks_of(pieces)))),
    ]


def grad_shapes(pieces, cols, extra=0):
    count, rows = len(blocks_of(pieces)), block_rows(pieces)
    if count == 1:
        return [jax.ShapeDtypeStruct((1, rows, cols), F32)]
    return [jax.ShapeDtypeStruct((count // 2, rows + extra, cols), BF16)] * 2


def turn_scratch(pieces, rows):
    return [pltpu.VMEM((len(blocks_of(pieces)), block_rows(pieces), rows), BF16)] * 2


def turn(value, table, plain, turned):
    plain[...] = value.T.reshape(plain.shape)
    for r in range(plain.shape[0]):
        turned[r] = plain[table[r]]


def stage_scratch(pieces, cols):
    return [
        pltpu.VMEM((g.shape[0], block_rows(pieces), cols), g.dtype)
        for g in grad_shapes(pieces, cols)
    ]


def store_grad(turned, right, stages, at, writes=None, outs=None):
    count, rows, _ = turned.shape
    grad = dot(turned[...].reshape(count * rows, -1), right, NN)
    half, cols = count // len(stages), right.shape[1]
    for r in range(count):
        stage = stages[r // half]
        part = grad[r * rows : (r + 1) * rows].astype(stage.dtype)
        stage[r % half, :rows, at : at + cols] = part
    if writes is not None:
        for stage, out in zip(stages, outs):
            writes.start(
                stage.at[:, :, pl.ds(at, cols)],
                out.at[:, pl.ds(0, rows), pl.ds(at, cols)],
            )


class Writes:
    def __init__(self, sems):
        self.sems, self.copies = sems, []

    def start(self, source, target):
        copy = pltpu.make_async_copy(source, target, self.sems.at[len(self.copies)])
        copy.start()
        self.copies.append(copy)

    def finish(self):
        for copy in self.copies:
            copy.wait()


class Reads:
    def __init__(self, sources, targets, sems):
        self.targets, self.copies = targets, []
        for i, (source, target) in enumerate(zip(sources, targets)):
            copy = pltpu.make_async_copy(source, target, sems.at[i])
            copy.start()
            self.copies.append(copy)

    def get(self, i):
        self.copies[i].wait()
        return self.targets[i]


def read_scratch(arrays):
    return [pltpu.VMEM(a.shape, a.dtype) for a in arrays] + [
        pltpu.SemaphoreType.DMA((len(arrays),))
    ]


def cost(micros):
    return pl.CostEstimate(
        flops=int(micros * 1.1e9 * CS), bytes_accessed=int(micros * 1e5 * CS), transcendentals=0
    )


def call(body, name, micros, outs, arrays, table, pieces, scratch, far=0):
    vmem = pl.BlockSpec(memory_space=pltpu.VMEM)
    away = pl.BlockSpec(memory_space=pl.ANY)
    return pl.pallas_call(
        body,
        out_shape=tuple(outs),
        in_specs=[pl.BlockSpec(memory_space=pltpu.SMEM)]
        + [vmem] * len(arrays)
        + [away] * len(pieces),
        out_specs=(vmem,) * (len(outs) - far) + (away,) * far,
        scratch_shapes=scratch,
        compiler_params=pltpu.CompilerParams(vmem_limit_bytes=60 << 20),
        cost_estimate=cost(micros),
        name=name,
    )(table, *arrays, *pieces)


def like(shape, kind):
    return jax.ShapeDtypeStruct(shape, kind)


def attend_kernel(q_ref, k_ref, v_ref, kp_ref, vp_ref, bias_ref, o_ref, lse_ref):
    rows = q_ref.shape[0]
    keys = jnp.concatenate([k_ref[...], kp_ref[...]], axis=0)
    values = jnp.concatenate([v_ref[...], vp_ref[...]], axis=0)
    bias = bias_ref[...]
    tile = min(rows, Q_TILE)
    low = lax.broadcasted_iota(jnp.int32, (tile, LANES), 1) < HEAD
    for start in range(0, rows, tile):
        q = q_ref[start : start + tile, :]
        outs, logs = [], []
        for half in range(2):
            here = low if half == 0 else ~low
            q_here = jnp.where(here, q, jnp.zeros_like(q))
            scores = dot(q_here, keys, NT) + bias
            top = jnp.max(scores, axis=-1, keepdims=True)
            raised = jnp.exp(scores - top)
            total = jnp.sum(raised, axis=-1, keepdims=True)
            mixed = dot(raised.astype(BF16), values, NN)
            outs.append(mixed / total)
            logs.append(top + jnp.log(total))
        o_ref[start : start + tile, :] = jnp.where(low, outs[0], outs[1]).astype(BF16)
        lse_ref[start : start + tile, :] = jnp.where(low, logs[0], logs[1])


def attend(qkv, kv_other, bias):
    rows, width = qkv.shape[0], qkv.shape[1] // 3
    pairs = width // LANES
    spec = lambda base: pl.BlockSpec((rows, LANES), lambda p: (0, base + p))
    return pl.pallas_call(
        attend_kernel,
        out_shape=(
            jax.ShapeDtypeStruct((rows, width), BF16),
            jax.ShapeDtypeStruct((rows, width), F32),
        ),
        grid=(pairs,),
        in_specs=[
            spec(0),
            spec(pairs),
            spec(2 * pairs),
            spec(0),
            spec(pairs),
            pl.BlockSpec((1, 2 * rows), lambda p: (0, 0)),
        ],
        out_specs=(spec(0), spec(0)),
        compiler_params=pltpu.CompilerParams(vmem_limit_bytes=56 << 20),
        cost_estimate=cost(15),
        name="attend",
    )(qkv, qkv, qkv, kv_other, kv_other, bias)


def attend_back_kernel(
    q_ref, k_ref, v_ref, kp_ref, vp_ref, bias_ref, o_ref, lse_ref, do_ref,
    dq_ref, own_ref, other_ref,
):
    rows = q_ref.shape[0]
    keys = jnp.concatenate([k_ref[...], kp_ref[...]], axis=0)
    values = jnp.concatenate([v_ref[...], vp_ref[...]], axis=0)
    bias = bias_ref[...]
    tile = min(rows, Q_TILE)
    low = lax.broadcasted_iota(jnp.int32, (tile, LANES), 1) < HEAD
    dk = jnp.zeros((LANES, 2 * rows), F32)
    dv = jnp.zeros((LANES, 2 * rows), F32)
    for start in range(0, rows, tile):
        at = slice(start, start + tile)
        q, do = q_ref[at, :], do_ref[at, :]
        product = o_ref[at, :].astype(F32) * do.astype(F32)
        lse = lse_ref[at, :]
        outs = []
        for half in range(2):
            here = low if half == 0 else ~low
            q_here = jnp.where(here, q, jnp.zeros_like(q))
            do_here = jnp.where(here, do, jnp.zeros_like(do))
            inner = jnp.sum(jnp.where(here, product, 0.0), axis=-1, keepdims=True)
            log = lse[:, half * HEAD : half * HEAD + 1]
            soft = jnp.exp(dot(q_here, keys, NT) + bias - log)
            grad = (soft * (dot(do_here, values, NT) - inner)).astype(BF16)
            outs.append(dot(grad, keys, NN))
            dk = dk + dot(q_here, grad, TN)
            dv = dv + dot(do_here, soft.astype(BF16), TN)
        dq_ref[at, :] = (jnp.where(low, outs[0], outs[1]) * SCALE).astype(BF16)
    for i, value in enumerate((dk.T, dv.T)):
        at = slice(i * LANES, (i + 1) * LANES)
        own_ref[:, at] = value[:rows]
        other_ref[:, at] = value[rows:].astype(BF16)


def attend_back(qkv, kv_other, bias, out, lse, grad_out, first, count):
    rows, width = out.shape
    pairs = width // LANES
    spec = lambda base: pl.BlockSpec((rows, LANES), lambda p: (0, base + first + p))
    result = lambda cols: pl.BlockSpec((rows, cols), lambda p: (0, p))
    return pl.pallas_call(
        attend_back_kernel,
        out_shape=(
            jax.ShapeDtypeStruct((rows, count * LANES), BF16),
            jax.ShapeDtypeStruct((rows, 2 * count * LANES), F32),
            jax.ShapeDtypeStruct((rows, 2 * count * LANES), BF16),
        ),
        grid=(count,),
        in_specs=[
            spec(0),
            spec(pairs),
            spec(2 * pairs),
            spec(0),
            spec(pairs),
            pl.BlockSpec((1, 2 * rows), lambda p: (0, 0)),
            spec(0),
            spec(0),
            spec(0),
        ],
        out_specs=(result(LANES), result(2 * LANES), result(2 * LANES)),
        compiler_params=pltpu.CompilerParams(vmem_limit_bytes=56 << 20),
        cost_estimate=cost(3 * count),
        name="attend_back",
    )(qkv, qkv, qkv, kv_other, kv_other, bias, out, lse, grad_out)


def gelu_parts(v):
    cdf = 0.5 * (1.0 + lax.erf(v * (2.0 ** -0.5)))
    pdf = jnp.exp(-0.5 * v * v) * 0.3989422804014327
    return v * cdf, cdf + v * pdf


def norm(values):
    center = values - jnp.mean(values, axis=-1, keepdims=True)
    inv_dev = lax.rsqrt(jnp.mean(center * center, axis=-1, keepdims=True) + EPS)
    return center * inv_dev, inv_dev


def norm_back(scaled, normed, inv_dev):
    return inv_dev * (
        scaled
        - jnp.mean(scaled, axis=-1, keepdims=True)
        - normed * jnp.mean(scaled * normed, axis=-1, keepdims=True)
    )


def total(value):
    return jnp.sum(value, axis=0, keepdims=True)


def join(parts, starts, size, micros):
    rows, cols = parts[0].shape[0], len(starts) * len(parts) * size

    def body(*refs):
        parts, out = refs[:-1], refs[-1]
        at = 0
        for start in starts:
            for part in parts:
                out[:, at : at + size] = part[:, start : start + size]
                at += size

    vmem = pl.BlockSpec(memory_space=pltpu.VMEM)
    return pl.pallas_call(
        body,
        out_shape=like((rows, cols), parts[0].dtype),
        in_specs=[vmem] * len(parts),
        out_specs=vmem,
        cost_estimate=cost(micros),
        name="join",
    )(*parts)


def project(x_parts, head_row, table, pieces):
    block, width = x_parts[0].shape
    rows = block * len(x_parts)
    n = len(pieces)

    def body(table, *refs):
        part_refs, bias_ref, refs = refs[:N_MP], refs[N_MP], refs[N_MP + 1 :]
        pieces, (x_ref, qkv_ref, kv_ref, held, sems) = refs[:n], refs[n:]
        weights = Weights(pieces, table, held, sems, 0, width)
        for i, part in enumerate(part_refs):
            x_ref[i * block : (i + 1) * block, :] = part[...]
        x = x_ref[...]
        for i in range(3):
            value = dot(x, weights.get(i), NN) + bias_ref[:, i * width : (i + 1) * width]
            value = value.astype(BF16)
            if i == 0:
                value = (value.astype(F32) * SCALE).astype(BF16)
            else:
                kv_ref[:, (i - 1) * width : i * width] = value
            qkv_ref[:, i * width : (i + 1) * width] = value

    return call(
        body,
        "project",
        7,
        [
            like((rows, width), BF16),
            like((rows, 3 * width), BF16),
            like((rows, 2 * width), BF16),
        ],
        list(x_parts) + [head_row],
        table,
        pieces,
        weight_scratch(pieces, 3 * width, 3),
    )


def feed(x, mixed, cot_parts, smalls, small_row, table, out_pieces, feed_pieces):
    rows, width = x.shape
    hidden = feed_pieces[0].shape[1] // 2
    count = 6
    tile = hidden // count
    spans = [slice(t * tile, (t + 1) * tile) for t in range(count)]
    cols = hidden + width
    n_out, n_up, n = len(out_pieces), len(feed_pieces), len(smalls)
    down_grads = grad_shapes(feed_pieces, hidden)
    mid_grads = grad_shapes(feed_pieces, cols, SHARED)
    g = len(mid_grads)

    def body(table, x_ref, mixed_ref, *refs):
        cot_far, small_far, refs = refs[:N_MP], refs[N_MP : N_MP + n], refs[N_MP + n :]
        out_p, up_p = refs[:n_out], refs[n_out : n_out + n_up]
        refs = refs[n_out + n_up :]
        shared_ref, result_out, da_out, do_out = refs[:4]
        down_outs, mid_outs, refs = refs[4 : 4 + g], refs[4 + g : 4 + 2 * g], refs[4 + 2 * g :]
        w_out, sems_out, w_up, sems_up, w_down, sems_down = refs[:6]
        plain, turned, plain_h, turned_h = refs[6:10]
        small_ref, cot_ref, read_sems = refs[10:13]
        n1_ref, dz_ref, h_ref, act_ref, slope_ref, result_ref, low_ref, do_ref = refs[13:21]
        down_stages, mid_stages = refs[21 : 21 + g], refs[21 + g : 21 + 2 * g]
        shared_low, sems = refs[21 + 2 * g :]
        out_w = Weights(out_p, table, w_out, sems_out, 3 * width, width)
        smalls = [small.at[pl.ds(small_row, SMALL)] for small in small_far]
        reads = Reads(smalls, [small_ref.at[i] for i in range(n)], read_sems)
        up_w = Weights(up_p, table, w_up, sems_up, 0, tile)
        down_w = Weights(up_p, table, w_down, sems_down, hidden, tile)
        block = rows // N_MP
        cots = Reads(
            cot_far,
            [cot_ref.at[pl.ds(i * block, block)] for i in range(N_MP)],
            read_sems.at[pl.ds(n, N_MP)],
        )
        writes = Writes(sems)

        attention = dot(mixed_ref[...], out_w.get(0), NT)
        for i in range(n):
            reads.get(i)
        small = jnp.sum(small_ref[...].astype(F32), axis=0)
        row_vals = sum(small[:, i * width : (i + 1) * width] for i in range(2 * N_MP))
        row = lambda i: row_vals[i : i + 1, :]
        up_b = small[6:7, :hidden]
        n1, r1 = norm(x_ref[...].astype(F32) + attention + row(0))
        n1_ref[...] = n1
        h_ref[...] = (n1 * row(1) + row(2)).astype(BF16)
        feed = jnp.zeros((rows, width), F32)
        u = dot(h_ref[...], up_w.get(0), NN)
        for t, at in enumerate(spans):
            down = down_w.get(t)
            later = dot(h_ref[...], up_w.get(t + 1), NN) if t + 1 < count else None
            act, slope = gelu_parts(u + up_b[:, at])
            act_ref[:, at] = act.astype(BF16)
            slope_ref[:, at] = slope.astype(BF16)
            feed = feed + dot(act_ref[:, at], down, NT)
            u = later
        h = n1_ref[...] * row(1) + row(2)
        n2, r2 = norm(h + feed + row(3))
        result_ref[...] = (n2 * row(4) + row(5)).astype(BF16)
        writes.start(result_ref, result_out)
        for i in range(N_MP):
            cots.get(i)
        gy = cot_ref[...].astype(F32)
        dz = norm_back(gy * row(4), n2, r2)
        dz_ref[...] = dz
        low_ref[...] = dz.astype(BF16)
        sums = [total(dz), total(gy * n2), total(gy)]

        turn(low_ref[...], table, plain, turned)
        turn(h_ref[...], table, plain_h, turned_h)
        shared_ref[...] = jnp.zeros_like(shared_ref)
        dh = dz_ref[...]
        for t, at in enumerate(spans):
            dact = dot(low_ref[...], down_w.get(t), NN)
            store_grad(turned, act_ref[:, at], down_stages, at.start, writes, down_outs)
            du = (dact * slope_ref[:, at].astype(F32)).astype(BF16)
            shared_ref[0:1, at] = total(du.astype(F32))
            dh = dh + dot(du, up_w.get(t), NT)
            store_grad(turned_h, du, mid_stages, at.start, writes, mid_outs)
        n1 = n1_ref[...]
        da = norm_back(dh * row(1), n1, r1)
        dz_ref[...] = da
        writes.start(dz_ref, da_out)
        low_ref[...] = da.astype(BF16)
        do_ref[...] = dot(low_ref[...], out_w.get(0), NN).astype(BF16)
        writes.start(do_ref, do_out)
        sums = [total(da), total(dh * n1), total(dh)] + sums
        for j in range(hidden // width):
            for i, value in enumerate(sums):
                shared_ref[1 + i : 2 + i, j * width : (j + 1) * width] = value
        if g > 1:
            shared_low[...] = shared_ref[...].astype(BF16)
            for out in mid_outs:
                for r in range(out.shape[0]):
                    writes.start(shared_low, out.at[r, pl.ds(block_rows(feed_pieces), SHARED)])
        turn(low_ref[...], table, plain, turned)
        store_grad(turned, mixed_ref[...], mid_stages, hidden, writes, mid_outs)
        writes.finish()

    near = [((rows, width), F32)] * 2 + [((rows, width), BF16)]
    near += [((rows, hidden), BF16)] * 2 + [((rows, width), BF16)] * 3
    return call(
        body,
        "feed",
        33,
        [
            like((SHARED, cols), F32),
            like((rows, width), BF16),
            like((rows, width), F32),
            like((rows, width), BF16),
        ]
        + down_grads
        + mid_grads,
        [x, mixed],
        table,
        list(cot_parts) + list(smalls) + list(out_pieces) + list(feed_pieces),
        weight_scratch(out_pieces, width)
        + weight_scratch(feed_pieces, hidden) * 2
        + turn_scratch(feed_pieces, rows) * 2
        + [
            pltpu.VMEM((n, SMALL, 2 * hidden), BF16),
            pltpu.VMEM((rows, width), BF16),
            pltpu.SemaphoreType.DMA((n + N_MP,)),
        ]
        + [pltpu.VMEM(*spec) for spec in near]
        + stage_scratch(feed_pieces, hidden)
        + stage_scratch(feed_pieces, cols)
        + [
            pltpu.VMEM((SHARED, cols), BF16),
            pltpu.SemaphoreType.DMA((3 + g * (2 * count + 1) + n_up,)),
        ],
        far=3 + 2 * g,
    )


def project_back(da, parts, table, pieces):
    rows, width = da.shape
    n = len(pieces)
    flat = [value for part in parts for value in part]

    def body(table, da_ref, *refs):
        part_refs, refs = refs[: len(flat)], refs[len(flat) :]
        pieces, (out_ref, dqkv_ref, held, sems) = refs[:n], refs[n:]
        weights = Weights(pieces, table, held, sems, 0, width)
        pair = 0
        for i in range(0, len(flat), 3):
            q_ref, own_ref, back_ref = part_refs[i : i + 3]
            cols = q_ref.shape[1]
            dqkv_ref[:, pair * LANES : pair * LANES + cols] = q_ref[...]
            for p in range(cols // LANES):
                for which in range(2):
                    at = slice((2 * p + which) * LANES, (2 * p + which + 1) * LANES)
                    to = (which + 1) * width + (pair + p) * LANES
                    value = own_ref[:, at] + back_ref[:, at].astype(F32)
                    dqkv_ref[:, to : to + LANES] = value.astype(BF16)
            pair += cols // LANES
        value = da_ref[...]
        for i in range(3):
            value = value + dot(dqkv_ref[:, i * width : (i + 1) * width], weights.get(i), NT)
        out_ref[...] = value.astype(BF16)

    return call(
        body,
        "project_back",
        9,
        [like((rows, width), BF16), like((rows, 3 * width), BF16)],
        [da] + flat,
        table,
        pieces,
        weight_scratch(pieces, 3 * width, 3),
    )


def project_grads(x, dqkv, table, pieces):
    rows, width = x.shape
    grads = grad_shapes(pieces, 3 * width, SHARED)
    g = len(grads)

    def body(table, x_ref, dqkv_ref, *refs):
        shared_ref, grad_outs, refs = refs[0], refs[1 : 1 + g], refs[1 + g :]
        plain, turned = refs[:2]
        stages, shared_low, sems = refs[2 : 2 + g], refs[2 + g], refs[3 + g]
        writes = Writes(sems)
        turn(x_ref[...], table, plain, turned)
        for i in range(3):
            at = i * width
            store_grad(turned, dqkv_ref[:, at : at + width], stages, at, writes, grad_outs)
        shared_ref[...] = jnp.zeros_like(shared_ref)
        shared_ref[0:1, :] = total(dqkv_ref[...].astype(F32))
        if g > 1:
            shared_low[...] = shared_ref[...].astype(BF16)
            for out in grad_outs:
                for r in range(out.shape[0]):
                    writes.start(shared_low, out.at[r, pl.ds(block_rows(pieces), SHARED)])
        writes.finish()

    return call(
        body,
        "project_grads",
        7,
        [like((SHARED, 3 * width), F32)] + grads,
        [x, dqkv],
        table,
        [],
        turn_scratch(pieces, rows)
        + stage_scratch(pieces, 3 * width)
        + [
            pltpu.VMEM((SHARED, 3 * width), BF16),
            pltpu.SemaphoreType.DMA((3 * g + len(blocks_of(pieces)),)),
        ],
        far=g,
    )


def at_column(values, rows, width, column):
    return lax.dynamic_update_slice(jnp.zeros((rows, width), values.dtype), values, (0, column))


def small_block(row_params, expand_bias, mine, depth):
    high = lax.reduce_precision(row_params, 8, 7)
    column = (mine * N_MP + depth) * row_params.shape[1]
    high_low = [
        at_column(part.astype(BF16), 6, WIDTH, column) for part in (high, row_params - high)
    ]
    bias = at_column(expand_bias, 2, 2 * WIDTH, mine * expand_bias.shape[1])
    return jnp.concatenate([jnp.concatenate(high_low, axis=1), bias])


def key_bias(length_long, length_short, block, core, depth):
    lengths = jnp.concatenate([length_long, length_short])
    other = core_swap(lengths)
    longs = jnp.where(core == 0, jnp.stack([lengths[0], other[0]]), jnp.stack([other[0], lengths[0]]))
    length = jnp.concatenate([longs, lengths[1:]])[depth]
    is_long = depth < 2
    place = lax.broadcasted_iota(jnp.int32, (1, 2 * N_MP * block), 1)
    row = place % (N_MP * block)
    is_own = place < N_MP * block
    source = (row // block) ^ depth
    whose = jnp.where(is_own, core, 1 - core)
    frame = row % block + jnp.where(is_long, (2 * source + whose) * block, source * block)
    counted = (frame < length) & (is_own | is_long)
    return jnp.where(counted, 0.0, NEG_FILL).astype(F32)


def on_device(
    frames_long,
    frames_short,
    length_long,
    length_short,
    input_proj,
    output_proj,
    expand_weight,
    shrink_weight,
    head_bias,
    expand_bias,
    row_params,
    cotangent_long,
    cotangent_short,
):
    mine = lax.axis_index("dp")
    depth = lax.axis_index("mp")
    n_dp = lax.axis_size("dp")
    fast = n_dp == 8
    core = mine % 2
    block = frames_short.shape[1]
    shard, group = input_proj.shape[1:]
    units = expand_weight.shape[1]
    width = group * N_MP
    hidden = units * N_MP
    table = block_table(mine, n_dp)

    joined = jnp.concatenate(
        [input_proj[0], input_proj[1], input_proj[2], output_proj.T], axis=1
    )
    heads = at_column(head_bias[:, 0], SMALL, WIDTH, mine * head_bias.shape[2])
    attn_parts = mp_gather(jnp.concatenate([joined, heads]))
    x_blocks = clip_blocks(frames_long[0], frames_short, core)
    cot_blocks = clip_blocks(cotangent_long[0], cotangent_short, core)
    bias = key_bias(length_long, length_short, block, core, depth)
    feed_shard = jnp.concatenate(
        [
            jnp.concatenate([expand_weight, shrink_weight.T], axis=1),
            small_block(row_params, expand_bias, mine, depth),
        ]
    )
    *attn_parts, feed_shard, bias, x_blocks, cot_blocks = tie(
        *attn_parts, feed_shard, bias, x_blocks, cot_blocks
    )
    order = [p[:shard, i * group : (i + 1) * group] for i in range(4) for p in attn_parts]
    attn_slab = jnp.concatenate([to_slab(order), to_slab([p[shard:] for p in attn_parts])])
    feed_parts = mp_gather(feed_shard)
    feed_order = [p[:, i * units : (i + 1) * units] for i in range(2) for p in feed_parts]
    if fast:
        attn_p = [attn_slab] + [dp_swap(attn_slab, to) for to in (early, late, across)]
        x_pieces = clip_pieces(x_blocks, depth)
        attn_p += [core_swap(piece) for piece in attn_p]
        both = tie(*attn_p, *x_pieces, *feed_order)
        attn_p, x_pieces, feed_order = both[:8], both[8:12], both[12:]
        feed_slab = to_slab(feed_order)
        feed_one = dp_swap(feed_slab, early)
        feed_two = dp_swap(feed_slab, late)
        x_parts = [x_pieces[0]] + [mp_swap(x_pieces[i], i) for i in range(1, N_MP)]
        *x_parts, cot_blocks, own_slab = tie(*x_parts, cot_blocks, feed_slab)
        heads = sum(p[shard:].astype(F32) for p in attn_p)
    else:
        x_parts = to_clips(x_blocks, depth)
        gather = lambda slab: lax.all_gather(slab, "dp", axis=0)
        whole = gather(attn_slab)
        heads = jnp.sum(whole[:, shard:].astype(F32), axis=0)
        attn_p = [whole[:, :shard].reshape(width, 4 * width)]
        whole = gather(to_slab(feed_order))
        small = jnp.sum(whole[:, shard:].astype(F32), axis=0)
        feed_p = [whole[:, :shard].reshape(width, 2 * hidden)]
    cot_parts = to_clips(cot_blocks, depth)
    heads = jnp.concatenate(
        [heads[:2, i * width : i * width + group] for i in range(N_MP)], axis=1
    )
    head_row = jnp.concatenate([heads[:1], jnp.zeros_like(heads[:1]), heads[1:]], axis=1)

    x, qkv, kv = project(x_parts, head_row, table, attn_p)
    if fast:
        kv, feed_one, feed_two, cot_parts[3], own_slab = tie(
            kv, feed_one, feed_two, cot_parts[3], core_swap(own_slab)
        )
    kv_other = core_swap(kv)
    if fast:
        feed_three = dp_swap(feed_one, late)
        feed_p = [feed_slab, feed_one, feed_two]
        backs = [own_slab] + [core_swap(piece) for piece in feed_p[1:]]
    mixed, lse = attend(qkv, kv_other, bias)
    if fast:
        mixed, feed_three, *both = tie(mixed, feed_three, *backs, *cot_parts)
        backs, cot_parts = both[:3], both[3:]
        feed_p = feed_p + [feed_three] + backs + [core_swap(feed_three)]
        smalls, small_row = feed_p, shard
    else:
        smalls, small_row = [small.astype(BF16)], 0
    outs = feed(x, mixed, cot_parts, smalls, small_row, table, attn_p, feed_p)
    mid_shared, result, da, do, *grads = outs
    g_down, g_mid = grads[: len(grads) // 2], grads[len(grads) // 2 :]

    def by_group_of(value, sizes):
        starts = [N_MP * sum(sizes[:i]) for i in range(len(sizes))]
        return [
            jnp.concatenate(
                [value[:, a + j * n : a + (j + 1) * n] for a, n in zip(starts, sizes)], axis=1
            )
            for j in range(N_MP)
        ]

    def last_sum(terms):
        return sum(term[0].astype(F32) for term in terms)

    result_parts = from_clips(result)
    if fast:
        b_down, b_mid = core_swap(g_down[1]), core_swap(g_mid[1])
    pairs = width // LANES
    first = pairs // 2
    dq_a, own_a, other_a = attend_back(qkv, kv_other, bias, mixed, lse, do, 0, first)
    if fast:
        other_a, b_down, b_mid, result_parts[3] = tie(other_a, b_down, b_mid, result_parts[3])
        t_down = [g_down[0], b_down]
        a_down = goes_on(t_down)
        do, a_down = tie(do, a_down)
        b_down = dp_swap(a_down, late)
        t_mid = [g_mid[0], b_mid]
        a_mid = goes_on(t_mid)
        do, a_mid = tie(do, a_mid)
        b_mid = dp_swap(a_mid, late)
    back_a = core_swap(other_a)
    dq_b, own_b, other_b = attend_back(
        qkv, kv_other, bias, mixed, lse, do, first, pairs - first
    )
    if fast:
        other_b, back_a, *result_parts = tie(other_b, back_a, *result_parts)
    back_b = core_swap(other_b)
    parts = [(dq_a, own_a, back_a), (dq_b, own_b, back_b)]
    frames_grad, dqkv = project_back(da, parts, table, attn_p)
    grad_parts = from_clips(frames_grad)
    if fast:
        dqkv, b_down, b_mid = tie(dqkv, b_down, b_mid)
        t_down, t_mid = stays(t_down, b_down), stays(t_mid, b_mid)
        a_down, a_mid = goes_on(t_down), goes_on(t_mid)
        dqkv, a_down, a_mid = tie(dqkv, a_down, a_mid)
        b_down = dp_swap(a_down, early)
        b_mid = dp_swap(a_mid, early)
    attn_shared, *g_attn = project_grads(x, dqkv, table, attn_p)
    if fast:
        both = tie(*g_attn, b_down, b_mid, *grad_parts)
        g_attn, b_down, b_mid, grad_parts = both[:2], both[2], both[3], both[4:]
        b_attn = core_swap(g_attn[1])
        s_down = by_group_of(last_sum(stays(t_down, b_down)), [units])
        t_attn = [g_attn[0], b_attn]
        a_attn = goes_on(t_attn)
        a_attn, *s_down = tie(a_attn, *s_down)
        b_attn = dp_swap(a_attn, late)
        z_down = mp_away(s_down)
        s_mid = by_group_of(last_sum(stays(t_mid, b_mid)), [units, group])
        b_attn, *z_down = tie(b_attn, *z_down)
        t_attn = stays(t_attn, b_attn)
        a_attn = goes_on(t_attn)
        z_mid = mp_away(s_mid)
        b_attn, *both = tie(dp_swap(a_attn, early), *z_mid, *result_parts)
        z_mid, result_parts = both[: N_MP - 1], both[N_MP - 1 :]
        s_attn = last_sum(stays(t_attn, b_attn))
    else:
        scatter = lambda g: lax.psum_scatter(g[0][0], "dp", scatter_dimension=0, tiled=True)
        s_down = by_group_of(scatter(g_down), [units])
        z_down = mp_away(s_down)
        s_mid = jnp.concatenate([scatter(g_mid), lax.psum(mid_shared, "dp")])
        s_mid = by_group_of(s_mid, [units, group])
        z_mid = mp_away(s_mid)
        s_attn = jnp.concatenate([scatter(g_attn), lax.psum(attn_shared, "dp")])
    s_attn = by_group_of(s_attn, [group] * 3)
    grad_long, grad_short = frames_of(grad_parts, core, depth)
    result_long, result_short = frames_of(result_parts, core, depth)
    attn_share = mp_total(s_attn[0], mp_away(s_attn))
    down_share = mp_total(s_down[0], z_down).T
    mid_share = mp_total(s_mid[0], z_mid)
    up_share = mid_share[:shard, :units]
    output_share = mid_share[:shard, units:].T
    input_share = jnp.stack(
        [attn_share[:shard, i * group : (i + 1) * group] for i in range(3)]
    )
    up_cols, head_cols, row_cols = units // n_dp, group // n_dp, width // (n_dp * N_MP)
    rank = mine * N_MP + depth
    up_b_share = lax.dynamic_slice(mid_share, (shard, mine * up_cols), (1, up_cols))
    row_share = lax.dynamic_slice(mid_share, (shard + 1, rank * row_cols), (6, row_cols))
    head_share = jnp.stack(
        [
            lax.dynamic_slice(attn_share, (shard, at + mine * head_cols), (1, head_cols))
            for at in (0, 2 * group)
        ]
    )
    return (
        result_long,
        result_short,
        grad_long.astype(F32),
        grad_short.astype(F32),
        input_share,
        output_share,
        up_share,
        down_share,
        head_share,
        up_b_share,
        row_share,
    )


def solution(mesh):
    return jax.shard_map(
        on_device,
        mesh=mesh,
        in_specs=(
            P("dp", "mp", None),
            P("dp", "mp", None),
            P("dp"),
            P("dp"),
            P(None, "dp", "mp"),
            P("mp", "dp"),
            P("dp", "mp"),
            P("mp", "dp"),
            P(None, "mp", "dp"),
            P("mp", "dp"),
            P(None, ("dp", "mp")),
            P("dp", "mp", None),
            P("dp", "mp", None),
        ),
        out_specs=(
            P("dp", "mp", None),
            P("dp", "mp", None),
            P("dp", "mp", None),
            P("dp", "mp", None),
            P(None, "dp", "mp"),
            P("mp", "dp"),
            P("dp", "mp"),
            P("mp", "dp"),
            P(None, "mp", "dp"),
            P("mp", "dp"),
            P(None, ("dp", "mp")),
        ),
        check_vma=False,
    )
```

```python
import functools

import jax
import jax.numpy as jnp
from jax import lax
from jax.experimental import pallas as pl
from jax.experimental.pallas import tpu as pltpu
from jax.sharding import PartitionSpec as P

HEAD = 64
EPS = 1e-05
NEG_FILL = -1e30
SCALE = HEAD ** (-0.5)
N_MP = 4
PARTS = 1
CS = 0.3
WIDTH = 768
SMALL = 8
SHARED = 8
LANES = 128
Q_TILE = 256
F32 = jnp.float32
BF16 = jnp.bfloat16
NT = (((1,), (1,)), ((), ()))
NN = (((1,), (0,)), ((), ()))
TN = (((0,), (0,)), ((), ()))


def dot(left, right, dims):
    return lax.dot_general(left, right, dims, preferred_element_type=F32)


def mp_swap(value, step):
    return lax.ppermute(value, "mp", [(i, i ^ step) for i in range(N_MP)])


def dp_swap(value, target):
    size = lax.axis_size("dp")
    return lax.ppermute(value, "dp", [(i, target(i)) for i in range(size)])


def core_swap(value):
    return dp_swap(value, lambda i: i ^ 1)


def clip_blocks(long_rows, short_rows, core):
    block = short_rows.shape[1]
    keep = lax.dynamic_slice_in_dim(long_rows, core * block, block, 0)
    away = lax.dynamic_slice_in_dim(long_rows, (1 - core) * block, block, 0)
    back = core_swap(away)
    first = jnp.where(core == 0, keep, back)
    second = jnp.where(core == 0, back, keep)
    return jnp.stack([first, second, short_rows[0], short_rows[1]])


def clip_pieces(blocks, depth):
    return [
        lax.dynamic_index_in_dim(blocks, depth ^ step, 0, keepdims=False) for step in range(N_MP)
    ]


def to_clips(blocks, depth):
    pieces = clip_pieces(blocks, depth)
    return pieces[:1] + [mp_swap(pieces[step], step) for step in range(1, N_MP)]


def from_clips(rows):
    block = rows.shape[0] // N_MP
    parts = []
    for step in range(N_MP):
        piece = rows[step * block : (step + 1) * block]
        parts.append(piece if step == 0 else mp_swap(piece, step))
    return parts


def frames_of(parts, core, depth):
    blocks = jnp.stack(parts)
    first, second, short_a, short_b = (
        lax.dynamic_index_in_dim(blocks, depth ^ i, 0, keepdims=False) for i in range(N_MP)
    )
    keep = jnp.where(core == 0, first, second)
    away = jnp.where(core == 0, second, first)
    back = core_swap(away)
    low = jnp.where(core == 0, keep, back)
    high = jnp.where(core == 0, back, keep)
    return jnp.concatenate([low, high], axis=0)[None], jnp.stack([short_a, short_b])


def flip(index, late):
    return index ^ ((4 if late else 2) if index % 2 == 0 else (2 if late else 4))


def block_table(mine, size):
    if size != 8:
        return jnp.zeros((1,), jnp.int32)
    early = jnp.where(mine % 2 == 0, 2, 4)
    late = 6 - early
    relative = [0, early, late, 6, 1, 1 ^ late, 1 ^ early, 7]
    return jnp.stack([mine ^ r for r in relative]).astype(jnp.int32)


def early(i):
    return flip(i, False)


def late(i):
    return flip(i, True)


def across(i):
    return i ^ 6


def tie(*values):
    return lax.optimization_barrier(values)


def swap_plane(plane):
    return plane + [core_swap(piece) for piece in plane]


def to_slab(parts):
    return jnp.concatenate(parts, axis=1)


def mp_gather(shard):
    return [shard] + [mp_swap(shard, step) for step in range(1, N_MP)]


def goes_on(terms):
    half = terms[0].shape[0] // 2
    return sum(term[half:].astype(F32) for term in terms).astype(BF16)


def stays(terms, back):
    half = terms[0].shape[0] // 2
    return [term[:half] for term in terms] + [back]


def mp_away(parts):
    return [mp_swap(parts[step].astype(BF16), step) for step in range(1, N_MP)]


def mp_total(own, backs):
    for back in backs:
        own = own + back.astype(F32)
    return own


def blocks_of(pieces):
    step = pieces[0].shape[0]
    return [(p, k * step) for p in pieces for k in range(p.shape[0] // step)]


def block_rows(pieces):
    return WIDTH // len(blocks_of(pieces))


class Weights:
    def __init__(self, pieces, table, held, sems, lo, tile):
        self.held, self.tile = held, tile
        cols, parts = held.shape[2], sems.shape[0]
        self.span, self.copies = cols // parts, []
        for t in range(parts):
            row = []
            for k, (piece, first) in enumerate(blocks_of(pieces)):
                copy = pltpu.make_async_copy(
                    piece.at[pl.ds(first, held.shape[1]), pl.ds(lo + t * self.span, self.span)],
                    held.at[table[k], :, pl.ds(t * self.span, self.span)],
                    sems.at[t, k],
                )
                copy.start()
                row.append(copy)
            self.copies.append(row)
        self.waited = 0

    def get(self, t):
        at = t * self.tile
        while self.waited * self.span < at + self.tile:
            for copy in self.copies[self.waited]:
                copy.wait()
            self.waited += 1
        count, rows, _ = self.held.shape
        return self.held[:, :, at : at + self.tile].reshape(count * rows, self.tile)


def weight_scratch(pieces, cols, parts=1):
    return [
        pltpu.VMEM((len(blocks_of(pieces)), block_rows(pieces), cols), BF16),
        pltpu.SemaphoreType.DMA((parts, len(blocks_of(pieces)))),
    ]


def grad_shapes(pieces, cols, extra=0):
    count, rows = len(blocks_of(pieces)), block_rows(pieces)
    if count == 1:
        return [jax.ShapeDtypeStruct((1, rows, cols), F32)]
    return [jax.ShapeDtypeStruct((count // 2, rows + extra, cols), BF16)] * 2


def turn_scratch(pieces, rows):
    return [pltpu.VMEM((len(blocks_of(pieces)), block_rows(pieces), rows), BF16)] * 2


def turn(value, table, plain, turned):
    plain[...] = value.T.reshape(plain.shape)
    for r in range(plain.shape[0]):
        turned[r] = plain[table[r]]


def stage_scratch(pieces, cols):
    return [
        pltpu.VMEM((g.shape[0], block_rows(pieces), cols), g.dtype)
        for g in grad_shapes(pieces, cols)
    ]


def store_grad(turned, right, stages, at, writes=None, outs=None):
    count, rows, _ = turned.shape
    grad = dot(turned[...].reshape(count * rows, -1), right, NN)
    half, cols = count // len(stages), right.shape[1]
    for r in range(count):
        stage = stages[r // half]
        part = grad[r * rows : (r + 1) * rows].astype(stage.dtype)
        stage[r % half, :rows, at : at + cols] = part
    if writes is not None:
        for stage, out in zip(stages, outs):
            writes.start(
                stage.at[:, :, pl.ds(at, cols)],
                out.at[:, pl.ds(0, rows), pl.ds(at, cols)],
            )


class Writes:
    def __init__(self, sems):
        self.sems, self.copies = sems, []

    def start(self, source, target):
        copy = pltpu.make_async_copy(source, target, self.sems.at[len(self.copies)])
        copy.start()
        self.copies.append(copy)

    def finish(self):
        for copy in self.copies:
            copy.wait()


class Reads:
    def __init__(self, sources, targets, sems):
        self.targets, self.copies = targets, []
        for i, (source, target) in enumerate(zip(sources, targets)):
            copy = pltpu.make_async_copy(source, target, sems.at[i])
            copy.start()
            self.copies.append(copy)

    def get(self, i):
        self.copies[i].wait()
        return self.targets[i]


def read_scratch(arrays):
    return [pltpu.VMEM(a.shape, a.dtype) for a in arrays] + [
        pltpu.SemaphoreType.DMA((len(arrays),))
    ]


def cost(micros):
    return pl.CostEstimate(
        flops=int(micros * 1.1e9 * CS), bytes_accessed=int(micros * 1e5 * CS), transcendentals=0
    )


def call(body, name, micros, outs, arrays, table, pieces, scratch, far=0):
    vmem = pl.BlockSpec(memory_space=pltpu.VMEM)
    away = pl.BlockSpec(memory_space=pl.ANY)
    return pl.pallas_call(
        body,
        out_shape=tuple(outs),
        in_specs=[pl.BlockSpec(memory_space=pltpu.SMEM)]
        + [vmem] * len(arrays)
        + [away] * len(pieces),
        out_specs=(vmem,) * (len(outs) - far) + (away,) * far,
        scratch_shapes=scratch,
        compiler_params=pltpu.CompilerParams(vmem_limit_bytes=60 << 20),
        cost_estimate=cost(micros),
        name=name,
    )(table, *arrays, *pieces)


def like(shape, kind):
    return jax.ShapeDtypeStruct(shape, kind)


def attend_kernel(q_ref, k_ref, v_ref, kp_ref, vp_ref, bias_ref, o_ref, lse_ref):
    rows = q_ref.shape[0]
    keys = jnp.concatenate([k_ref[...], kp_ref[...]], axis=0)
    values = jnp.concatenate([v_ref[...], vp_ref[...]], axis=0)
    bias = bias_ref[...]
    tile = min(rows, Q_TILE)
    low = lax.broadcasted_iota(jnp.int32, (tile, LANES), 1) < HEAD
    for start in range(0, rows, tile):
        q = q_ref[start : start + tile, :]
        outs, logs = [], []
        for half in range(2):
            here = low if half == 0 else ~low
            q_here = jnp.where(here, q, jnp.zeros_like(q))
            scores = dot(q_here, keys, NT) + bias
            top = jnp.max(scores, axis=-1, keepdims=True)
            raised = jnp.exp(scores - top)
            total = jnp.sum(raised, axis=-1, keepdims=True)
            mixed = dot(raised.astype(BF16), values, NN)
            outs.append(mixed / total)
            logs.append(top + jnp.log(total))
        o_ref[start : start + tile, :] = jnp.where(low, outs[0], outs[1]).astype(BF16)
        lse_ref[start : start + tile, :] = jnp.where(low, logs[0], logs[1])


def attend(qkv, kv_other, bias):
    rows, width = qkv.shape[0], qkv.shape[1] // 3
    pairs = width // LANES
    spec = lambda base: pl.BlockSpec((rows, LANES), lambda p: (0, base + p))
    return pl.pallas_call(
        attend_kernel,
        out_shape=(
            jax.ShapeDtypeStruct((rows, width), BF16),
            jax.ShapeDtypeStruct((rows, width), F32),
        ),
        grid=(pairs,),
        in_specs=[
            spec(0),
            spec(pairs),
            spec(2 * pairs),
            spec(0),
            spec(pairs),
            pl.BlockSpec((1, 2 * rows), lambda p: (0, 0)),
        ],
        out_specs=(spec(0), spec(0)),
        compiler_params=pltpu.CompilerParams(vmem_limit_bytes=56 << 20),
        cost_estimate=cost(15),
        name="attend",
    )(qkv, qkv, qkv, kv_other, kv_other, bias)


def attend_back_kernel(
    q_ref, k_ref, v_ref, kp_ref, vp_ref, bias_ref, o_ref, lse_ref, do_ref,
    dq_ref, own_ref, other_ref,
):
    rows = q_ref.shape[0]
    keys = jnp.concatenate([k_ref[...], kp_ref[...]], axis=0)
    values = jnp.concatenate([v_ref[...], vp_ref[...]], axis=0)
    bias = bias_ref[...]
    tile = min(rows, Q_TILE)
    low = lax.broadcasted_iota(jnp.int32, (tile, LANES), 1) < HEAD
    dk = jnp.zeros((LANES, 2 * rows), F32)
    dv = jnp.zeros((LANES, 2 * rows), F32)
    for start in range(0, rows, tile):
        at = slice(start, start + tile)
        q, do = q_ref[at, :], do_ref[at, :]
        product = o_ref[at, :].astype(F32) * do.astype(F32)
        lse = lse_ref[at, :]
        outs = []
        for half in range(2):
            here = low if half == 0 else ~low
            q_here = jnp.where(here, q, jnp.zeros_like(q))
            do_here = jnp.where(here, do, jnp.zeros_like(do))
            inner = jnp.sum(jnp.where(here, product, 0.0), axis=-1, keepdims=True)
            log = lse[:, half * HEAD : half * HEAD + 1]
            soft = jnp.exp(dot(q_here, keys, NT) + bias - log)
            grad = (soft * (dot(do_here, values, NT) - inner)).astype(BF16)
            outs.append(dot(grad, keys, NN))
            dk = dk + dot(q_here, grad, TN)
            dv = dv + dot(do_here, soft.astype(BF16), TN)
        dq_ref[at, :] = (jnp.where(low, outs[0], outs[1]) * SCALE).astype(BF16)
    for i, value in enumerate((dk.T, dv.T)):
        at = slice(i * LANES, (i + 1) * LANES)
        own_ref[:, at] = value[:rows]
        other_ref[:, at] = value[rows:].astype(BF16)


def attend_back(qkv, kv_other, bias, out, lse, grad_out, first, count):
    rows, width = out.shape
    pairs = width // LANES
    spec = lambda base: pl.BlockSpec((rows, LANES), lambda p: (0, base + first + p))
    result = lambda cols: pl.BlockSpec((rows, cols), lambda p: (0, p))
    return pl.pallas_call(
        attend_back_kernel,
        out_shape=(
            jax.ShapeDtypeStruct((rows, count * LANES), BF16),
            jax.ShapeDtypeStruct((rows, 2 * count * LANES), F32),
            jax.ShapeDtypeStruct((rows, 2 * count * LANES), BF16),
        ),
        grid=(count,),
        in_specs=[
            spec(0),
            spec(pairs),
            spec(2 * pairs),
            spec(0),
            spec(pairs),
            pl.BlockSpec((1, 2 * rows), lambda p: (0, 0)),
            spec(0),
            spec(0),
            spec(0),
        ],
        out_specs=(result(LANES), result(2 * LANES), result(2 * LANES)),
        compiler_params=pltpu.CompilerParams(vmem_limit_bytes=56 << 20),
        cost_estimate=cost(3 * count),
        name="attend_back",
    )(qkv, qkv, qkv, kv_other, kv_other, bias, out, lse, grad_out)


def gelu_parts(v):
    cdf = 0.5 * (1.0 + lax.erf(v * (2.0 ** -0.5)))
    pdf = jnp.exp(-0.5 * v * v) * 0.3989422804014327
    return v * cdf, cdf + v * pdf


def norm(values):
    center = values - jnp.mean(values, axis=-1, keepdims=True)
    inv_dev = lax.rsqrt(jnp.mean(center * center, axis=-1, keepdims=True) + EPS)
    return center * inv_dev, inv_dev


def norm_back(scaled, normed, inv_dev):
    return inv_dev * (
        scaled
        - jnp.mean(scaled, axis=-1, keepdims=True)
        - normed * jnp.mean(scaled * normed, axis=-1, keepdims=True)
    )


def total(value):
    return jnp.sum(value, axis=0, keepdims=True)


def project(x_parts, head_row, table, pieces):
    block, width = x_parts[0].shape
    rows = block * len(x_parts)
    n = len(pieces)

    def body(table, *refs):
        part_refs, bias_ref, refs = refs[:N_MP], refs[N_MP], refs[N_MP + 1 :]
        pieces, (x_ref, qkv_ref, kv_ref, held, sems) = refs[:n], refs[n:]
        weights = Weights(pieces, table, held, sems, 0, width)
        for i, part in enumerate(part_refs):
            x_ref[i * block : (i + 1) * block, :] = part[...]
        x = x_ref[...]
        for i in range(3):
            value = dot(x, weights.get(i), NN) + bias_ref[:, i * width : (i + 1) * width]
            value = value.astype(BF16)
            if i == 0:
                value = (value.astype(F32) * SCALE).astype(BF16)
            else:
                kv_ref[:, (i - 1) * width : i * width] = value
            qkv_ref[:, i * width : (i + 1) * width] = value

    return call(
        body,
        "project",
        7,
        [
            like((rows, width), BF16),
            like((rows, 3 * width), BF16),
            like((rows, 2 * width), BF16),
        ],
        list(x_parts) + [head_row],
        table,
        pieces,
        weight_scratch(pieces, 3 * width, 3),
    )


def feed(x, mixed, cot_parts, smalls, small_row, table, out_pieces, feed_pieces):
    rows, width = x.shape
    hidden = feed_pieces[0].shape[1] // 2
    count = 6
    tile = hidden // count
    spans = [slice(t * tile, (t + 1) * tile) for t in range(count)]
    cols = hidden + width
    n_out, n_up, n = len(out_pieces), len(feed_pieces), len(smalls)
    down_grads = grad_shapes(feed_pieces, hidden)
    mid_grads = grad_shapes(feed_pieces, cols, SHARED)
    g = len(mid_grads)

    def body(table, x_ref, mixed_ref, *refs):
        cot_far, small_far, refs = refs[:N_MP], refs[N_MP : N_MP + n], refs[N_MP + n :]
        out_p, up_p = refs[:n_out], refs[n_out : n_out + n_up]
        refs = refs[n_out + n_up :]
        shared_ref, result_out, da_out, do_out = refs[:4]
        down_outs, mid_outs, refs = refs[4 : 4 + g], refs[4 + g : 4 + 2 * g], refs[4 + 2 * g :]
        w_out, sems_out, w_up, sems_up, w_down, sems_down = refs[:6]
        plain, turned, plain_h, turned_h = refs[6:10]
        small_ref, cot_ref, read_sems = refs[10:13]
        n1_ref, dz_ref, h_ref, act_ref, slope_ref, result_ref, low_ref, do_ref = refs[13:21]
        down_stages, mid_stages = refs[21 : 21 + g], refs[21 + g : 21 + 2 * g]
        shared_low, sems = refs[21 + 2 * g :]
        out_w = Weights(out_p, table, w_out, sems_out, 3 * width, width)
        smalls = [small.at[pl.ds(small_row, SMALL)] for small in small_far]
        reads = Reads(smalls, [small_ref.at[i] for i in range(n)], read_sems)
        up_w = Weights(up_p, table, w_up, sems_up, 0, tile)
        down_w = Weights(up_p, table, w_down, sems_down, hidden, tile)
        block = rows // N_MP
        cots = Reads(
            cot_far,
            [cot_ref.at[pl.ds(i * block, block)] for i in range(N_MP)],
            read_sems.at[pl.ds(n, N_MP)],
        )
        writes = Writes(sems)

        attention = dot(mixed_ref[...], out_w.get(0), NT)
        for i in range(n):
            reads.get(i)
        small = jnp.sum(small_ref[...].astype(F32), axis=0)
        row_vals = sum(small[:, i * width : (i + 1) * width] for i in range(2 * N_MP))
        row = lambda i: row_vals[i : i + 1, :]
        up_b = small[6:7, :hidden]
        n1, r1 = norm(x_ref[...].astype(F32) + attention + row(0))
        n1_ref[...] = n1
        h_ref[...] = (n1 * row(1) + row(2)).astype(BF16)
        feed = jnp.zeros((rows, width), F32)
        u = dot(h_ref[...], up_w.get(0), NN)
        for t, at in enumerate(spans):
            down = down_w.get(t)
            later = dot(h_ref[...], up_w.get(t + 1), NN) if t + 1 < count else None
            act, slope = gelu_parts(u + up_b[:, at])
            act_ref[:, at] = act.astype(BF16)
            slope_ref[:, at] = slope.astype(BF16)
            feed = feed + dot(act_ref[:, at], down, NT)
            u = later
        h = n1_ref[...] * row(1) + row(2)
        n2, r2 = norm(h + feed + row(3))
        result_ref[...] = (n2 * row(4) + row(5)).astype(BF16)
        writes.start(result_ref, result_out)
        for i in range(N_MP):
            cots.get(i)
        gy = cot_ref[...].astype(F32)
        dz = norm_back(gy * row(4), n2, r2)
        dz_ref[...] = dz
        low_ref[...] = dz.astype(BF16)
        sums = [total(dz), total(gy * n2), total(gy)]

        turn(low_ref[...], table, plain, turned)
        turn(h_ref[...], table, plain_h, turned_h)
        shared_ref[...] = jnp.zeros_like(shared_ref)
        dh = dz_ref[...]
        for t, at in enumerate(spans):
            dact = dot(low_ref[...], down_w.get(t), NN)
            store_grad(turned, act_ref[:, at], down_stages, at.start, writes, down_outs)
            du = (dact * slope_ref[:, at].astype(F32)).astype(BF16)
            shared_ref[0:1, at] = total(du.astype(F32))
            dh = dh + dot(du, up_w.get(t), NT)
            store_grad(turned_h, du, mid_stages, at.start, writes, mid_outs)
        n1 = n1_ref[...]
        da = norm_back(dh * row(1), n1, r1)
        dz_ref[...] = da
        writes.start(dz_ref, da_out)
        low_ref[...] = da.astype(BF16)
        do_ref[...] = dot(low_ref[...], out_w.get(0), NN).astype(BF16)
        writes.start(do_ref, do_out)
        sums = [total(da), total(dh * n1), total(dh)] + sums
        for j in range(hidden // width):
            for i, value in enumerate(sums):
                shared_ref[1 + i : 2 + i, j * width : (j + 1) * width] = value
        if g > 1:
            shared_low[...] = shared_ref[...].astype(BF16)
            for out in mid_outs:
                for r in range(out.shape[0]):
                    writes.start(shared_low, out.at[r, pl.ds(block_rows(feed_pieces), SHARED)])
        turn(low_ref[...], table, plain, turned)
        store_grad(turned, mixed_ref[...], mid_stages, hidden, writes, mid_outs)
        writes.finish()

    near = [((rows, width), F32)] * 2 + [((rows, width), BF16)]
    near += [((rows, hidden), BF16)] * 2 + [((rows, width), BF16)] * 3
    return call(
        body,
        "feed",
        33,
        [
            like((SHARED, cols), F32),
            like((rows, width), BF16),
            like((rows, width), F32),
            like((rows, width), BF16),
        ]
        + down_grads
        + mid_grads,
        [x, mixed],
        table,
        list(cot_parts) + list(smalls) + list(out_pieces) + list(feed_pieces),
        weight_scratch(out_pieces, width)
        + weight_scratch(feed_pieces, hidden) * 2
        + turn_scratch(feed_pieces, rows) * 2
        + [
            pltpu.VMEM((n, SMALL, 2 * hidden), BF16),
            pltpu.VMEM((rows, width), BF16),
            pltpu.SemaphoreType.DMA((n + N_MP,)),
        ]
        + [pltpu.VMEM(*spec) for spec in near]
        + stage_scratch(feed_pieces, hidden)
        + stage_scratch(feed_pieces, cols)
        + [
            pltpu.VMEM((SHARED, cols), BF16),
            pltpu.SemaphoreType.DMA((3 + g * (2 * count + 1) + n_up,)),
        ],
        far=3 + 2 * g,
    )


def project_back(da, parts, table, pieces):
    rows, width = da.shape
    n = len(pieces)
    flat = [value for part in parts for value in part]

    def body(table, da_ref, *refs):
        part_refs, refs = refs[: len(flat)], refs[len(flat) :]
        pieces, (out_ref, dqkv_ref, held, sems) = refs[:n], refs[n:]
        weights = Weights(pieces, table, held, sems, 0, width)
        pair = 0
        for i in range(0, len(flat), 3):
            q_ref, own_ref, back_ref = part_refs[i : i + 3]
            cols = q_ref.shape[1]
            dqkv_ref[:, pair * LANES : pair * LANES + cols] = q_ref[...]
            for p in range(cols // LANES):
                for which in range(2):
                    at = slice((2 * p + which) * LANES, (2 * p + which + 1) * LANES)
                    to = (which + 1) * width + (pair + p) * LANES
                    value = own_ref[:, at] + back_ref[:, at].astype(F32)
                    dqkv_ref[:, to : to + LANES] = value.astype(BF16)
            pair += cols // LANES
        value = da_ref[...]
        for i in range(3):
            value = value + dot(dqkv_ref[:, i * width : (i + 1) * width], weights.get(i), NT)
        out_ref[...] = value.astype(BF16)

    return call(
        body,
        "project_back",
        9,
        [like((rows, width), BF16), like((rows, 3 * width), BF16)],
        [da] + flat,
        table,
        pieces,
        weight_scratch(pieces, 3 * width, 3),
    )


def project_grads(x, dqkv, table, pieces):
    rows, width = x.shape
    grads = grad_shapes(pieces, 3 * width, SHARED)
    g = len(grads)

    def body(table, x_ref, dqkv_ref, *refs):
        shared_ref, grad_outs, refs = refs[0], refs[1 : 1 + g], refs[1 + g :]
        plain, turned = refs[:2]
        stages, shared_low, sems = refs[2 : 2 + g], refs[2 + g], refs[3 + g]
        writes = Writes(sems)
        turn(x_ref[...], table, plain, turned)
        for i in range(3):
            at = i * width
            store_grad(turned, dqkv_ref[:, at : at + width], stages, at, writes, grad_outs)
        shared_ref[...] = jnp.zeros_like(shared_ref)
        shared_ref[0:1, :] = total(dqkv_ref[...].astype(F32))
        if g > 1:
            shared_low[...] = shared_ref[...].astype(BF16)
            for out in grad_outs:
                for r in range(out.shape[0]):
                    writes.start(shared_low, out.at[r, pl.ds(block_rows(pieces), SHARED)])
        writes.finish()

    return call(
        body,
        "project_grads",
        7,
        [like((SHARED, 3 * width), F32)] + grads,
        [x, dqkv],
        table,
        [],
        turn_scratch(pieces, rows)
        + stage_scratch(pieces, 3 * width)
        + [
            pltpu.VMEM((SHARED, 3 * width), BF16),
            pltpu.SemaphoreType.DMA((3 * g + len(blocks_of(pieces)),)),
        ],
        far=g,
    )


def at_column(values, rows, width, column):
    return lax.dynamic_update_slice(jnp.zeros((rows, width), values.dtype), values, (0, column))


def small_block(row_params, expand_bias, mine, depth):
    high = lax.reduce_precision(row_params, 8, 7)
    column = (mine * N_MP + depth) * row_params.shape[1]
    high_low = [
        at_column(part.astype(BF16), 6, WIDTH, column) for part in (high, row_params - high)
    ]
    bias = at_column(expand_bias, 2, 2 * WIDTH, mine * expand_bias.shape[1])
    return jnp.concatenate([jnp.concatenate(high_low, axis=1), bias])


def key_bias(length_long, length_short, block, core, depth):
    lengths = jnp.concatenate([length_long, length_short])
    other = core_swap(lengths)
    longs = jnp.where(core == 0, jnp.stack([lengths[0], other[0]]), jnp.stack([other[0], lengths[0]]))
    length = jnp.concatenate([longs, lengths[1:]])[depth]
    is_long = depth < 2
    place = lax.broadcasted_iota(jnp.int32, (1, 2 * N_MP * block), 1)
    row = place % (N_MP * block)
    is_own = place < N_MP * block
    source = (row // block) ^ depth
    whose = jnp.where(is_own, core, 1 - core)
    frame = row % block + jnp.where(is_long, (2 * source + whose) * block, source * block)
    counted = (frame < length) & (is_own | is_long)
    return jnp.where(counted, 0.0, NEG_FILL).astype(F32)


def on_device(
    frames_long,
    frames_short,
    length_long,
    length_short,
    input_proj,
    output_proj,
    expand_weight,
    shrink_weight,
    head_bias,
    expand_bias,
    row_params,
    cotangent_long,
    cotangent_short,
):
    mine = lax.axis_index("dp")
    depth = lax.axis_index("mp")
    n_dp = lax.axis_size("dp")
    fast = n_dp == 8
    core = mine % 2
    block = frames_short.shape[1]
    shard, group = input_proj.shape[1:]
    units = expand_weight.shape[1]
    width = group * N_MP
    hidden = units * N_MP
    table = block_table(mine, n_dp)

    joined = jnp.concatenate(
        [input_proj[0], input_proj[1], input_proj[2], output_proj.T], axis=1
    )
    heads = at_column(head_bias[:, 0], SMALL, WIDTH, mine * head_bias.shape[2])
    attn_parts = mp_gather(jnp.concatenate([joined, heads]))
    x_blocks = clip_blocks(frames_long[0], frames_short, core)
    cot_blocks = clip_blocks(cotangent_long[0], cotangent_short, core)
    bias = key_bias(length_long, length_short, block, core, depth)
    feed_shard = jnp.concatenate(
        [
            jnp.concatenate([expand_weight, shrink_weight.T], axis=1),
            small_block(row_params, expand_bias, mine, depth),
        ]
    )
    *attn_parts, feed_shard, bias, x_blocks, cot_blocks = tie(
        *attn_parts, feed_shard, bias, x_blocks, cot_blocks
    )
    order = [p[:shard, i * group : (i + 1) * group] for i in range(4) for p in attn_parts]
    attn_slab = jnp.concatenate([to_slab(order), to_slab([p[shard:] for p in attn_parts])])
    feed_parts = mp_gather(feed_shard)
    feed_order = [p[:, i * units : (i + 1) * units] for i in range(2) for p in feed_parts]
    if fast:
        attn_p = [attn_slab] + [dp_swap(attn_slab, to) for to in (early, late, across)]
        x_pieces = clip_pieces(x_blocks, depth)
        attn_p += [core_swap(piece) for piece in attn_p]
        both = tie(*attn_p, *x_pieces, *feed_order)
        attn_p, x_pieces, feed_order = both[:8], both[8:12], both[12:]
        feed_slab = to_slab(feed_order)
        feed_one = dp_swap(feed_slab, early)
        feed_two = dp_swap(feed_slab, late)
        x_parts = [x_pieces[0]] + [mp_swap(x_pieces[i], i) for i in range(1, N_MP)]
        *x_parts, cot_blocks, own_slab = tie(*x_parts, cot_blocks, feed_slab)
        heads = sum(p[shard:].astype(F32) for p in attn_p)
    else:
        x_parts = to_clips(x_blocks, depth)
        gather = lambda slab: lax.all_gather(slab, "dp", axis=0)
        whole = gather(attn_slab)
        heads = jnp.sum(whole[:, shard:].astype(F32), axis=0)
        attn_p = [whole[:, :shard].reshape(width, 4 * width)]
        whole = gather(to_slab(feed_order))
        small = jnp.sum(whole[:, shard:].astype(F32), axis=0)
        feed_p = [whole[:, :shard].reshape(width, 2 * hidden)]
    cot_parts = to_clips(cot_blocks, depth)
    heads = jnp.concatenate(
        [heads[:2, i * width : i * width + group] for i in range(N_MP)], axis=1
    )
    head_row = jnp.concatenate([heads[:1], jnp.zeros_like(heads[:1]), heads[1:]], axis=1)

    x, qkv, kv = project(x_parts, head_row, table, attn_p)
    if fast:
        kv, feed_one, feed_two, cot_parts[3], own_slab = tie(
            kv, feed_one, feed_two, cot_parts[3], core_swap(own_slab)
        )
    kv_other = core_swap(kv)
    if fast:
        feed_three = dp_swap(feed_one, late)
        feed_p = [feed_slab, feed_one, feed_two]
        backs = [own_slab] + [core_swap(piece) for piece in feed_p[1:]]
    mixed, lse = attend(qkv, kv_other, bias)
    if fast:
        mixed, feed_three, *both = tie(mixed, feed_three, *backs, *cot_parts)
        backs, cot_parts = both[:3], both[3:]
        feed_p = feed_p + [feed_three] + backs + [core_swap(feed_three)]
        smalls, small_row = feed_p, shard
    else:
        smalls, small_row = [small.astype(BF16)], 0
    outs = feed(x, mixed, cot_parts, smalls, small_row, table, attn_p, feed_p)
    mid_shared, result, da, do, *grads = outs
    g_down, g_mid = grads[: len(grads) // 2], grads[len(grads) // 2 :]

    def by_group_of(value, sizes):
        starts = [N_MP * sum(sizes[:i]) for i in range(len(sizes))]
        return [
            jnp.concatenate(
                [value[:, a + j * n : a + (j + 1) * n] for a, n in zip(starts, sizes)], axis=1
            )
            for j in range(N_MP)
        ]

    def feed_groups(down, mid):
        down = jnp.pad(down, ((0, SHARED), (0, 0)))
        return by_group_of(jnp.concatenate([mid, down], axis=1), [units, group, units])

    def last_sum(terms):
        return sum(term[0].astype(F32) for term in terms)

    if fast:
        b_down, b_mid = core_swap(g_down[1]), core_swap(g_mid[1])
    pairs = width // LANES
    first = pairs // 2
    dq_a, own_a, other_a = attend_back(qkv, kv_other, bias, mixed, lse, do, 0, first)
    if fast:
        other_a, b_down = tie(other_a, b_down)
        t_down = [g_down[0], b_down]
        a_down = goes_on(t_down)
        do, a_down = tie(do, a_down)
        b_down = dp_swap(a_down, late)
    back_a = core_swap(other_a)
    dq_b, own_b, other_b = attend_back(
        qkv, kv_other, bias, mixed, lse, do, first, pairs - first
    )
    if fast:
        other_b, back_a, b_down, b_mid = tie(other_b, back_a, b_down, b_mid)
    back_b = core_swap(other_b)
    if fast:
        t_down, t_mid = stays(t_down, b_down), [g_mid[0], b_mid]
        back_b, a_down, a_mid = tie(back_b, goes_on(t_down), goes_on(t_mid))
        b_mid = dp_swap(a_mid, late)
        b_down = dp_swap(a_down, early)
    parts = [(dq_a, own_a, back_a), (dq_b, own_b, back_b)]
    frames_grad, dqkv = project_back(da, parts, table, attn_p)
    frames_grad, result = tie(frames_grad, result)
    result_parts = from_clips(result)
    if fast:
        dqkv, b_down, b_mid, result_parts[3] = tie(dqkv, b_down, b_mid, result_parts[3])
        t_down, t_mid = stays(t_down, b_down), stays(t_mid, b_mid)
        dqkv, a_mid, frames_grad = tie(dqkv, goes_on(t_mid), frames_grad)
        b_mid = dp_swap(a_mid, early)
    grad_parts = from_clips(frames_grad)
    attn_shared, *g_attn = project_grads(x, dqkv, table, attn_p)
    if fast:
        both = tie(*g_attn, b_mid, *grad_parts, *result_parts)
        g_attn, b_mid, grad_parts, result_parts = both[:2], both[2], both[3:7], both[7:]
        t_attn = [g_attn[0], core_swap(g_attn[1])]
        both = tie(goes_on(t_attn), *t_down, *stays(t_mid, b_mid))
        b_attn = dp_swap(both[0], late)
        s_down, s_mid = last_sum(both[1:5]), last_sum(both[5:])
        s_feed = feed_groups(s_down, s_mid)
        z_feed = mp_away(s_feed)
        t_attn = stays(t_attn, b_attn)
        b_attn, *z_feed = tie(dp_swap(goes_on(t_attn), early), *z_feed)
        s_attn = last_sum(stays(t_attn, b_attn))
    else:
        scatter = lambda g: lax.psum_scatter(g[0][0], "dp", scatter_dimension=0, tiled=True)
        s_mid = jnp.concatenate([scatter(g_mid), lax.psum(mid_shared, "dp")])
        s_feed = feed_groups(scatter(g_down), s_mid)
        z_feed = mp_away(s_feed)
        s_attn = jnp.concatenate([scatter(g_attn), lax.psum(attn_shared, "dp")])
    s_attn = by_group_of(s_attn, [group] * 3)
    grad_long, grad_short = frames_of(grad_parts, core, depth)
    result_long, result_short = frames_of(result_parts, core, depth)
    feed_share = mp_total(s_feed[0], z_feed)
    mid_share, down_share = feed_share[:, : units + group], feed_share[:shard, units + group :].T
    attn_share = mp_total(s_attn[0], mp_away(s_attn))
    up_share = mid_share[:shard, :units]
    output_share = mid_share[:shard, units:].T
    input_share = jnp.stack(
        [attn_share[:shard, i * group : (i + 1) * group] for i in range(3)]
    )
    up_cols, head_cols, row_cols = units // n_dp, group // n_dp, width // (n_dp * N_MP)
    rank = mine * N_MP + depth
    up_b_share = lax.dynamic_slice(mid_share, (shard, mine * up_cols), (1, up_cols))
    row_share = lax.dynamic_slice(mid_share, (shard + 1, rank * row_cols), (6, row_cols))
    head_share = jnp.stack(
        [
            lax.dynamic_slice(attn_share, (shard, at + mine * head_cols), (1, head_cols))
            for at in (0, 2 * group)
        ]
    )
    return (
        result_long,
        result_short,
        grad_long.astype(F32),
        grad_short.astype(F32),
        input_share,
        output_share,
        up_share,
        down_share,
        head_share,
        up_b_share,
        row_share,
    )


def solution(mesh):
    return jax.shard_map(
        on_device,
        mesh=mesh,
        in_specs=(
            P("dp", "mp", None),
            P("dp", "mp", None),
            P("dp"),
            P("dp"),
            P(None, "dp", "mp"),
            P("mp", "dp"),
            P("dp", "mp"),
            P("mp", "dp"),
            P(None, "mp", "dp"),
            P("mp", "dp"),
            P(None, ("dp", "mp")),
            P("dp", "mp", None),
            P("dp", "mp", None),
        ),
        out_specs=(
            P("dp", "mp", None),
            P("dp", "mp", None),
            P("dp", "mp", None),
            P("dp", "mp", None),
            P(None, "dp", "mp"),
            P("mp", "dp"),
            P("dp", "mp"),
            P("mp", "dp"),
            P(None, "mp", "dp"),
            P("mp", "dp"),
            P(None, ("dp", "mp")),
        ),
        check_vma=False,
    )
```

```python
import functools

import jax
import jax.numpy as jnp
from jax import lax
from jax.experimental import pallas as pl
from jax.experimental.pallas import tpu as pltpu
from jax.sharding import PartitionSpec as P

HEAD = 64
EPS = 1e-05
NEG_FILL = -1e30
SCALE = HEAD ** (-0.5)
N_MP = 4
PARTS = 1
CS = 0.3
WIDTH = 768
SMALL = 8
SHARED = 8
LANES = 128
Q_TILE = 256
F32 = jnp.float32
BF16 = jnp.bfloat16
NT = (((1,), (1,)), ((), ()))
NN = (((1,), (0,)), ((), ()))
TN = (((0,), (0,)), ((), ()))


def dot(left, right, dims):
    return lax.dot_general(left, right, dims, preferred_element_type=F32)


def mp_swap(value, step):
    return lax.ppermute(value, "mp", [(i, i ^ step) for i in range(N_MP)])


def dp_swap(value, target):
    size = lax.axis_size("dp")
    return lax.ppermute(value, "dp", [(i, target(i)) for i in range(size)])


def core_swap(value):
    return dp_swap(value, lambda i: i ^ 1)


def clip_blocks(long_rows, short_rows, core):
    block = short_rows.shape[1]
    keep = lax.dynamic_slice_in_dim(long_rows, core * block, block, 0)
    away = lax.dynamic_slice_in_dim(long_rows, (1 - core) * block, block, 0)
    back = core_swap(away)
    first = jnp.where(core == 0, keep, back)
    second = jnp.where(core == 0, back, keep)
    return jnp.stack([first, second, short_rows[0], short_rows[1]])


def clip_pieces(blocks, depth):
    return [
        lax.dynamic_index_in_dim(blocks, depth ^ step, 0, keepdims=False) for step in range(N_MP)
    ]


def to_clips(blocks, depth):
    pieces = clip_pieces(blocks, depth)
    return pieces[:1] + [mp_swap(pieces[step], step) for step in range(1, N_MP)]


def from_clips(rows):
    block = rows.shape[0] // N_MP
    parts = []
    for step in range(N_MP):
        piece = rows[step * block : (step + 1) * block]
        parts.append(piece if step == 0 else mp_swap(piece, step))
    return parts


def frames_of(parts, core, depth):
    blocks = jnp.stack(parts)
    first, second, short_a, short_b = (
        lax.dynamic_index_in_dim(blocks, depth ^ i, 0, keepdims=False) for i in range(N_MP)
    )
    keep = jnp.where(core == 0, first, second)
    away = jnp.where(core == 0, second, first)
    back = core_swap(away)
    low = jnp.where(core == 0, keep, back)
    high = jnp.where(core == 0, back, keep)
    return jnp.concatenate([low, high], axis=0)[None], jnp.stack([short_a, short_b])


def flip(index, late):
    return index ^ ((4 if late else 2) if index % 2 == 0 else (2 if late else 4))


def block_table(mine, size):
    if size != 8:
        return jnp.zeros((1,), jnp.int32)
    early = jnp.where(mine % 2 == 0, 2, 4)
    late = 6 - early
    relative = [0, early, late, 6, 1, 1 ^ late, 1 ^ early, 7]
    return jnp.stack([mine ^ r for r in relative]).astype(jnp.int32)


def early(i):
    return flip(i, False)


def late(i):
    return flip(i, True)


def across(i):
    return i ^ 6


def tie(*values):
    return lax.optimization_barrier(values)


def swap_plane(plane):
    return plane + [core_swap(piece) for piece in plane]


def to_slab(parts):
    return jnp.concatenate(parts, axis=1)


def mp_gather(shard):
    return [shard] + [mp_swap(shard, step) for step in range(1, N_MP)]


def goes_on(terms):
    half = terms[0].shape[0] // 2
    return sum(term[half:].astype(F32) for term in terms).astype(BF16)


def stays(terms, back):
    half = terms[0].shape[0] // 2
    return [term[:half] for term in terms] + [back]


def mp_away(parts):
    return [mp_swap(parts[step].astype(BF16), step) for step in range(1, N_MP)]


def mp_total(own, backs):
    for back in backs:
        own = own + back.astype(F32)
    return own


def blocks_of(pieces):
    step = pieces[0].shape[0]
    return [(p, k * step) for p in pieces for k in range(p.shape[0] // step)]


def block_rows(pieces):
    return WIDTH // len(blocks_of(pieces))


class Weights:
    def __init__(self, pieces, table, held, sems, lo, tile):
        self.held, self.tile = held, tile
        cols, parts = held.shape[2], sems.shape[0]
        self.span, self.copies = cols // parts, []
        for t in range(parts):
            row = []
            for k, (piece, first) in enumerate(blocks_of(pieces)):
                copy = pltpu.make_async_copy(
                    piece.at[pl.ds(first, held.shape[1]), pl.ds(lo + t * self.span, self.span)],
                    held.at[table[k], :, pl.ds(t * self.span, self.span)],
                    sems.at[t, k],
                )
                copy.start()
                row.append(copy)
            self.copies.append(row)
        self.waited = 0

    def get(self, t):
        at = t * self.tile
        while self.waited * self.span < at + self.tile:
            for copy in self.copies[self.waited]:
                copy.wait()
            self.waited += 1
        count, rows, _ = self.held.shape
        return self.held[:, :, at : at + self.tile].reshape(count * rows, self.tile)


def weight_scratch(pieces, cols, parts=1):
    return [
        pltpu.VMEM((len(blocks_of(pieces)), block_rows(pieces), cols), BF16),
        pltpu.SemaphoreType.DMA((parts, len(blocks_of(pieces)))),
    ]


def grad_shapes(pieces, cols, extra=0):
    count, rows = len(blocks_of(pieces)), block_rows(pieces)
    if count == 1:
        return [jax.ShapeDtypeStruct((1, rows, cols), F32)]
    return [jax.ShapeDtypeStruct((count // 2, rows + extra, cols), BF16)] * 2


def turn_scratch(pieces, rows):
    return [pltpu.VMEM((len(blocks_of(pieces)), block_rows(pieces), rows), BF16)] * 2


def turn(value, table, plain, turned):
    plain[...] = value.T.reshape(plain.shape)
    for r in range(plain.shape[0]):
        turned[r] = plain[table[r]]


def stage_scratch(pieces, cols):
    return [
        pltpu.VMEM((g.shape[0], block_rows(pieces), cols), g.dtype)
        for g in grad_shapes(pieces, cols)
    ]


def store_grad(turned, right, stages, at, writes=None, outs=None):
    count, rows, _ = turned.shape
    grad = dot(turned[...].reshape(count * rows, -1), right, NN)
    half, cols = count // len(stages), right.shape[1]
    for r in range(count):
        stage = stages[r // half]
        part = grad[r * rows : (r + 1) * rows].astype(stage.dtype)
        stage[r % half, :rows, at : at + cols] = part
    if writes is not None:
        for stage, out in zip(stages, outs):
            writes.start(
                stage.at[:, :, pl.ds(at, cols)],
                out.at[:, pl.ds(0, rows), pl.ds(at, cols)],
            )


class Writes:
    def __init__(self, sems):
        self.sems, self.copies = sems, []

    def start(self, source, target):
        copy = pltpu.make_async_copy(source, target, self.sems.at[len(self.copies)])
        copy.start()
        self.copies.append(copy)

    def finish(self):
        for copy in self.copies:
            copy.wait()


class Reads:
    def __init__(self, sources, targets, sems):
        self.targets, self.copies = targets, []
        for i, (source, target) in enumerate(zip(sources, targets)):
            copy = pltpu.make_async_copy(source, target, sems.at[i])
            copy.start()
            self.copies.append(copy)

    def get(self, i):
        self.copies[i].wait()
        return self.targets[i]


def read_scratch(arrays):
    return [pltpu.VMEM(a.shape, a.dtype) for a in arrays] + [
        pltpu.SemaphoreType.DMA((len(arrays),))
    ]


def cost(micros):
    return pl.CostEstimate(
        flops=int(micros * 1.1e9 * CS), bytes_accessed=int(micros * 1e5 * CS), transcendentals=0
    )


def call(body, name, micros, outs, arrays, table, pieces, scratch, far=0):
    vmem = pl.BlockSpec(memory_space=pltpu.VMEM)
    away = pl.BlockSpec(memory_space=pl.ANY)
    return pl.pallas_call(
        body,
        out_shape=tuple(outs),
        in_specs=[pl.BlockSpec(memory_space=pltpu.SMEM)]
        + [vmem] * len(arrays)
        + [away] * len(pieces),
        out_specs=(vmem,) * (len(outs) - far) + (away,) * far,
        scratch_shapes=scratch,
        compiler_params=pltpu.CompilerParams(vmem_limit_bytes=60 << 20),
        cost_estimate=cost(micros),
        name=name,
    )(table, *arrays, *pieces)


def like(shape, kind):
    return jax.ShapeDtypeStruct(shape, kind)


def attend_kernel(q_ref, k_ref, v_ref, kp_ref, vp_ref, bias_ref, o_ref, lse_ref):
    rows = q_ref.shape[0]
    keys = jnp.concatenate([k_ref[...], kp_ref[...]], axis=0)
    values = jnp.concatenate([v_ref[...], vp_ref[...]], axis=0)
    bias = bias_ref[...]
    tile = min(rows, Q_TILE)
    low = lax.broadcasted_iota(jnp.int32, (tile, LANES), 1) < HEAD
    for start in range(0, rows, tile):
        q = q_ref[start : start + tile, :]
        outs, logs = [], []
        for half in range(2):
            here = low if half == 0 else ~low
            q_here = jnp.where(here, q, jnp.zeros_like(q))
            scores = dot(q_here, keys, NT) + bias
            top = jnp.max(scores, axis=-1, keepdims=True)
            raised = jnp.exp(scores - top)
            total = jnp.sum(raised, axis=-1, keepdims=True)
            mixed = dot(raised.astype(BF16), values, NN)
            outs.append(mixed / total)
            logs.append(top + jnp.log(total))
        o_ref[start : start + tile, :] = jnp.where(low, outs[0], outs[1]).astype(BF16)
        lse_ref[start : start + tile, :] = jnp.where(low, logs[0], logs[1])


def attend(qkv, kv_other, bias):
    rows, width = qkv.shape[0], qkv.shape[1] // 3
    pairs = width // LANES
    spec = lambda base: pl.BlockSpec((rows, LANES), lambda p: (0, base + p))
    return pl.pallas_call(
        attend_kernel,
        out_shape=(
            jax.ShapeDtypeStruct((rows, width), BF16),
            jax.ShapeDtypeStruct((rows, width), F32),
        ),
        grid=(pairs,),
        in_specs=[
            spec(0),
            spec(pairs),
            spec(2 * pairs),
            spec(0),
            spec(pairs),
            pl.BlockSpec((1, 2 * rows), lambda p: (0, 0)),
        ],
        out_specs=(spec(0), spec(0)),
        compiler_params=pltpu.CompilerParams(vmem_limit_bytes=56 << 20),
        cost_estimate=cost(15),
        name="attend",
    )(qkv, qkv, qkv, kv_other, kv_other, bias)


def attend_back_kernel(
    q_ref, k_ref, v_ref, kp_ref, vp_ref, bias_ref, o_ref, lse_ref, do_ref,
    dq_ref, own_ref, other_ref,
):
    rows = q_ref.shape[0]
    keys = jnp.concatenate([k_ref[...], kp_ref[...]], axis=0)
    values = jnp.concatenate([v_ref[...], vp_ref[...]], axis=0)
    bias = bias_ref[...]
    tile = min(rows, Q_TILE)
    low = lax.broadcasted_iota(jnp.int32, (tile, LANES), 1) < HEAD
    dk = jnp.zeros((LANES, 2 * rows), F32)
    dv = jnp.zeros((LANES, 2 * rows), F32)
    for start in range(0, rows, tile):
        at = slice(start, start + tile)
        q, do = q_ref[at, :], do_ref[at, :]
        product = o_ref[at, :].astype(F32) * do.astype(F32)
        lse = lse_ref[at, :]
        outs = []
        for half in range(2):
            here = low if half == 0 else ~low
            q_here = jnp.where(here, q, jnp.zeros_like(q))
            do_here = jnp.where(here, do, jnp.zeros_like(do))
            inner = jnp.sum(jnp.where(here, product, 0.0), axis=-1, keepdims=True)
            log = lse[:, half * HEAD : half * HEAD + 1]
            soft = jnp.exp(dot(q_here, keys, NT) + bias - log)
            grad = (soft * (dot(do_here, values, NT) - inner)).astype(BF16)
            outs.append(dot(grad, keys, NN))
            dk = dk + dot(q_here, grad, TN)
            dv = dv + dot(do_here, soft.astype(BF16), TN)
        dq_ref[at, :] = (jnp.where(low, outs[0], outs[1]) * SCALE).astype(BF16)
    for i, value in enumerate((dk.T, dv.T)):
        at = slice(i * LANES, (i + 1) * LANES)
        own_ref[:, at] = value[:rows]
        other_ref[:, at] = value[rows:].astype(BF16)


def attend_back(qkv, kv_other, bias, out, lse, grad_out, first, count):
    rows, width = out.shape
    pairs = width // LANES
    spec = lambda base: pl.BlockSpec((rows, LANES), lambda p: (0, base + first + p))
    result = lambda cols: pl.BlockSpec((rows, cols), lambda p: (0, p))
    return pl.pallas_call(
        attend_back_kernel,
        out_shape=(
            jax.ShapeDtypeStruct((rows, count * LANES), BF16),
            jax.ShapeDtypeStruct((rows, 2 * count * LANES), F32),
            jax.ShapeDtypeStruct((rows, 2 * count * LANES), BF16),
        ),
        grid=(count,),
        in_specs=[
            spec(0),
            spec(pairs),
            spec(2 * pairs),
            spec(0),
            spec(pairs),
            pl.BlockSpec((1, 2 * rows), lambda p: (0, 0)),
            spec(0),
            spec(0),
            spec(0),
        ],
        out_specs=(result(LANES), result(2 * LANES), result(2 * LANES)),
        compiler_params=pltpu.CompilerParams(vmem_limit_bytes=56 << 20),
        cost_estimate=cost(3 * count),
        name="attend_back",
    )(qkv, qkv, qkv, kv_other, kv_other, bias, out, lse, grad_out)


def gelu_parts(v):
    cdf = 0.5 * (1.0 + lax.erf(v * (2.0 ** -0.5)))
    pdf = jnp.exp(-0.5 * v * v) * 0.3989422804014327
    return v * cdf, cdf + v * pdf


def norm(values):
    center = values - jnp.mean(values, axis=-1, keepdims=True)
    inv_dev = lax.rsqrt(jnp.mean(center * center, axis=-1, keepdims=True) + EPS)
    return center * inv_dev, inv_dev


def norm_back(scaled, normed, inv_dev):
    return inv_dev * (
        scaled
        - jnp.mean(scaled, axis=-1, keepdims=True)
        - normed * jnp.mean(scaled * normed, axis=-1, keepdims=True)
    )


def total(value):
    return jnp.sum(value, axis=0, keepdims=True)


def join(parts, starts, size, micros):
    rows, cols = parts[0].shape[0], len(starts) * len(parts) * size

    def body(*refs):
        parts, out = refs[:-1], refs[-1]
        at = 0
        for start in starts:
            for part in parts:
                out[:, at : at + size] = part[:, start : start + size]
                at += size

    vmem = pl.BlockSpec(memory_space=pltpu.VMEM)
    return pl.pallas_call(
        body,
        out_shape=like((rows, cols), parts[0].dtype),
        in_specs=[vmem] * len(parts),
        out_specs=vmem,
        cost_estimate=cost(micros),
        name="join",
    )(*parts)


def project(x_parts, head_row, table, pieces):
    block, width = x_parts[0].shape
    rows = block * len(x_parts)
    n = len(pieces)

    def body(table, *refs):
        part_refs, bias_ref, refs = refs[:N_MP], refs[N_MP], refs[N_MP + 1 :]
        pieces, (x_ref, qkv_ref, kv_ref, held, sems) = refs[:n], refs[n:]
        weights = Weights(pieces, table, held, sems, 0, width)
        for i, part in enumerate(part_refs):
            x_ref[i * block : (i + 1) * block, :] = part[...]
        x = x_ref[...]
        for i in range(3):
            value = dot(x, weights.get(i), NN) + bias_ref[:, i * width : (i + 1) * width]
            value = value.astype(BF16)
            if i == 0:
                value = (value.astype(F32) * SCALE).astype(BF16)
            else:
                kv_ref[:, (i - 1) * width : i * width] = value
            qkv_ref[:, i * width : (i + 1) * width] = value

    return call(
        body,
        "project",
        7,
        [
            like((rows, width), BF16),
            like((rows, 3 * width), BF16),
            like((rows, 2 * width), BF16),
        ],
        list(x_parts) + [head_row],
        table,
        pieces,
        weight_scratch(pieces, 3 * width, 3),
    )


def feed(x, mixed, cot_parts, smalls, small_row, table, out_pieces, feed_pieces):
    rows, width = x.shape
    hidden = feed_pieces[0].shape[1] // 2
    count = 6
    tile = hidden // count
    spans = [slice(t * tile, (t + 1) * tile) for t in range(count)]
    cols = hidden + width
    n_out, n_up, n = len(out_pieces), len(feed_pieces), len(smalls)
    down_grads = grad_shapes(feed_pieces, hidden)
    mid_grads = grad_shapes(feed_pieces, cols, SHARED)
    g = len(mid_grads)

    def body(table, x_ref, mixed_ref, *refs):
        cot_far, small_far, refs = refs[:N_MP], refs[N_MP : N_MP + n], refs[N_MP + n :]
        out_p, up_p = refs[:n_out], refs[n_out : n_out + n_up]
        refs = refs[n_out + n_up :]
        shared_ref, result_out, da_out, do_out = refs[:4]
        down_outs, mid_outs, refs = refs[4 : 4 + g], refs[4 + g : 4 + 2 * g], refs[4 + 2 * g :]
        w_out, sems_out, w_up, sems_up, w_down, sems_down = refs[:6]
        plain, turned, plain_h, turned_h = refs[6:10]
        small_ref, cot_ref, read_sems = refs[10:13]
        n1_ref, dz_ref, h_ref, act_ref, slope_ref, result_ref, low_ref, do_ref = refs[13:21]
        down_stages, mid_stages = refs[21 : 21 + g], refs[21 + g : 21 + 2 * g]
        shared_low, sems = refs[21 + 2 * g :]
        out_w = Weights(out_p, table, w_out, sems_out, 3 * width, width)
        smalls = [small.at[pl.ds(small_row, SMALL)] for small in small_far]
        reads = Reads(smalls, [small_ref.at[i] for i in range(n)], read_sems)
        up_w = Weights(up_p, table, w_up, sems_up, 0, tile)
        down_w = Weights(up_p, table, w_down, sems_down, hidden, tile)
        block = rows // N_MP
        cots = Reads(
            cot_far,
            [cot_ref.at[pl.ds(i * block, block)] for i in range(N_MP)],
            read_sems.at[pl.ds(n, N_MP)],
        )
        writes = Writes(sems)

        attention = dot(mixed_ref[...], out_w.get(0), NT)
        for i in range(n):
            reads.get(i)
        small = jnp.sum(small_ref[...].astype(F32), axis=0)
        row_vals = sum(small[:, i * width : (i + 1) * width] for i in range(2 * N_MP))
        row = lambda i: row_vals[i : i + 1, :]
        up_b = small[6:7, :hidden]
        n1, r1 = norm(x_ref[...].astype(F32) + attention + row(0))
        n1_ref[...] = n1
        h_ref[...] = (n1 * row(1) + row(2)).astype(BF16)
        feed = jnp.zeros((rows, width), F32)
        u = dot(h_ref[...], up_w.get(0), NN)
        for t, at in enumerate(spans):
            down = down_w.get(t)
            later = dot(h_ref[...], up_w.get(t + 1), NN) if t + 1 < count else None
            act, slope = gelu_parts(u + up_b[:, at])
            act_ref[:, at] = act.astype(BF16)
            slope_ref[:, at] = slope.astype(BF16)
            feed = feed + dot(act_ref[:, at], down, NT)
            u = later
        h = n1_ref[...] * row(1) + row(2)
        n2, r2 = norm(h + feed + row(3))
        result_ref[...] = (n2 * row(4) + row(5)).astype(BF16)
        writes.start(result_ref, result_out)
        for i in range(N_MP):
            cots.get(i)
        gy = cot_ref[...].astype(F32)
        dz = norm_back(gy * row(4), n2, r2)
        dz_ref[...] = dz
        low_ref[...] = dz.astype(BF16)
        sums = [total(dz), total(gy * n2), total(gy)]

        turn(low_ref[...], table, plain, turned)
        turn(h_ref[...], table, plain_h, turned_h)
        shared_ref[...] = jnp.zeros_like(shared_ref)
        dh = dz_ref[...]
        for t, at in enumerate(spans):
            dact = dot(low_ref[...], down_w.get(t), NN)
            store_grad(turned, act_ref[:, at], down_stages, at.start, writes, down_outs)
            du = (dact * slope_ref[:, at].astype(F32)).astype(BF16)
            shared_ref[0:1, at] = total(du.astype(F32))
            dh = dh + dot(du, up_w.get(t), NT)
            store_grad(turned_h, du, mid_stages, at.start, writes, mid_outs)
        n1 = n1_ref[...]
        da = norm_back(dh * row(1), n1, r1)
        dz_ref[...] = da
        writes.start(dz_ref, da_out)
        low_ref[...] = da.astype(BF16)
        do_ref[...] = dot(low_ref[...], out_w.get(0), NN).astype(BF16)
        writes.start(do_ref, do_out)
        sums = [total(da), total(dh * n1), total(dh)] + sums
        for j in range(hidden // width):
            for i, value in enumerate(sums):
                shared_ref[1 + i : 2 + i, j * width : (j + 1) * width] = value
        if g > 1:
            shared_low[...] = shared_ref[...].astype(BF16)
            for out in mid_outs:
                for r in range(out.shape[0]):
                    writes.start(shared_low, out.at[r, pl.ds(block_rows(feed_pieces), SHARED)])
        turn(low_ref[...], table, plain, turned)
        store_grad(turned, mixed_ref[...], mid_stages, hidden, writes, mid_outs)
        writes.finish()

    near = [((rows, width), F32)] * 2 + [((rows, width), BF16)]
    near += [((rows, hidden), BF16)] * 2 + [((rows, width), BF16)] * 3
    return call(
        body,
        "feed",
        33,
        [
            like((SHARED, cols), F32),
            like((rows, width), BF16),
            like((rows, width), F32),
            like((rows, width), BF16),
        ]
        + down_grads
        + mid_grads,
        [x, mixed],
        table,
        list(cot_parts) + list(smalls) + list(out_pieces) + list(feed_pieces),
        weight_scratch(out_pieces, width)
        + weight_scratch(feed_pieces, hidden) * 2
        + turn_scratch(feed_pieces, rows) * 2
        + [
            pltpu.VMEM((n, SMALL, 2 * hidden), BF16),
            pltpu.VMEM((rows, width), BF16),
            pltpu.SemaphoreType.DMA((n + N_MP,)),
        ]
        + [pltpu.VMEM(*spec) for spec in near]
        + stage_scratch(feed_pieces, hidden)
        + stage_scratch(feed_pieces, cols)
        + [
            pltpu.VMEM((SHARED, cols), BF16),
            pltpu.SemaphoreType.DMA((3 + g * (2 * count + 1) + n_up,)),
        ],
        far=3 + 2 * g,
    )


def project_back(da, parts, table, pieces):
    rows, width = da.shape
    n = len(pieces)
    flat = [value for part in parts for value in part]

    def body(table, da_ref, *refs):
        part_refs, refs = refs[: len(flat)], refs[len(flat) :]
        pieces, (out_ref, dqkv_ref, held, sems) = refs[:n], refs[n:]
        weights = Weights(pieces, table, held, sems, 0, width)
        pair = 0
        for i in range(0, len(flat), 3):
            q_ref, own_ref, back_ref = part_refs[i : i + 3]
            cols = q_ref.shape[1]
            dqkv_ref[:, pair * LANES : pair * LANES + cols] = q_ref[...]
            for p in range(cols // LANES):
                for which in range(2):
                    at = slice((2 * p + which) * LANES, (2 * p + which + 1) * LANES)
                    to = (which + 1) * width + (pair + p) * LANES
                    value = own_ref[:, at] + back_ref[:, at].astype(F32)
                    dqkv_ref[:, to : to + LANES] = value.astype(BF16)
            pair += cols // LANES
        value = da_ref[...]
        for i in range(3):
            value = value + dot(dqkv_ref[:, i * width : (i + 1) * width], weights.get(i), NT)
        out_ref[...] = value.astype(BF16)

    return call(
        body,
        "project_back",
        9,
        [like((rows, width), BF16), like((rows, 3 * width), BF16)],
        [da] + flat,
        table,
        pieces,
        weight_scratch(pieces, 3 * width, 3),
    )


def project_grads(x, dqkv, table, pieces):
    rows, width = x.shape
    grads = grad_shapes(pieces, 3 * width, SHARED)
    g = len(grads)

    def body(table, x_ref, dqkv_ref, *refs):
        shared_ref, grad_outs, refs = refs[0], refs[1 : 1 + g], refs[1 + g :]
        plain, turned = refs[:2]
        stages, shared_low, sems = refs[2 : 2 + g], refs[2 + g], refs[3 + g]
        writes = Writes(sems)
        turn(x_ref[...], table, plain, turned)
        for i in range(3):
            at = i * width
            store_grad(turned, dqkv_ref[:, at : at + width], stages, at, writes, grad_outs)
        shared_ref[...] = jnp.zeros_like(shared_ref)
        shared_ref[0:1, :] = total(dqkv_ref[...].astype(F32))
        if g > 1:
            shared_low[...] = shared_ref[...].astype(BF16)
            for out in grad_outs:
                for r in range(out.shape[0]):
                    writes.start(shared_low, out.at[r, pl.ds(block_rows(pieces), SHARED)])
        writes.finish()

    return call(
        body,
        "project_grads",
        7,
        [like((SHARED, 3 * width), F32)] + grads,
        [x, dqkv],
        table,
        [],
        turn_scratch(pieces, rows)
        + stage_scratch(pieces, 3 * width)
        + [
            pltpu.VMEM((SHARED, 3 * width), BF16),
            pltpu.SemaphoreType.DMA((3 * g + len(blocks_of(pieces)),)),
        ],
        far=g,
    )


def at_column(values, rows, width, column):
    return lax.dynamic_update_slice(jnp.zeros((rows, width), values.dtype), values, (0, column))


def small_block(row_params, expand_bias, mine, depth):
    high = lax.reduce_precision(row_params, 8, 7)
    column = (mine * N_MP + depth) * row_params.shape[1]
    high_low = [
        at_column(part.astype(BF16), 6, WIDTH, column) for part in (high, row_params - high)
    ]
    bias = at_column(expand_bias, 2, 2 * WIDTH, mine * expand_bias.shape[1])
    return jnp.concatenate([jnp.concatenate(high_low, axis=1), bias])


def key_bias(length_long, length_short, block, core, depth):
    lengths = jnp.concatenate([length_long, length_short])
    other = core_swap(lengths)
    longs = jnp.where(core == 0, jnp.stack([lengths[0], other[0]]), jnp.stack([other[0], lengths[0]]))
    length = jnp.concatenate([longs, lengths[1:]])[depth]
    is_long = depth < 2
    place = lax.broadcasted_iota(jnp.int32, (1, 2 * N_MP * block), 1)
    row = place % (N_MP * block)
    is_own = place < N_MP * block
    source = (row // block) ^ depth
    whose = jnp.where(is_own, core, 1 - core)
    frame = row % block + jnp.where(is_long, (2 * source + whose) * block, source * block)
    counted = (frame < length) & (is_own | is_long)
    return jnp.where(counted, 0.0, NEG_FILL).astype(F32)


def on_device(
    frames_long,
    frames_short,
    length_long,
    length_short,
    input_proj,
    output_proj,
    expand_weight,
    shrink_weight,
    head_bias,
    expand_bias,
    row_params,
    cotangent_long,
    cotangent_short,
):
    mine = lax.axis_index("dp")
    depth = lax.axis_index("mp")
    n_dp = lax.axis_size("dp")
    fast = n_dp == 8
    core = mine % 2
    block = frames_short.shape[1]
    shard, group = input_proj.shape[1:]
    units = expand_weight.shape[1]
    width = group * N_MP
    hidden = units * N_MP
    table = block_table(mine, n_dp)

    joined = jnp.concatenate(
        [input_proj[0], input_proj[1], input_proj[2], output_proj.T], axis=1
    )
    heads = at_column(head_bias[:, 0], SMALL, WIDTH, mine * head_bias.shape[2])
    attn_parts = mp_gather(jnp.concatenate([joined, heads]))
    x_blocks = clip_blocks(frames_long[0], frames_short, core)
    cot_blocks = clip_blocks(cotangent_long[0], cotangent_short, core)
    bias = key_bias(length_long, length_short, block, core, depth)
    feed_shard = jnp.concatenate(
        [
            jnp.concatenate([expand_weight, shrink_weight.T], axis=1),
            small_block(row_params, expand_bias, mine, depth),
        ]
    )
    *attn_parts, feed_shard, bias, x_blocks, cot_blocks = tie(
        *attn_parts, feed_shard, bias, x_blocks, cot_blocks
    )
    order = [p[:shard, i * group : (i + 1) * group] for i in range(4) for p in attn_parts]
    attn_slab = jnp.concatenate([to_slab(order), to_slab([p[shard:] for p in attn_parts])])
    feed_parts = mp_gather(feed_shard)
    feed_order = [p[:, i * units : (i + 1) * units] for i in range(2) for p in feed_parts]
    if fast:
        attn_p = [attn_slab] + [dp_swap(attn_slab, to) for to in (early, late, across)]
        x_pieces = clip_pieces(x_blocks, depth)
        attn_p += [core_swap(piece) for piece in attn_p]
        both = tie(*attn_p, *x_pieces, *feed_order)
        attn_p, x_pieces, feed_order = both[:8], both[8:12], both[12:]
        feed_slab = to_slab(feed_order)
        feed_one = dp_swap(feed_slab, early)
        feed_two = dp_swap(feed_slab, late)
        x_parts = [x_pieces[0]] + [mp_swap(x_pieces[i], i) for i in range(1, N_MP)]
        *x_parts, cot_blocks, own_slab = tie(*x_parts, cot_blocks, feed_slab)
        heads = sum(p[shard:].astype(F32) for p in attn_p)
    else:
        x_parts = to_clips(x_blocks, depth)
        gather = lambda slab: lax.all_gather(slab, "dp", axis=0)
        whole = gather(attn_slab)
        heads = jnp.sum(whole[:, shard:].astype(F32), axis=0)
        attn_p = [whole[:, :shard].reshape(width, 4 * width)]
        whole = gather(to_slab(feed_order))
        small = jnp.sum(whole[:, shard:].astype(F32), axis=0)
        feed_p = [whole[:, :shard].reshape(width, 2 * hidden)]
    cot_parts = to_clips(cot_blocks, depth)
    heads = jnp.concatenate(
        [heads[:2, i * width : i * width + group] for i in range(N_MP)], axis=1
    )
    head_row = jnp.concatenate([heads[:1], jnp.zeros_like(heads[:1]), heads[1:]], axis=1)

    x, qkv, kv = project(x_parts, head_row, table, attn_p)
    if fast:
        kv, feed_one, feed_two, cot_parts[3], own_slab = tie(
            kv, feed_one, feed_two, cot_parts[3], core_swap(own_slab)
        )
    kv_other = core_swap(kv)
    if fast:
        feed_three = dp_swap(feed_one, late)
        feed_p = [feed_slab, feed_one, feed_two]
        backs = [own_slab] + [core_swap(piece) for piece in feed_p[1:]]
    mixed, lse = attend(qkv, kv_other, bias)
    if fast:
        mixed, feed_three, *both = tie(mixed, feed_three, *backs, *cot_parts)
        backs, cot_parts = both[:3], both[3:]
        feed_p = feed_p + [feed_three] + backs + [core_swap(feed_three)]
        smalls, small_row = feed_p, shard
    else:
        smalls, small_row = [small.astype(BF16)], 0
    outs = feed(x, mixed, cot_parts, smalls, small_row, table, attn_p, feed_p)
    mid_shared, result, da, do, *grads = outs
    g_down, g_mid = grads[: len(grads) // 2], grads[len(grads) // 2 :]

    def by_group_of(value, sizes):
        starts = [N_MP * sum(sizes[:i]) for i in range(len(sizes))]
        return [
            jnp.concatenate(
                [value[:, a + j * n : a + (j + 1) * n] for a, n in zip(starts, sizes)], axis=1
            )
            for j in range(N_MP)
        ]

    def last_sum(terms):
        return sum(term[0].astype(F32) for term in terms)

    result_parts = from_clips(result)
    if fast:
        b_down, b_mid = core_swap(g_down[1]), core_swap(g_mid[1])
    pairs = width // LANES
    first = pairs // 2
    dq_a, own_a, other_a = attend_back(qkv, kv_other, bias, mixed, lse, do, 0, first)
    if fast:
        other_a, b_down, b_mid, result_parts[3] = tie(other_a, b_down, b_mid, result_parts[3])
        t_down = [g_down[0], b_down]
        a_down = goes_on(t_down)
        do, a_down = tie(do, a_down)
        b_down = dp_swap(a_down, late)
    back_a = core_swap(other_a)
    dq_b, own_b, other_b = attend_back(
        qkv, kv_other, bias, mixed, lse, do, first, pairs - first
    )
    if fast:
        other_b, back_a, b_down, *result_parts = tie(other_b, back_a, b_down, *result_parts)
    back_b = core_swap(other_b)
    if fast:
        t_down, t_mid = stays(t_down, b_down), [g_mid[0], b_mid]
        back_b, a_down, a_mid = tie(back_b, goes_on(t_down), goes_on(t_mid))
        b_down = dp_swap(a_down, early)
        b_mid = dp_swap(a_mid, late)
    parts = [(dq_a, own_a, back_a), (dq_b, own_b, back_b)]
    frames_grad, dqkv = project_back(da, parts, table, attn_p)
    if fast:
        frames_grad, dqkv, b_down = tie(frames_grad, dqkv, b_down)
        s_down = by_group_of(last_sum(stays(t_down, b_down)), [units])
        frames_grad, dqkv, *s_down = tie(frames_grad, dqkv, *s_down)
        z_down = mp_away(s_down)
        dqkv, frames_grad, b_mid, z_down[1], z_down[2] = tie(
            dqkv, frames_grad, b_mid, z_down[1], z_down[2]
        )
        t_mid = stays(t_mid, b_mid)
        dqkv, frames_grad, a_mid = tie(dqkv, frames_grad, goes_on(t_mid))
        b_mid = dp_swap(a_mid, early)
    grad_parts = from_clips(frames_grad)
    attn_shared, *g_attn = project_grads(x, dqkv, table, attn_p)
    if fast:
        both = tie(*g_attn, b_mid, *grad_parts, *z_down)
        g_attn, b_mid, grad_parts, z_down = both[:2], both[2], both[3:7], both[7:]
        t_attn = [g_attn[0], core_swap(g_attn[1])]
        a_attn, *t_mid = tie(goes_on(t_attn), *stays(t_mid, b_mid))
        b_attn = dp_swap(a_attn, late)
        s_mid = by_group_of(last_sum(t_mid), [units, group])
        z_mid = mp_away(s_mid)
        b_attn, z_mid[2] = tie(b_attn, z_mid[2])
        t_attn = stays(t_attn, b_attn)
        b_attn = dp_swap(goes_on(t_attn), early)
        b_attn, *both = tie(b_attn, *z_mid, *result_parts)
        z_mid, result_parts = both[: N_MP - 1], both[N_MP - 1 :]
        s_attn = last_sum(stays(t_attn, b_attn))
    else:
        scatter = lambda g: lax.psum_scatter(g[0][0], "dp", scatter_dimension=0, tiled=True)
        s_down = by_group_of(scatter(g_down), [units])
        z_down = mp_away(s_down)
        s_mid = jnp.concatenate([scatter(g_mid), lax.psum(mid_shared, "dp")])
        s_mid = by_group_of(s_mid, [units, group])
        z_mid = mp_away(s_mid)
        s_attn = jnp.concatenate([scatter(g_attn), lax.psum(attn_shared, "dp")])
    s_attn = by_group_of(s_attn, [group] * 3)
    grad_long, grad_short = frames_of(grad_parts, core, depth)
    result_long, result_short = frames_of(result_parts, core, depth)
    attn_share = mp_total(s_attn[0], mp_away(s_attn))
    down_share = mp_total(s_down[0], z_down).T
    mid_share = mp_total(s_mid[0], z_mid)
    up_share = mid_share[:shard, :units]
    output_share = mid_share[:shard, units:].T
    input_share = jnp.stack(
        [attn_share[:shard, i * group : (i + 1) * group] for i in range(3)]
    )
    up_cols, head_cols, row_cols = units // n_dp, group // n_dp, width // (n_dp * N_MP)
    rank = mine * N_MP + depth
    up_b_share = lax.dynamic_slice(mid_share, (shard, mine * up_cols), (1, up_cols))
    row_share = lax.dynamic_slice(mid_share, (shard + 1, rank * row_cols), (6, row_cols))
    head_share = jnp.stack(
        [
            lax.dynamic_slice(attn_share, (shard, at + mine * head_cols), (1, head_cols))
            for at in (0, 2 * group)
        ]
    )
    return (
        result_long,
        result_short,
        grad_long.astype(F32),
        grad_short.astype(F32),
        input_share,
        output_share,
        up_share,
        down_share,
        head_share,
        up_b_share,
        row_share,
    )


def solution(mesh):
    return jax.shard_map(
        on_device,
        mesh=mesh,
        in_specs=(
            P("dp", "mp", None),
            P("dp", "mp", None),
            P("dp"),
            P("dp"),
            P(None, "dp", "mp"),
            P("mp", "dp"),
            P("dp", "mp"),
            P("mp", "dp"),
            P(None, "mp", "dp"),
            P("mp", "dp"),
            P(None, ("dp", "mp")),
            P("dp", "mp", None),
            P("dp", "mp", None),
        ),
        out_specs=(
            P("dp", "mp", None),
            P("dp", "mp", None),
            P("dp", "mp", None),
            P("dp", "mp", None),
            P(None, "dp", "mp"),
            P("mp", "dp"),
            P("dp", "mp"),
            P("mp", "dp"),
            P(None, "mp", "dp"),
            P("mp", "dp"),
            P(None, ("dp", "mp")),
        ),
        check_vma=False,
    )
```

```python
import functools

import jax
import jax.numpy as jnp
from jax import lax
from jax.experimental import pallas as pl
from jax.experimental.pallas import tpu as pltpu
from jax.sharding import PartitionSpec as P

HEAD = 64
EPS = 1e-05
NEG_FILL = -1e30
SCALE = HEAD ** (-0.5)
N_MP = 4
PARTS = 1
CS = 0.3
WIDTH = 768
SMALL = 8
SHARED = 8
LANES = 128
Q_TILE = 256
F32 = jnp.float32
BF16 = jnp.bfloat16
NT = (((1,), (1,)), ((), ()))
NN = (((1,), (0,)), ((), ()))
TN = (((0,), (0,)), ((), ()))


def dot(left, right, dims):
    return lax.dot_general(left, right, dims, preferred_element_type=F32)


def mp_swap(value, step):
    return lax.ppermute(value, "mp", [(i, i ^ step) for i in range(N_MP)])


def dp_swap(value, target):
    size = lax.axis_size("dp")
    return lax.ppermute(value, "dp", [(i, target(i)) for i in range(size)])


def core_swap(value):
    return dp_swap(value, lambda i: i ^ 1)


def clip_blocks(long_rows, short_rows, core):
    block = short_rows.shape[1]
    keep = lax.dynamic_slice_in_dim(long_rows, core * block, block, 0)
    away = lax.dynamic_slice_in_dim(long_rows, (1 - core) * block, block, 0)
    back = core_swap(away)
    first = jnp.where(core == 0, keep, back)
    second = jnp.where(core == 0, back, keep)
    return jnp.stack([first, second, short_rows[0], short_rows[1]])


def clip_pieces(blocks, depth):
    return [
        lax.dynamic_index_in_dim(blocks, depth ^ step, 0, keepdims=False) for step in range(N_MP)
    ]


def to_clips(blocks, depth):
    pieces = clip_pieces(blocks, depth)
    return pieces[:1] + [mp_swap(pieces[step], step) for step in range(1, N_MP)]


def from_clips(rows):
    block = rows.shape[0] // N_MP
    parts = []
    for step in range(N_MP):
        piece = rows[step * block : (step + 1) * block]
        parts.append(piece if step == 0 else mp_swap(piece, step))
    return parts


def frames_of(parts, core, depth):
    blocks = jnp.stack(parts)
    first, second, short_a, short_b = (
        lax.dynamic_index_in_dim(blocks, depth ^ i, 0, keepdims=False) for i in range(N_MP)
    )
    keep = jnp.where(core == 0, first, second)
    away = jnp.where(core == 0, second, first)
    back = core_swap(away)
    low = jnp.where(core == 0, keep, back)
    high = jnp.where(core == 0, back, keep)
    return jnp.concatenate([low, high], axis=0)[None], jnp.stack([short_a, short_b])


def flip(index, late):
    return index ^ ((4 if late else 2) if index % 2 == 0 else (2 if late else 4))


def block_table(mine, size):
    if size != 8:
        return jnp.zeros((1,), jnp.int32)
    early = jnp.where(mine % 2 == 0, 2, 4)
    late = 6 - early
    relative = [0, early, late, 6, 1, 1 ^ late, 1 ^ early, 7]
    return jnp.stack([mine ^ r for r in relative]).astype(jnp.int32)


def early(i):
    return flip(i, False)


def late(i):
    return flip(i, True)


def across(i):
    return i ^ 6


def tie(*values):
    return lax.optimization_barrier(values)


def swap_plane(plane):
    return plane + [core_swap(piece) for piece in plane]


def to_slab(parts):
    return jnp.concatenate(parts, axis=1)


def mp_gather(shard):
    return [shard] + [mp_swap(shard, step) for step in range(1, N_MP)]


def goes_on(terms):
    half = terms[-1].shape[0] // 2
    return sum(term[half : 2 * half].astype(F32) for term in terms).astype(BF16)


def mp_away(parts):
    return [mp_swap(parts[step].astype(BF16), step) for step in range(1, N_MP)]


def mp_total(own, backs):
    for back in backs:
        own = own + back.astype(F32)
    return own


def blocks_of(pieces):
    step = pieces[0].shape[0]
    return [(p, k * step) for p in pieces for k in range(p.shape[0] // step)]


def block_rows(pieces):
    return WIDTH // len(blocks_of(pieces))


class Weights:
    def __init__(self, pieces, table, held, sems, lo, tile):
        self.held, self.tile = held, tile
        cols, parts = held.shape[2], sems.shape[0]
        self.span, self.copies = cols // parts, []
        for t in range(parts):
            row = []
            for k, (piece, first) in enumerate(blocks_of(pieces)):
                copy = pltpu.make_async_copy(
                    piece.at[pl.ds(first, held.shape[1]), pl.ds(lo + t * self.span, self.span)],
                    held.at[table[k], :, pl.ds(t * self.span, self.span)],
                    sems.at[t, k],
                )
                copy.start()
                row.append(copy)
            self.copies.append(row)
        self.waited = 0

    def get(self, t):
        at = t * self.tile
        while self.waited * self.span < at + self.tile:
            for copy in self.copies[self.waited]:
                copy.wait()
            self.waited += 1
        count, rows, _ = self.held.shape
        return self.held[:, :, at : at + self.tile].reshape(count * rows, self.tile)


def weight_scratch(pieces, cols, parts=1):
    return [
        pltpu.VMEM((len(blocks_of(pieces)), block_rows(pieces), cols), BF16),
        pltpu.SemaphoreType.DMA((parts, len(blocks_of(pieces)))),
    ]


def grad_shapes(pieces, cols, extra=0):
    count, rows = len(blocks_of(pieces)), block_rows(pieces)
    if count == 1:
        return [jax.ShapeDtypeStruct((1, rows, cols), F32)]
    return [jax.ShapeDtypeStruct((count // 2, rows + extra, cols), BF16)] * 2


def turn_scratch(pieces, rows):
    return [pltpu.VMEM((len(blocks_of(pieces)), block_rows(pieces), rows), BF16)] * 2


def turn(value, table, plain, turned):
    plain[...] = value.T.reshape(plain.shape)
    for r in range(plain.shape[0]):
        turned[r] = plain[table[r]]


def stage_scratch(pieces, cols):
    return [
        pltpu.VMEM((g.shape[0], block_rows(pieces), cols), g.dtype)
        for g in grad_shapes(pieces, cols)
    ]


def store_grad(turned, right, stages, at, writes=None, outs=None):
    count, rows, _ = turned.shape
    grad = dot(turned[...].reshape(count * rows, -1), right, NN)
    half, cols = count // len(stages), right.shape[1]
    for r in range(count):
        stage = stages[r // half]
        part = grad[r * rows : (r + 1) * rows].astype(stage.dtype)
        stage[r % half, :rows, at : at + cols] = part
    if writes is not None:
        for stage, out in zip(stages, outs):
            writes.start(
                stage.at[:, :, pl.ds(at, cols)],
                out.at[:, pl.ds(0, rows), pl.ds(at, cols)],
            )


class Writes:
    def __init__(self, sems):
        self.sems, self.copies = sems, []

    def start(self, source, target):
        copy = pltpu.make_async_copy(source, target, self.sems.at[len(self.copies)])
        copy.start()
        self.copies.append(copy)

    def finish(self):
        for copy in self.copies:
            copy.wait()


class Reads:
    def __init__(self, sources, targets, sems):
        self.targets, self.copies = targets, []
        for i, (source, target) in enumerate(zip(sources, targets)):
            copy = pltpu.make_async_copy(source, target, sems.at[i])
            copy.start()
            self.copies.append(copy)

    def get(self, i):
        self.copies[i].wait()
        return self.targets[i]


def read_scratch(arrays):
    return [pltpu.VMEM(a.shape, a.dtype) for a in arrays] + [
        pltpu.SemaphoreType.DMA((len(arrays),))
    ]


def cost(micros):
    return pl.CostEstimate(
        flops=int(micros * 1.1e9 * CS), bytes_accessed=int(micros * 1e5 * CS), transcendentals=0
    )


def call(body, name, micros, outs, arrays, table, pieces, scratch, far=0):
    vmem = pl.BlockSpec(memory_space=pltpu.VMEM)
    away = pl.BlockSpec(memory_space=pl.ANY)
    return pl.pallas_call(
        body,
        out_shape=tuple(outs),
        in_specs=[pl.BlockSpec(memory_space=pltpu.SMEM)]
        + [vmem] * len(arrays)
        + [away] * len(pieces),
        out_specs=(vmem,) * (len(outs) - far) + (away,) * far,
        scratch_shapes=scratch,
        compiler_params=pltpu.CompilerParams(vmem_limit_bytes=60 << 20),
        cost_estimate=cost(micros),
        name=name,
    )(table, *arrays, *pieces)


def like(shape, kind):
    return jax.ShapeDtypeStruct(shape, kind)


def attend_kernel(q_ref, k_ref, v_ref, kp_ref, vp_ref, bias_ref, o_ref, lse_ref):
    rows = q_ref.shape[0]
    keys = jnp.concatenate([k_ref[...], kp_ref[...]], axis=0)
    values = jnp.concatenate([v_ref[...], vp_ref[...]], axis=0)
    bias = bias_ref[...]
    tile = min(rows, Q_TILE)
    low = lax.broadcasted_iota(jnp.int32, (tile, LANES), 1) < HEAD
    for start in range(0, rows, tile):
        q = q_ref[start : start + tile, :]
        outs, logs = [], []
        for half in range(2):
            here = low if half == 0 else ~low
            q_here = jnp.where(here, q, jnp.zeros_like(q))
            scores = dot(q_here, keys, NT) + bias
            top = jnp.max(scores, axis=-1, keepdims=True)
            raised = jnp.exp(scores - top)
            total = jnp.sum(raised, axis=-1, keepdims=True)
            mixed = dot(raised.astype(BF16), values, NN)
            outs.append(mixed / total)
            logs.append(top + jnp.log(total))
        o_ref[start : start + tile, :] = jnp.where(low, outs[0], outs[1]).astype(BF16)
        lse_ref[start : start + tile, :] = jnp.where(low, logs[0], logs[1])


def attend(qkv, kv_other, bias):
    rows, width = qkv.shape[0], qkv.shape[1] // 3
    pairs = width // LANES
    spec = lambda base: pl.BlockSpec((rows, LANES), lambda p: (0, base + p))
    return pl.pallas_call(
        attend_kernel,
        out_shape=(
            jax.ShapeDtypeStruct((rows, width), BF16),
            jax.ShapeDtypeStruct((rows, width), F32),
        ),
        grid=(pairs,),
        in_specs=[
            spec(0),
            spec(pairs),
            spec(2 * pairs),
            spec(0),
            spec(pairs),
            pl.BlockSpec((1, 2 * rows), lambda p: (0, 0)),
        ],
        out_specs=(spec(0), spec(0)),
        compiler_params=pltpu.CompilerParams(vmem_limit_bytes=56 << 20),
        cost_estimate=cost(15),
        name="attend",
    )(qkv, qkv, qkv, kv_other, kv_other, bias)


def attend_back_kernel(
    q_ref, k_ref, v_ref, kp_ref, vp_ref, bias_ref, o_ref, lse_ref, do_ref,
    dq_ref, own_ref, other_ref,
):
    rows = q_ref.shape[0]
    keys = jnp.concatenate([k_ref[...], kp_ref[...]], axis=0)
    values = jnp.concatenate([v_ref[...], vp_ref[...]], axis=0)
    bias = bias_ref[...]
    tile = min(rows, Q_TILE)
    low = lax.broadcasted_iota(jnp.int32, (tile, LANES), 1) < HEAD
    dk = jnp.zeros((LANES, 2 * rows), F32)
    dv = jnp.zeros((LANES, 2 * rows), F32)
    for start in range(0, rows, tile):
        at = slice(start, start + tile)
        q, do = q_ref[at, :], do_ref[at, :]
        product = o_ref[at, :].astype(F32) * do.astype(F32)
        lse = lse_ref[at, :]
        outs = []
        for half in range(2):
            here = low if half == 0 else ~low
            q_here = jnp.where(here, q, jnp.zeros_like(q))
            do_here = jnp.where(here, do, jnp.zeros_like(do))
            inner = jnp.sum(jnp.where(here, product, 0.0), axis=-1, keepdims=True)
            log = lse[:, half * HEAD : half * HEAD + 1]
            soft = jnp.exp(dot(q_here, keys, NT) + bias - log)
            grad = (soft * (dot(do_here, values, NT) - inner)).astype(BF16)
            outs.append(dot(grad, keys, NN))
            dk = dk + dot(q_here, grad, TN)
            dv = dv + dot(do_here, soft.astype(BF16), TN)
        dq_ref[at, :] = (jnp.where(low, outs[0], outs[1]) * SCALE).astype(BF16)
    for i, value in enumerate((dk.T, dv.T)):
        at = slice(i * LANES, (i + 1) * LANES)
        own_ref[:, at] = value[:rows]
        other_ref[:, at] = value[rows:].astype(BF16)


def attend_back(qkv, kv_other, bias, out, lse, grad_out, first, count):
    rows, width = out.shape
    pairs = width // LANES
    spec = lambda base: pl.BlockSpec((rows, LANES), lambda p: (0, base + first + p))
    result = lambda cols: pl.BlockSpec((rows, cols), lambda p: (0, p))
    return pl.pallas_call(
        attend_back_kernel,
        out_shape=(
            jax.ShapeDtypeStruct((rows, count * LANES), BF16),
            jax.ShapeDtypeStruct((rows, 2 * count * LANES), F32),
            jax.ShapeDtypeStruct((rows, 2 * count * LANES), BF16),
        ),
        grid=(count,),
        in_specs=[
            spec(0),
            spec(pairs),
            spec(2 * pairs),
            spec(0),
            spec(pairs),
            pl.BlockSpec((1, 2 * rows), lambda p: (0, 0)),
            spec(0),
            spec(0),
            spec(0),
        ],
        out_specs=(result(LANES), result(2 * LANES), result(2 * LANES)),
        compiler_params=pltpu.CompilerParams(vmem_limit_bytes=56 << 20),
        cost_estimate=cost(3 * count),
        name="attend_back",
    )(qkv, qkv, qkv, kv_other, kv_other, bias, out, lse, grad_out)


def gelu_parts(v):
    cdf = 0.5 * (1.0 + lax.erf(v * (2.0 ** -0.5)))
    pdf = jnp.exp(-0.5 * v * v) * 0.3989422804014327
    return v * cdf, cdf + v * pdf


def norm(values):
    center = values - jnp.mean(values, axis=-1, keepdims=True)
    inv_dev = lax.rsqrt(jnp.mean(center * center, axis=-1, keepdims=True) + EPS)
    return center * inv_dev, inv_dev


def norm_back(scaled, normed, inv_dev):
    return inv_dev * (
        scaled
        - jnp.mean(scaled, axis=-1, keepdims=True)
        - normed * jnp.mean(scaled * normed, axis=-1, keepdims=True)
    )


def total(value):
    return jnp.sum(value, axis=0, keepdims=True)


def join(parts, starts, size, micros):
    rows, cols = parts[0].shape[0], len(starts) * len(parts) * size

    def body(*refs):
        parts, out = refs[:-1], refs[-1]
        at = 0
        for start in starts:
            for part in parts:
                out[:, at : at + size] = part[:, start : start + size]
                at += size

    vmem = pl.BlockSpec(memory_space=pltpu.VMEM)
    return pl.pallas_call(
        body,
        out_shape=like((rows, cols), parts[0].dtype),
        in_specs=[vmem] * len(parts),
        out_specs=vmem,
        cost_estimate=cost(micros),
        name="join",
    )(*parts)


def project(x_parts, head_row, table, pieces):
    block, width = x_parts[0].shape
    rows = block * len(x_parts)
    n = len(pieces)

    def body(table, *refs):
        part_refs, bias_ref, refs = refs[:N_MP], refs[N_MP], refs[N_MP + 1 :]
        pieces, (x_ref, qkv_ref, kv_ref, held, sems) = refs[:n], refs[n:]
        weights = Weights(pieces, table, held, sems, 0, width)
        for i, part in enumerate(part_refs):
            x_ref[i * block : (i + 1) * block, :] = part[...]
        x = x_ref[...]
        for i in range(3):
            value = dot(x, weights.get(i), NN) + bias_ref[:, i * width : (i + 1) * width]
            value = value.astype(BF16)
            if i == 0:
                value = (value.astype(F32) * SCALE).astype(BF16)
            else:
                kv_ref[:, (i - 1) * width : i * width] = value
            qkv_ref[:, i * width : (i + 1) * width] = value

    return call(
        body,
        "project",
        7,
        [
            like((rows, width), BF16),
            like((rows, 3 * width), BF16),
            like((rows, 2 * width), BF16),
        ],
        list(x_parts) + [head_row],
        table,
        pieces,
        weight_scratch(pieces, 3 * width, 3),
    )


def feed(x, mixed, cot_parts, smalls, small_row, table, out_pieces, feed_pieces):
    rows, width = x.shape
    hidden = feed_pieces[0].shape[1] // 2
    count = 6
    tile = hidden // count
    spans = [slice(t * tile, (t + 1) * tile) for t in range(count)]
    cols = hidden + width
    n_out, n_up, n = len(out_pieces), len(feed_pieces), len(smalls)
    down_grads = grad_shapes(feed_pieces, hidden)
    mid_grads = grad_shapes(feed_pieces, cols, SHARED)
    g = len(mid_grads)

    def body(table, x_ref, mixed_ref, *refs):
        cot_far, small_far, refs = refs[:N_MP], refs[N_MP : N_MP + n], refs[N_MP + n :]
        out_p, up_p = refs[:n_out], refs[n_out : n_out + n_up]
        refs = refs[n_out + n_up :]
        shared_ref, result_out, da_out, do_out = refs[:4]
        down_outs, mid_outs, refs = refs[4 : 4 + g], refs[4 + g : 4 + 2 * g], refs[4 + 2 * g :]
        w_out, sems_out, w_up, sems_up, w_down, sems_down = refs[:6]
        plain, turned, plain_h, turned_h = refs[6:10]
        small_ref, cot_ref, read_sems = refs[10:13]
        n1_ref, dz_ref, h_ref, act_ref, slope_ref, result_ref, low_ref, do_ref = refs[13:21]
        down_stages, mid_stages = refs[21 : 21 + g], refs[21 + g : 21 + 2 * g]
        shared_low, sems = refs[21 + 2 * g :]
        out_w = Weights(out_p, table, w_out, sems_out, 3 * width, width)
        smalls = [small.at[pl.ds(small_row, SMALL)] for small in small_far]
        reads = Reads(smalls, [small_ref.at[i] for i in range(n)], read_sems)
        up_w = Weights(up_p, table, w_up, sems_up, 0, tile)
        down_w = Weights(up_p, table, w_down, sems_down, hidden, tile)
        block = rows // N_MP
        cots = Reads(
            cot_far,
            [cot_ref.at[pl.ds(i * block, block)] for i in range(N_MP)],
            read_sems.at[pl.ds(n, N_MP)],
        )
        writes = Writes(sems)

        attention = dot(mixed_ref[...], out_w.get(0), NT)
        for i in range(n):
            reads.get(i)
        small = jnp.sum(small_ref[...].astype(F32), axis=0)
        row_vals = sum(small[:, i * width : (i + 1) * width] for i in range(2 * N_MP))
        row = lambda i: row_vals[i : i + 1, :]
        up_b = small[6:7, :hidden]
        n1, r1 = norm(x_ref[...].astype(F32) + attention + row(0))
        n1_ref[...] = n1
        h_ref[...] = (n1 * row(1) + row(2)).astype(BF16)
        feed = jnp.zeros((rows, width), F32)
        u = dot(h_ref[...], up_w.get(0), NN)
        for t, at in enumerate(spans):
            down = down_w.get(t)
            later = dot(h_ref[...], up_w.get(t + 1), NN) if t + 1 < count else None
            act, slope = gelu_parts(u + up_b[:, at])
            act_ref[:, at] = act.astype(BF16)
            slope_ref[:, at] = slope.astype(BF16)
            feed = feed + dot(act_ref[:, at], down, NT)
            u = later
        h = n1_ref[...] * row(1) + row(2)
        n2, r2 = norm(h + feed + row(3))
        result_ref[...] = (n2 * row(4) + row(5)).astype(BF16)
        writes.start(result_ref, result_out)
        for i in range(N_MP):
            cots.get(i)
        gy = cot_ref[...].astype(F32)
        dz = norm_back(gy * row(4), n2, r2)
        dz_ref[...] = dz
        low_ref[...] = dz.astype(BF16)
        sums = [total(dz), total(gy * n2), total(gy)]

        turn(low_ref[...], table, plain, turned)
        turn(h_ref[...], table, plain_h, turned_h)
        shared_ref[...] = jnp.zeros_like(shared_ref)
        dh = dz_ref[...]
        for t, at in enumerate(spans):
            dact = dot(low_ref[...], down_w.get(t), NN)
            store_grad(turned, act_ref[:, at], down_stages, at.start, writes, down_outs)
            du = (dact * slope_ref[:, at].astype(F32)).astype(BF16)
            shared_ref[0:1, at] = total(du.astype(F32))
            dh = dh + dot(du, up_w.get(t), NT)
            store_grad(turned_h, du, mid_stages, at.start, writes, mid_outs)
        n1 = n1_ref[...]
        da = norm_back(dh * row(1), n1, r1)
        dz_ref[...] = da
        writes.start(dz_ref, da_out)
        low_ref[...] = da.astype(BF16)
        do_ref[...] = dot(low_ref[...], out_w.get(0), NN).astype(BF16)
        writes.start(do_ref, do_out)
        sums = [total(da), total(dh * n1), total(dh)] + sums
        for j in range(hidden // width):
            for i, value in enumerate(sums):
                shared_ref[1 + i : 2 + i, j * width : (j + 1) * width] = value
        if g > 1:
            shared_low[...] = shared_ref[...].astype(BF16)
            for out in mid_outs:
                for r in range(out.shape[0]):
                    writes.start(shared_low, out.at[r, pl.ds(block_rows(feed_pieces), SHARED)])
        turn(low_ref[...], table, plain, turned)
        store_grad(turned, mixed_ref[...], mid_stages, hidden, writes, mid_outs)
        writes.finish()

    near = [((rows, width), F32)] * 2 + [((rows, width), BF16)]
    near += [((rows, hidden), BF16)] * 2 + [((rows, width), BF16)] * 3
    return call(
        body,
        "feed",
        33,
        [
            like((SHARED, cols), F32),
            like((rows, width), BF16),
            like((rows, width), F32),
            like((rows, width), BF16),
        ]
        + down_grads
        + mid_grads,
        [x, mixed],
        table,
        list(cot_parts) + list(smalls) + list(out_pieces) + list(feed_pieces),
        weight_scratch(out_pieces, width)
        + weight_scratch(feed_pieces, hidden) * 2
        + turn_scratch(feed_pieces, rows) * 2
        + [
            pltpu.VMEM((n, SMALL, 2 * hidden), BF16),
            pltpu.VMEM((rows, width), BF16),
            pltpu.SemaphoreType.DMA((n + N_MP,)),
        ]
        + [pltpu.VMEM(*spec) for spec in near]
        + stage_scratch(feed_pieces, hidden)
        + stage_scratch(feed_pieces, cols)
        + [
            pltpu.VMEM((SHARED, cols), BF16),
            pltpu.SemaphoreType.DMA((3 + g * (2 * count + 1) + n_up,)),
        ],
        far=3 + 2 * g,
    )


def project_back(da, parts, table, pieces):
    rows, width = da.shape
    n = len(pieces)
    flat = [value for part in parts for value in part]

    def body(table, da_ref, *refs):
        part_refs, refs = refs[: len(flat)], refs[len(flat) :]
        pieces, (out_ref, dqkv_ref, held, sems) = refs[:n], refs[n:]
        weights = Weights(pieces, table, held, sems, 0, width)
        pair = 0
        for i in range(0, len(flat), 3):
            q_ref, own_ref, back_ref = part_refs[i : i + 3]
            cols = q_ref.shape[1]
            dqkv_ref[:, pair * LANES : pair * LANES + cols] = q_ref[...]
            for p in range(cols // LANES):
                for which in range(2):
                    at = slice((2 * p + which) * LANES, (2 * p + which + 1) * LANES)
                    to = (which + 1) * width + (pair + p) * LANES
                    value = own_ref[:, at] + back_ref[:, at].astype(F32)
                    dqkv_ref[:, to : to + LANES] = value.astype(BF16)
            pair += cols // LANES
        value = da_ref[...]
        for i in range(3):
            value = value + dot(dqkv_ref[:, i * width : (i + 1) * width], weights.get(i), NT)
        out_ref[...] = value.astype(BF16)

    return call(
        body,
        "project_back",
        9,
        [like((rows, width), BF16), like((rows, 3 * width), BF16)],
        [da] + flat,
        table,
        pieces,
        weight_scratch(pieces, 3 * width, 3),
    )


def project_grads(x, dqkv, table, pieces):
    rows, width = x.shape
    grads = grad_shapes(pieces, 3 * width, SHARED)
    g = len(grads)

    def body(table, x_ref, dqkv_ref, *refs):
        shared_ref, grad_outs, refs = refs[0], refs[1 : 1 + g], refs[1 + g :]
        plain, turned = refs[:2]
        stages, shared_low, sems = refs[2 : 2 + g], refs[2 + g], refs[3 + g]
        writes = Writes(sems)
        turn(x_ref[...], table, plain, turned)
        for i in range(3):
            at = i * width
            store_grad(turned, dqkv_ref[:, at : at + width], stages, at, writes, grad_outs)
        shared_ref[...] = jnp.zeros_like(shared_ref)
        shared_ref[0:1, :] = total(dqkv_ref[...].astype(F32))
        if g > 1:
            shared_low[...] = shared_ref[...].astype(BF16)
            for out in grad_outs:
                for r in range(out.shape[0]):
                    writes.start(shared_low, out.at[r, pl.ds(block_rows(pieces), SHARED)])
        writes.finish()

    return call(
        body,
        "project_grads",
        7,
        [like((SHARED, 3 * width), F32)] + grads,
        [x, dqkv],
        table,
        [],
        turn_scratch(pieces, rows)
        + stage_scratch(pieces, 3 * width)
        + [
            pltpu.VMEM((SHARED, 3 * width), BF16),
            pltpu.SemaphoreType.DMA((3 * g + len(blocks_of(pieces)),)),
        ],
        far=g,
    )


def at_column(values, rows, width, column):
    return lax.dynamic_update_slice(jnp.zeros((rows, width), values.dtype), values, (0, column))


def small_block(row_params, expand_bias, mine, depth):
    high = lax.reduce_precision(row_params, 8, 7)
    column = (mine * N_MP + depth) * row_params.shape[1]
    high_low = [
        at_column(part.astype(BF16), 6, WIDTH, column) for part in (high, row_params - high)
    ]
    bias = at_column(expand_bias, 2, 2 * WIDTH, mine * expand_bias.shape[1])
    return jnp.concatenate([jnp.concatenate(high_low, axis=1), bias])


def key_bias(length_long, length_short, block, core, depth):
    lengths = jnp.concatenate([length_long, length_short])
    other = core_swap(lengths)
    longs = jnp.where(core == 0, jnp.stack([lengths[0], other[0]]), jnp.stack([other[0], lengths[0]]))
    length = jnp.concatenate([longs, lengths[1:]])[depth]
    is_long = depth < 2
    place = lax.broadcasted_iota(jnp.int32, (1, 2 * N_MP * block), 1)
    row = place % (N_MP * block)
    is_own = place < N_MP * block
    source = (row // block) ^ depth
    whose = jnp.where(is_own, core, 1 - core)
    frame = row % block + jnp.where(is_long, (2 * source + whose) * block, source * block)
    counted = (frame < length) & (is_own | is_long)
    return jnp.where(counted, 0.0, NEG_FILL).astype(F32)


def on_device(
    frames_long,
    frames_short,
    length_long,
    length_short,
    input_proj,
    output_proj,
    expand_weight,
    shrink_weight,
    head_bias,
    expand_bias,
    row_params,
    cotangent_long,
    cotangent_short,
):
    mine = lax.axis_index("dp")
    depth = lax.axis_index("mp")
    n_dp = lax.axis_size("dp")
    fast = n_dp == 8
    core = mine % 2
    block = frames_short.shape[1]
    shard, group = input_proj.shape[1:]
    units = expand_weight.shape[1]
    width = group * N_MP
    hidden = units * N_MP
    table = block_table(mine, n_dp)

    joined = jnp.concatenate(
        [input_proj[0], input_proj[1], input_proj[2], output_proj.T], axis=1
    )
    heads = at_column(head_bias[:, 0], SMALL, WIDTH, mine * head_bias.shape[2])
    attn_parts = mp_gather(jnp.concatenate([joined, heads]))
    x_blocks = clip_blocks(frames_long[0], frames_short, core)
    cot_blocks = clip_blocks(cotangent_long[0], cotangent_short, core)
    bias = key_bias(length_long, length_short, block, core, depth)
    feed_shard = jnp.concatenate(
        [
            jnp.concatenate([expand_weight, shrink_weight.T], axis=1),
            small_block(row_params, expand_bias, mine, depth),
        ]
    )
    *attn_parts, feed_shard, bias, x_blocks, cot_blocks = tie(
        *attn_parts, feed_shard, bias, x_blocks, cot_blocks
    )
    order = [p[:shard, i * group : (i + 1) * group] for i in range(4) for p in attn_parts]
    attn_slab = jnp.concatenate([to_slab(order), to_slab([p[shard:] for p in attn_parts])])
    feed_parts = mp_gather(feed_shard)
    feed_order = [p[:, i * units : (i + 1) * units] for i in range(2) for p in feed_parts]
    if fast:
        attn_p = [attn_slab] + [dp_swap(attn_slab, to) for to in (early, late, across)]
        x_pieces = clip_pieces(x_blocks, depth)
        attn_p += [core_swap(piece) for piece in attn_p]
        both = tie(*attn_p, *x_pieces, *feed_order)
        attn_p, x_pieces, feed_order = both[:8], both[8:12], both[12:]
        feed_slab = to_slab(feed_order)
        feed_one = dp_swap(feed_slab, early)
        feed_two = dp_swap(feed_slab, late)
        x_parts = [x_pieces[0]] + [mp_swap(x_pieces[i], i) for i in range(1, N_MP)]
        *x_parts, cot_blocks, own_slab = tie(*x_parts, cot_blocks, feed_slab)
        heads = sum(p[shard:].astype(F32) for p in attn_p)
    else:
        x_parts = to_clips(x_blocks, depth)
        gather = lambda slab: lax.all_gather(slab, "dp", axis=0)
        whole = gather(attn_slab)
        heads = jnp.sum(whole[:, shard:].astype(F32), axis=0)
        attn_p = [whole[:, :shard].reshape(width, 4 * width)]
        whole = gather(to_slab(feed_order))
        small = jnp.sum(whole[:, shard:].astype(F32), axis=0)
        feed_p = [whole[:, :shard].reshape(width, 2 * hidden)]
    cot_parts = to_clips(cot_blocks, depth)
    heads = jnp.concatenate(
        [heads[:2, i * width : i * width + group] for i in range(N_MP)], axis=1
    )
    head_row = jnp.concatenate([heads[:1], jnp.zeros_like(heads[:1]), heads[1:]], axis=1)

    x, qkv, kv = project(x_parts, head_row, table, attn_p)
    if fast:
        kv, feed_one, feed_two, cot_parts[3], own_slab = tie(
            kv, feed_one, feed_two, cot_parts[3], core_swap(own_slab)
        )
    kv_other = core_swap(kv)
    if fast:
        feed_three = dp_swap(feed_one, late)
        feed_p = [feed_slab, feed_one, feed_two]
        backs = [own_slab] + [core_swap(piece) for piece in feed_p[1:]]
    mixed, lse = attend(qkv, kv_other, bias)
    if fast:
        mixed, feed_three, *both = tie(mixed, feed_three, *backs, *cot_parts)
        backs, cot_parts = both[:3], both[3:]
        feed_p = feed_p + [feed_three] + backs + [core_swap(feed_three)]
        smalls, small_row = feed_p, shard
    else:
        smalls, small_row = [small.astype(BF16)], 0
    outs = feed(x, mixed, cot_parts, smalls, small_row, table, attn_p, feed_p)
    mid_shared, result, da, do, *grads = outs
    g_down, g_mid = grads[: len(grads) // 2], grads[len(grads) // 2 :]

    def by_group_of(value, sizes):
        starts = [N_MP * sum(sizes[:i]) for i in range(len(sizes))]
        return [
            jnp.concatenate(
                [value[:, a + j * n : a + (j + 1) * n] for a, n in zip(starts, sizes)], axis=1
            )
            for j in range(N_MP)
        ]

    def last_sum(terms):
        return sum(term[0].astype(F32) for term in terms)

    result_parts = from_clips(result)
    if fast:
        b_down, b_mid = core_swap(g_down[1]), core_swap(g_mid[1])
    pairs = width // LANES
    first = pairs // 2
    dq_a, own_a, other_a = attend_back(qkv, kv_other, bias, mixed, lse, do, 0, first)
    if fast:
        other_a, b_down, b_mid, result_parts[3] = tie(other_a, b_down, b_mid, result_parts[3])
        t_down = [g_down[0], b_down]
        a_down = goes_on(t_down)
        do, a_down = tie(do, a_down)
        b_down = dp_swap(a_down, late)
        t_mid = [g_mid[0], b_mid]
        a_mid = goes_on(t_mid)
        do, a_mid = tie(do, a_mid)
        b_mid = dp_swap(a_mid, late)
    back_a = core_swap(other_a)
    dq_b, own_b, other_b = attend_back(
        qkv, kv_other, bias, mixed, lse, do, first, pairs - first
    )
    if fast:
        other_b, back_a, *result_parts = tie(other_b, back_a, *result_parts)
    back_b = core_swap(other_b)
    parts = [(dq_a, own_a, back_a), (dq_b, own_b, back_b)]
    frames_grad, dqkv = project_back(da, parts, table, attn_p)
    grad_parts = from_clips(frames_grad)
    if fast:
        dqkv, b_down, b_mid = tie(dqkv, b_down, b_mid)
        t_down, t_mid = t_down + [b_down], t_mid + [b_mid]
        a_down, a_mid = goes_on(t_down), goes_on(t_mid)
        dqkv, a_down, a_mid = tie(dqkv, a_down, a_mid)
        b_down = dp_swap(a_down, early)
        b_mid = dp_swap(a_mid, early)
    attn_shared, *g_attn = project_grads(x, dqkv, table, attn_p)
    if fast:
        both = tie(*g_attn, b_down, b_mid, *grad_parts)
        g_attn, b_down, b_mid, grad_parts = both[:2], both[2], both[3], both[4:]
        t_attn = [g_attn[0], core_swap(g_attn[1])]
        both = tie(goes_on(t_attn), *t_down, b_down, *t_mid, b_mid)
        b_attn = dp_swap(both[0], late)
        t_down, t_mid = both[1:5], both[5:]
        s_down = by_group_of(last_sum(t_down), [units])
        z_down = mp_away(s_down)
        s_mid = by_group_of(last_sum(t_mid), [units, group])
        b_attn, z_down[2] = tie(b_attn, z_down[2])
        t_attn = t_attn + [b_attn]
        a_attn, *s_mid = tie(goes_on(t_attn), *s_mid)
        z_mid = mp_away(s_mid)
        b_attn = dp_swap(a_attn, early)
        b_attn, *both = tie(b_attn, *z_down, *z_mid, *result_parts)
        z_down, z_mid, result_parts = both[:3], both[3:6], both[6:]
        s_attn = last_sum(t_attn + [b_attn])
    else:
        scatter = lambda g: lax.psum_scatter(g[0][0], "dp", scatter_dimension=0, tiled=True)
        s_down = by_group_of(scatter(g_down), [units])
        z_down = mp_away(s_down)
        s_mid = jnp.concatenate([scatter(g_mid), lax.psum(mid_shared, "dp")])
        s_mid = by_group_of(s_mid, [units, group])
        z_mid = mp_away(s_mid)
        s_attn = jnp.concatenate([scatter(g_attn), lax.psum(attn_shared, "dp")])
    s_attn = by_group_of(s_attn, [group] * 3)
    grad_long, grad_short = frames_of(grad_parts, core, depth)
    result_long, result_short = frames_of(result_parts, core, depth)
    attn_share = mp_total(s_attn[0], mp_away(s_attn))
    down_share = mp_total(s_down[0], z_down).T
    mid_share = mp_total(s_mid[0], z_mid)
    up_share = mid_share[:shard, :units]
    output_share = mid_share[:shard, units:].T
    input_share = jnp.stack(
        [attn_share[:shard, i * group : (i + 1) * group] for i in range(3)]
    )
    up_cols, head_cols, row_cols = units // n_dp, group // n_dp, width // (n_dp * N_MP)
    rank = mine * N_MP + depth
    up_b_share = lax.dynamic_slice(mid_share, (shard, mine * up_cols), (1, up_cols))
    row_share = lax.dynamic_slice(mid_share, (shard + 1, rank * row_cols), (6, row_cols))
    head_share = jnp.stack(
        [
            lax.dynamic_slice(attn_share, (shard, at + mine * head_cols), (1, head_cols))
            for at in (0, 2 * group)
        ]
    )
    return (
        result_long,
        result_short,
        grad_long.astype(F32),
        grad_short.astype(F32),
        input_share,
        output_share,
        up_share,
        down_share,
        head_share,
        up_b_share,
        row_share,
    )


def solution(mesh):
    return jax.shard_map(
        on_device,
        mesh=mesh,
        in_specs=(
            P("dp", "mp", None),
            P("dp", "mp", None),
            P("dp"),
            P("dp"),
            P(None, "dp", "mp"),
            P("mp", "dp"),
            P("dp", "mp"),
            P("mp", "dp"),
            P(None, "mp", "dp"),
            P("mp", "dp"),
            P(None, ("dp", "mp")),
            P("dp", "mp", None),
            P("dp", "mp", None),
        ),
        out_specs=(
            P("dp", "mp", None),
            P("dp", "mp", None),
            P("dp", "mp", None),
            P("dp", "mp", None),
            P(None, "dp", "mp"),
            P("mp", "dp"),
            P("dp", "mp"),
            P("mp", "dp"),
            P(None, "mp", "dp"),
            P("mp", "dp"),
            P(None, ("dp", "mp")),
        ),
        check_vma=False,
    )
```

```python
import functools

import jax
import jax.numpy as jnp
from jax import lax
from jax.experimental import pallas as pl
from jax.experimental.pallas import tpu as pltpu
from jax.sharding import PartitionSpec as P

HEAD = 64
EPS = 1e-05
NEG_FILL = -1e30
SCALE = HEAD ** (-0.5)
N_MP = 4
PARTS = 1
CS = 0.3
WIDTH = 768
SMALL = 8
SHARED = 8
LANES = 128
Q_TILE = 256
F32 = jnp.float32
BF16 = jnp.bfloat16
NT = (((1,), (1,)), ((), ()))
NN = (((1,), (0,)), ((), ()))
TN = (((0,), (0,)), ((), ()))


def dot(left, right, dims):
    return lax.dot_general(left, right, dims, preferred_element_type=F32)


def mp_swap(value, step):
    return lax.ppermute(value, "mp", [(i, i ^ step) for i in range(N_MP)])


def dp_swap(value, target):
    size = lax.axis_size("dp")
    return lax.ppermute(value, "dp", [(i, target(i)) for i in range(size)])


def core_swap(value):
    return dp_swap(value, lambda i: i ^ 1)


def clip_blocks(long_rows, short_rows, core):
    block = short_rows.shape[1]
    keep = lax.dynamic_slice_in_dim(long_rows, core * block, block, 0)
    away = lax.dynamic_slice_in_dim(long_rows, (1 - core) * block, block, 0)
    back = core_swap(away)
    first = jnp.where(core == 0, keep, back)
    second = jnp.where(core == 0, back, keep)
    return jnp.stack([first, second, short_rows[0], short_rows[1]])


def clip_pieces(blocks, depth):
    return [
        lax.dynamic_index_in_dim(blocks, depth ^ step, 0, keepdims=False) for step in range(N_MP)
    ]


def to_clips(blocks, depth):
    pieces = clip_pieces(blocks, depth)
    return pieces[:1] + [mp_swap(pieces[step], step) for step in range(1, N_MP)]


def from_clips(rows):
    block = rows.shape[0] // N_MP
    parts = []
    for step in range(N_MP):
        piece = rows[step * block : (step + 1) * block]
        parts.append(piece if step == 0 else mp_swap(piece, step))
    return parts


def frames_of(parts, core, depth):
    blocks = jnp.stack(parts)
    first, second, short_a, short_b = (
        lax.dynamic_index_in_dim(blocks, depth ^ i, 0, keepdims=False) for i in range(N_MP)
    )
    keep = jnp.where(core == 0, first, second)
    away = jnp.where(core == 0, second, first)
    back = core_swap(away)
    low = jnp.where(core == 0, keep, back)
    high = jnp.where(core == 0, back, keep)
    return jnp.concatenate([low, high], axis=0)[None], jnp.stack([short_a, short_b])


def flip(index, late):
    return index ^ ((4 if late else 2) if index % 2 == 0 else (2 if late else 4))


def block_table(mine, size):
    if size != 8:
        return jnp.zeros((1,), jnp.int32)
    early = jnp.where(mine % 2 == 0, 2, 4)
    late = 6 - early
    relative = [0, early, late, 6, 1, 1 ^ late, 1 ^ early, 7]
    return jnp.stack([mine ^ r for r in relative]).astype(jnp.int32)


def early(i):
    return flip(i, False)


def late(i):
    return flip(i, True)


def across(i):
    return i ^ 6


def tie(*values):
    return lax.optimization_barrier(values)


def swap_plane(plane):
    return plane + [core_swap(piece) for piece in plane]


def to_slab(parts):
    return jnp.concatenate(parts, axis=1)


def mp_gather(shard):
    return [shard] + [mp_swap(shard, step) for step in range(1, N_MP)]


def goes_on(terms):
    half = terms[0].shape[0] // 2
    return sum(term[half:].astype(F32) for term in terms).astype(BF16)


def stays(terms, back):
    half = terms[0].shape[0] // 2
    return [term[:half] for term in terms] + [back]


def mp_away(parts):
    return [mp_swap(parts[step].astype(BF16), step) for step in range(1, N_MP)]


def mp_total(own, backs):
    for back in backs:
        own = own + back.astype(F32)
    return own


def blocks_of(pieces):
    step = pieces[0].shape[0]
    return [(p, k * step) for p in pieces for k in range(p.shape[0] // step)]


def block_rows(pieces):
    return WIDTH // len(blocks_of(pieces))


class Weights:
    def __init__(self, pieces, table, held, sems, lo, tile):
        self.held, self.tile = held, tile
        cols, parts = held.shape[2], sems.shape[0]
        self.span, self.copies = cols // parts, []
        for t in range(parts):
            row = []
            for k, (piece, first) in enumerate(blocks_of(pieces)):
                copy = pltpu.make_async_copy(
                    piece.at[pl.ds(first, held.shape[1]), pl.ds(lo + t * self.span, self.span)],
                    held.at[table[k], :, pl.ds(t * self.span, self.span)],
                    sems.at[t, k],
                )
                copy.start()
                row.append(copy)
            self.copies.append(row)
        self.waited = 0

    def whole(self):
        for row in self.copies[self.waited :]:
            for copy in row:
                copy.wait()
        self.waited = len(self.copies)

    def at(self, at):
        count, rows, _ = self.held.shape
        return self.held[:, :, pl.ds(at, self.tile)].reshape(count * rows, self.tile)

    def get(self, t):
        at = t * self.tile
        while self.waited * self.span < at + self.tile:
            for copy in self.copies[self.waited]:
                copy.wait()
            self.waited += 1
        count, rows, _ = self.held.shape
        return self.held[:, :, at : at + self.tile].reshape(count * rows, self.tile)


def weight_scratch(pieces, cols, parts=1):
    return [
        pltpu.VMEM((len(blocks_of(pieces)), block_rows(pieces), cols), BF16),
        pltpu.SemaphoreType.DMA((parts, len(blocks_of(pieces)))),
    ]


def grad_shapes(pieces, cols, extra=0):
    count, rows = len(blocks_of(pieces)), block_rows(pieces)
    if count == 1:
        return [jax.ShapeDtypeStruct((1, rows, cols), F32)]
    return [jax.ShapeDtypeStruct((count // 2, rows + extra, cols), BF16)] * 2


def turn_scratch(pieces, rows):
    return [pltpu.VMEM((len(blocks_of(pieces)), block_rows(pieces), rows), BF16)] * 2


def turn(value, table, plain, turned):
    plain[...] = value.T.reshape(plain.shape)
    for r in range(plain.shape[0]):
        turned[r] = plain[table[r]]


def stage_scratch(pieces, cols):
    return [
        pltpu.VMEM((g.shape[0], block_rows(pieces), cols), g.dtype)
        for g in grad_shapes(pieces, cols)
    ]


def store_grad(turned, right, stages, at):
    count, rows, _ = turned.shape
    grad = dot(turned[...].reshape(count * rows, -1), right, NN)
    half, cols = count // len(stages), right.shape[1]
    for r in range(count):
        stage = stages[r // half]
        part = grad[r * rows : (r + 1) * rows].astype(stage.dtype)
        stage[r % half, :rows, pl.ds(at, cols)] = part


def grad_copies(stages, outs, at, cols, sems, first):
    return [
        pltpu.make_async_copy(
            stage.at[:, :, pl.ds(at, cols)],
            out.at[:, pl.ds(0, stage.shape[1]), pl.ds(at, cols)],
            sems.at[first + i],
        )
        for i, (stage, out) in enumerate(zip(stages, outs))
    ]


def start_all(copies):
    for copy in copies:
        copy.start()


def wait_all(copies):
    for copy in copies:
        copy.wait()


class Writes:
    def __init__(self, sems):
        self.sems, self.copies = sems, []

    def start(self, source, target):
        copy = pltpu.make_async_copy(source, target, self.sems.at[len(self.copies)])
        copy.start()
        self.copies.append(copy)

    def finish(self):
        for copy in self.copies:
            copy.wait()


class Reads:
    def __init__(self, sources, targets, sems):
        self.targets, self.copies = targets, []
        for i, (source, target) in enumerate(zip(sources, targets)):
            copy = pltpu.make_async_copy(source, target, sems.at[i])
            copy.start()
            self.copies.append(copy)

    def get(self, i):
        self.copies[i].wait()
        return self.targets[i]


def read_scratch(arrays):
    return [pltpu.VMEM(a.shape, a.dtype) for a in arrays] + [
        pltpu.SemaphoreType.DMA((len(arrays),))
    ]


def cost(micros):
    return pl.CostEstimate(
        flops=int(micros * 1.1e9 * CS), bytes_accessed=int(micros * 1e5 * CS), transcendentals=0
    )


def call(body, name, micros, outs, arrays, table, pieces, scratch, far=0):
    vmem = pl.BlockSpec(memory_space=pltpu.VMEM)
    away = pl.BlockSpec(memory_space=pl.ANY)
    return pl.pallas_call(
        body,
        out_shape=tuple(outs),
        in_specs=[pl.BlockSpec(memory_space=pltpu.SMEM)]
        + [vmem] * len(arrays)
        + [away] * len(pieces),
        out_specs=(vmem,) * (len(outs) - far) + (away,) * far,
        scratch_shapes=scratch,
        compiler_params=pltpu.CompilerParams(vmem_limit_bytes=60 << 20),
        cost_estimate=cost(micros),
        name=name,
    )(table, *arrays, *pieces)


def like(shape, kind):
    return jax.ShapeDtypeStruct(shape, kind)


def attend_kernel(q_ref, k_ref, v_ref, kp_ref, vp_ref, bias_ref, o_ref, lse_ref):
    rows = q_ref.shape[0]
    keys = jnp.concatenate([k_ref[...], kp_ref[...]], axis=0)
    values = jnp.concatenate([v_ref[...], vp_ref[...]], axis=0)
    bias = bias_ref[...]
    tile = min(rows, Q_TILE)
    low = lax.broadcasted_iota(jnp.int32, (tile, LANES), 1) < HEAD
    for start in range(0, rows, tile):
        q = q_ref[start : start + tile, :]
        outs, logs = [], []
        for half in range(2):
            here = low if half == 0 else ~low
            q_here = jnp.where(here, q, jnp.zeros_like(q))
            scores = dot(q_here, keys, NT) + bias
            top = jnp.max(scores, axis=-1, keepdims=True)
            raised = jnp.exp(scores - top)
            total = jnp.sum(raised, axis=-1, keepdims=True)
            mixed = dot(raised.astype(BF16), values, NN)
            outs.append(mixed / total)
            logs.append(top + jnp.log(total))
        o_ref[start : start + tile, :] = jnp.where(low, outs[0], outs[1]).astype(BF16)
        lse_ref[start : start + tile, :] = jnp.where(low, logs[0], logs[1])


def attend(qkv, kv_other, bias):
    rows, width = qkv.shape[0], qkv.shape[1] // 3
    pairs = width // LANES
    spec = lambda base: pl.BlockSpec((rows, LANES), lambda p: (0, base + p))
    return pl.pallas_call(
        attend_kernel,
        out_shape=(
            jax.ShapeDtypeStruct((rows, width), BF16),
            jax.ShapeDtypeStruct((rows, width), F32),
        ),
        grid=(pairs,),
        in_specs=[
            spec(0),
            spec(pairs),
            spec(2 * pairs),
            spec(0),
            spec(pairs),
            pl.BlockSpec((1, 2 * rows), lambda p: (0, 0)),
        ],
        out_specs=(spec(0), spec(0)),
        compiler_params=pltpu.CompilerParams(vmem_limit_bytes=56 << 20),
        cost_estimate=cost(15),
        name="attend",
    )(qkv, qkv, qkv, kv_other, kv_other, bias)


def attend_back_kernel(
    q_ref, k_ref, v_ref, kp_ref, vp_ref, bias_ref, o_ref, lse_ref, do_ref,
    dq_ref, own_ref, other_ref,
):
    rows = q_ref.shape[0]
    keys = jnp.concatenate([k_ref[...], kp_ref[...]], axis=0)
    values = jnp.concatenate([v_ref[...], vp_ref[...]], axis=0)
    bias = bias_ref[...]
    tile = min(rows, Q_TILE)
    low = lax.broadcasted_iota(jnp.int32, (tile, LANES), 1) < HEAD
    dk = jnp.zeros((LANES, 2 * rows), F32)
    dv = jnp.zeros((LANES, 2 * rows), F32)
    for start in range(0, rows, tile):
        at = slice(start, start + tile)
        q, do = q_ref[at, :], do_ref[at, :]
        product = o_ref[at, :].astype(F32) * do.astype(F32)
        lse = lse_ref[at, :]
        outs = []
        for half in range(2):
            here = low if half == 0 else ~low
            q_here = jnp.where(here, q, jnp.zeros_like(q))
            do_here = jnp.where(here, do, jnp.zeros_like(do))
            inner = jnp.sum(jnp.where(here, product, 0.0), axis=-1, keepdims=True)
            log = lse[:, half * HEAD : half * HEAD + 1]
            soft = jnp.exp(dot(q_here, keys, NT) + bias - log)
            grad = (soft * (dot(do_here, values, NT) - inner)).astype(BF16)
            outs.append(dot(grad, keys, NN))
            dk = dk + dot(q_here, grad, TN)
            dv = dv + dot(do_here, soft.astype(BF16), TN)
        dq_ref[at, :] = (jnp.where(low, outs[0], outs[1]) * SCALE).astype(BF16)
    for i, value in enumerate((dk.T, dv.T)):
        at = slice(i * LANES, (i + 1) * LANES)
        own_ref[:, at] = value[:rows]
        other_ref[:, at] = value[rows:].astype(BF16)


def attend_back(qkv, kv_other, bias, out, lse, grad_out, first, count):
    rows, width = out.shape
    pairs = width // LANES
    spec = lambda base: pl.BlockSpec((rows, LANES), lambda p: (0, base + first + p))
    result = lambda cols: pl.BlockSpec((rows, cols), lambda p: (0, p))
    return pl.pallas_call(
        attend_back_kernel,
        out_shape=(
            jax.ShapeDtypeStruct((rows, count * LANES), BF16),
            jax.ShapeDtypeStruct((rows, 2 * count * LANES), F32),
            jax.ShapeDtypeStruct((rows, 2 * count * LANES), BF16),
        ),
        grid=(count,),
        in_specs=[
            spec(0),
            spec(pairs),
            spec(2 * pairs),
            spec(0),
            spec(pairs),
            pl.BlockSpec((1, 2 * rows), lambda p: (0, 0)),
            spec(0),
            spec(0),
            spec(0),
        ],
        out_specs=(result(LANES), result(2 * LANES), result(2 * LANES)),
        compiler_params=pltpu.CompilerParams(vmem_limit_bytes=56 << 20),
        cost_estimate=cost(3 * count),
        name="attend_back",
    )(qkv, qkv, qkv, kv_other, kv_other, bias, out, lse, grad_out)


def gelu_parts(v):
    cdf = 0.5 * (1.0 + lax.erf(v * (2.0 ** -0.5)))
    pdf = jnp.exp(-0.5 * v * v) * 0.3989422804014327
    return v * cdf, cdf + v * pdf


def norm(values):
    center = values - jnp.mean(values, axis=-1, keepdims=True)
    inv_dev = lax.rsqrt(jnp.mean(center * center, axis=-1, keepdims=True) + EPS)
    return center * inv_dev, inv_dev


def norm_back(scaled, normed, inv_dev):
    return inv_dev * (
        scaled
        - jnp.mean(scaled, axis=-1, keepdims=True)
        - normed * jnp.mean(scaled * normed, axis=-1, keepdims=True)
    )


def total(value):
    return jnp.sum(value, axis=0, keepdims=True)


def join(parts, starts, size, micros):
    rows, cols = parts[0].shape[0], len(starts) * len(parts) * size

    def body(*refs):
        parts, out = refs[:-1], refs[-1]
        at = 0
        for start in starts:
            for part in parts:
                out[:, at : at + size] = part[:, start : start + size]
                at += size

    vmem = pl.BlockSpec(memory_space=pltpu.VMEM)
    return pl.pallas_call(
        body,
        out_shape=like((rows, cols), parts[0].dtype),
        in_specs=[vmem] * len(parts),
        out_specs=vmem,
        cost_estimate=cost(micros),
        name="join",
    )(*parts)


def project(x_parts, head_row, table, pieces):
    block, width = x_parts[0].shape
    rows = block * len(x_parts)
    n = len(pieces)

    def body(table, *refs):
        part_refs, bias_ref, refs = refs[:N_MP], refs[N_MP], refs[N_MP + 1 :]
        pieces, (x_ref, qkv_ref, kv_ref, held, sems) = refs[:n], refs[n:]
        weights = Weights(pieces, table, held, sems, 0, width)
        for i, part in enumerate(part_refs):
            x_ref[i * block : (i + 1) * block, :] = part[...]
        x = x_ref[...]
        for i in range(3):
            value = dot(x, weights.get(i), NN) + bias_ref[:, i * width : (i + 1) * width]
            value = value.astype(BF16)
            if i == 0:
                value = (value.astype(F32) * SCALE).astype(BF16)
            else:
                kv_ref[:, (i - 1) * width : i * width] = value
            qkv_ref[:, i * width : (i + 1) * width] = value

    return call(
        body,
        "project",
        7,
        [
            like((rows, width), BF16),
            like((rows, 3 * width), BF16),
            like((rows, 2 * width), BF16),
        ],
        list(x_parts) + [head_row],
        table,
        pieces,
        weight_scratch(pieces, 3 * width, 3),
    )


def feed(x, mixed, cot_parts, smalls, small_row, table, out_pieces, feed_pieces):
    rows, width = x.shape
    hidden = feed_pieces[0].shape[1] // 2
    count = 6
    tile = hidden // count
    cols = hidden + width
    n_out, n_up, n = len(out_pieces), len(feed_pieces), len(smalls)
    down_grads = grad_shapes(feed_pieces, hidden)
    mid_grads = grad_shapes(feed_pieces, cols, SHARED)
    g = len(mid_grads)

    def body(table, x_ref, mixed_ref, *refs):
        cot_far, small_far, refs = refs[:N_MP], refs[N_MP : N_MP + n], refs[N_MP + n :]
        out_p, up_p = refs[:n_out], refs[n_out : n_out + n_up]
        refs = refs[n_out + n_up :]
        shared_ref, result_out, da_out, do_out = refs[:4]
        down_outs, mid_outs, refs = refs[4 : 4 + g], refs[4 + g : 4 + 2 * g], refs[4 + 2 * g :]
        w_out, sems_out, w_up, sems_up, w_down, sems_down = refs[:6]
        plain, turned, plain_h, turned_h = refs[6:10]
        small_ref, cot_ref, read_sems = refs[10:13]
        n1_ref, dz_ref, h_ref, act_ref, slope_ref, result_ref, low_ref, do_ref = refs[13:21]
        down_stages, mid_stages = refs[21 : 21 + g], refs[21 + g : 21 + 2 * g]
        shared_low, sems, grad_sems, up_b_ref = refs[21 + 2 * g :]
        out_w = Weights(out_p, table, w_out, sems_out, 3 * width, width)
        smalls = [small.at[pl.ds(small_row, SMALL)] for small in small_far]
        reads = Reads(smalls, [small_ref.at[i] for i in range(n)], read_sems)
        up_w = Weights(up_p, table, w_up, sems_up, 0, tile)
        down_w = Weights(up_p, table, w_down, sems_down, hidden, tile)
        block = rows // N_MP
        cots = Reads(
            cot_far,
            [cot_ref.at[pl.ds(i * block, block)] for i in range(N_MP)],
            read_sems.at[pl.ds(n, N_MP)],
        )
        writes = Writes(sems)

        attention = dot(mixed_ref[...], out_w.get(0), NT)
        for i in range(n):
            reads.get(i)
        small = jnp.sum(small_ref[...].astype(F32), axis=0)
        row_vals = sum(small[:, i * width : (i + 1) * width] for i in range(2 * N_MP))
        row = lambda i: row_vals[i : i + 1, :]
        up_b = small[6:7, :hidden]
        n1, r1 = norm(x_ref[...].astype(F32) + attention + row(0))
        n1_ref[...] = n1
        h_ref[...] = (n1 * row(1) + row(2)).astype(BF16)
        up_b_ref[...] = up_b
        dz_ref[...] = jnp.zeros_like(dz_ref)
        up_w.whole()
        down_w.whole()

        @pl.loop(0, count)
        def _(t):
            at = pl.multiple_of(t * tile, tile)
            u = dot(h_ref[...], up_w.at(at), NN)
            act, slope = gelu_parts(u + up_b_ref[:, pl.ds(at, tile)])
            act_ref[:, pl.ds(at, tile)] = act.astype(BF16)
            slope_ref[:, pl.ds(at, tile)] = slope.astype(BF16)
            dz_ref[...] += dot(act_ref[:, pl.ds(at, tile)], down_w.at(at), NT)

        feed = dz_ref[...]
        h = n1_ref[...] * row(1) + row(2)
        n2, r2 = norm(h + feed + row(3))
        result_ref[...] = (n2 * row(4) + row(5)).astype(BF16)
        writes.start(result_ref, result_out)
        for i in range(N_MP):
            cots.get(i)
        gy = cot_ref[...].astype(F32)
        dz = norm_back(gy * row(4), n2, r2)
        dz_ref[...] = dz
        low_ref[...] = dz.astype(BF16)
        sums = [total(dz), total(gy * n2), total(gy)]

        turn(low_ref[...], table, plain, turned)
        turn(h_ref[...], table, plain_h, turned_h)
        shared_ref[...] = jnp.zeros_like(shared_ref)
        def tile_copies(t):
            at = t * tile if isinstance(t, int) else pl.multiple_of(t * tile, tile)
            down = grad_copies(down_stages, down_outs, at, tile, grad_sems, 2 * g * t)
            return down + grad_copies(mid_stages, mid_outs, at, tile, grad_sems, 2 * g * t + g)

        @pl.loop(0, count)
        def _(t):
            at = pl.multiple_of(t * tile, tile)
            dact = dot(low_ref[...], down_w.at(at), NN)
            store_grad(turned, act_ref[:, pl.ds(at, tile)], down_stages, at)
            du = (dact * slope_ref[:, pl.ds(at, tile)].astype(F32)).astype(BF16)
            shared_ref[0:1, pl.ds(at, tile)] = total(du.astype(F32))
            dz_ref[...] += dot(du, up_w.at(at), NT)
            store_grad(turned_h, du, mid_stages, at)
            start_all(tile_copies(t))

        dh = dz_ref[...]
        n1 = n1_ref[...]
        da = norm_back(dh * row(1), n1, r1)
        dz_ref[...] = da
        writes.start(dz_ref, da_out)
        low_ref[...] = da.astype(BF16)
        do_ref[...] = dot(low_ref[...], out_w.get(0), NN).astype(BF16)
        writes.start(do_ref, do_out)
        sums = [total(da), total(dh * n1), total(dh)] + sums
        for j in range(hidden // width):
            for i, value in enumerate(sums):
                shared_ref[1 + i : 2 + i, j * width : (j + 1) * width] = value
        if g > 1:
            shared_low[...] = shared_ref[...].astype(BF16)
            for out in mid_outs:
                for r in range(out.shape[0]):
                    writes.start(shared_low, out.at[r, pl.ds(block_rows(feed_pieces), SHARED)])
        turn(low_ref[...], table, plain, turned)
        store_grad(turned, mixed_ref[...], mid_stages, hidden)
        last = grad_copies(mid_stages, mid_outs, hidden, width, grad_sems, 2 * g * count)
        start_all(last)
        for t in range(count):
            wait_all(tile_copies(t))
        wait_all(last)
        writes.finish()

    near = [((rows, width), F32)] * 2 + [((rows, width), BF16)]
    near += [((rows, hidden), BF16)] * 2 + [((rows, width), BF16)] * 3
    return call(
        body,
        "feed",
        33,
        [
            like((SHARED, cols), F32),
            like((rows, width), BF16),
            like((rows, width), F32),
            like((rows, width), BF16),
        ]
        + down_grads
        + mid_grads,
        [x, mixed],
        table,
        list(cot_parts) + list(smalls) + list(out_pieces) + list(feed_pieces),
        weight_scratch(out_pieces, width)
        + weight_scratch(feed_pieces, hidden) * 2
        + turn_scratch(feed_pieces, rows) * 2
        + [
            pltpu.VMEM((n, SMALL, 2 * hidden), BF16),
            pltpu.VMEM((rows, width), BF16),
            pltpu.SemaphoreType.DMA((n + N_MP,)),
        ]
        + [pltpu.VMEM(*spec) for spec in near]
        + stage_scratch(feed_pieces, hidden)
        + stage_scratch(feed_pieces, cols)
        + [
            pltpu.VMEM((SHARED, cols), BF16),
            pltpu.SemaphoreType.DMA((3 + n_up,)),
            pltpu.SemaphoreType.DMA((g * (2 * count + 1),)),
            pltpu.VMEM((1, hidden), F32),
        ],
        far=3 + 2 * g,
    )


def project_back(da, parts, table, pieces):
    rows, width = da.shape
    n = len(pieces)
    flat = [value for part in parts for value in part]

    def body(table, da_ref, *refs):
        part_refs, refs = refs[: len(flat)], refs[len(flat) :]
        pieces, (out_ref, dqkv_ref, held, sems) = refs[:n], refs[n:]
        weights = Weights(pieces, table, held, sems, 0, width)
        pair = 0
        for i in range(0, len(flat), 3):
            q_ref, own_ref, back_ref = part_refs[i : i + 3]
            cols = q_ref.shape[1]
            dqkv_ref[:, pair * LANES : pair * LANES + cols] = q_ref[...]
            for p in range(cols // LANES):
                for which in range(2):
                    at = slice((2 * p + which) * LANES, (2 * p + which + 1) * LANES)
                    to = (which + 1) * width + (pair + p) * LANES
                    value = own_ref[:, at] + back_ref[:, at].astype(F32)
                    dqkv_ref[:, to : to + LANES] = value.astype(BF16)
            pair += cols // LANES
        value = da_ref[...]
        for i in range(3):
            value = value + dot(dqkv_ref[:, i * width : (i + 1) * width], weights.get(i), NT)
        out_ref[...] = value.astype(BF16)

    return call(
        body,
        "project_back",
        9,
        [like((rows, width), BF16), like((rows, 3 * width), BF16)],
        [da] + flat,
        table,
        pieces,
        weight_scratch(pieces, 3 * width, 3),
    )


def project_grads(x, dqkv, table, pieces):
    rows, width = x.shape
    grads = grad_shapes(pieces, 3 * width, SHARED)
    g = len(grads)

    def body(table, x_ref, dqkv_ref, *refs):
        shared_ref, grad_outs, refs = refs[0], refs[1 : 1 + g], refs[1 + g :]
        plain, turned = refs[:2]
        stages, shared_low, sems = refs[2 : 2 + g], refs[2 + g], refs[3 + g]
        writes = Writes(sems.at[pl.ds(3 * g, len(blocks_of(pieces)))])
        turn(x_ref[...], table, plain, turned)

        @pl.loop(0, 3)
        def _(i):
            at = pl.multiple_of(i * width, width)
            store_grad(turned, dqkv_ref[:, pl.ds(at, width)], stages, at)
            start_all(grad_copies(stages, grad_outs, at, width, sems, g * i))

        shared_ref[...] = jnp.zeros_like(shared_ref)
        shared_ref[0:1, :] = total(dqkv_ref[...].astype(F32))
        if g > 1:
            shared_low[...] = shared_ref[...].astype(BF16)
            for out in grad_outs:
                for r in range(out.shape[0]):
                    writes.start(shared_low, out.at[r, pl.ds(block_rows(pieces), SHARED)])
        for i in range(3):
            wait_all(grad_copies(stages, grad_outs, i * width, width, sems, g * i))
        writes.finish()

    return call(
        body,
        "project_grads",
        7,
        [like((SHARED, 3 * width), F32)] + grads,
        [x, dqkv],
        table,
        [],
        turn_scratch(pieces, rows)
        + stage_scratch(pieces, 3 * width)
        + [
            pltpu.VMEM((SHARED, 3 * width), BF16),
            pltpu.SemaphoreType.DMA((3 * g + len(blocks_of(pieces)),)),
        ],
        far=g,
    )


def at_column(values, rows, width, column):
    return lax.dynamic_update_slice(jnp.zeros((rows, width), values.dtype), values, (0, column))


def small_block(row_params, expand_bias, mine, depth):
    high = lax.reduce_precision(row_params, 8, 7)
    column = (mine * N_MP + depth) * row_params.shape[1]
    high_low = [
        at_column(part.astype(BF16), 6, WIDTH, column) for part in (high, row_params - high)
    ]
    bias = at_column(expand_bias, 2, 2 * WIDTH, mine * expand_bias.shape[1])
    return jnp.concatenate([jnp.concatenate(high_low, axis=1), bias])


def key_bias(length_long, length_short, block, core, depth):
    lengths = jnp.concatenate([length_long, length_short])
    other = core_swap(lengths)
    longs = jnp.where(core == 0, jnp.stack([lengths[0], other[0]]), jnp.stack([other[0], lengths[0]]))
    length = jnp.concatenate([longs, lengths[1:]])[depth]
    is_long = depth < 2
    place = lax.broadcasted_iota(jnp.int32, (1, 2 * N_MP * block), 1)
    row = place % (N_MP * block)
    is_own = place < N_MP * block
    source = (row // block) ^ depth
    whose = jnp.where(is_own, core, 1 - core)
    frame = row % block + jnp.where(is_long, (2 * source + whose) * block, source * block)
    counted = (frame < length) & (is_own | is_long)
    return jnp.where(counted, 0.0, NEG_FILL).astype(F32)


def on_device(
    frames_long,
    frames_short,
    length_long,
    length_short,
    input_proj,
    output_proj,
    expand_weight,
    shrink_weight,
    head_bias,
    expand_bias,
    row_params,
    cotangent_long,
    cotangent_short,
):
    mine = lax.axis_index("dp")
    depth = lax.axis_index("mp")
    n_dp = lax.axis_size("dp")
    fast = n_dp == 8
    core = mine % 2
    block = frames_short.shape[1]
    shard, group = input_proj.shape[1:]
    units = expand_weight.shape[1]
    width = group * N_MP
    hidden = units * N_MP
    table = block_table(mine, n_dp)

    joined = jnp.concatenate(
        [input_proj[0], input_proj[1], input_proj[2], output_proj.T], axis=1
    )
    heads = at_column(head_bias[:, 0], SMALL, WIDTH, mine * head_bias.shape[2])
    attn_parts = mp_gather(jnp.concatenate([joined, heads]))
    x_blocks = clip_blocks(frames_long[0], frames_short, core)
    cot_blocks = clip_blocks(cotangent_long[0], cotangent_short, core)
    bias = key_bias(length_long, length_short, block, core, depth)
    feed_shard = jnp.concatenate(
        [
            jnp.concatenate([expand_weight, shrink_weight.T], axis=1),
            small_block(row_params, expand_bias, mine, depth),
        ]
    )
    *attn_parts, feed_shard, bias, x_blocks, cot_blocks = tie(
        *attn_parts, feed_shard, bias, x_blocks, cot_blocks
    )
    order = [p[:shard, i * group : (i + 1) * group] for i in range(4) for p in attn_parts]
    attn_slab = jnp.concatenate([to_slab(order), to_slab([p[shard:] for p in attn_parts])])
    feed_parts = mp_gather(feed_shard)
    feed_order = [p[:, i * units : (i + 1) * units] for i in range(2) for p in feed_parts]
    if fast:
        attn_p = [attn_slab] + [dp_swap(attn_slab, to) for to in (early, late, across)]
        x_pieces = clip_pieces(x_blocks, depth)
        attn_p += [core_swap(piece) for piece in attn_p]
        both = tie(*attn_p, *x_pieces, *feed_order)
        attn_p, x_pieces, feed_order = both[:8], both[8:12], both[12:]
        feed_slab = to_slab(feed_order)
        feed_one = dp_swap(feed_slab, early)
        feed_two = dp_swap(feed_slab, late)
        x_parts = [x_pieces[0]] + [mp_swap(x_pieces[i], i) for i in range(1, N_MP)]
        *x_parts, cot_blocks, own_slab = tie(*x_parts, cot_blocks, feed_slab)
        heads = sum(p[shard:].astype(F32) for p in attn_p)
    else:
        x_parts = to_clips(x_blocks, depth)
        gather = lambda slab: lax.all_gather(slab, "dp", axis=0)
        whole = gather(attn_slab)
        heads = jnp.sum(whole[:, shard:].astype(F32), axis=0)
        attn_p = [whole[:, :shard].reshape(width, 4 * width)]
        whole = gather(to_slab(feed_order))
        small = jnp.sum(whole[:, shard:].astype(F32), axis=0)
        feed_p = [whole[:, :shard].reshape(width, 2 * hidden)]
    cot_parts = to_clips(cot_blocks, depth)
    heads = jnp.concatenate(
        [heads[:2, i * width : i * width + group] for i in range(N_MP)], axis=1
    )
    head_row = jnp.concatenate([heads[:1], jnp.zeros_like(heads[:1]), heads[1:]], axis=1)

    x, qkv, kv = project(x_parts, head_row, table, attn_p)
    if fast:
        kv, feed_one, feed_two, cot_parts[3], own_slab = tie(
            kv, feed_one, feed_two, cot_parts[3], core_swap(own_slab)
        )
    kv_other = core_swap(kv)
    if fast:
        feed_three = dp_swap(feed_one, late)
        feed_p = [feed_slab, feed_one, feed_two]
        backs = [own_slab] + [core_swap(piece) for piece in feed_p[1:]]
    mixed, lse = attend(qkv, kv_other, bias)
    if fast:
        mixed, feed_three, *both = tie(mixed, feed_three, *backs, *cot_parts)
        backs, cot_parts = both[:3], both[3:]
        feed_p = feed_p + [feed_three] + backs + [core_swap(feed_three)]
        smalls, small_row = feed_p, shard
    else:
        smalls, small_row = [small.astype(BF16)], 0
    outs = feed(x, mixed, cot_parts, smalls, small_row, table, attn_p, feed_p)
    mid_shared, result, da, do, *grads = outs
    g_down, g_mid = grads[: len(grads) // 2], grads[len(grads) // 2 :]

    def by_group_of(value, sizes):
        starts = [N_MP * sum(sizes[:i]) for i in range(len(sizes))]
        return [
            jnp.concatenate(
                [value[:, a + j * n : a + (j + 1) * n] for a, n in zip(starts, sizes)], axis=1
            )
            for j in range(N_MP)
        ]

    def last_sum(terms):
        return sum(term[0].astype(F32) for term in terms)

    result_parts = from_clips(result)
    if fast:
        b_down, b_mid = core_swap(g_down[1]), core_swap(g_mid[1])
    pairs = width // LANES
    first = pairs // 2
    dq_a, own_a, other_a = attend_back(qkv, kv_other, bias, mixed, lse, do, 0, first)
    if fast:
        other_a, b_down, b_mid, result_parts[3] = tie(other_a, b_down, b_mid, result_parts[3])
        t_down = [g_down[0], b_down]
        a_down = goes_on(t_down)
        do, a_down = tie(do, a_down)
        b_down = dp_swap(a_down, late)
        t_mid = [g_mid[0], b_mid]
        a_mid = goes_on(t_mid)
        do, a_mid = tie(do, a_mid)
        b_mid = dp_swap(a_mid, late)
    back_a = core_swap(other_a)
    dq_b, own_b, other_b = attend_back(
        qkv, kv_other, bias, mixed, lse, do, first, pairs - first
    )
    if fast:
        other_b, back_a, *result_parts = tie(other_b, back_a, *result_parts)
    back_b = core_swap(other_b)
    parts = [(dq_a, own_a, back_a), (dq_b, own_b, back_b)]
    frames_grad, dqkv = project_back(da, parts, table, attn_p)
    grad_parts = from_clips(frames_grad)
    if fast:
        dqkv, b_down, b_mid = tie(dqkv, b_down, b_mid)
        t_down, t_mid = stays(t_down, b_down), stays(t_mid, b_mid)
        a_down, a_mid = goes_on(t_down), goes_on(t_mid)
        dqkv, a_down, a_mid = tie(dqkv, a_down, a_mid)
        b_down = dp_swap(a_down, early)
        b_mid = dp_swap(a_mid, early)
    attn_shared, *g_attn = project_grads(x, dqkv, table, attn_p)
    if fast:
        both = tie(*g_attn, b_down, b_mid, *grad_parts)
        g_attn, b_down, b_mid, grad_parts = both[:2], both[2], both[3], both[4:]
        b_attn = core_swap(g_attn[1])
        s_down = by_group_of(last_sum(stays(t_down, b_down)), [units])
        t_attn = [g_attn[0], b_attn]
        a_attn = goes_on(t_attn)
        a_attn, *s_down = tie(a_attn, *s_down)
        b_attn = dp_swap(a_attn, late)
        z_down = mp_away(s_down)
        s_mid = by_group_of(last_sum(stays(t_mid, b_mid)), [units, group])
        b_attn, *z_down = tie(b_attn, *z_down)
        t_attn = stays(t_attn, b_attn)
        a_attn = goes_on(t_attn)
        z_mid = mp_away(s_mid)
        b_attn, *both = tie(dp_swap(a_attn, early), *z_mid, *result_parts)
        z_mid, result_parts = both[: N_MP - 1], both[N_MP - 1 :]
        s_attn = last_sum(stays(t_attn, b_attn))
    else:
        scatter = lambda g: lax.psum_scatter(g[0][0], "dp", scatter_dimension=0, tiled=True)
        s_down = by_group_of(scatter(g_down), [units])
        z_down = mp_away(s_down)
        s_mid = jnp.concatenate([scatter(g_mid), lax.psum(mid_shared, "dp")])
        s_mid = by_group_of(s_mid, [units, group])
        z_mid = mp_away(s_mid)
        s_attn = jnp.concatenate([scatter(g_attn), lax.psum(attn_shared, "dp")])
    s_attn = by_group_of(s_attn, [group] * 3)
    grad_long, grad_short = frames_of(grad_parts, core, depth)
    result_long, result_short = frames_of(result_parts, core, depth)
    attn_share = mp_total(s_attn[0], mp_away(s_attn))
    down_share = mp_total(s_down[0], z_down).T
    mid_share = mp_total(s_mid[0], z_mid)
    up_share = mid_share[:shard, :units]
    output_share = mid_share[:shard, units:].T
    input_share = jnp.stack(
        [attn_share[:shard, i * group : (i + 1) * group] for i in range(3)]
    )
    up_cols, head_cols, row_cols = units // n_dp, group // n_dp, width // (n_dp * N_MP)
    rank = mine * N_MP + depth
    up_b_share = lax.dynamic_slice(mid_share, (shard, mine * up_cols), (1, up_cols))
    row_share = lax.dynamic_slice(mid_share, (shard + 1, rank * row_cols), (6, row_cols))
    head_share = jnp.stack(
        [
            lax.dynamic_slice(attn_share, (shard, at + mine * head_cols), (1, head_cols))
            for at in (0, 2 * group)
        ]
    )
    return (
        result_long,
        result_short,
        grad_long.astype(F32),
        grad_short.astype(F32),
        input_share,
        output_share,
        up_share,
        down_share,
        head_share,
        up_b_share,
        row_share,
    )


def solution(mesh):
    return jax.shard_map(
        on_device,
        mesh=mesh,
        in_specs=(
            P("dp", "mp", None),
            P("dp", "mp", None),
            P("dp"),
            P("dp"),
            P(None, "dp", "mp"),
            P("mp", "dp"),
            P("dp", "mp"),
            P("mp", "dp"),
            P(None, "mp", "dp"),
            P("mp", "dp"),
            P(None, ("dp", "mp")),
            P("dp", "mp", None),
            P("dp", "mp", None),
        ),
        out_specs=(
            P("dp", "mp", None),
            P("dp", "mp", None),
            P("dp", "mp", None),
            P("dp", "mp", None),
            P(None, "dp", "mp"),
            P("mp", "dp"),
            P("dp", "mp"),
            P("mp", "dp"),
            P(None, "mp", "dp"),
            P("mp", "dp"),
            P(None, ("dp", "mp")),
        ),
        check_vma=False,
    )
```

```python
import functools

import jax
import jax.numpy as jnp
from jax import lax
from jax.experimental import pallas as pl
from jax.experimental.pallas import tpu as pltpu
from jax.sharding import PartitionSpec as P

HEAD = 64
EPS = 1e-05
NEG_FILL = -1e30
SCALE = HEAD ** (-0.5)
N_MP = 4
PARTS = 1
CS = 0.3
WIDTH = 768
SMALL = 8
SHARED = 8
LANES = 128
Q_TILE = 256
F32 = jnp.float32
BF16 = jnp.bfloat16
NT = (((1,), (1,)), ((), ()))
NN = (((1,), (0,)), ((), ()))
TN = (((0,), (0,)), ((), ()))


def dot(left, right, dims):
    return lax.dot_general(left, right, dims, preferred_element_type=F32)


def mp_swap(value, step):
    return lax.ppermute(value, "mp", [(i, i ^ step) for i in range(N_MP)])


def dp_swap(value, target):
    size = lax.axis_size("dp")
    return lax.ppermute(value, "dp", [(i, target(i)) for i in range(size)])


def core_swap(value):
    return dp_swap(value, lambda i: i ^ 1)


def clip_blocks(long_rows, short_rows, core):
    block = short_rows.shape[1]
    keep = lax.dynamic_slice_in_dim(long_rows, core * block, block, 0)
    away = lax.dynamic_slice_in_dim(long_rows, (1 - core) * block, block, 0)
    back = core_swap(away)
    first = jnp.where(core == 0, keep, back)
    second = jnp.where(core == 0, back, keep)
    return jnp.stack([first, second, short_rows[0], short_rows[1]])


def clip_pieces(blocks, depth):
    return [
        lax.dynamic_index_in_dim(blocks, depth ^ step, 0, keepdims=False) for step in range(N_MP)
    ]


def to_clips(blocks, depth):
    pieces = clip_pieces(blocks, depth)
    return pieces[:1] + [mp_swap(pieces[step], step) for step in range(1, N_MP)]


def from_clips(rows):
    block = rows.shape[0] // N_MP
    parts = []
    for step in range(N_MP):
        piece = rows[step * block : (step + 1) * block]
        parts.append(piece if step == 0 else mp_swap(piece, step))
    return parts


def frames_of(parts, core, depth):
    blocks = jnp.stack(parts)
    first, second, short_a, short_b = (
        lax.dynamic_index_in_dim(blocks, depth ^ i, 0, keepdims=False) for i in range(N_MP)
    )
    keep = jnp.where(core == 0, first, second)
    away = jnp.where(core == 0, second, first)
    back = core_swap(away)
    low = jnp.where(core == 0, keep, back)
    high = jnp.where(core == 0, back, keep)
    return jnp.concatenate([low, high], axis=0)[None], jnp.stack([short_a, short_b])


def flip(index, late):
    return index ^ ((4 if late else 2) if index % 2 == 0 else (2 if late else 4))


def block_table(mine, size):
    if size != 8:
        return jnp.zeros((1,), jnp.int32)
    early = jnp.where(mine % 2 == 0, 2, 4)
    late = 6 - early
    relative = [0, early, late, 6, 1, 1 ^ late, 1 ^ early, 7]
    return jnp.stack([mine ^ r for r in relative]).astype(jnp.int32)


def early(i):
    return flip(i, False)


def late(i):
    return flip(i, True)


def across(i):
    return i ^ 6


def tie(*values):
    return lax.optimization_barrier(values)


def swap_plane(plane):
    return plane + [core_swap(piece) for piece in plane]


def to_slab(parts):
    return jnp.concatenate(parts, axis=1)


def mp_gather(shard):
    return [shard] + [mp_swap(shard, step) for step in range(1, N_MP)]


def goes_on(terms):
    half = terms[0].shape[0] // 2
    return sum(term[half:].astype(F32) for term in terms).astype(BF16)


def stays(terms, back):
    half = terms[0].shape[0] // 2
    return [term[:half] for term in terms] + [back]


def mp_away(parts):
    return [mp_swap(parts[step].astype(BF16), step) for step in range(1, N_MP)]


def mp_total(own, backs):
    for back in backs:
        own = own + back.astype(F32)
    return own


def blocks_of(pieces):
    step = pieces[0].shape[0]
    return [(p, k * step) for p in pieces for k in range(p.shape[0] // step)]


def block_rows(pieces):
    return WIDTH // len(blocks_of(pieces))


class Weights:
    def __init__(self, pieces, table, held, sems, lo, tile):
        self.held, self.tile = held, tile
        cols, parts = held.shape[2], sems.shape[0]
        self.span, self.copies = cols // parts, []
        for t in range(parts):
            row = []
            for k, (piece, first) in enumerate(blocks_of(pieces)):
                copy = pltpu.make_async_copy(
                    piece.at[pl.ds(first, held.shape[1]), pl.ds(lo + t * self.span, self.span)],
                    held.at[table[k], :, pl.ds(t * self.span, self.span)],
                    sems.at[t, k],
                )
                copy.start()
                row.append(copy)
            self.copies.append(row)
        self.waited = 0

    def whole(self):
        for row in self.copies[self.waited :]:
            for copy in row:
                copy.wait()
        self.waited = len(self.copies)

    def at(self, at):
        count, rows, _ = self.held.shape
        return self.held[:, :, pl.ds(at, self.tile)].reshape(count * rows, self.tile)

    def get(self, t):
        at = t * self.tile
        while self.waited * self.span < at + self.tile:
            for copy in self.copies[self.waited]:
                copy.wait()
            self.waited += 1
        count, rows, _ = self.held.shape
        return self.held[:, :, at : at + self.tile].reshape(count * rows, self.tile)


def weight_scratch(pieces, cols, parts=1):
    return [
        pltpu.VMEM((len(blocks_of(pieces)), block_rows(pieces), cols), BF16),
        pltpu.SemaphoreType.DMA((parts, len(blocks_of(pieces)))),
    ]


def grad_shapes(pieces, cols, extra=0):
    count, rows = len(blocks_of(pieces)), block_rows(pieces)
    if count == 1:
        return [jax.ShapeDtypeStruct((1, rows, cols), F32)]
    return [jax.ShapeDtypeStruct((count // 2, rows + extra, cols), BF16)] * 2


def turn_scratch(pieces, rows):
    return [pltpu.VMEM((len(blocks_of(pieces)), block_rows(pieces), rows), BF16)] * 2


def turn(value, table, plain, turned):
    plain[...] = value.T.reshape(plain.shape)
    for r in range(plain.shape[0]):
        turned[r] = plain[table[r]]


def stage_scratch(pieces, cols):
    return [
        pltpu.VMEM((g.shape[0], block_rows(pieces), cols), g.dtype)
        for g in grad_shapes(pieces, cols)
    ]


def store_grad(turned, right, stages, at):
    count, rows, _ = turned.shape
    grad = dot(turned[...].reshape(count * rows, -1), right, NN)
    half, cols = count // len(stages), right.shape[1]
    for r in range(count):
        stage = stages[r // half]
        part = grad[r * rows : (r + 1) * rows].astype(stage.dtype)
        stage[r % half, :rows, pl.ds(at, cols)] = part


def grad_copies(stages, outs, at, cols, sems, first):
    return [
        pltpu.make_async_copy(
            stage.at[:, :, pl.ds(at, cols)],
            out.at[:, pl.ds(0, stage.shape[1]), pl.ds(at, cols)],
            sems.at[first + i],
        )
        for i, (stage, out) in enumerate(zip(stages, outs))
    ]


def start_all(copies):
    for copy in copies:
        copy.start()


def wait_all(copies):
    for copy in copies:
        copy.wait()


class Writes:
    def __init__(self, sems):
        self.sems, self.copies = sems, []

    def start(self, source, target):
        copy = pltpu.make_async_copy(source, target, self.sems.at[len(self.copies)])
        copy.start()
        self.copies.append(copy)

    def finish(self):
        for copy in self.copies:
            copy.wait()


class Reads:
    def __init__(self, sources, targets, sems):
        self.targets, self.copies = targets, []
        for i, (source, target) in enumerate(zip(sources, targets)):
            copy = pltpu.make_async_copy(source, target, sems.at[i])
            copy.start()
            self.copies.append(copy)

    def get(self, i):
        self.copies[i].wait()
        return self.targets[i]


def read_scratch(arrays):
    return [pltpu.VMEM(a.shape, a.dtype) for a in arrays] + [
        pltpu.SemaphoreType.DMA((len(arrays),))
    ]


def cost(micros):
    return pl.CostEstimate(
        flops=int(micros * 1.1e9 * CS), bytes_accessed=int(micros * 1e5 * CS), transcendentals=0
    )


def call(body, name, micros, outs, arrays, table, pieces, scratch, far=0):
    vmem = pl.BlockSpec(memory_space=pltpu.VMEM)
    away = pl.BlockSpec(memory_space=pl.ANY)
    return pl.pallas_call(
        body,
        out_shape=tuple(outs),
        in_specs=[pl.BlockSpec(memory_space=pltpu.SMEM)]
        + [vmem] * len(arrays)
        + [away] * len(pieces),
        out_specs=(vmem,) * (len(outs) - far) + (away,) * far,
        scratch_shapes=scratch,
        compiler_params=pltpu.CompilerParams(vmem_limit_bytes=60 << 20),
        cost_estimate=cost(micros),
        name=name,
    )(table, *arrays, *pieces)


def like(shape, kind):
    return jax.ShapeDtypeStruct(shape, kind)


def attend_kernel(q_ref, k_ref, v_ref, kp_ref, vp_ref, bias_ref, o_ref, lse_ref):
    rows = q_ref.shape[0]
    keys = jnp.concatenate([k_ref[...], kp_ref[...]], axis=0)
    values = jnp.concatenate([v_ref[...], vp_ref[...]], axis=0)
    bias = bias_ref[...]
    tile = min(rows, Q_TILE)
    low = lax.broadcasted_iota(jnp.int32, (tile, LANES), 1) < HEAD
    for start in range(0, rows, tile):
        q = q_ref[start : start + tile, :]
        outs, logs = [], []
        for half in range(2):
            here = low if half == 0 else ~low
            q_here = jnp.where(here, q, jnp.zeros_like(q))
            scores = dot(q_here, keys, NT) + bias
            top = jnp.max(scores, axis=-1, keepdims=True)
            raised = jnp.exp(scores - top)
            total = jnp.sum(raised, axis=-1, keepdims=True)
            mixed = dot(raised.astype(BF16), values, NN)
            outs.append(mixed / total)
            logs.append(top + jnp.log(total))
        o_ref[start : start + tile, :] = jnp.where(low, outs[0], outs[1]).astype(BF16)
        lse_ref[start : start + tile, :] = jnp.where(low, logs[0], logs[1])


def attend(qkv, kv_other, bias):
    rows, width = qkv.shape[0], qkv.shape[1] // 3
    pairs = width // LANES
    spec = lambda base: pl.BlockSpec((rows, LANES), lambda p: (0, base + p))
    return pl.pallas_call(
        attend_kernel,
        out_shape=(
            jax.ShapeDtypeStruct((rows, width), BF16),
            jax.ShapeDtypeStruct((rows, width), F32),
        ),
        grid=(pairs,),
        in_specs=[
            spec(0),
            spec(pairs),
            spec(2 * pairs),
            spec(0),
            spec(pairs),
            pl.BlockSpec((1, 2 * rows), lambda p: (0, 0)),
        ],
        out_specs=(spec(0), spec(0)),
        compiler_params=pltpu.CompilerParams(vmem_limit_bytes=56 << 20),
        cost_estimate=cost(15),
        name="attend",
    )(qkv, qkv, qkv, kv_other, kv_other, bias)


def attend_back_kernel(
    q_ref, k_ref, v_ref, kp_ref, vp_ref, bias_ref, o_ref, lse_ref, do_ref,
    dq_ref, own_ref, other_ref,
):
    rows = q_ref.shape[0]
    keys = jnp.concatenate([k_ref[...], kp_ref[...]], axis=0)
    values = jnp.concatenate([v_ref[...], vp_ref[...]], axis=0)
    bias = bias_ref[...]
    tile = min(rows, Q_TILE)
    low = lax.broadcasted_iota(jnp.int32, (tile, LANES), 1) < HEAD
    dk = jnp.zeros((LANES, 2 * rows), F32)
    dv = jnp.zeros((LANES, 2 * rows), F32)
    for start in range(0, rows, tile):
        at = slice(start, start + tile)
        q, do = q_ref[at, :], do_ref[at, :]
        product = o_ref[at, :].astype(F32) * do.astype(F32)
        lse = lse_ref[at, :]
        outs = []
        for half in range(2):
            here = low if half == 0 else ~low
            q_here = jnp.where(here, q, jnp.zeros_like(q))
            do_here = jnp.where(here, do, jnp.zeros_like(do))
            inner = jnp.sum(jnp.where(here, product, 0.0), axis=-1, keepdims=True)
            log = lse[:, half * HEAD : half * HEAD + 1]
            soft = jnp.exp(dot(q_here, keys, NT) + bias - log)
            grad = (soft * (dot(do_here, values, NT) - inner)).astype(BF16)
            outs.append(dot(grad, keys, NN))
            dk = dk + dot(q_here, grad, TN)
            dv = dv + dot(do_here, soft.astype(BF16), TN)
        dq_ref[at, :] = (jnp.where(low, outs[0], outs[1]) * SCALE).astype(BF16)
    for i, value in enumerate((dk.T, dv.T)):
        at = slice(i * LANES, (i + 1) * LANES)
        own_ref[:, at] = value[:rows]
        other_ref[:, at] = value[rows:].astype(BF16)


def attend_back(qkv, kv_other, bias, out, lse, grad_out, first, count):
    rows, width = out.shape
    pairs = width // LANES
    spec = lambda base: pl.BlockSpec((rows, LANES), lambda p: (0, base + first + p))
    result = lambda cols: pl.BlockSpec((rows, cols), lambda p: (0, p))
    return pl.pallas_call(
        attend_back_kernel,
        out_shape=(
            jax.ShapeDtypeStruct((rows, count * LANES), BF16),
            jax.ShapeDtypeStruct((rows, 2 * count * LANES), F32),
            jax.ShapeDtypeStruct((rows, 2 * count * LANES), BF16),
        ),
        grid=(count,),
        in_specs=[
            spec(0),
            spec(pairs),
            spec(2 * pairs),
            spec(0),
            spec(pairs),
            pl.BlockSpec((1, 2 * rows), lambda p: (0, 0)),
            spec(0),
            spec(0),
            spec(0),
        ],
        out_specs=(result(LANES), result(2 * LANES), result(2 * LANES)),
        compiler_params=pltpu.CompilerParams(vmem_limit_bytes=56 << 20),
        cost_estimate=cost(3 * count),
        name="attend_back",
    )(qkv, qkv, qkv, kv_other, kv_other, bias, out, lse, grad_out)


def gelu_parts(v):
    cdf = 0.5 * (1.0 + lax.erf(v * (2.0 ** -0.5)))
    pdf = jnp.exp(-0.5 * v * v) * 0.3989422804014327
    return v * cdf, cdf + v * pdf


def norm(values):
    center = values - jnp.mean(values, axis=-1, keepdims=True)
    inv_dev = lax.rsqrt(jnp.mean(center * center, axis=-1, keepdims=True) + EPS)
    return center * inv_dev, inv_dev


def norm_back(scaled, normed, inv_dev):
    return inv_dev * (
        scaled
        - jnp.mean(scaled, axis=-1, keepdims=True)
        - normed * jnp.mean(scaled * normed, axis=-1, keepdims=True)
    )


def total(value):
    return jnp.sum(value, axis=0, keepdims=True)


def join(parts, starts, size, micros):
    rows, cols = parts[0].shape[0], len(starts) * len(parts) * size

    def body(*refs):
        parts, out = refs[:-1], refs[-1]
        at = 0
        for start in starts:
            for part in parts:
                out[:, at : at + size] = part[:, start : start + size]
                at += size

    vmem = pl.BlockSpec(memory_space=pltpu.VMEM)
    return pl.pallas_call(
        body,
        out_shape=like((rows, cols), parts[0].dtype),
        in_specs=[vmem] * len(parts),
        out_specs=vmem,
        cost_estimate=cost(micros),
        name="join",
    )(*parts)


def project(x_parts, head_row, table, pieces):
    block, width = x_parts[0].shape
    rows = block * len(x_parts)
    n = len(pieces)

    def body(table, *refs):
        part_refs, bias_ref, refs = refs[:N_MP], refs[N_MP], refs[N_MP + 1 :]
        pieces, (x_ref, qkv_ref, kv_ref, held, sems) = refs[:n], refs[n:]
        weights = Weights(pieces, table, held, sems, 0, width)
        for i, part in enumerate(part_refs):
            x_ref[i * block : (i + 1) * block, :] = part[...]
        x = x_ref[...]
        for i in range(3):
            value = dot(x, weights.get(i), NN) + bias_ref[:, i * width : (i + 1) * width]
            value = value.astype(BF16)
            if i == 0:
                value = (value.astype(F32) * SCALE).astype(BF16)
            else:
                kv_ref[:, (i - 1) * width : i * width] = value
            qkv_ref[:, i * width : (i + 1) * width] = value

    return call(
        body,
        "project",
        7,
        [
            like((rows, width), BF16),
            like((rows, 3 * width), BF16),
            like((rows, 2 * width), BF16),
        ],
        list(x_parts) + [head_row],
        table,
        pieces,
        weight_scratch(pieces, 3 * width, 3),
    )


def feed(x, mixed, cot_parts, smalls, small_row, table, out_pieces, feed_pieces):
    rows, width = x.shape
    hidden = feed_pieces[0].shape[1] // 2
    count = 6
    tile = hidden // count
    cols = hidden + width
    n_out, n_up, n = len(out_pieces), len(feed_pieces), len(smalls)
    down_grads = grad_shapes(feed_pieces, hidden)
    mid_grads = grad_shapes(feed_pieces, cols, SHARED)
    g = len(mid_grads)

    def body(table, x_ref, mixed_ref, *refs):
        cot_far, small_far, refs = refs[:N_MP], refs[N_MP : N_MP + n], refs[N_MP + n :]
        out_p, up_p = refs[:n_out], refs[n_out : n_out + n_up]
        refs = refs[n_out + n_up :]
        shared_ref, result_out, da_out, do_out = refs[:4]
        down_outs, mid_outs, refs = refs[4 : 4 + g], refs[4 + g : 4 + 2 * g], refs[4 + 2 * g :]
        w_out, sems_out, w_up, sems_up, w_down, sems_down = refs[:6]
        plain, turned, plain_h, turned_h = refs[6:10]
        small_ref, cot_ref, read_sems = refs[10:13]
        n1_ref, dz_ref, h_ref, act_ref, slope_ref, result_ref, low_ref, do_ref = refs[13:21]
        down_stages, mid_stages = refs[21 : 21 + g], refs[21 + g : 21 + 2 * g]
        shared_low, sems, grad_sems, up_b_ref = refs[21 + 2 * g :]
        out_w = Weights(out_p, table, w_out, sems_out, 3 * width, width)
        smalls = [small.at[pl.ds(small_row, SMALL)] for small in small_far]
        reads = Reads(smalls, [small_ref.at[i] for i in range(n)], read_sems)
        up_w = Weights(up_p, table, w_up, sems_up, 0, tile)
        down_w = Weights(up_p, table, w_down, sems_down, hidden, tile)
        block = rows // N_MP
        cots = Reads(
            cot_far,
            [cot_ref.at[pl.ds(i * block, block)] for i in range(N_MP)],
            read_sems.at[pl.ds(n, N_MP)],
        )
        writes = Writes(sems)

        attention = dot(mixed_ref[...], out_w.get(0), NT)
        for i in range(n):
            reads.get(i)
        small = jnp.sum(small_ref[...].astype(F32), axis=0)
        row_vals = sum(small[:, i * width : (i + 1) * width] for i in range(2 * N_MP))
        row = lambda i: row_vals[i : i + 1, :]
        up_b = small[6:7, :hidden]
        n1, r1 = norm(x_ref[...].astype(F32) + attention + row(0))
        n1_ref[...] = n1
        h_ref[...] = (n1 * row(1) + row(2)).astype(BF16)
        up_b_ref[...] = up_b
        dz_ref[...] = jnp.zeros_like(dz_ref)
        up_w.whole()
        down_w.whole()

        @pl.loop(0, count // 2)
        def _(i):
            ats = [pl.multiple_of((2 * i + k) * tile, tile) for k in range(2)]
            us = [dot(h_ref[...], up_w.at(at), NN) for at in ats]
            for at, u in zip(ats, us):
                act, slope = gelu_parts(u + up_b_ref[:, pl.ds(at, tile)])
                act_ref[:, pl.ds(at, tile)] = act.astype(BF16)
                slope_ref[:, pl.ds(at, tile)] = slope.astype(BF16)
                dz_ref[...] += dot(act_ref[:, pl.ds(at, tile)], down_w.at(at), NT)

        feed = dz_ref[...]
        h = n1_ref[...] * row(1) + row(2)
        n2, r2 = norm(h + feed + row(3))
        result_ref[...] = (n2 * row(4) + row(5)).astype(BF16)
        writes.start(result_ref, result_out)
        for i in range(N_MP):
            cots.get(i)
        gy = cot_ref[...].astype(F32)
        dz = norm_back(gy * row(4), n2, r2)
        dz_ref[...] = dz
        low_ref[...] = dz.astype(BF16)
        sums = [total(dz), total(gy * n2), total(gy)]

        turn(low_ref[...], table, plain, turned)
        turn(h_ref[...], table, plain_h, turned_h)
        shared_ref[...] = jnp.zeros_like(shared_ref)
        def tile_copies(t):
            at = t * tile if isinstance(t, int) else pl.multiple_of(t * tile, tile)
            down = grad_copies(down_stages, down_outs, at, tile, grad_sems, 2 * g * t)
            return down + grad_copies(mid_stages, mid_outs, at, tile, grad_sems, 2 * g * t + g)

        @pl.loop(0, count)
        def _(t):
            at = pl.multiple_of(t * tile, tile)
            dact = dot(low_ref[...], down_w.at(at), NN)
            store_grad(turned, act_ref[:, pl.ds(at, tile)], down_stages, at)
            du = (dact * slope_ref[:, pl.ds(at, tile)].astype(F32)).astype(BF16)
            shared_ref[0:1, pl.ds(at, tile)] = total(du.astype(F32))
            dz_ref[...] += dot(du, up_w.at(at), NT)
            store_grad(turned_h, du, mid_stages, at)
            start_all(tile_copies(t))

        dh = dz_ref[...]
        n1 = n1_ref[...]
        da = norm_back(dh * row(1), n1, r1)
        dz_ref[...] = da
        writes.start(dz_ref, da_out)
        low_ref[...] = da.astype(BF16)
        do_ref[...] = dot(low_ref[...], out_w.get(0), NN).astype(BF16)
        writes.start(do_ref, do_out)
        sums = [total(da), total(dh * n1), total(dh)] + sums
        for j in range(hidden // width):
            for i, value in enumerate(sums):
                shared_ref[1 + i : 2 + i, j * width : (j + 1) * width] = value
        if g > 1:
            shared_low[...] = shared_ref[...].astype(BF16)
            for out in mid_outs:
                for r in range(out.shape[0]):
                    writes.start(shared_low, out.at[r, pl.ds(block_rows(feed_pieces), SHARED)])
        turn(low_ref[...], table, plain, turned)
        store_grad(turned, mixed_ref[...], mid_stages, hidden)
        last = grad_copies(mid_stages, mid_outs, hidden, width, grad_sems, 2 * g * count)
        start_all(last)
        for t in range(count):
            wait_all(tile_copies(t))
        wait_all(last)
        writes.finish()

    near = [((rows, width), F32)] * 2 + [((rows, width), BF16)]
    near += [((rows, hidden), BF16)] * 2 + [((rows, width), BF16)] * 3
    return call(
        body,
        "feed",
        33,
        [
            like((SHARED, cols), F32),
            like((rows, width), BF16),
            like((rows, width), F32),
            like((rows, width), BF16),
        ]
        + down_grads
        + mid_grads,
        [x, mixed],
        table,
        list(cot_parts) + list(smalls) + list(out_pieces) + list(feed_pieces),
        weight_scratch(out_pieces, width)
        + weight_scratch(feed_pieces, hidden) * 2
        + turn_scratch(feed_pieces, rows) * 2
        + [
            pltpu.VMEM((n, SMALL, 2 * hidden), BF16),
            pltpu.VMEM((rows, width), BF16),
            pltpu.SemaphoreType.DMA((n + N_MP,)),
        ]
        + [pltpu.VMEM(*spec) for spec in near]
        + stage_scratch(feed_pieces, hidden)
        + stage_scratch(feed_pieces, cols)
        + [
            pltpu.VMEM((SHARED, cols), BF16),
            pltpu.SemaphoreType.DMA((3 + n_up,)),
            pltpu.SemaphoreType.DMA((g * (2 * count + 1),)),
            pltpu.VMEM((1, hidden), F32),
        ],
        far=3 + 2 * g,
    )


def project_back(da, parts, table, pieces):
    rows, width = da.shape
    n = len(pieces)
    flat = [value for part in parts for value in part]

    def body(table, da_ref, *refs):
        part_refs, refs = refs[: len(flat)], refs[len(flat) :]
        pieces, (out_ref, dqkv_ref, held, sems) = refs[:n], refs[n:]
        weights = Weights(pieces, table, held, sems, 0, width)
        pair = 0
        for i in range(0, len(flat), 3):
            q_ref, own_ref, back_ref = part_refs[i : i + 3]
            cols = q_ref.shape[1]
            dqkv_ref[:, pair * LANES : pair * LANES + cols] = q_ref[...]
            for p in range(cols // LANES):
                for which in range(2):
                    at = slice((2 * p + which) * LANES, (2 * p + which + 1) * LANES)
                    to = (which + 1) * width + (pair + p) * LANES
                    value = own_ref[:, at] + back_ref[:, at].astype(F32)
                    dqkv_ref[:, to : to + LANES] = value.astype(BF16)
            pair += cols // LANES
        value = da_ref[...]
        for i in range(3):
            value = value + dot(dqkv_ref[:, i * width : (i + 1) * width], weights.get(i), NT)
        out_ref[...] = value.astype(BF16)

    return call(
        body,
        "project_back",
        9,
        [like((rows, width), BF16), like((rows, 3 * width), BF16)],
        [da] + flat,
        table,
        pieces,
        weight_scratch(pieces, 3 * width, 3),
    )


def project_grads(x, dqkv, table, pieces):
    rows, width = x.shape
    grads = grad_shapes(pieces, 3 * width, SHARED)
    g = len(grads)

    def body(table, x_ref, dqkv_ref, *refs):
        shared_ref, grad_outs, refs = refs[0], refs[1 : 1 + g], refs[1 + g :]
        plain, turned = refs[:2]
        stages, shared_low, sems = refs[2 : 2 + g], refs[2 + g], refs[3 + g]
        writes = Writes(sems.at[pl.ds(3 * g, len(blocks_of(pieces)))])
        turn(x_ref[...], table, plain, turned)

        @pl.loop(0, 3)
        def _(i):
            at = pl.multiple_of(i * width, width)
            store_grad(turned, dqkv_ref[:, pl.ds(at, width)], stages, at)
            start_all(grad_copies(stages, grad_outs, at, width, sems, g * i))

        shared_ref[...] = jnp.zeros_like(shared_ref)
        shared_ref[0:1, :] = total(dqkv_ref[...].astype(F32))
        if g > 1:
            shared_low[...] = shared_ref[...].astype(BF16)
            for out in grad_outs:
                for r in range(out.shape[0]):
                    writes.start(shared_low, out.at[r, pl.ds(block_rows(pieces), SHARED)])
        for i in range(3):
            wait_all(grad_copies(stages, grad_outs, i * width, width, sems, g * i))
        writes.finish()

    return call(
        body,
        "project_grads",
        7,
        [like((SHARED, 3 * width), F32)] + grads,
        [x, dqkv],
        table,
        [],
        turn_scratch(pieces, rows)
        + stage_scratch(pieces, 3 * width)
        + [
            pltpu.VMEM((SHARED, 3 * width), BF16),
            pltpu.SemaphoreType.DMA((3 * g + len(blocks_of(pieces)),)),
        ],
        far=g,
    )


def at_column(values, rows, width, column):
    return lax.dynamic_update_slice(jnp.zeros((rows, width), values.dtype), values, (0, column))


def small_block(row_params, expand_bias, mine, depth):
    high = lax.reduce_precision(row_params, 8, 7)
    column = (mine * N_MP + depth) * row_params.shape[1]
    high_low = [
        at_column(part.astype(BF16), 6, WIDTH, column) for part in (high, row_params - high)
    ]
    bias = at_column(expand_bias, 2, 2 * WIDTH, mine * expand_bias.shape[1])
    return jnp.concatenate([jnp.concatenate(high_low, axis=1), bias])


def key_bias(length_long, length_short, block, core, depth):
    lengths = jnp.concatenate([length_long, length_short])
    other = core_swap(lengths)
    longs = jnp.where(core == 0, jnp.stack([lengths[0], other[0]]), jnp.stack([other[0], lengths[0]]))
    length = jnp.concatenate([longs, lengths[1:]])[depth]
    is_long = depth < 2
    place = lax.broadcasted_iota(jnp.int32, (1, 2 * N_MP * block), 1)
    row = place % (N_MP * block)
    is_own = place < N_MP * block
    source = (row // block) ^ depth
    whose = jnp.where(is_own, core, 1 - core)
    frame = row % block + jnp.where(is_long, (2 * source + whose) * block, source * block)
    counted = (frame < length) & (is_own | is_long)
    return jnp.where(counted, 0.0, NEG_FILL).astype(F32)


def on_device(
    frames_long,
    frames_short,
    length_long,
    length_short,
    input_proj,
    output_proj,
    expand_weight,
    shrink_weight,
    head_bias,
    expand_bias,
    row_params,
    cotangent_long,
    cotangent_short,
):
    mine = lax.axis_index("dp")
    depth = lax.axis_index("mp")
    n_dp = lax.axis_size("dp")
    fast = n_dp == 8
    core = mine % 2
    block = frames_short.shape[1]
    shard, group = input_proj.shape[1:]
    units = expand_weight.shape[1]
    width = group * N_MP
    hidden = units * N_MP
    table = block_table(mine, n_dp)

    joined = jnp.concatenate(
        [input_proj[0], input_proj[1], input_proj[2], output_proj.T], axis=1
    )
    heads = at_column(head_bias[:, 0], SMALL, WIDTH, mine * head_bias.shape[2])
    attn_parts = mp_gather(jnp.concatenate([joined, heads]))
    x_blocks = clip_blocks(frames_long[0], frames_short, core)
    cot_blocks = clip_blocks(cotangent_long[0], cotangent_short, core)
    bias = key_bias(length_long, length_short, block, core, depth)
    feed_shard = jnp.concatenate(
        [
            jnp.concatenate([expand_weight, shrink_weight.T], axis=1),
            small_block(row_params, expand_bias, mine, depth),
        ]
    )
    *attn_parts, feed_shard, bias, x_blocks, cot_blocks = tie(
        *attn_parts, feed_shard, bias, x_blocks, cot_blocks
    )
    order = [p[:shard, i * group : (i + 1) * group] for i in range(4) for p in attn_parts]
    attn_slab = jnp.concatenate([to_slab(order), to_slab([p[shard:] for p in attn_parts])])
    feed_parts = mp_gather(feed_shard)
    feed_order = [p[:, i * units : (i + 1) * units] for i in range(2) for p in feed_parts]
    if fast:
        attn_p = [attn_slab] + [dp_swap(attn_slab, to) for to in (early, late, across)]
        x_pieces = clip_pieces(x_blocks, depth)
        attn_p += [core_swap(piece) for piece in attn_p]
        both = tie(*attn_p, *x_pieces, *feed_order)
        attn_p, x_pieces, feed_order = both[:8], both[8:12], both[12:]
        feed_slab = to_slab(feed_order)
        feed_one = dp_swap(feed_slab, early)
        feed_two = dp_swap(feed_slab, late)
        x_parts = [x_pieces[0]] + [mp_swap(x_pieces[i], i) for i in range(1, N_MP)]
        *x_parts, cot_blocks, own_slab = tie(*x_parts, cot_blocks, feed_slab)
        heads = sum(p[shard:].astype(F32) for p in attn_p)
    else:
        x_parts = to_clips(x_blocks, depth)
        gather = lambda slab: lax.all_gather(slab, "dp", axis=0)
        whole = gather(attn_slab)
        heads = jnp.sum(whole[:, shard:].astype(F32), axis=0)
        attn_p = [whole[:, :shard].reshape(width, 4 * width)]
        whole = gather(to_slab(feed_order))
        small = jnp.sum(whole[:, shard:].astype(F32), axis=0)
        feed_p = [whole[:, :shard].reshape(width, 2 * hidden)]
    cot_parts = to_clips(cot_blocks, depth)
    heads = jnp.concatenate(
        [heads[:2, i * width : i * width + group] for i in range(N_MP)], axis=1
    )
    head_row = jnp.concatenate([heads[:1], jnp.zeros_like(heads[:1]), heads[1:]], axis=1)

    x, qkv, kv = project(x_parts, head_row, table, attn_p)
    if fast:
        kv, feed_one, feed_two, cot_parts[3], own_slab = tie(
            kv, feed_one, feed_two, cot_parts[3], core_swap(own_slab)
        )
    kv_other = core_swap(kv)
    if fast:
        feed_three = dp_swap(feed_one, late)
        feed_p = [feed_slab, feed_one, feed_two]
        backs = [own_slab] + [core_swap(piece) for piece in feed_p[1:]]
    mixed, lse = attend(qkv, kv_other, bias)
    if fast:
        mixed, feed_three, *both = tie(mixed, feed_three, *backs, *cot_parts)
        backs, cot_parts = both[:3], both[3:]
        feed_p = feed_p + [feed_three] + backs + [core_swap(feed_three)]
        smalls, small_row = feed_p, shard
    else:
        smalls, small_row = [small.astype(BF16)], 0
    outs = feed(x, mixed, cot_parts, smalls, small_row, table, attn_p, feed_p)
    mid_shared, result, da, do, *grads = outs
    g_down, g_mid = grads[: len(grads) // 2], grads[len(grads) // 2 :]

    def by_group_of(value, sizes):
        starts = [N_MP * sum(sizes[:i]) for i in range(len(sizes))]
        return [
            jnp.concatenate(
                [value[:, a + j * n : a + (j + 1) * n] for a, n in zip(starts, sizes)], axis=1
            )
            for j in range(N_MP)
        ]

    def last_sum(terms):
        return sum(term[0].astype(F32) for term in terms)

    result_parts = from_clips(result)
    if fast:
        b_down, b_mid = core_swap(g_down[1]), core_swap(g_mid[1])
    pairs = width // LANES
    first = pairs // 2
    dq_a, own_a, other_a = attend_back(qkv, kv_other, bias, mixed, lse, do, 0, first)
    if fast:
        other_a, b_down, b_mid, result_parts[3] = tie(other_a, b_down, b_mid, result_parts[3])
        t_down = [g_down[0], b_down]
        a_down = goes_on(t_down)
        do, a_down = tie(do, a_down)
        b_down = dp_swap(a_down, late)
        t_mid = [g_mid[0], b_mid]
        a_mid = goes_on(t_mid)
        do, a_mid = tie(do, a_mid)
        b_mid = dp_swap(a_mid, late)
    back_a = core_swap(other_a)
    dq_b, own_b, other_b = attend_back(
        qkv, kv_other, bias, mixed, lse, do, first, pairs - first
    )
    if fast:
        other_b, back_a, *result_parts = tie(other_b, back_a, *result_parts)
    back_b = core_swap(other_b)
    parts = [(dq_a, own_a, back_a), (dq_b, own_b, back_b)]
    frames_grad, dqkv = project_back(da, parts, table, attn_p)
    grad_parts = from_clips(frames_grad)
    if fast:
        dqkv, b_down, b_mid = tie(dqkv, b_down, b_mid)
        t_down, t_mid = stays(t_down, b_down), stays(t_mid, b_mid)
        a_down, a_mid = goes_on(t_down), goes_on(t_mid)
        dqkv, a_down, a_mid = tie(dqkv, a_down, a_mid)
        b_down = dp_swap(a_down, early)
        b_mid = dp_swap(a_mid, early)
    attn_shared, *g_attn = project_grads(x, dqkv, table, attn_p)
    if fast:
        both = tie(*g_attn, b_down, b_mid, grad_parts[3])
        g_attn, b_down, b_mid, grad_parts[3] = both[:2], both[2], both[3], both[4]
        b_attn = core_swap(g_attn[1])
        s_down = by_group_of(last_sum(stays(t_down, b_down)), [units])
        t_attn = [g_attn[0], b_attn]
        a_attn = goes_on(t_attn)
        a_attn, *s_down = tie(a_attn, *s_down)
        b_attn = dp_swap(a_attn, late)
        z_down = mp_away(s_down)
        s_mid = by_group_of(last_sum(stays(t_mid, b_mid)), [units, group])
        b_attn, *z_down = tie(b_attn, *z_down)
        t_attn = stays(t_attn, b_attn)
        a_attn = goes_on(t_attn)
        z_mid = mp_away(s_mid)
        b_attn, *both = tie(dp_swap(a_attn, early), *z_mid, *result_parts)
        z_mid, result_parts = both[: N_MP - 1], both[N_MP - 1 :]
        s_attn = last_sum(stays(t_attn, b_attn))
    else:
        scatter = lambda g: lax.psum_scatter(g[0][0], "dp", scatter_dimension=0, tiled=True)
        s_down = by_group_of(scatter(g_down), [units])
        z_down = mp_away(s_down)
        s_mid = jnp.concatenate([scatter(g_mid), lax.psum(mid_shared, "dp")])
        s_mid = by_group_of(s_mid, [units, group])
        z_mid = mp_away(s_mid)
        s_attn = jnp.concatenate([scatter(g_attn), lax.psum(attn_shared, "dp")])
    s_attn = by_group_of(s_attn, [group] * 3)
    grad_long, grad_short = frames_of(grad_parts, core, depth)
    result_long, result_short = frames_of(result_parts, core, depth)
    attn_share = mp_total(s_attn[0], mp_away(s_attn))
    down_share = mp_total(s_down[0], z_down).T
    mid_share = mp_total(s_mid[0], z_mid)
    up_share = mid_share[:shard, :units]
    output_share = mid_share[:shard, units:].T
    input_share = jnp.stack(
        [attn_share[:shard, i * group : (i + 1) * group] for i in range(3)]
    )
    up_cols, head_cols, row_cols = units // n_dp, group // n_dp, width // (n_dp * N_MP)
    rank = mine * N_MP + depth
    up_b_share = lax.dynamic_slice(mid_share, (shard, mine * up_cols), (1, up_cols))
    row_share = lax.dynamic_slice(mid_share, (shard + 1, rank * row_cols), (6, row_cols))
    head_share = jnp.stack(
        [
            lax.dynamic_slice(attn_share, (shard, at + mine * head_cols), (1, head_cols))
            for at in (0, 2 * group)
        ]
    )
    return (
        result_long,
        result_short,
        grad_long.astype(F32),
        grad_short.astype(F32),
        input_share,
        output_share,
        up_share,
        down_share,
        head_share,
        up_b_share,
        row_share,
    )


def solution(mesh):
    return jax.shard_map(
        on_device,
        mesh=mesh,
        in_specs=(
            P("dp", "mp", None),
            P("dp", "mp", None),
            P("dp"),
            P("dp"),
            P(None, "dp", "mp"),
            P("mp", "dp"),
            P("dp", "mp"),
            P("mp", "dp"),
            P(None, "mp", "dp"),
            P("mp", "dp"),
            P(None, ("dp", "mp")),
            P("dp", "mp", None),
            P("dp", "mp", None),
        ),
        out_specs=(
            P("dp", "mp", None),
            P("dp", "mp", None),
            P("dp", "mp", None),
            P("dp", "mp", None),
            P(None, "dp", "mp"),
            P("mp", "dp"),
            P("dp", "mp"),
            P("mp", "dp"),
            P(None, "mp", "dp"),
            P("mp", "dp"),
            P(None, ("dp", "mp")),
        ),
        check_vma=False,
    )
```

```python
import functools

import jax
import jax.numpy as jnp
from jax import lax
from jax.experimental import pallas as pl
from jax.experimental.pallas import tpu as pltpu
from jax.sharding import PartitionSpec as P

HEAD = 64
EPS = 1e-05
NEG_FILL = -1e30
SCALE = HEAD ** (-0.5)
N_MP = 4
PARTS = 1
CS = 0.3
WIDTH = 768
SMALL = 8
SHARED = 8
LANES = 128
Q_TILE = 256
F32 = jnp.float32
BF16 = jnp.bfloat16
NT = (((1,), (1,)), ((), ()))
NN = (((1,), (0,)), ((), ()))
TN = (((0,), (0,)), ((), ()))


def dot(left, right, dims):
    return lax.dot_general(left, right, dims, preferred_element_type=F32)


def mp_swap(value, step):
    return lax.ppermute(value, "mp", [(i, i ^ step) for i in range(N_MP)])


def dp_swap(value, target):
    size = lax.axis_size("dp")
    return lax.ppermute(value, "dp", [(i, target(i)) for i in range(size)])


def core_swap(value):
    return dp_swap(value, lambda i: i ^ 1)


def clip_blocks(long_rows, short_rows, core):
    block = short_rows.shape[1]
    keep = lax.dynamic_slice_in_dim(long_rows, core * block, block, 0)
    away = lax.dynamic_slice_in_dim(long_rows, (1 - core) * block, block, 0)
    back = core_swap(away)
    first = jnp.where(core == 0, keep, back)
    second = jnp.where(core == 0, back, keep)
    return jnp.stack([first, second, short_rows[0], short_rows[1]])


def clip_pieces(blocks, depth):
    return [
        lax.dynamic_index_in_dim(blocks, depth ^ step, 0, keepdims=False) for step in range(N_MP)
    ]


def to_clips(blocks, depth):
    pieces = clip_pieces(blocks, depth)
    return pieces[:1] + [mp_swap(pieces[step], step) for step in range(1, N_MP)]


def from_clips(parts):
    return parts[:1] + [mp_swap(parts[step], step) for step in range(1, N_MP)]


def frames_of(parts, core, depth):
    blocks = jnp.stack(parts)
    first, second, short_a, short_b = (
        lax.dynamic_index_in_dim(blocks, depth ^ i, 0, keepdims=False) for i in range(N_MP)
    )
    keep = jnp.where(core == 0, first, second)
    away = jnp.where(core == 0, second, first)
    back = core_swap(away)
    low = jnp.where(core == 0, keep, back)
    high = jnp.where(core == 0, back, keep)
    return jnp.concatenate([low, high], axis=0)[None], jnp.stack([short_a, short_b])


def flip(index, late):
    return index ^ ((4 if late else 2) if index % 2 == 0 else (2 if late else 4))


def block_table(mine, size):
    if size != 8:
        return jnp.zeros((1,), jnp.int32)
    early = jnp.where(mine % 2 == 0, 2, 4)
    late = 6 - early
    relative = [0, early, late, 6, 1, 1 ^ late, 1 ^ early, 7]
    return jnp.stack([mine ^ r for r in relative]).astype(jnp.int32)


def early(i):
    return flip(i, False)


def late(i):
    return flip(i, True)


def across(i):
    return i ^ 6


def tie(*values):
    return lax.optimization_barrier(values)


def swap_plane(plane):
    return plane + [core_swap(piece) for piece in plane]


def to_slab(parts):
    return jnp.concatenate(parts, axis=1)


def mp_gather(shard):
    return [shard] + [mp_swap(shard, step) for step in range(1, N_MP)]


def goes_on(terms):
    half = terms[0].shape[0] // 2
    return sum(term[half:].astype(F32) for term in terms).astype(BF16)


def stays(terms, back):
    half = terms[0].shape[0] // 2
    return [term[:half] for term in terms] + [back]


def mp_away(parts):
    return [mp_swap(parts[step].astype(BF16), step) for step in range(1, N_MP)]


def mp_total(own, backs):
    for back in backs:
        own = own + back.astype(F32)
    return own


def blocks_of(pieces):
    step = pieces[0].shape[0]
    return [(p, k * step) for p in pieces for k in range(p.shape[0] // step)]


def block_rows(pieces):
    return WIDTH // len(blocks_of(pieces))


class Weights:
    def __init__(self, pieces, table, held, sems, lo, tile):
        self.held, self.tile = held, tile
        cols, parts = held.shape[2], sems.shape[0]
        self.span, self.copies = cols // parts, []
        for t in range(parts):
            row = []
            for k, (piece, first) in enumerate(blocks_of(pieces)):
                copy = pltpu.make_async_copy(
                    piece.at[pl.ds(first, held.shape[1]), pl.ds(lo + t * self.span, self.span)],
                    held.at[table[k], :, pl.ds(t * self.span, self.span)],
                    sems.at[t, k],
                )
                copy.start()
                row.append(copy)
            self.copies.append(row)
        self.waited = 0

    def whole(self):
        for row in self.copies[self.waited :]:
            for copy in row:
                copy.wait()
        self.waited = len(self.copies)

    def at(self, at):
        count, rows, _ = self.held.shape
        return self.held[:, :, pl.ds(at, self.tile)].reshape(count * rows, self.tile)

    def get(self, t):
        at = t * self.tile
        while self.waited * self.span < at + self.tile:
            for copy in self.copies[self.waited]:
                copy.wait()
            self.waited += 1
        count, rows, _ = self.held.shape
        return self.held[:, :, at : at + self.tile].reshape(count * rows, self.tile)


def weight_scratch(pieces, cols, parts=1):
    return [
        pltpu.VMEM((len(blocks_of(pieces)), block_rows(pieces), cols), BF16),
        pltpu.SemaphoreType.DMA((parts, len(blocks_of(pieces)))),
    ]


def grad_shapes(pieces, cols, extra=0):
    count, rows = len(blocks_of(pieces)), block_rows(pieces)
    if count == 1:
        return [jax.ShapeDtypeStruct((1, rows, cols), F32)]
    return [jax.ShapeDtypeStruct((count // 2, rows + extra, cols), BF16)] * 2


def turn_scratch(pieces, rows):
    return [pltpu.VMEM((len(blocks_of(pieces)), block_rows(pieces), rows), BF16)] * 2


def turn(value, table, plain, turned):
    plain[...] = value.T.reshape(plain.shape)
    for r in range(plain.shape[0]):
        turned[r] = plain[table[r]]


def stage_scratch(pieces, cols):
    return [
        pltpu.VMEM((g.shape[0], block_rows(pieces), cols), g.dtype)
        for g in grad_shapes(pieces, cols)
    ]


def store_grad(turned, right, stages, at):
    count, rows, _ = turned.shape
    grad = dot(turned[...].reshape(count * rows, -1), right, NN)
    half, cols = count // len(stages), right.shape[1]
    for r in range(count):
        stage = stages[r // half]
        part = grad[r * rows : (r + 1) * rows].astype(stage.dtype)
        stage[r % half, :rows, pl.ds(at, cols)] = part


def grad_copies(stages, outs, at, cols, sems, first):
    return [
        pltpu.make_async_copy(
            stage.at[:, :, pl.ds(at, cols)],
            out.at[:, pl.ds(0, stage.shape[1]), pl.ds(at, cols)],
            sems.at[first + i],
        )
        for i, (stage, out) in enumerate(zip(stages, outs))
    ]


def start_all(copies):
    for copy in copies:
        copy.start()


def wait_all(copies):
    for copy in copies:
        copy.wait()


class Writes:
    def __init__(self, sems):
        self.sems, self.copies = sems, []

    def start(self, source, target):
        copy = pltpu.make_async_copy(source, target, self.sems.at[len(self.copies)])
        copy.start()
        self.copies.append(copy)

    def finish(self):
        for copy in self.copies:
            copy.wait()


class Reads:
    def __init__(self, sources, targets, sems):
        self.targets, self.copies = targets, []
        for i, (source, target) in enumerate(zip(sources, targets)):
            copy = pltpu.make_async_copy(source, target, sems.at[i])
            copy.start()
            self.copies.append(copy)

    def get(self, i):
        self.copies[i].wait()
        return self.targets[i]


def read_scratch(arrays):
    return [pltpu.VMEM(a.shape, a.dtype) for a in arrays] + [
        pltpu.SemaphoreType.DMA((len(arrays),))
    ]


def cost(micros):
    return pl.CostEstimate(
        flops=int(micros * 1.1e9 * CS), bytes_accessed=int(micros * 1e5 * CS), transcendentals=0
    )


def call(body, name, micros, outs, arrays, table, pieces, scratch, far=0):
    vmem = pl.BlockSpec(memory_space=pltpu.VMEM)
    away = pl.BlockSpec(memory_space=pl.ANY)
    return pl.pallas_call(
        body,
        out_shape=tuple(outs),
        in_specs=[pl.BlockSpec(memory_space=pltpu.SMEM)]
        + [vmem] * len(arrays)
        + [away] * len(pieces),
        out_specs=(vmem,) * (len(outs) - far) + (away,) * far,
        scratch_shapes=scratch,
        compiler_params=pltpu.CompilerParams(vmem_limit_bytes=60 << 20),
        cost_estimate=cost(micros),
        name=name,
    )(table, *arrays, *pieces)


def like(shape, kind):
    return jax.ShapeDtypeStruct(shape, kind)


def attend_kernel(q_ref, k_ref, v_ref, kp_ref, vp_ref, bias_ref, o_ref, lse_ref):
    rows = q_ref.shape[0]
    keys = jnp.concatenate([k_ref[...], kp_ref[...]], axis=0)
    values = jnp.concatenate([v_ref[...], vp_ref[...]], axis=0)
    bias = bias_ref[...]
    tile = min(rows, Q_TILE)
    low = lax.broadcasted_iota(jnp.int32, (tile, LANES), 1) < HEAD
    for start in range(0, rows, tile):
        q = q_ref[start : start + tile, :]
        outs, logs = [], []
        for half in range(2):
            here = low if half == 0 else ~low
            q_here = jnp.where(here, q, jnp.zeros_like(q))
            scores = dot(q_here, keys, NT) + bias
            top = jnp.max(scores, axis=-1, keepdims=True)
            raised = jnp.exp(scores - top)
            total = jnp.sum(raised, axis=-1, keepdims=True)
            mixed = dot(raised.astype(BF16), values, NN)
            outs.append(mixed / total)
            logs.append(top + jnp.log(total))
        o_ref[start : start + tile, :] = jnp.where(low, outs[0], outs[1]).astype(BF16)
        lse_ref[start : start + tile, :] = jnp.where(low, logs[0], logs[1])


def attend(qkv, kv_other, bias):
    rows, width = qkv.shape[0], qkv.shape[1] // 3
    pairs = width // LANES
    spec = lambda base: pl.BlockSpec((rows, LANES), lambda p: (0, base + p))
    return pl.pallas_call(
        attend_kernel,
        out_shape=(
            jax.ShapeDtypeStruct((rows, width), BF16),
            jax.ShapeDtypeStruct((rows, width), F32),
        ),
        grid=(pairs,),
        in_specs=[
            spec(0),
            spec(pairs),
            spec(2 * pairs),
            spec(0),
            spec(pairs),
            pl.BlockSpec((1, 2 * rows), lambda p: (0, 0)),
        ],
        out_specs=(spec(0), spec(0)),
        compiler_params=pltpu.CompilerParams(vmem_limit_bytes=56 << 20),
        cost_estimate=cost(15),
        name="attend",
    )(qkv, qkv, qkv, kv_other, kv_other, bias)


def attend_back_kernel(
    q_ref, k_ref, v_ref, kp_ref, vp_ref, bias_ref, o_ref, lse_ref, do_ref,
    dq_ref, own_ref, other_ref,
):
    rows = q_ref.shape[0]
    keys = jnp.concatenate([k_ref[...], kp_ref[...]], axis=0)
    values = jnp.concatenate([v_ref[...], vp_ref[...]], axis=0)
    bias = bias_ref[...]
    tile = min(rows, Q_TILE)
    low = lax.broadcasted_iota(jnp.int32, (tile, LANES), 1) < HEAD
    dk = jnp.zeros((LANES, 2 * rows), F32)
    dv = jnp.zeros((LANES, 2 * rows), F32)
    for start in range(0, rows, tile):
        at = slice(start, start + tile)
        q, do = q_ref[at, :], do_ref[at, :]
        product = o_ref[at, :].astype(F32) * do.astype(F32)
        lse = lse_ref[at, :]
        outs = []
        for half in range(2):
            here = low if half == 0 else ~low
            q_here = jnp.where(here, q, jnp.zeros_like(q))
            do_here = jnp.where(here, do, jnp.zeros_like(do))
            inner = jnp.sum(jnp.where(here, product, 0.0), axis=-1, keepdims=True)
            log = lse[:, half * HEAD : half * HEAD + 1]
            soft = jnp.exp(dot(q_here, keys, NT) + bias - log)
            grad = (soft * (dot(do_here, values, NT) - inner)).astype(BF16)
            outs.append(dot(grad, keys, NN))
            dk = dk + dot(q_here, grad, TN)
            dv = dv + dot(do_here, soft.astype(BF16), TN)
        dq_ref[at, :] = (jnp.where(low, outs[0], outs[1]) * SCALE).astype(BF16)
    for i, value in enumerate((dk.T, dv.T)):
        at = slice(i * LANES, (i + 1) * LANES)
        own_ref[:, at] = value[:rows]
        other_ref[:, at] = value[rows:].astype(BF16)


def attend_back(qkv, kv_other, bias, out, lse, grad_out, first, count):
    rows, width = out.shape
    pairs = width // LANES
    spec = lambda base: pl.BlockSpec((rows, LANES), lambda p: (0, base + first + p))
    result = lambda cols: pl.BlockSpec((rows, cols), lambda p: (0, p))
    return pl.pallas_call(
        attend_back_kernel,
        out_shape=(
            jax.ShapeDtypeStruct((rows, count * LANES), BF16),
            jax.ShapeDtypeStruct((rows, 2 * count * LANES), F32),
            jax.ShapeDtypeStruct((rows, 2 * count * LANES), BF16),
        ),
        grid=(count,),
        in_specs=[
            spec(0),
            spec(pairs),
            spec(2 * pairs),
            spec(0),
            spec(pairs),
            pl.BlockSpec((1, 2 * rows), lambda p: (0, 0)),
            spec(0),
            spec(0),
            spec(0),
        ],
        out_specs=(result(LANES), result(2 * LANES), result(2 * LANES)),
        compiler_params=pltpu.CompilerParams(vmem_limit_bytes=56 << 20),
        cost_estimate=cost(3 * count),
        name="attend_back",
    )(qkv, qkv, qkv, kv_other, kv_other, bias, out, lse, grad_out)


def gelu_parts(v):
    cdf = 0.5 * (1.0 + lax.erf(v * (2.0 ** -0.5)))
    pdf = jnp.exp(-0.5 * v * v) * 0.3989422804014327
    return v * cdf, cdf + v * pdf


def norm(values):
    center = values - jnp.mean(values, axis=-1, keepdims=True)
    inv_dev = lax.rsqrt(jnp.mean(center * center, axis=-1, keepdims=True) + EPS)
    return center * inv_dev, inv_dev


def norm_back(scaled, normed, inv_dev):
    return inv_dev * (
        scaled
        - jnp.mean(scaled, axis=-1, keepdims=True)
        - normed * jnp.mean(scaled * normed, axis=-1, keepdims=True)
    )


def total(value):
    return jnp.sum(value, axis=0, keepdims=True)


def join(parts, starts, size, micros):
    rows, cols = parts[0].shape[0], len(starts) * len(parts) * size

    def body(*refs):
        parts, out = refs[:-1], refs[-1]
        at = 0
        for start in starts:
            for part in parts:
                out[:, at : at + size] = part[:, start : start + size]
                at += size

    vmem = pl.BlockSpec(memory_space=pltpu.VMEM)
    return pl.pallas_call(
        body,
        out_shape=like((rows, cols), parts[0].dtype),
        in_specs=[vmem] * len(parts),
        out_specs=vmem,
        cost_estimate=cost(micros),
        name="join",
    )(*parts)


def project(x_parts, head_row, table, pieces):
    block, width = x_parts[0].shape
    rows = block * len(x_parts)
    n = len(pieces)

    def body(table, *refs):
        part_refs, bias_ref, refs = refs[:N_MP], refs[N_MP], refs[N_MP + 1 :]
        pieces, (x_ref, qkv_ref, kv_ref, held, sems) = refs[:n], refs[n:]
        weights = Weights(pieces, table, held, sems, 0, width)
        for i, part in enumerate(part_refs):
            x_ref[i * block : (i + 1) * block, :] = part[...]
        x = x_ref[...]
        for i in range(3):
            value = dot(x, weights.get(i), NN) + bias_ref[:, i * width : (i + 1) * width]
            value = value.astype(BF16)
            if i == 0:
                value = (value.astype(F32) * SCALE).astype(BF16)
            else:
                kv_ref[:, (i - 1) * width : i * width] = value
            qkv_ref[:, i * width : (i + 1) * width] = value

    return call(
        body,
        "project",
        7,
        [
            like((rows, width), BF16),
            like((rows, 3 * width), BF16),
            like((rows, 2 * width), BF16),
        ],
        list(x_parts) + [head_row],
        table,
        pieces,
        weight_scratch(pieces, 3 * width, 3),
    )


def feed(x, mixed, cot_parts, smalls, small_row, table, out_pieces, feed_pieces):
    rows, width = x.shape
    hidden = feed_pieces[0].shape[1] // 2
    count = 6
    tile = hidden // count
    cols = hidden + width
    n_out, n_up, n = len(out_pieces), len(feed_pieces), len(smalls)
    down_grads = grad_shapes(feed_pieces, hidden)
    mid_grads = grad_shapes(feed_pieces, cols, SHARED)
    g = len(mid_grads)

    def body(table, x_ref, mixed_ref, *refs):
        cot_far, small_far, refs = refs[:N_MP], refs[N_MP : N_MP + n], refs[N_MP + n :]
        out_p, up_p = refs[:n_out], refs[n_out : n_out + n_up]
        refs = refs[n_out + n_up :]
        result_outs, shared_ref, da_out, do_out = refs[1 : 1 + N_MP], refs[0], *refs[5:7]
        down_outs, mid_outs, refs = refs[7 : 7 + g], refs[7 + g : 7 + 2 * g], refs[7 + 2 * g :]
        w_out, sems_out, w_up, sems_up, w_down, sems_down = refs[:6]
        plain, turned, plain_h, turned_h = refs[6:10]
        small_ref, cot_ref, read_sems = refs[10:13]
        n1_ref, dz_ref, h_ref, act_ref, slope_ref, result_ref, low_ref, do_ref = refs[13:21]
        down_stages, mid_stages = refs[21 : 21 + g], refs[21 + g : 21 + 2 * g]
        shared_low, sems, grad_sems, up_b_ref = refs[21 + 2 * g :]
        out_w = Weights(out_p, table, w_out, sems_out, 3 * width, width)
        smalls = [small.at[pl.ds(small_row, SMALL)] for small in small_far]
        reads = Reads(smalls, [small_ref.at[i] for i in range(n)], read_sems)
        up_w = Weights(up_p, table, w_up, sems_up, 0, tile)
        down_w = Weights(up_p, table, w_down, sems_down, hidden, tile)
        block = rows // N_MP
        cots = Reads(
            cot_far,
            [cot_ref.at[pl.ds(i * block, block)] for i in range(N_MP)],
            read_sems.at[pl.ds(n, N_MP)],
        )
        writes = Writes(sems)

        attention = dot(mixed_ref[...], out_w.get(0), NT)
        for i in range(n):
            reads.get(i)
        small = jnp.sum(small_ref[...].astype(F32), axis=0)
        row_vals = sum(small[:, i * width : (i + 1) * width] for i in range(2 * N_MP))
        row = lambda i: row_vals[i : i + 1, :]
        up_b = small[6:7, :hidden]
        n1, r1 = norm(x_ref[...].astype(F32) + attention + row(0))
        n1_ref[...] = n1
        h_ref[...] = (n1 * row(1) + row(2)).astype(BF16)
        up_b_ref[...] = up_b
        dz_ref[...] = jnp.zeros_like(dz_ref)
        up_w.whole()
        down_w.whole()

        @pl.loop(0, count // 2)
        def _(i):
            ats = [pl.multiple_of((2 * i + k) * tile, tile) for k in range(2)]
            us = [dot(h_ref[...], up_w.at(at), NN) for at in ats]
            for at, u in zip(ats, us):
                act, slope = gelu_parts(u + up_b_ref[:, pl.ds(at, tile)])
                act_ref[:, pl.ds(at, tile)] = act.astype(BF16)
                slope_ref[:, pl.ds(at, tile)] = slope.astype(BF16)
                dz_ref[...] += dot(act_ref[:, pl.ds(at, tile)], down_w.at(at), NT)

        feed = dz_ref[...]
        h = n1_ref[...] * row(1) + row(2)
        n2, r2 = norm(h + feed + row(3))
        result_ref[...] = (n2 * row(4) + row(5)).astype(BF16)
        for i, out in enumerate(result_outs):
            writes.start(result_ref.at[pl.ds(i * block, block)], out)
        for i in range(N_MP):
            cots.get(i)
        gy = cot_ref[...].astype(F32)
        dz = norm_back(gy * row(4), n2, r2)
        dz_ref[...] = dz
        low_ref[...] = dz.astype(BF16)
        sums = [total(dz), total(gy * n2), total(gy)]

        turn(low_ref[...], table, plain, turned)
        turn(h_ref[...], table, plain_h, turned_h)
        shared_ref[...] = jnp.zeros_like(shared_ref)
        def tile_copies(t):
            at = t * tile if isinstance(t, int) else pl.multiple_of(t * tile, tile)
            down = grad_copies(down_stages, down_outs, at, tile, grad_sems, 2 * g * t)
            return down + grad_copies(mid_stages, mid_outs, at, tile, grad_sems, 2 * g * t + g)

        @pl.loop(0, count)
        def _(t):
            at = pl.multiple_of(t * tile, tile)
            dact = dot(low_ref[...], down_w.at(at), NN)
            store_grad(turned, act_ref[:, pl.ds(at, tile)], down_stages, at)
            du = (dact * slope_ref[:, pl.ds(at, tile)].astype(F32)).astype(BF16)
            shared_ref[0:1, pl.ds(at, tile)] = total(du.astype(F32))
            dz_ref[...] += dot(du, up_w.at(at), NT)
            store_grad(turned_h, du, mid_stages, at)
            start_all(tile_copies(t))

        dh = dz_ref[...]
        n1 = n1_ref[...]
        da = norm_back(dh * row(1), n1, r1)
        dz_ref[...] = da
        writes.start(dz_ref, da_out)
        low_ref[...] = da.astype(BF16)
        do_ref[...] = dot(low_ref[...], out_w.get(0), NN).astype(BF16)
        writes.start(do_ref, do_out)
        sums = [total(da), total(dh * n1), total(dh)] + sums
        for j in range(hidden // width):
            for i, value in enumerate(sums):
                shared_ref[1 + i : 2 + i, j * width : (j + 1) * width] = value
        if g > 1:
            shared_low[...] = shared_ref[...].astype(BF16)
            for out in mid_outs:
                for r in range(out.shape[0]):
                    writes.start(shared_low, out.at[r, pl.ds(block_rows(feed_pieces), SHARED)])
        turn(low_ref[...], table, plain, turned)
        store_grad(turned, mixed_ref[...], mid_stages, hidden)
        last = grad_copies(mid_stages, mid_outs, hidden, width, grad_sems, 2 * g * count)
        start_all(last)
        for t in range(count):
            wait_all(tile_copies(t))
        wait_all(last)
        writes.finish()

    near = [((rows, width), F32)] * 2 + [((rows, width), BF16)]
    near += [((rows, hidden), BF16)] * 2 + [((rows, width), BF16)] * 3
    return call(
        body,
        "feed",
        33,
        [
            like((SHARED, cols), F32),
        ]
        + [like((rows // N_MP, width), BF16)] * N_MP
        + [
            like((rows, width), F32),
            like((rows, width), BF16),
        ]
        + down_grads
        + mid_grads,
        [x, mixed],
        table,
        list(cot_parts) + list(smalls) + list(out_pieces) + list(feed_pieces),
        weight_scratch(out_pieces, width)
        + weight_scratch(feed_pieces, hidden) * 2
        + turn_scratch(feed_pieces, rows) * 2
        + [
            pltpu.VMEM((n, SMALL, 2 * hidden), BF16),
            pltpu.VMEM((rows, width), BF16),
            pltpu.SemaphoreType.DMA((n + N_MP,)),
        ]
        + [pltpu.VMEM(*spec) for spec in near]
        + stage_scratch(feed_pieces, hidden)
        + stage_scratch(feed_pieces, cols)
        + [
            pltpu.VMEM((SHARED, cols), BF16),
            pltpu.SemaphoreType.DMA((2 + N_MP + n_up,)),
            pltpu.SemaphoreType.DMA((g * (2 * count + 1),)),
            pltpu.VMEM((1, hidden), F32),
        ],
        far=2 + N_MP + 2 * g,
    )


def project_back(da, parts, table, pieces):
    rows, width = da.shape
    n = len(pieces)
    flat = [value for part in parts for value in part]

    def body(table, da_ref, *refs):
        part_refs, refs = refs[: len(flat)], refs[len(flat) :]
        pieces, out_refs, refs = refs[:n], refs[n : n + N_MP], refs[n + N_MP :]
        dqkv_ref, held, sems = refs
        weights = Weights(pieces, table, held, sems, 0, width)
        pair = 0
        for i in range(0, len(flat), 3):
            q_ref, own_ref, back_ref = part_refs[i : i + 3]
            cols = q_ref.shape[1]
            dqkv_ref[:, pair * LANES : pair * LANES + cols] = q_ref[...]
            for p in range(cols // LANES):
                for which in range(2):
                    at = slice((2 * p + which) * LANES, (2 * p + which + 1) * LANES)
                    to = (which + 1) * width + (pair + p) * LANES
                    value = own_ref[:, at] + back_ref[:, at].astype(F32)
                    dqkv_ref[:, to : to + LANES] = value.astype(BF16)
            pair += cols // LANES
        value = da_ref[...]
        for i in range(3):
            value = value + dot(dqkv_ref[:, i * width : (i + 1) * width], weights.get(i), NT)
        block = rows // N_MP
        for i, out_ref in enumerate(out_refs):
            out_ref[...] = value[i * block : (i + 1) * block].astype(BF16)

    return call(
        body,
        "project_back",
        9,
        [like((rows // N_MP, width), BF16)] * N_MP + [like((rows, 3 * width), BF16)],
        [da] + flat,
        table,
        pieces,
        weight_scratch(pieces, 3 * width, 3),
    )


def project_grads(x, dqkv, table, pieces):
    rows, width = x.shape
    grads = grad_shapes(pieces, 3 * width, SHARED)
    g = len(grads)

    def body(table, x_ref, dqkv_ref, *refs):
        shared_ref, grad_outs, refs = refs[0], refs[1 : 1 + g], refs[1 + g :]
        plain, turned = refs[:2]
        stages, shared_low, sems = refs[2 : 2 + g], refs[2 + g], refs[3 + g]
        writes = Writes(sems.at[pl.ds(3 * g, len(blocks_of(pieces)))])
        turn(x_ref[...], table, plain, turned)

        @pl.loop(0, 3)
        def _(i):
            at = pl.multiple_of(i * width, width)
            store_grad(turned, dqkv_ref[:, pl.ds(at, width)], stages, at)
            start_all(grad_copies(stages, grad_outs, at, width, sems, g * i))

        shared_ref[...] = jnp.zeros_like(shared_ref)
        shared_ref[0:1, :] = total(dqkv_ref[...].astype(F32))
        if g > 1:
            shared_low[...] = shared_ref[...].astype(BF16)
            for out in grad_outs:
                for r in range(out.shape[0]):
                    writes.start(shared_low, out.at[r, pl.ds(block_rows(pieces), SHARED)])
        for i in range(3):
            wait_all(grad_copies(stages, grad_outs, i * width, width, sems, g * i))
        writes.finish()

    return call(
        body,
        "project_grads",
        7,
        [like((SHARED, 3 * width), F32)] + grads,
        [x, dqkv],
        table,
        [],
        turn_scratch(pieces, rows)
        + stage_scratch(pieces, 3 * width)
        + [
            pltpu.VMEM((SHARED, 3 * width), BF16),
            pltpu.SemaphoreType.DMA((3 * g + len(blocks_of(pieces)),)),
        ],
        far=g,
    )


def at_column(values, rows, width, column):
    return lax.dynamic_update_slice(jnp.zeros((rows, width), values.dtype), values, (0, column))


def small_block(row_params, expand_bias, mine, depth):
    high = lax.reduce_precision(row_params, 8, 7)
    column = (mine * N_MP + depth) * row_params.shape[1]
    high_low = [
        at_column(part.astype(BF16), 6, WIDTH, column) for part in (high, row_params - high)
    ]
    bias = at_column(expand_bias, 2, 2 * WIDTH, mine * expand_bias.shape[1])
    return jnp.concatenate([jnp.concatenate(high_low, axis=1), bias])


def key_bias(length_long, length_short, block, core, depth):
    lengths = jnp.concatenate([length_long, length_short])
    other = core_swap(lengths)
    longs = jnp.where(core == 0, jnp.stack([lengths[0], other[0]]), jnp.stack([other[0], lengths[0]]))
    length = jnp.concatenate([longs, lengths[1:]])[depth]
    is_long = depth < 2
    place = lax.broadcasted_iota(jnp.int32, (1, 2 * N_MP * block), 1)
    row = place % (N_MP * block)
    is_own = place < N_MP * block
    source = (row // block) ^ depth
    whose = jnp.where(is_own, core, 1 - core)
    frame = row % block + jnp.where(is_long, (2 * source + whose) * block, source * block)
    counted = (frame < length) & (is_own | is_long)
    return jnp.where(counted, 0.0, NEG_FILL).astype(F32)


def on_device(
    frames_long,
    frames_short,
    length_long,
    length_short,
    input_proj,
    output_proj,
    expand_weight,
    shrink_weight,
    head_bias,
    expand_bias,
    row_params,
    cotangent_long,
    cotangent_short,
):
    mine = lax.axis_index("dp")
    depth = lax.axis_index("mp")
    n_dp = lax.axis_size("dp")
    fast = n_dp == 8
    core = mine % 2
    block = frames_short.shape[1]
    shard, group = input_proj.shape[1:]
    units = expand_weight.shape[1]
    width = group * N_MP
    hidden = units * N_MP
    table = block_table(mine, n_dp)

    joined = jnp.concatenate(
        [input_proj[0], input_proj[1], input_proj[2], output_proj.T], axis=1
    )
    heads = at_column(head_bias[:, 0], SMALL, WIDTH, mine * head_bias.shape[2])
    attn_parts = mp_gather(jnp.concatenate([joined, heads]))
    x_blocks = clip_blocks(frames_long[0], frames_short, core)
    cot_blocks = clip_blocks(cotangent_long[0], cotangent_short, core)
    bias = key_bias(length_long, length_short, block, core, depth)
    feed_shard = jnp.concatenate(
        [
            jnp.concatenate([expand_weight, shrink_weight.T], axis=1),
            small_block(row_params, expand_bias, mine, depth),
        ]
    )
    *attn_parts, feed_shard, bias, x_blocks, cot_blocks = tie(
        *attn_parts, feed_shard, bias, x_blocks, cot_blocks
    )
    order = [p[:shard, i * group : (i + 1) * group] for i in range(4) for p in attn_parts]
    attn_slab = jnp.concatenate([to_slab(order), to_slab([p[shard:] for p in attn_parts])])
    feed_parts = mp_gather(feed_shard)
    feed_order = [p[:, i * units : (i + 1) * units] for i in range(2) for p in feed_parts]
    if fast:
        attn_p = [attn_slab] + [dp_swap(attn_slab, to) for to in (early, late, across)]
        x_pieces = clip_pieces(x_blocks, depth)
        attn_p += [core_swap(piece) for piece in attn_p]
        both = tie(*attn_p, *x_pieces, *feed_order)
        attn_p, x_pieces, feed_order = both[:8], both[8:12], both[12:]
        feed_slab = to_slab(feed_order)
        feed_one = dp_swap(feed_slab, early)
        feed_two = dp_swap(feed_slab, late)
        x_parts = [x_pieces[0]] + [mp_swap(x_pieces[i], i) for i in range(1, N_MP)]
        *x_parts, cot_blocks, own_slab = tie(*x_parts, cot_blocks, feed_slab)
        heads = sum(p[shard:].astype(F32) for p in attn_p)
    else:
        x_parts = to_clips(x_blocks, depth)
        gather = lambda slab: lax.all_gather(slab, "dp", axis=0)
        whole = gather(attn_slab)
        heads = jnp.sum(whole[:, shard:].astype(F32), axis=0)
        attn_p = [whole[:, :shard].reshape(width, 4 * width)]
        whole = gather(to_slab(feed_order))
        small = jnp.sum(whole[:, shard:].astype(F32), axis=0)
        feed_p = [whole[:, :shard].reshape(width, 2 * hidden)]
    cot_parts = to_clips(cot_blocks, depth)
    heads = jnp.concatenate(
        [heads[:2, i * width : i * width + group] for i in range(N_MP)], axis=1
    )
    head_row = jnp.concatenate([heads[:1], jnp.zeros_like(heads[:1]), heads[1:]], axis=1)

    x, qkv, kv = project(x_parts, head_row, table, attn_p)
    if fast:
        kv, feed_one, feed_two, cot_parts[3], own_slab = tie(
            kv, feed_one, feed_two, cot_parts[3], core_swap(own_slab)
        )
    kv_other = core_swap(kv)
    if fast:
        feed_three = dp_swap(feed_one, late)
        feed_p = [feed_slab, feed_one, feed_two]
        backs = [own_slab] + [core_swap(piece) for piece in feed_p[1:]]
    mixed, lse = attend(qkv, kv_other, bias)
    if fast:
        mixed, feed_three, *both = tie(mixed, feed_three, *backs, *cot_parts)
        backs, cot_parts = both[:3], both[3:]
        feed_p = feed_p + [feed_three] + backs + [core_swap(feed_three)]
        smalls, small_row = feed_p, shard
    else:
        smalls, small_row = [small.astype(BF16)], 0
    outs = feed(x, mixed, cot_parts, smalls, small_row, table, attn_p, feed_p)
    mid_shared, result, (da, do), grads = outs[0], list(outs[1:5]), outs[5:7], outs[7:]
    g_down, g_mid = grads[: len(grads) // 2], grads[len(grads) // 2 :]

    def by_group_of(value, sizes):
        starts = [N_MP * sum(sizes[:i]) for i in range(len(sizes))]
        return [
            jnp.concatenate(
                [value[:, a + j * n : a + (j + 1) * n] for a, n in zip(starts, sizes)], axis=1
            )
            for j in range(N_MP)
        ]

    def last_sum(terms):
        return sum(term[0].astype(F32) for term in terms)

    result_parts = from_clips(result)
    if fast:
        b_down, b_mid = core_swap(g_down[1]), core_swap(g_mid[1])
    pairs = width // LANES
    first = pairs // 2
    dq_a, own_a, other_a = attend_back(qkv, kv_other, bias, mixed, lse, do, 0, first)
    if fast:
        other_a, b_down, b_mid, result_parts[3] = tie(other_a, b_down, b_mid, result_parts[3])
        t_down = [g_down[0], b_down]
        a_down = goes_on(t_down)
        do, a_down = tie(do, a_down)
        b_down = dp_swap(a_down, late)
        t_mid = [g_mid[0], b_mid]
        a_mid = goes_on(t_mid)
        do, a_mid = tie(do, a_mid)
        b_mid = dp_swap(a_mid, late)
    back_a = core_swap(other_a)
    dq_b, own_b, other_b = attend_back(
        qkv, kv_other, bias, mixed, lse, do, first, pairs - first
    )
    if fast:
        other_b, back_a, *result_parts = tie(other_b, back_a, *result_parts)
    back_b = core_swap(other_b)
    parts = [(dq_a, own_a, back_a), (dq_b, own_b, back_b)]
    *frames_grad, dqkv = project_back(da, parts, table, attn_p)
    grad_parts = from_clips(frames_grad)
    if fast:
        dqkv, b_down, b_mid = tie(dqkv, b_down, b_mid)
        t_down, t_mid = stays(t_down, b_down), stays(t_mid, b_mid)
        a_down, a_mid = goes_on(t_down), goes_on(t_mid)
        dqkv, a_down, a_mid = tie(dqkv, a_down, a_mid)
        b_down = dp_swap(a_down, early)
        b_mid = dp_swap(a_mid, early)
    attn_shared, *g_attn = project_grads(x, dqkv, table, attn_p)
    if fast:
        both = tie(*g_attn, b_down, b_mid, grad_parts[3])
        g_attn, b_down, b_mid, grad_parts[3] = both[:2], both[2], both[3], both[4]
        b_attn = core_swap(g_attn[1])
        s_down = by_group_of(last_sum(stays(t_down, b_down)), [units])
        t_attn = [g_attn[0], b_attn]
        a_attn = goes_on(t_attn)
        a_attn, *s_down = tie(a_attn, *s_down)
        b_attn = dp_swap(a_attn, late)
        z_down = mp_away(s_down)
        s_mid = by_group_of(last_sum(stays(t_mid, b_mid)), [units, group])
        b_attn, *z_down = tie(b_attn, *z_down)
        t_attn = stays(t_attn, b_attn)
        a_attn = goes_on(t_attn)
        z_mid = mp_away(s_mid)
        b_attn, *both = tie(dp_swap(a_attn, early), *z_mid, *result_parts)
        z_mid, result_parts = both[: N_MP - 1], both[N_MP - 1 :]
        s_attn = last_sum(stays(t_attn, b_attn))
    else:
        scatter = lambda g: lax.psum_scatter(g[0][0], "dp", scatter_dimension=0, tiled=True)
        s_down = by_group_of(scatter(g_down), [units])
        z_down = mp_away(s_down)
        s_mid = jnp.concatenate([scatter(g_mid), lax.psum(mid_shared, "dp")])
        s_mid = by_group_of(s_mid, [units, group])
        z_mid = mp_away(s_mid)
        s_attn = jnp.concatenate([scatter(g_attn), lax.psum(attn_shared, "dp")])
    s_attn = by_group_of(s_attn, [group] * 3)
    grad_long, grad_short = frames_of(grad_parts, core, depth)
    result_long, result_short = frames_of(result_parts, core, depth)
    attn_share = mp_total(s_attn[0], mp_away(s_attn))
    down_share = mp_total(s_down[0], z_down).T
    mid_share = mp_total(s_mid[0], z_mid)
    up_share = mid_share[:shard, :units]
    output_share = mid_share[:shard, units:].T
    input_share = jnp.stack(
        [attn_share[:shard, i * group : (i + 1) * group] for i in range(3)]
    )
    up_cols, head_cols, row_cols = units // n_dp, group // n_dp, width // (n_dp * N_MP)
    rank = mine * N_MP + depth
    up_b_share = lax.dynamic_slice(mid_share, (shard, mine * up_cols), (1, up_cols))
    row_share = lax.dynamic_slice(mid_share, (shard + 1, rank * row_cols), (6, row_cols))
    head_share = jnp.stack(
        [
            lax.dynamic_slice(attn_share, (shard, at + mine * head_cols), (1, head_cols))
            for at in (0, 2 * group)
        ]
    )
    return (
        result_long,
        result_short,
        grad_long.astype(F32),
        grad_short.astype(F32),
        input_share,
        output_share,
        up_share,
        down_share,
        head_share,
        up_b_share,
        row_share,
    )


def solution(mesh):
    return jax.shard_map(
        on_device,
        mesh=mesh,
        in_specs=(
            P("dp", "mp", None),
            P("dp", "mp", None),
            P("dp"),
            P("dp"),
            P(None, "dp", "mp"),
            P("mp", "dp"),
            P("dp", "mp"),
            P("mp", "dp"),
            P(None, "mp", "dp"),
            P("mp", "dp"),
            P(None, ("dp", "mp")),
            P("dp", "mp", None),
            P("dp", "mp", None),
        ),
        out_specs=(
            P("dp", "mp", None),
            P("dp", "mp", None),
            P("dp", "mp", None),
            P("dp", "mp", None),
            P(None, "dp", "mp"),
            P("mp", "dp"),
            P("dp", "mp"),
            P("mp", "dp"),
            P(None, "mp", "dp"),
            P("mp", "dp"),
            P(None, ("dp", "mp")),
        ),
        check_vma=False,
    )
```

```python
import functools

import jax
import jax.numpy as jnp
from jax import lax
from jax.experimental import pallas as pl
from jax.experimental.pallas import tpu as pltpu
from jax.sharding import PartitionSpec as P

HEAD = 64
EPS = 1e-05
NEG_FILL = -1e30
SCALE = HEAD ** (-0.5)
N_MP = 4
PARTS = 1
CS = 0.3
WIDTH = 768
SMALL = 8
SHARED = 8
LANES = 128
Q_TILE = 256
F32 = jnp.float32
BF16 = jnp.bfloat16
NT = (((1,), (1,)), ((), ()))
NN = (((1,), (0,)), ((), ()))
TN = (((0,), (0,)), ((), ()))


def dot(left, right, dims):
    return lax.dot_general(left, right, dims, preferred_element_type=F32)


def mp_swap(value, step):
    return lax.ppermute(value, "mp", [(i, i ^ step) for i in range(N_MP)])


def dp_swap(value, target):
    size = lax.axis_size("dp")
    return lax.ppermute(value, "dp", [(i, target(i)) for i in range(size)])


def core_swap(value):
    return dp_swap(value, lambda i: i ^ 1)


def clip_blocks(long_rows, short_rows, core):
    block = short_rows.shape[1]
    keep = lax.dynamic_slice_in_dim(long_rows, core * block, block, 0)
    away = lax.dynamic_slice_in_dim(long_rows, (1 - core) * block, block, 0)
    back = core_swap(away)
    first = jnp.where(core == 0, keep, back)
    second = jnp.where(core == 0, back, keep)
    return jnp.stack([first, second, short_rows[0], short_rows[1]])


def clip_pieces(blocks, depth):
    return [
        lax.dynamic_index_in_dim(blocks, depth ^ step, 0, keepdims=False) for step in range(N_MP)
    ]


def to_clips(blocks, depth):
    pieces = clip_pieces(blocks, depth)
    return pieces[:1] + [mp_swap(pieces[step], step) for step in range(1, N_MP)]


def from_clips(parts):
    return parts[:1] + [mp_swap(parts[step], step) for step in range(1, N_MP)]


def frames_of(parts, core, depth):
    blocks = jnp.stack(parts)
    first, second, short_a, short_b = (
        lax.dynamic_index_in_dim(blocks, depth ^ i, 0, keepdims=False) for i in range(N_MP)
    )
    keep = jnp.where(core == 0, first, second)
    away = jnp.where(core == 0, second, first)
    back = core_swap(away)
    low = jnp.where(core == 0, keep, back)
    high = jnp.where(core == 0, back, keep)
    return jnp.concatenate([low, high], axis=0)[None], jnp.stack([short_a, short_b])


def flip(index, late):
    return index ^ ((4 if late else 2) if index % 2 == 0 else (2 if late else 4))


def block_table(mine, size):
    if size != 8:
        return jnp.zeros((1,), jnp.int32)
    early = jnp.where(mine % 2 == 0, 2, 4)
    late = 6 - early
    relative = [0, early, late, 6, 1, 1 ^ late, 1 ^ early, 7]
    return jnp.stack([mine ^ r for r in relative]).astype(jnp.int32)


def early(i):
    return flip(i, False)


def late(i):
    return flip(i, True)


def across(i):
    return i ^ 6


def tie(*values):
    return lax.optimization_barrier(values)


def swap_plane(plane):
    return plane + [core_swap(piece) for piece in plane]


def to_slab(parts):
    return jnp.concatenate(parts, axis=1)


def mp_gather(shard):
    return [shard] + [mp_swap(shard, step) for step in range(1, N_MP)]


def goes_on(terms):
    half = terms[0].shape[0] // 2
    return sum(term[half:].astype(F32) for term in terms).astype(BF16)


def stays(terms, back):
    half = terms[0].shape[0] // 2
    return [term[:half] for term in terms] + [back]


def mp_away(parts):
    return [mp_swap(parts[step].astype(BF16), step) for step in range(1, N_MP)]


def mp_total(own, backs):
    for back in backs:
        own = own + back.astype(F32)
    return own


def blocks_of(pieces):
    step = pieces[0].shape[0]
    return [(p, k * step) for p in pieces for k in range(p.shape[0] // step)]


def block_rows(pieces):
    return WIDTH // len(blocks_of(pieces))


class Weights:
    def __init__(self, pieces, table, held, sems, lo, tile):
        self.held, self.tile = held, tile
        cols, parts = held.shape[2], sems.shape[0]
        self.span, self.copies = cols // parts, []
        for t in range(parts):
            row = []
            for k, (piece, first) in enumerate(blocks_of(pieces)):
                copy = pltpu.make_async_copy(
                    piece.at[pl.ds(first, held.shape[1]), pl.ds(lo + t * self.span, self.span)],
                    held.at[table[k], :, pl.ds(t * self.span, self.span)],
                    sems.at[t, k],
                )
                copy.start()
                row.append(copy)
            self.copies.append(row)
        self.waited = 0

    def whole(self):
        for row in self.copies[self.waited :]:
            for copy in row:
                copy.wait()
        self.waited = len(self.copies)

    def at(self, at):
        count, rows, _ = self.held.shape
        return self.held[:, :, pl.ds(at, self.tile)].reshape(count * rows, self.tile)

    def get(self, t):
        at = t * self.tile
        while self.waited * self.span < at + self.tile:
            for copy in self.copies[self.waited]:
                copy.wait()
            self.waited += 1
        count, rows, _ = self.held.shape
        return self.held[:, :, at : at + self.tile].reshape(count * rows, self.tile)


def weight_scratch(pieces, cols, parts=1):
    return [
        pltpu.VMEM((len(blocks_of(pieces)), block_rows(pieces), cols), BF16),
        pltpu.SemaphoreType.DMA((parts, len(blocks_of(pieces)))),
    ]


def grad_shapes(pieces, cols, extra=0):
    count, rows = len(blocks_of(pieces)), block_rows(pieces)
    if count == 1:
        return [jax.ShapeDtypeStruct((1, rows, cols), F32)]
    return [jax.ShapeDtypeStruct((count // 2, rows + extra, cols), BF16)] * 2


def turn_scratch(pieces, rows):
    return [pltpu.VMEM((len(blocks_of(pieces)), block_rows(pieces), rows), BF16)] * 2


def turn(value, table, plain, turned):
    plain[...] = value.T.reshape(plain.shape)
    for r in range(plain.shape[0]):
        turned[r] = plain[table[r]]


def stage_scratch(pieces, cols):
    return [
        pltpu.VMEM((g.shape[0], block_rows(pieces), cols), g.dtype)
        for g in grad_shapes(pieces, cols)
    ]


def store_grad(turned, right, stages, at):
    count, rows, _ = turned.shape
    grad = dot(turned[...].reshape(count * rows, -1), right, NN)
    half, cols = count // len(stages), right.shape[1]
    for r in range(count):
        stage = stages[r // half]
        part = grad[r * rows : (r + 1) * rows].astype(stage.dtype)
        stage[r % half, :rows, pl.ds(at, cols)] = part


def grad_copies(stages, outs, at, cols, sems, first):
    return [
        pltpu.make_async_copy(
            stage.at[:, :, pl.ds(at, cols)],
            out.at[:, pl.ds(0, stage.shape[1]), pl.ds(at, cols)],
            sems.at[first + i],
        )
        for i, (stage, out) in enumerate(zip(stages, outs))
    ]


def start_all(copies):
    for copy in copies:
        copy.start()


def wait_all(copies):
    for copy in copies:
        copy.wait()


class Writes:
    def __init__(self, sems):
        self.sems, self.copies = sems, []

    def start(self, source, target):
        copy = pltpu.make_async_copy(source, target, self.sems.at[len(self.copies)])
        copy.start()
        self.copies.append(copy)

    def finish(self):
        for copy in self.copies:
            copy.wait()


class Reads:
    def __init__(self, sources, targets, sems):
        self.targets, self.copies = targets, []
        for i, (source, target) in enumerate(zip(sources, targets)):
            copy = pltpu.make_async_copy(source, target, sems.at[i])
            copy.start()
            self.copies.append(copy)

    def get(self, i):
        self.copies[i].wait()
        return self.targets[i]


def read_scratch(arrays):
    return [pltpu.VMEM(a.shape, a.dtype) for a in arrays] + [
        pltpu.SemaphoreType.DMA((len(arrays),))
    ]


def cost(micros):
    return pl.CostEstimate(
        flops=int(micros * 1.1e9 * CS), bytes_accessed=int(micros * 1e5 * CS), transcendentals=0
    )


def call(body, name, micros, outs, arrays, table, pieces, scratch, far=0):
    vmem = pl.BlockSpec(memory_space=pltpu.VMEM)
    away = pl.BlockSpec(memory_space=pl.ANY)
    return pl.pallas_call(
        body,
        out_shape=tuple(outs),
        in_specs=[pl.BlockSpec(memory_space=pltpu.SMEM)]
        + [vmem] * len(arrays)
        + [away] * len(pieces),
        out_specs=(vmem,) * (len(outs) - far) + (away,) * far,
        scratch_shapes=scratch,
        compiler_params=pltpu.CompilerParams(vmem_limit_bytes=60 << 20),
        cost_estimate=cost(micros),
        name=name,
    )(table, *arrays, *pieces)


def like(shape, kind):
    return jax.ShapeDtypeStruct(shape, kind)


def attend_kernel(q_ref, k_ref, v_ref, kp_ref, vp_ref, bias_ref, o_ref, lse_ref):
    rows = q_ref.shape[0]
    keys = jnp.concatenate([k_ref[...], kp_ref[...]], axis=0)
    values = jnp.concatenate([v_ref[...], vp_ref[...]], axis=0)
    bias = bias_ref[...]
    tile = min(rows, Q_TILE)
    low = lax.broadcasted_iota(jnp.int32, (tile, LANES), 1) < HEAD
    for start in range(0, rows, tile):
        q = q_ref[start : start + tile, :]
        outs, logs = [], []
        for half in range(2):
            here = low if half == 0 else ~low
            q_here = jnp.where(here, q, jnp.zeros_like(q))
            scores = dot(q_here, keys, NT) + bias
            top = jnp.max(scores, axis=-1, keepdims=True)
            raised = jnp.exp(scores - top)
            total = jnp.sum(raised, axis=-1, keepdims=True)
            mixed = dot(raised.astype(BF16), values, NN)
            outs.append(mixed / total)
            logs.append(top + jnp.log(total))
        o_ref[start : start + tile, :] = jnp.where(low, outs[0], outs[1]).astype(BF16)
        lse_ref[start : start + tile, :] = jnp.where(low, logs[0], logs[1])


def attend(qkv, kv_other, bias):
    rows, width = qkv.shape[0], qkv.shape[1] // 3
    pairs = width // LANES
    spec = lambda base: pl.BlockSpec((rows, LANES), lambda p: (0, base + p))
    return pl.pallas_call(
        attend_kernel,
        out_shape=(
            jax.ShapeDtypeStruct((rows, width), BF16),
            jax.ShapeDtypeStruct((rows, width), F32),
        ),
        grid=(pairs,),
        in_specs=[
            spec(0),
            spec(pairs),
            spec(2 * pairs),
            spec(0),
            spec(pairs),
            pl.BlockSpec((1, 2 * rows), lambda p: (0, 0)),
        ],
        out_specs=(spec(0), spec(0)),
        compiler_params=pltpu.CompilerParams(vmem_limit_bytes=56 << 20),
        cost_estimate=cost(15),
        name="attend",
    )(qkv, qkv, qkv, kv_other, kv_other, bias)


def attend_back_kernel(
    q_ref, k_ref, v_ref, kp_ref, vp_ref, bias_ref, o_ref, lse_ref, do_ref,
    dq_ref, own_ref, other_ref,
):
    rows = q_ref.shape[0]
    keys = jnp.concatenate([k_ref[...], kp_ref[...]], axis=0)
    values = jnp.concatenate([v_ref[...], vp_ref[...]], axis=0)
    bias = bias_ref[...]
    tile = min(rows, Q_TILE)
    low = lax.broadcasted_iota(jnp.int32, (tile, LANES), 1) < HEAD
    dk = jnp.zeros((LANES, 2 * rows), F32)
    dv = jnp.zeros((LANES, 2 * rows), F32)
    for start in range(0, rows, tile):
        at = slice(start, start + tile)
        q, do = q_ref[at, :], do_ref[at, :]
        product = o_ref[at, :].astype(F32) * do.astype(F32)
        lse = lse_ref[at, :]
        outs = []
        for half in range(2):
            here = low if half == 0 else ~low
            q_here = jnp.where(here, q, jnp.zeros_like(q))
            do_here = jnp.where(here, do, jnp.zeros_like(do))
            inner = jnp.sum(jnp.where(here, product, 0.0), axis=-1, keepdims=True)
            log = lse[:, half * HEAD : half * HEAD + 1]
            soft = jnp.exp(dot(q_here, keys, NT) + bias - log)
            grad = (soft * (dot(do_here, values, NT) - inner)).astype(BF16)
            outs.append(dot(grad, keys, NN))
            dk = dk + dot(q_here, grad, TN)
            dv = dv + dot(do_here, soft.astype(BF16), TN)
        dq_ref[at, :] = (jnp.where(low, outs[0], outs[1]) * SCALE).astype(BF16)
    for i, value in enumerate((dk.T, dv.T)):
        at = slice(i * LANES, (i + 1) * LANES)
        own_ref[:, at] = value[:rows]
        other_ref[:, at] = value[rows:].astype(BF16)


def attend_back(qkv, kv_other, bias, out, lse, grad_out, first, count):
    rows, width = out.shape
    pairs = width // LANES
    spec = lambda base: pl.BlockSpec((rows, LANES), lambda p: (0, base + first + p))
    result = lambda cols: pl.BlockSpec((rows, cols), lambda p: (0, p))
    return pl.pallas_call(
        attend_back_kernel,
        out_shape=(
            jax.ShapeDtypeStruct((rows, count * LANES), BF16),
            jax.ShapeDtypeStruct((rows, 2 * count * LANES), F32),
            jax.ShapeDtypeStruct((rows, 2 * count * LANES), BF16),
        ),
        grid=(count,),
        in_specs=[
            spec(0),
            spec(pairs),
            spec(2 * pairs),
            spec(0),
            spec(pairs),
            pl.BlockSpec((1, 2 * rows), lambda p: (0, 0)),
            spec(0),
            spec(0),
            spec(0),
        ],
        out_specs=(result(LANES), result(2 * LANES), result(2 * LANES)),
        compiler_params=pltpu.CompilerParams(vmem_limit_bytes=56 << 20),
        cost_estimate=cost(3 * count),
        name="attend_back",
    )(qkv, qkv, qkv, kv_other, kv_other, bias, out, lse, grad_out)


def gelu_parts(v):
    cdf = 0.5 * (1.0 + lax.erf(v * (2.0 ** -0.5)))
    pdf = jnp.exp(-0.5 * v * v) * 0.3989422804014327
    return v * cdf, cdf + v * pdf


def norm(values):
    center = values - jnp.mean(values, axis=-1, keepdims=True)
    inv_dev = lax.rsqrt(jnp.mean(center * center, axis=-1, keepdims=True) + EPS)
    return center * inv_dev, inv_dev


def norm_back(scaled, normed, inv_dev):
    return inv_dev * (
        scaled
        - jnp.mean(scaled, axis=-1, keepdims=True)
        - normed * jnp.mean(scaled * normed, axis=-1, keepdims=True)
    )


def total(value):
    return jnp.sum(value, axis=0, keepdims=True)


def join(parts, starts, size, micros):
    rows, cols = parts[0].shape[0], len(starts) * len(parts) * size

    def body(*refs):
        parts, out = refs[:-1], refs[-1]
        at = 0
        for start in starts:
            for part in parts:
                out[:, at : at + size] = part[:, start : start + size]
                at += size

    vmem = pl.BlockSpec(memory_space=pltpu.VMEM)
    return pl.pallas_call(
        body,
        out_shape=like((rows, cols), parts[0].dtype),
        in_specs=[vmem] * len(parts),
        out_specs=vmem,
        cost_estimate=cost(micros),
        name="join",
    )(*parts)


def project(x_parts, head_row, table, pieces):
    block, width = x_parts[0].shape
    rows = block * len(x_parts)
    n = len(pieces)

    def body(table, *refs):
        part_refs, bias_ref, refs = refs[:N_MP], refs[N_MP], refs[N_MP + 1 :]
        pieces, (x_ref, qkv_ref, kv_ref, held, sems) = refs[:n], refs[n:]
        weights = Weights(pieces, table, held, sems, 0, width)
        for i, part in enumerate(part_refs):
            x_ref[i * block : (i + 1) * block, :] = part[...]
        x = x_ref[...]
        for i in range(3):
            value = dot(x, weights.get(i), NN) + bias_ref[:, i * width : (i + 1) * width]
            value = value.astype(BF16)
            if i == 0:
                value = (value.astype(F32) * SCALE).astype(BF16)
            else:
                kv_ref[:, (i - 1) * width : i * width] = value
            qkv_ref[:, i * width : (i + 1) * width] = value

    return call(
        body,
        "project",
        7,
        [
            like((rows, width), BF16),
            like((rows, 3 * width), BF16),
            like((rows, 2 * width), BF16),
        ],
        list(x_parts) + [head_row],
        table,
        pieces,
        weight_scratch(pieces, 3 * width, 3),
    )


def feed(x, mixed, cot_parts, smalls, small_row, table, out_pieces, feed_pieces):
    rows, width = x.shape
    hidden = feed_pieces[0].shape[1] // 2
    count = 6
    tile = hidden // count
    cols = hidden + width
    n_out, n_up, n = len(out_pieces), len(feed_pieces), len(smalls)
    down_grads = grad_shapes(feed_pieces, hidden)
    mid_grads = grad_shapes(feed_pieces, cols, SHARED)
    g = len(mid_grads)

    def body(table, x_ref, mixed_ref, *refs):
        cot_far, small_far, refs = refs[:N_MP], refs[N_MP : N_MP + n], refs[N_MP + n :]
        out_p, up_p = refs[:n_out], refs[n_out : n_out + n_up]
        refs = refs[n_out + n_up :]
        result_outs, shared_ref, da_out, do_out = refs[1 : 1 + N_MP], refs[0], *refs[5:7]
        down_outs, mid_outs, refs = refs[7 : 7 + g], refs[7 + g : 7 + 2 * g], refs[7 + 2 * g :]
        w_out, sems_out, w_up, sems_up, w_down, sems_down = refs[:6]
        plain, turned, plain_h, turned_h = refs[6:10]
        small_ref, cot_ref, read_sems = refs[10:13]
        n1_ref, dz_ref, h_ref, act_ref, slope_ref, result_ref, low_ref, do_ref = refs[13:21]
        down_stages, mid_stages = refs[21 : 21 + g], refs[21 + g : 21 + 2 * g]
        shared_low, sems, grad_sems, up_b_ref = refs[21 + 2 * g :]
        out_w = Weights(out_p, table, w_out, sems_out, 3 * width, width)
        smalls = [small.at[pl.ds(small_row, SMALL)] for small in small_far]
        reads = Reads(smalls, [small_ref.at[i] for i in range(n)], read_sems)
        up_w = Weights(up_p, table, w_up, sems_up, 0, tile)
        down_w = Weights(up_p, table, w_down, sems_down, hidden, tile)
        block = rows // N_MP
        cots = Reads(
            cot_far,
            [cot_ref.at[pl.ds(i * block, block)] for i in range(N_MP)],
            read_sems.at[pl.ds(n, N_MP)],
        )
        writes = Writes(sems)

        attention = dot(mixed_ref[...], out_w.get(0), NT)
        for i in range(n):
            reads.get(i)
        small = jnp.sum(small_ref[...].astype(F32), axis=0)
        row_vals = sum(small[:, i * width : (i + 1) * width] for i in range(2 * N_MP))
        row = lambda i: row_vals[i : i + 1, :]
        up_b = small[6:7, :hidden]
        n1, r1 = norm(x_ref[...].astype(F32) + attention + row(0))
        n1_ref[...] = n1
        h_ref[...] = (n1 * row(1) + row(2)).astype(BF16)
        up_b_ref[...] = up_b
        dz_ref[...] = jnp.zeros_like(dz_ref)
        up_w.whole()
        down_w.whole()

        @pl.loop(0, count // 2)
        def _(i):
            ats = [pl.multiple_of((2 * i + k) * tile, tile) for k in range(2)]
            us = [dot(h_ref[...], up_w.at(at), NN) for at in ats]
            for at, u in zip(ats, us):
                act, slope = gelu_parts(u + up_b_ref[:, pl.ds(at, tile)])
                act_ref[:, pl.ds(at, tile)] = act.astype(BF16)
                slope_ref[:, pl.ds(at, tile)] = slope.astype(BF16)
                dz_ref[...] += dot(act_ref[:, pl.ds(at, tile)], down_w.at(at), NT)

        feed = dz_ref[...]
        h = n1_ref[...] * row(1) + row(2)
        n2, r2 = norm(h + feed + row(3))
        result_ref[...] = (n2 * row(4) + row(5)).astype(BF16)
        for i, out in enumerate(result_outs):
            writes.start(result_ref.at[pl.ds(i * block, block)], out)
        for i in range(N_MP):
            cots.get(i)
        gy = cot_ref[...].astype(F32)
        dz = norm_back(gy * row(4), n2, r2)
        dz_ref[...] = dz
        low_ref[...] = dz.astype(BF16)
        sums = [total(dz), total(gy * n2), total(gy)]

        turn(low_ref[...], table, plain, turned)
        turn(h_ref[...], table, plain_h, turned_h)
        shared_ref[...] = jnp.zeros_like(shared_ref)
        def tile_copies(t):
            at = t * tile if isinstance(t, int) else pl.multiple_of(t * tile, tile)
            down = grad_copies(down_stages, down_outs, at, tile, grad_sems, 2 * g * t)
            return down + grad_copies(mid_stages, mid_outs, at, tile, grad_sems, 2 * g * t + g)

        @pl.loop(0, count)
        def _(t):
            at = pl.multiple_of(t * tile, tile)
            dact = dot(low_ref[...], down_w.at(at), NN)
            store_grad(turned, act_ref[:, pl.ds(at, tile)], down_stages, at)
            du = (dact * slope_ref[:, pl.ds(at, tile)].astype(F32)).astype(BF16)
            shared_ref[0:1, pl.ds(at, tile)] = total(du.astype(F32))
            dz_ref[...] += dot(du, up_w.at(at), NT)
            store_grad(turned_h, du, mid_stages, at)
            start_all(tile_copies(t))

        dh = dz_ref[...]
        n1 = n1_ref[...]
        da = norm_back(dh * row(1), n1, r1)
        dz_ref[...] = da
        writes.start(dz_ref, da_out)
        low_ref[...] = da.astype(BF16)
        do_ref[...] = dot(low_ref[...], out_w.get(0), NN).astype(BF16)
        writes.start(do_ref, do_out)
        sums = [total(da), total(dh * n1), total(dh)] + sums
        for j in range(hidden // width):
            for i, value in enumerate(sums):
                shared_ref[1 + i : 2 + i, j * width : (j + 1) * width] = value
        if g > 1:
            shared_low[...] = shared_ref[...].astype(BF16)
            for out in mid_outs:
                for r in range(out.shape[0]):
                    writes.start(shared_low, out.at[r, pl.ds(block_rows(feed_pieces), SHARED)])
        turn(low_ref[...], table, plain, turned)
        store_grad(turned, mixed_ref[...], mid_stages, hidden)
        last = grad_copies(mid_stages, mid_outs, hidden, width, grad_sems, 2 * g * count)
        start_all(last)
        for t in range(count):
            wait_all(tile_copies(t))
        wait_all(last)
        writes.finish()

    near = [((rows, width), F32)] * 2 + [((rows, width), BF16)]
    near += [((rows, hidden), BF16)] * 2 + [((rows, width), BF16)] * 3
    return call(
        body,
        "feed",
        33,
        [
            like((SHARED, cols), F32),
        ]
        + [like((rows // N_MP, width), BF16)] * N_MP
        + [
            like((rows, width), F32),
            like((rows, width), BF16),
        ]
        + down_grads
        + mid_grads,
        [x, mixed],
        table,
        list(cot_parts) + list(smalls) + list(out_pieces) + list(feed_pieces),
        weight_scratch(out_pieces, width)
        + weight_scratch(feed_pieces, hidden) * 2
        + turn_scratch(feed_pieces, rows) * 2
        + [
            pltpu.VMEM((n, SMALL, 2 * hidden), BF16),
            pltpu.VMEM((rows, width), BF16),
            pltpu.SemaphoreType.DMA((n + N_MP,)),
        ]
        + [pltpu.VMEM(*spec) for spec in near]
        + stage_scratch(feed_pieces, hidden)
        + stage_scratch(feed_pieces, cols)
        + [
            pltpu.VMEM((SHARED, cols), BF16),
            pltpu.SemaphoreType.DMA((2 + N_MP + n_up,)),
            pltpu.SemaphoreType.DMA((g * (2 * count + 1),)),
            pltpu.VMEM((1, hidden), F32),
        ],
        far=2 + N_MP + 2 * g,
    )


def project_back(da, parts, table, pieces):
    rows, width = da.shape
    n = len(pieces)
    flat = [value for part in parts for value in part]

    def body(table, da_ref, *refs):
        part_refs, refs = refs[: len(flat)], refs[len(flat) :]
        pieces, out_refs, refs = refs[:n], refs[n : n + N_MP], refs[n + N_MP :]
        dqkv_ref, held, sems = refs
        weights = Weights(pieces, table, held, sems, 0, width)
        pair = 0
        for i in range(0, len(flat), 3):
            q_ref, own_ref, back_ref = part_refs[i : i + 3]
            cols = q_ref.shape[1]
            dqkv_ref[:, pair * LANES : pair * LANES + cols] = q_ref[...]
            for p in range(cols // LANES):
                for which in range(2):
                    at = slice((2 * p + which) * LANES, (2 * p + which + 1) * LANES)
                    to = (which + 1) * width + (pair + p) * LANES
                    value = own_ref[:, at] + back_ref[:, at].astype(F32)
                    dqkv_ref[:, to : to + LANES] = value.astype(BF16)
            pair += cols // LANES
        value = da_ref[...]
        for i in range(3):
            value = value + dot(dqkv_ref[:, i * width : (i + 1) * width], weights.get(i), NT)
        block = rows // N_MP
        for i, out_ref in enumerate(out_refs):
            out_ref[...] = value[i * block : (i + 1) * block].astype(BF16)

    return call(
        body,
        "project_back",
        9,
        [like((rows // N_MP, width), BF16)] * N_MP + [like((rows, 3 * width), BF16)],
        [da] + flat,
        table,
        pieces,
        weight_scratch(pieces, 3 * width, 3),
    )


def project_grads(x, dqkv, table, pieces):
    rows, width = x.shape
    grads = grad_shapes(pieces, 3 * width, SHARED)
    g = len(grads)

    def body(table, x_ref, dqkv_ref, *refs):
        shared_ref, grad_outs, refs = refs[0], refs[1 : 1 + g], refs[1 + g :]
        plain, turned = refs[:2]
        stages, shared_low, sems = refs[2 : 2 + g], refs[2 + g], refs[3 + g]
        writes = Writes(sems.at[pl.ds(3 * g, len(blocks_of(pieces)))])
        turn(x_ref[...], table, plain, turned)

        @pl.loop(0, 3)
        def _(i):
            at = pl.multiple_of(i * width, width)
            store_grad(turned, dqkv_ref[:, pl.ds(at, width)], stages, at)
            start_all(grad_copies(stages, grad_outs, at, width, sems, g * i))

        shared_ref[...] = jnp.zeros_like(shared_ref)
        shared_ref[0:1, :] = total(dqkv_ref[...].astype(F32))
        if g > 1:
            shared_low[...] = shared_ref[...].astype(BF16)
            for out in grad_outs:
                for r in range(out.shape[0]):
                    writes.start(shared_low, out.at[r, pl.ds(block_rows(pieces), SHARED)])
        for i in range(3):
            wait_all(grad_copies(stages, grad_outs, i * width, width, sems, g * i))
        writes.finish()

    return call(
        body,
        "project_grads",
        7,
        [like((SHARED, 3 * width), F32)] + grads,
        [x, dqkv],
        table,
        [],
        turn_scratch(pieces, rows)
        + stage_scratch(pieces, 3 * width)
        + [
            pltpu.VMEM((SHARED, 3 * width), BF16),
            pltpu.SemaphoreType.DMA((3 * g + len(blocks_of(pieces)),)),
        ],
        far=g,
    )


def at_column(values, rows, width, column):
    return lax.dynamic_update_slice(jnp.zeros((rows, width), values.dtype), values, (0, column))


def small_block(row_params, expand_bias, mine, depth):
    high = lax.reduce_precision(row_params, 8, 7)
    column = (mine * N_MP + depth) * row_params.shape[1]
    high_low = [
        at_column(part.astype(BF16), 6, WIDTH, column) for part in (high, row_params - high)
    ]
    bias = at_column(expand_bias, 2, 2 * WIDTH, mine * expand_bias.shape[1])
    return jnp.concatenate([jnp.concatenate(high_low, axis=1), bias])


def key_bias(length_long, length_short, block, core, depth):
    lengths = jnp.concatenate([length_long, length_short])
    other = core_swap(lengths)
    longs = jnp.where(core == 0, jnp.stack([lengths[0], other[0]]), jnp.stack([other[0], lengths[0]]))
    length = jnp.concatenate([longs, lengths[1:]])[depth]
    is_long = depth < 2
    place = lax.broadcasted_iota(jnp.int32, (1, 2 * N_MP * block), 1)
    row = place % (N_MP * block)
    is_own = place < N_MP * block
    source = (row // block) ^ depth
    whose = jnp.where(is_own, core, 1 - core)
    frame = row % block + jnp.where(is_long, (2 * source + whose) * block, source * block)
    counted = (frame < length) & (is_own | is_long)
    return jnp.where(counted, 0.0, NEG_FILL).astype(F32)


def on_device(
    frames_long,
    frames_short,
    length_long,
    length_short,
    input_proj,
    output_proj,
    expand_weight,
    shrink_weight,
    head_bias,
    expand_bias,
    row_params,
    cotangent_long,
    cotangent_short,
):
    mine = lax.axis_index("dp")
    depth = lax.axis_index("mp")
    n_dp = lax.axis_size("dp")
    fast = n_dp == 8
    core = mine % 2
    block = frames_short.shape[1]
    shard, group = input_proj.shape[1:]
    units = expand_weight.shape[1]
    width = group * N_MP
    hidden = units * N_MP
    table = block_table(mine, n_dp)

    joined = jnp.concatenate(
        [input_proj[0], input_proj[1], input_proj[2], output_proj.T], axis=1
    )
    heads = at_column(head_bias[:, 0], SMALL, WIDTH, mine * head_bias.shape[2])
    attn_parts = mp_gather(jnp.concatenate([joined, heads]))
    x_blocks = clip_blocks(frames_long[0], frames_short, core)
    cot_blocks = clip_blocks(cotangent_long[0], cotangent_short, core)
    bias = key_bias(length_long, length_short, block, core, depth)
    feed_shard = jnp.concatenate(
        [
            jnp.concatenate([expand_weight, shrink_weight.T], axis=1),
            small_block(row_params, expand_bias, mine, depth),
        ]
    )
    *attn_parts, feed_shard, bias, x_blocks, cot_blocks = tie(
        *attn_parts, feed_shard, bias, x_blocks, cot_blocks
    )
    order = [p[:shard, i * group : (i + 1) * group] for i in range(4) for p in attn_parts]
    attn_slab = jnp.concatenate([to_slab(order), to_slab([p[shard:] for p in attn_parts])])
    feed_parts = mp_gather(feed_shard)
    feed_order = [p[:, i * units : (i + 1) * units] for i in range(2) for p in feed_parts]
    if fast:
        attn_p = [attn_slab] + [dp_swap(attn_slab, to) for to in (early, late, across)]
        x_pieces = clip_pieces(x_blocks, depth)
        attn_p += [core_swap(piece) for piece in attn_p]
        both = tie(*attn_p, *x_pieces, *feed_order)
        attn_p, x_pieces, feed_order = both[:8], both[8:12], both[12:]
        feed_slab = to_slab(feed_order)
        feed_one = dp_swap(feed_slab, early)
        feed_two = dp_swap(feed_slab, late)
        x_parts = [x_pieces[0]] + [mp_swap(x_pieces[i], i) for i in range(1, N_MP)]
        *x_parts, cot_blocks, own_slab = tie(*x_parts, cot_blocks, feed_slab)
        heads = sum(p[shard:].astype(F32) for p in attn_p)
    else:
        x_parts = to_clips(x_blocks, depth)
        gather = lambda slab: lax.all_gather(slab, "dp", axis=0)
        whole = gather(attn_slab)
        heads = jnp.sum(whole[:, shard:].astype(F32), axis=0)
        attn_p = [whole[:, :shard].reshape(width, 4 * width)]
        whole = gather(to_slab(feed_order))
        small = jnp.sum(whole[:, shard:].astype(F32), axis=0)
        feed_p = [whole[:, :shard].reshape(width, 2 * hidden)]
    cot_parts = to_clips(cot_blocks, depth)
    heads = jnp.concatenate(
        [heads[:2, i * width : i * width + group] for i in range(N_MP)], axis=1
    )
    head_row = jnp.concatenate([heads[:1], jnp.zeros_like(heads[:1]), heads[1:]], axis=1)

    x, qkv, kv = project(x_parts, head_row, table, attn_p)
    if fast:
        kv, feed_one, feed_two, cot_parts[3], own_slab = tie(
            kv, feed_one, feed_two, cot_parts[3], core_swap(own_slab)
        )
    kv_other = core_swap(kv)
    if fast:
        feed_three = dp_swap(feed_one, late)
        feed_p = [feed_slab, feed_one, feed_two]
        backs = [own_slab] + [core_swap(piece) for piece in feed_p[1:]]
    mixed, lse = attend(qkv, kv_other, bias)
    if fast:
        mixed, feed_three, *both = tie(mixed, feed_three, *backs, *cot_parts)
        backs, cot_parts = both[:3], both[3:]
        feed_p = feed_p + [feed_three] + backs + [core_swap(feed_three)]
        smalls, small_row = feed_p, shard
    else:
        smalls, small_row = [small.astype(BF16)], 0
    outs = feed(x, mixed, cot_parts, smalls, small_row, table, attn_p, feed_p)
    mid_shared, result, (da, do), grads = outs[0], list(outs[1:5]), outs[5:7], outs[7:]
    g_down, g_mid = grads[: len(grads) // 2], grads[len(grads) // 2 :]

    def by_group_of(value, sizes):
        starts = [N_MP * sum(sizes[:i]) for i in range(len(sizes))]
        return [
            jnp.concatenate(
                [value[:, a + j * n : a + (j + 1) * n] for a, n in zip(starts, sizes)], axis=1
            )
            for j in range(N_MP)
        ]

    def last_sum(terms):
        return sum(term[0].astype(F32) for term in terms)

    result_parts = from_clips(result)
    if fast:
        b_down, b_mid = core_swap(g_down[1]), core_swap(g_mid[1])
    pairs = width // LANES
    first = pairs // 2
    dq_a, own_a, other_a = attend_back(qkv, kv_other, bias, mixed, lse, do, 0, first)
    if fast:
        other_a, b_down, b_mid, result_parts[3] = tie(other_a, b_down, b_mid, result_parts[3])
        t_down = [g_down[0], b_down]
        a_down = goes_on(t_down)
        do, a_down = tie(do, a_down)
        b_down = dp_swap(a_down, late)
        t_mid = [g_mid[0], b_mid]
        a_mid = goes_on(t_mid)
        do, a_mid = tie(do, a_mid)
        b_mid = dp_swap(a_mid, late)
    back_a = core_swap(other_a)
    dq_b, own_b, other_b = attend_back(
        qkv, kv_other, bias, mixed, lse, do, first, pairs - first
    )
    if fast:
        other_b, back_a, *result_parts = tie(other_b, back_a, *result_parts)
    back_b = core_swap(other_b)
    parts = [(dq_a, own_a, back_a), (dq_b, own_b, back_b)]
    *frames_grad, dqkv = project_back(da, parts, table, attn_p)
    grad_parts = from_clips(frames_grad)
    if fast:
        dqkv, b_down, b_mid = tie(dqkv, b_down, b_mid)
        t_down, t_mid = stays(t_down, b_down), stays(t_mid, b_mid)
        a_down, a_mid = goes_on(t_down), goes_on(t_mid)
        dqkv, a_down, a_mid = tie(dqkv, a_down, a_mid)
        b_down = dp_swap(a_down, early)
        b_mid = dp_swap(a_mid, early)
    attn_shared, *g_attn = project_grads(x, dqkv, table, attn_p)
    if fast:
        both = tie(*g_attn, b_down, b_mid, *grad_parts)
        g_attn, b_down, b_mid, grad_parts = both[:2], both[2], both[3], both[4:]
        b_attn = core_swap(g_attn[1])
        s_down = by_group_of(last_sum(stays(t_down, b_down)), [units])
        t_attn = [g_attn[0], b_attn]
        a_attn = goes_on(t_attn)
        a_attn, b_mid, *s_down = tie(a_attn, b_mid, *s_down)
        b_attn = dp_swap(a_attn, late)
        z_down = mp_away(s_down)
        s_mid = by_group_of(last_sum(stays(t_mid, b_mid)), [units, group])
        b_attn, *z_down = tie(b_attn, *z_down)
        t_attn = stays(t_attn, b_attn)
        a_attn = goes_on(t_attn)
        z_mid = mp_away(s_mid)
        b_attn, *both = tie(dp_swap(a_attn, early), *z_mid, *result_parts)
        z_mid, result_parts = both[: N_MP - 1], both[N_MP - 1 :]
        s_attn = last_sum(stays(t_attn, b_attn))
    else:
        scatter = lambda g: lax.psum_scatter(g[0][0], "dp", scatter_dimension=0, tiled=True)
        s_down = by_group_of(scatter(g_down), [units])
        z_down = mp_away(s_down)
        s_mid = jnp.concatenate([scatter(g_mid), lax.psum(mid_shared, "dp")])
        s_mid = by_group_of(s_mid, [units, group])
        z_mid = mp_away(s_mid)
        s_attn = jnp.concatenate([scatter(g_attn), lax.psum(attn_shared, "dp")])
    s_attn = by_group_of(s_attn, [group] * 3)
    grad_long, grad_short = frames_of(grad_parts, core, depth)
    result_long, result_short = frames_of(result_parts, core, depth)
    attn_share = mp_total(s_attn[0], mp_away(s_attn))
    down_share = mp_total(s_down[0], z_down).T
    mid_share = mp_total(s_mid[0], z_mid)
    up_share = mid_share[:shard, :units]
    output_share = mid_share[:shard, units:].T
    input_share = jnp.stack(
        [attn_share[:shard, i * group : (i + 1) * group] for i in range(3)]
    )
    up_cols, head_cols, row_cols = units // n_dp, group // n_dp, width // (n_dp * N_MP)
    rank = mine * N_MP + depth
    up_b_share = lax.dynamic_slice(mid_share, (shard, mine * up_cols), (1, up_cols))
    row_share = lax.dynamic_slice(mid_share, (shard + 1, rank * row_cols), (6, row_cols))
    head_share = jnp.stack(
        [
            lax.dynamic_slice(attn_share, (shard, at + mine * head_cols), (1, head_cols))
            for at in (0, 2 * group)
        ]
    )
    return (
        result_long,
        result_short,
        grad_long.astype(F32),
        grad_short.astype(F32),
        input_share,
        output_share,
        up_share,
        down_share,
        head_share,
        up_b_share,
        row_share,
    )


def solution(mesh):
    return jax.shard_map(
        on_device,
        mesh=mesh,
        in_specs=(
            P("dp", "mp", None),
            P("dp", "mp", None),
            P("dp"),
            P("dp"),
            P(None, "dp", "mp"),
            P("mp", "dp"),
            P("dp", "mp"),
            P("mp", "dp"),
            P(None, "mp", "dp"),
            P("mp", "dp"),
            P(None, ("dp", "mp")),
            P("dp", "mp", None),
            P("dp", "mp", None),
        ),
        out_specs=(
            P("dp", "mp", None),
            P("dp", "mp", None),
            P("dp", "mp", None),
            P("dp", "mp", None),
            P(None, "dp", "mp"),
            P("mp", "dp"),
            P("dp", "mp"),
            P("mp", "dp"),
            P(None, "mp", "dp"),
            P("mp", "dp"),
            P(None, ("dp", "mp")),
        ),
        check_vma=False,
    )
```
